32 devices in a mesh: dp: 8 (over y, x, core), seq: 4 (over z).
Axes of the slice: x: 2, y: 2, z: 4, core: 2. Of those that a mesh axis runs over, the one named last changes fastest.
Arguments:
- tokens: bfloat16 [16, 1024, 1024], P('dp', 'seq'), may hold values from -6 to 6
- cotangent: bfloat16 [16, 1024, 1024], P('dp', 'seq'), may hold values from -6 to 6
- species_index: int32 [16], P('dp'), may hold values from 0 to 849
- species_count: int32 [850], replicated, may hold values from 100 to 1599
- loss_weight: float32 [850], replicated, may hold values from 0.25 to 4
- query_weight: bfloat16 [1024, 1024], P(('dp', 'seq')), may hold values from -0.1875 to 0.1875
- key_weight: bfloat16 [1024, 1024], P(('dp', 'seq')), may hold values from -0.1875 to 0.1875
- value_weight: bfloat16 [1024, 1024], P(('dp', 'seq')), may hold values from -0.1875 to 0.1875
- out_weight: bfloat16 [1024, 1024], P(('dp', 'seq')), may hold values from -1.5 to 1.5
- gate_weight: bfloat16 [1024, 4096], P(('dp', 'seq')), may hold values from -0.1875 to 0.1875
- up_weight: bfloat16 [1024, 4096], P(('dp', 'seq')), may hold values from -0.1875 to 0.1875
- down_weight: bfloat16 [4096, 1024], P(('dp', 'seq')), may hold values from -0.09375 to 0.09375
- mixer_gain: bfloat16 [1024], P(('dp', 'seq')), may hold values from 0.5 to 1.5
- mixer_shift: bfloat16 [1024], P(('dp', 'seq')), may hold values from -1.5 to 1.5
- feeder_gain: bfloat16 [1024], P(('dp', 'seq')), may hold values from 0.5 to 1.5
- feeder_shift: bfloat16 [1024], P(('dp', 'seq')), may hold values from -1.5 to 1.5
Outputs:
- output: bfloat16 [16, 1024, 1024], P('dp', 'seq')
- input_gradient: float32 [16, 1024, 1024], P('dp', 'seq')
- query_gradient: float32 [1024, 1024], P(('dp', 'seq'))
- key_gradient: float32 [1024, 1024], P(('dp', 'seq'))
- value_gradient: float32 [1024, 1024], P(('dp', 'seq'))
- out_gradient: float32 [1024, 1024], P(('dp', 'seq'))
- gate_gradient: float32 [1024, 4096], P(('dp', 'seq'))
- up_gradient: float32 [1024, 4096], P(('dp', 'seq'))
- down_gradient: float32 [4096, 1024], P(('dp', 'seq'))
- mixer_gain_gradient: float32 [1024], P(('dp', 'seq'))
- mixer_shift_gradient: float32 [1024], P(('dp', 'seq'))
- feeder_gain_gradient: float32 [1024], P(('dp', 'seq'))
- feeder_shift_gradient: float32 [1024], P(('dp', 'seq'))
The draws below stay inside these ranges and needn't reach their ends.
All inputs are finite; a program needn't handle non-finite values.
Results may differ from the reference program's by a relative error of at most 0.017.
Values may be sent and summed in bfloat16 or wider, within the bound.
A program may use at most 256 MiB of HBM per device.

```python
import math
import jax
import jax.numpy as jnp
import numpy as np
from jax import lax

D = 1024
HEADS = 16
HD = 64
FF = 4096
SPECIES = 850
WINDOWS = 16
LENGTH = 1024


def plant(drawn, key, least, top_value):
    dims = drawn.shape
    place = [jax.random.randint(jax.random.fold_in(key, axis), (), 0, dims[axis]) for axis in range(len(dims))]
    drawn = drawn.at[tuple(place)].set(least)
    longest = dims.index(max(dims))
    place[longest] = (place[longest] + 1) % dims[longest]
    return drawn.at[tuple(place)].set(top_value)


def steps_of(rng, shape, cuts, low, largest):
    def one(axis_at, blocks):
        heights = jax.random.uniform(jax.random.fold_in(jax.random.fold_in(rng, 6), axis_at), (blocks,), jnp.float32, low / len(cuts), largest / len(cuts))
        return jnp.repeat(jnp.exp(heights), shape[axis_at] // blocks).reshape((-1,) + (1,) * (len(shape) - axis_at - 1))

    level = one(*cuts[0])
    for cut in cuts[1:]:
        level = level * one(*cut)
    return level


def cumulative_ranks(count, slope):
    portions = [(1 << 20) // math.isqrt(rank ** slope) + 1 for rank in range(1, count + 1)]
    spread = 1 + sum(portions) // (1 << 30)
    return np.cumsum(np.array([max(1, weight // spread) for weight in portions]))


def ranked_ids(stream_key, shape, number_of, lean):
    listing = cumulative_ranks(number_of, lean)
    ticket = jax.random.randint(jax.random.fold_in(stream_key, 1), shape, 0, int(listing[number_of - 1]))
    rank = jnp.searchsorted(jnp.asarray(listing, jnp.int32), ticket, side="right")
    return jax.random.permutation(jax.random.fold_in(stream_key, 2), number_of)[rank].astype(jnp.int32)


def scatter_about(stream_key, dims, deviation, reach, shards=(), held_as=jnp.bfloat16):
    entries = jax.random.normal(stream_key, dims, jnp.float32) * deviation
    if len(shards) > 0:
        entries = steps_of(stream_key, dims, shards, -0.22, 0.18) * entries
    return jnp.clip(entries, min=-reach, max=reach).astype(held_as)


def setup_inputs(seed: int = 0) -> dict:
    arg_keys = jax.random.split(jax.random.key(seed), 17)
    tokens = scatter_about(arg_keys[0], (WINDOWS, LENGTH, D), 1.0, 6.0, ((0, 8), (1, 4)))
    cotangent = scatter_about(arg_keys[1], (WINDOWS, LENGTH, D), 1.0, 6.0, ((0, 8), (1, 4)))
    species_index = plant(ranked_ids(arg_keys[2], (WINDOWS,), SPECIES, 2), jax.random.fold_in(arg_keys[2], 3), 0, SPECIES - 1).astype(jnp.int32)
    species_count = plant(jax.random.randint(arg_keys[3], (SPECIES,), 100, 1600), jax.random.fold_in(arg_keys[3], 1), 100, 1599).astype(jnp.int32)
    loss_weight = jnp.clip(jnp.exp(jax.random.uniform(arg_keys[4], (SPECIES,), jnp.float32, math.log(0.25), math.log(4.0))), 0.25, 4.0)
    query_weight = scatter_about(arg_keys[5], (D, D), D ** -0.5, 0.1875, ((0, 32),))
    key_weight = scatter_about(arg_keys[6], (D, D), D ** -0.5, 0.1875, ((0, 32),))
    value_weight = scatter_about(arg_keys[7], (D, D), D ** -0.5, 0.1875, ((0, 32),))
    out_weight = scatter_about(arg_keys[8], (D, D), (D * 16 // LENGTH) ** -0.5, 1.5, ((0, 32),))
    gate_weight = scatter_about(arg_keys[9], (D, FF), D ** -0.5, 0.1875, ((0, 32),))
    up_weight = scatter_about(arg_keys[10], (D, FF), D ** -0.5, 0.1875, ((0, 32),))
    down_weight = scatter_about(arg_keys[11], (FF, D), FF ** -0.5, 0.09375, ((0, 32),))
    mixer_gain = jnp.clip(1.0 + 0.1 * jax.random.normal(arg_keys[12], (D,), jnp.float32), 0.5, 1.5).astype(jnp.bfloat16)
    mixer_shift = scatter_about(arg_keys[13], (D,), 0.3, 1.5, ((0, 32),))
    feeder_gain = jnp.clip(1.0 + 0.1 * jax.random.normal(arg_keys[14], (D,), jnp.float32), 0.5, 1.5).astype(jnp.bfloat16)
    feeder_shift = scatter_about(arg_keys[15], (D,), 0.3, 1.5, ((0, 32),))
    return dict(tokens=tokens, cotangent=cotangent, species_index=species_index, species_count=species_count, loss_weight=loss_weight, query_weight=query_weight, key_weight=key_weight, value_weight=value_weight, out_weight=out_weight, gate_weight=gate_weight, up_weight=up_weight, down_weight=down_weight, mixer_gain=mixer_gain, mixer_shift=mixer_shift, feeder_gain=feeder_gain, feeder_shift=feeder_shift)


@jax.custom_vjp
def low(v):
    return lax.optimization_barrier(v.astype(jnp.bfloat16)).astype(jnp.float32)

@jax.custom_vjp
def low_back(v):
    return v

def low_keep(v):
    return (low(v), None)

def low_pass(kept, grad):
    return (grad,)

def back_keep(v):
    return (v, None)

def back_low(kept, grad):
    return (low(grad),)
low.defvjp(low_keep, low_pass)
low_back.defvjp(back_keep, back_low)

def matmul(left, right):
    return jnp.dot(left, right, precision=lax.Precision.HIGHEST, preferred_element_type=jnp.float32)

def layer_norm(values, gain, shift):
    center = lax.optimization_barrier(jnp.mean(values, axis=-1, keepdims=True))
    centered = values - center
    variance = lax.optimization_barrier(jnp.mean(centered * centered, axis=-1, keepdims=True))
    return centered * lax.rsqrt(variance + 1e-05) * gain + shift

def rotate(values, cosine, sine):
    half = HD // 2
    first = values[..., :half]
    second = values[..., half:]
    return jnp.concatenate([first * cosine - second * sine, second * cosine + first * sine], axis=-1)

def attend_head(query_head, key_head, value_head):
    scores = low_back(matmul(query_head, key_head.T) * HD ** (-0.5))
    peak = lax.optimization_barrier(jnp.max(scores, axis=-1, keepdims=True))
    raised = jnp.exp(scores - peak)
    probs = low(raised / lax.optimization_barrier(jnp.sum(raised, axis=-1, keepdims=True)))
    return matmul(probs, value_head)

def forward(inputs, params):
    wq, wk, wv, wo, wg, wu, wd, gain_one, shift_one, gain_two, shift_two = params
    length = inputs.shape[0]
    half = HD // 2
    positions = jnp.arange(length, dtype=jnp.float32)
    freqs = 10000.0 ** (-2.0 * jnp.arange(half, dtype=jnp.float32) / HD)
    angle = positions[:, None] * freqs[None, :]
    cosine = jnp.cos(angle)[:, None, :]
    sine = jnp.sin(angle)[:, None, :]
    norm_one = low(layer_norm(inputs, gain_one, shift_one))
    queries = low(rotate(low_back(matmul(norm_one, wq)).reshape(length, HEADS, HD), cosine, sine))
    keys = low(rotate(low_back(matmul(norm_one, wk)).reshape(length, HEADS, HD), cosine, sine))
    values = low(low_back(matmul(norm_one, wv))).reshape(length, HEADS, HD)
    head_fn = jax.checkpoint(attend_head)
    heads_out = lax.map(lambda trio: head_fn(trio[0], trio[1], trio[2]), (queries.transpose(1, 0, 2), keys.transpose(1, 0, 2), values.transpose(1, 0, 2)))
    attended = low(low_back(heads_out.transpose(1, 0, 2).reshape(length, HEADS * HD)))
    middle = inputs + low_back(matmul(attended, wo))
    norm_two = low(layer_norm(middle, gain_two, shift_two))
    gate = low_back(matmul(norm_two, wg))
    upward = low_back(matmul(norm_two, wu))
    hidden = low(gate * jax.nn.sigmoid(gate) * upward)
    return middle + low_back(matmul(hidden, wd))

def reference(tokens, cotangent, species_index, species_count, loss_weight, query_weight, key_weight, value_weight, out_weight, gate_weight, up_weight, down_weight, mixer_gain, mixer_shift, feeder_gain, feeder_shift):
    params = tuple((w.astype(jnp.float32) for w in (query_weight, key_weight, value_weight, out_weight, gate_weight, up_weight, down_weight, mixer_gain, mixer_shift, feeder_gain, feeder_shift)))
    table = loss_weight * lax.rsqrt(species_count.astype(jnp.float32) / 400.0)
    factor = table[species_index.astype(jnp.int32)]

    def window_step(totals, item):
        window, tangent, weight = item
        result, pullback = jax.vjp(forward, window.astype(jnp.float32), params)
        input_grad, param_grads = pullback(weight * tangent.astype(jnp.float32))
        totals = tuple((a + b for a, b in zip(totals, param_grads)))
        return (totals, (result.astype(jnp.bfloat16), input_grad))
    zeros = tuple((jnp.zeros(p.shape, jnp.float32) for p in params))
    totals, (outputs, input_grads) = lax.scan(window_step, zeros, (tokens, cotangent, factor))
    return (outputs, input_grads, totals[0], totals[1], totals[2], totals[3], totals[4], totals[5], totals[6], totals[7], totals[8], totals[9], totals[10])
```

```python
import jax
import jax.numpy as jnp
from jax import lax
from jax.experimental import pallas as pl
from jax.experimental.pallas import tpu as pltpu
from jax.sharding import PartitionSpec as P

HEADS = 16
HD = 64
MESH = pl.DeviceIdType.MESH
BF = jnp.bfloat16
F32 = jnp.float32
ANY = pl.BlockSpec(memory_space=pl.ANY)
VM = pl.BlockSpec(memory_space=pltpu.VMEM)
VMEM_BYTES = 60 << 20


def place():
    dp, z = lax.axis_index("dp"), lax.axis_index("seq")
    return dp // 4, (dp // 2) % 2, dp % 2, z


def dev(y, x, c, z):
    return ((y * 2 + x) * 2 + c, z)


def both(a, b):
    return jnp.logical_and(a, b)


def greet(y, x, c, z):
    barrier = pltpu.get_barrier_semaphore()
    peers = [dev(y, 1 - x, c, z), dev(1 - y, x, c, z), dev(y, x, 1 - c, z)]
    for k in (1, 2, 3):
        peers += [dev(y, x, c, (z + k) % 4), dev(y, x, 1 - c, (z + k) % 4)]
    for p in peers:
        pl.semaphore_signal(barrier, inc=1, device_id=p, device_id_type=MESH)
    pl.semaphore_wait(barrier, len(peers))


class Links:
    def __init__(self, send, recv, local):
        self.send, self.recv, self.local = send, recv, local
        self.n = 0
        self.m = 0
        self.open = []

    def take(self, count):
        self.n += count
        return self.n - count

    def copy(self, src, dst, device, send, recv):
        return pltpu.make_async_remote_copy(
            src_ref=src, dst_ref=dst, send_sem=self.send.at[send], recv_sem=self.recv.at[recv],
            device_id=device, device_id_type=MESH)

    def go(self, c, ok=None):
        if ok is None:
            c.start()
        else:
            pl.when(ok)(c.start)
        self.open.append((c, ok))
        return c

    def to(self, src, dst, device):
        i = self.take(1)
        return self.go(self.copy(src, dst, device, i, i))

    def here(self, src, dst):
        self.m += 1
        c = pltpu.make_async_copy(src, dst, self.local.at[self.m - 1])
        c.start()
        return c

    def drain(self):
        for c, ok in self.open:
            if ok is None:
                c.wait_send()
            else:
                pl.when(ok)(c.wait_send)
        self.open = []


def near(z):
    return [(z + side * d, both(z + side * d >= 0, z + side * d <= 3), side)
            for d in (1, 2, 3) for side in (-1, 1)]


class Chain:
    def __init__(self, links, me, at, yy, xx):
        self.links, self.me, self.at, self.yy, self.xx = links, me, at, yy, xx
        self.recv, self.send = links.take(4), links.take(8)

    def copy(self, zz, target, slot):
        y, x, c, _ = self.me
        p = self.at(self.yy, self.xx, zz)
        return self.links.copy(p, p, dev(y, x, c, target), self.send + slot, self.recv + zz)

    def own(self):
        z = self.me[3]
        self.links.go(self.copy(z, z - 1, 0), z > 0)
        self.links.go(self.copy(z, z + 1, 1), z < 3)

    def arrive(self, n, zz, ok, side, then):
        z = self.me[3]

        @pl.when(ok)
        def _():
            self.copy(zz, z, 0).wait_recv()
        self.links.go(self.copy(zz, z - side, 2 + n), both(ok, z < 3 if side < 0 else z > 0))
        then(zz, ok)


class Pair:
    def __init__(self, links, at, yy, xx, target):
        self.links, self.at, self.yy, self.xx, self.target = links, at, yy, xx, target
        self.base = links.take(4)

    def copy(self, zz):
        p = self.at(self.yy, self.xx, zz)
        return self.links.copy(p, p, self.target, self.base + zz, self.base + zz)

    def go(self, zz, ok=None):
        self.links.go(self.copy(zz), ok)

    def wait(self, zz, ok=None):
        c = self.copy(zz)
        if ok is None:
            c.wait_recv()
        else:
            pl.when(ok)(c.wait_recv)


def spread(links, at, me, route):
    y, x, c, z = me
    to_x, to_y = dev(y, 1 - x, c, z), dev(1 - y, x, c, z)
    order = near(z)
    if route == 0:
        chain = Chain(links, me, at, y, x)
        py, px, px2 = Pair(links, at, y, x, to_y), Pair(links, at, y, x, to_x), Pair(links, at, 1 - y, x, to_x)

        def start():
            chain.own()
            py.go(z)
            px.go(z)

        def first():
            py.wait(z)
            px2.go(z)

            def then(zz, ok):
                py.go(zz, ok)
                px.go(zz, ok)
            for n, (zz, ok, side) in enumerate(order):
                chain.arrive(n, zz, ok, side, then)

        def second():
            for zz, ok, side in order:
                py.wait(zz, ok)
                px2.go(zz, ok)

        def last():
            for p in (px, px2):
                for zz in range(4):
                    p.wait(zz)
    else:
        px = Pair(links, at, y, x, to_x)
        ch0, ch1 = Chain(links, me, at, y, x), Chain(links, me, at, y, 1 - x)
        py, py2 = Pair(links, at, y, x, to_y), Pair(links, at, y, 1 - x, to_y)

        def start():
            px.go(z)
            ch0.own()
            py.go(z)

        def first():
            px.wait(z)
            ch1.own()
            py2.go(z)
            for n, (zz, ok, side) in enumerate(order):
                ch0.arrive(n, zz, ok, side, py.go)

        def second():
            for n, (zz, ok, side) in enumerate(order):
                ch1.arrive(n, zz, ok, side, py2.go)

        def last():
            for p in (py, py2):
                for zz in range(4):
                    p.wait(zz)
    return start, first, second, last


class Incoming:
    def __init__(self, links, me, src, mid, dst):
        self.links, self.me, self.src, self.mid, self.dst = links, me, src, mid, dst
        y, x, c, z = me
        self.swap = [links.to(src.at[i, pl.ds((1 - c) * 128, 128)], mid.at[2 * c + i], dev(y, x, 1 - c, z))
                     for i in (0, 1)]
        self.base = links.take(4)

    def send(self):
        y, x, c, z = self.me
        for i in (0, 1):
            self.swap[i].wait_recv()
        self.kept = []
        for w in range(4):
            mine = c == w // 2
            for ok, s in ((mine, self.src.at[w % 2, pl.ds(c * 128, 128)]), (jnp.logical_not(mine), self.mid.at[w])):
                d = self.dst.at[0, z]
                self.links.go(self.links.copy(s, d, dev(y, x, c, w), self.base + w, self.base + z), both(ok, z != w))
                local = pltpu.make_async_copy(s, d, self.links.local.at[self.links.m])
                here = both(ok, z == w)
                pl.when(here)(local.start)
                self.kept.append((local, here))
        self.links.m += 1

    def arrive(self):
        y, x, c, z = self.me
        for local, here in self.kept:
            pl.when(here)(local.wait)
        for zz in range(4):
            d = self.dst.at[0, zz]
            pl.when(zz != z)(self.links.copy(d, d, dev(y, x, c, zz), self.base, self.base + zz).wait_recv)
        self.pair = self.links.to(self.dst.at[0], self.dst.at[1], dev(y, x, 1 - c, z))

    def finish(self):
        self.pair.wait_recv()


SPLIT = 1152


def gather_kernel(tok, cot, own_qkv, oth_qkv, own_gu, oth_gu, wo, wd, gp,
                  oqkv, ogu, oo, od, xw, cw, gains, tmid, cmid, send, recv, local):
    me = y, x, c, z = place()
    yx = y * 2 + x
    partner = dev(y, x, 1 - c, z)
    greet(y, x, c, z)
    links = Links(send, recv, local)
    a = links.to(oth_qkv, oqkv.at[yx, c, z], partner)
    tin = Incoming(links, me, tok, tmid, xw)
    b = links.to(oth_gu, ogu.at[yx, c, z], partner)
    cin = Incoming(links, me, cot, cmid, cw)
    loc = [links.here(own_qkv, oqkv.at[yx, c, z]), links.here(own_gu, ogu.at[yx, c, z]),
           links.here(wo, oo.at[yx, z]), links.here(wd, od.at[yx, z]), links.here(gp, gains.at[yx, c, z])]
    tin.send()
    for q in loc:
        q.wait()
    a.wait_recv()
    b.wait_recv()
    parts = []

    def add(at, route):
        parts.append(spread(links, at, me, route))
    for r in (0, 1):
        add(lambda y, x, z, r=r: oqkv.at[y * 2 + x, r, z], r)
        add(lambda y, x, z, r=r: oo.at[y * 2 + x, z, pl.ds(16 * r, 16)], r)
    add(lambda y, x, z: gains.at[y * 2 + x, c, z], 0)
    add(lambda y, x, z: ogu.at[y * 2 + x, 0, z], 0)
    add(lambda y, x, z: ogu.at[y * 2 + x, 1, z, :, pl.ds(0, SPLIT)], 0)
    add(lambda y, x, z: ogu.at[y * 2 + x, 1, z, :, pl.ds(SPLIT, 4096 - SPLIT)], 1)
    add(lambda y, x, z: od.at[y * 2 + x, z, pl.ds(0, 80)], 0)
    add(lambda y, x, z: od.at[y * 2 + x, z, pl.ds(80, 48)], 1)
    for s in parts:
        s[0]()
    for i, s in enumerate(parts):
        s[1]()
        if i == 3:
            tin.arrive()
    cin.send()
    for s in parts:
        s[2]()
    for s in parts:
        s[3]()
    cin.arrive()
    g = links.to(gains.at[:, c], gains.at[:, c], partner)
    g.wait_recv()
    tin.finish()
    cin.finish()
    links.drain()


def gather(tok, cot, own_qkv, oth_qkv, own_gu, oth_gu, wo, wd, gp):
    return pl.pallas_call(
        gather_kernel,
        out_shape=(
            jax.ShapeDtypeStruct((4, 2, 4, 32, 1536), BF),
            jax.ShapeDtypeStruct((4, 2, 4, 32, 4096), BF),
            jax.ShapeDtypeStruct((4, 4, 32, 1024), BF),
            jax.ShapeDtypeStruct((4, 4, 128, 1024), BF),
            jax.ShapeDtypeStruct((2, 4, 128, 1024), BF),
            jax.ShapeDtypeStruct((2, 4, 128, 1024), BF),
            jax.ShapeDtypeStruct((4, 2, 4, 8, 128), F32),
        ),
        in_specs=[VM] * 9,
        out_specs=[ANY] * 7,
        scratch_shapes=[
            pltpu.VMEM((4, 128, 1024), BF),
            pltpu.VMEM((4, 128, 1024), BF),
            pltpu.SemaphoreType.DMA((400,)),
            pltpu.SemaphoreType.DMA((400,)),
            pltpu.SemaphoreType.DMA((8,)),
        ],
        compiler_params=pltpu.CompilerParams(collective_id=0, has_side_effects=True, vmem_limit_bytes=VMEM_BYTES),
    )(tok, cot, own_qkv, oth_qkv, own_gu, oth_gu, wo, wd, gp)


def add_into(dst, a, b):
    def body(i, _):
        dst[i] = (a[i].astype(F32) + b[i].astype(F32)).astype(dst.dtype)
        return 0
    lax.fori_loop(0, dst.shape[0], body, 0)


def reduce_shapes(rows, cols, route, dtype=BF):
    big = pltpu.VMEM((2, 4, rows, cols), dtype)
    if route == 0:
        return [big, big, pltpu.VMEM((4, rows, cols), dtype), pltpu.VMEM((3, rows, cols), dtype),
                pltpu.VMEM((rows, cols), F32)]
    return [big, big, pltpu.VMEM((2, 3, rows, cols), dtype), pltpu.VMEM((2, rows, cols), dtype),
            pltpu.VMEM((rows, cols), F32)]


def collect(links, at, me, route, bufs, deliver):
    y, x, c, z = me
    to_x, to_y = dev(y, 1 - x, c, z), dev(1 - y, x, c, z)
    zs = [(z + k) % 4 for k in range(4)]
    S = {}
    own, got, third, fourth, total = bufs
    if route == 0:
        def start():
            for n, yy in ((0, 1 - y), (1, y)):
                S["l", n] = links.here(at(yy, x), own.at[n])
                S["r", n] = links.to(at(yy, 1 - x), got.at[n], to_x)

        def first():
            S["l", 0].wait()
            S["r", 0].wait_recv()
            add_into(own.at[0], own.at[0], got.at[0])
            S["y"] = links.to(own.at[0], third, to_y)

        def second():
            S["l", 1].wait()
            S["r", 1].wait_recv()
            add_into(own.at[1], own.at[1], got.at[1])
            S["y"].wait_recv()
            add_into(own.at[1], own.at[1], third)
            for k in (1, 2, 3):
                S["z", k] = links.to(own.at[1, zs[k]], fourth.at[k - 1], dev(y, x, c, zs[k]))

        def last():
            for k in (1, 2, 3):
                S["z", k].wait_recv()
            total[...] = (own[1, z].astype(F32) + fourth[0].astype(F32)
                          + (fourth[1].astype(F32) + fourth[2].astype(F32)))
            deliver(total)
        return start, first, second, last

    def start():
        for n, xx in ((0, 1 - x), (1, x)):
            S["l", n] = links.here(at(y, xx), own.at[n])
            S["r", n] = links.to(at(1 - y, xx), got.at[n], to_y)

    def first():
        for n in (0, 1):
            S["l", n].wait()
            S["r", n].wait_recv()
            add_into(own.at[n], own.at[n], got.at[n])
            for k in (1, 2, 3):
                S["z", n, k] = links.to(own.at[n, zs[k]], third.at[n, k - 1], dev(y, x, c, zs[k]))

    def second():
        for k in (1, 2, 3):
            S["z", 0, k].wait_recv()
        fourth[0] = (own[0, z].astype(F32) + third[0, 0].astype(F32)
                     + (third[0, 1].astype(F32) + third[0, 2].astype(F32))).astype(fourth.dtype)
        S["x"] = links.to(fourth.at[0], fourth.at[1], to_x)

    def last():
        for k in (1, 2, 3):
            S["z", 1, k].wait_recv()
        S["x"].wait_recv()
        total[...] = (own[1, z].astype(F32) + third[1, 0].astype(F32)
                      + (third[1, 1].astype(F32) + third[1, 2].astype(F32)) + fourth[1].astype(F32))
        deliver(total)
    return start, first, second, last


class Outgoing:
    def __init__(self, links, me, src, dst):
        y, x, c, z = me
        self.links, self.me, self.dst = links, me, dst
        self.recv, self.sendn = links.take(4), links.take(4)
        self.kept = []
        links.m += 1
        for k in range(4):
            zz = (z + k) % 4
            s, d = src.at[zz], dst.at[z % 2, c]
            remote = links.copy(s, d, dev(y, x, z // 2, zz), self.sendn + k, self.recv + (z % 2) * 2 + c)
            if k == 0:
                local = pltpu.make_async_copy(s, d, links.local.at[links.m - 1])
                self.here = here = c == z // 2
                pl.when(here)(local.start)
                links.go(remote, jnp.logical_not(here))
                self.local = local
            else:
                links.go(remote)

    def finish(self):
        y, x, c, z = self.me
        pl.when(self.here)(self.local.wait)
        for i in (0, 1):
            for h in (0, 1):
                d = self.dst.at[i, h]
                mine = both(z == 2 * c + i, h == c)
                w = self.links.copy(d, d, dev(y, x, 1 - c, z), self.sendn, self.recv + 2 * i + h)
                pl.when(jnp.logical_not(mine))(w.wait_recv)


RSPLIT = 2048
PIECES = (
    ("gu", 0, 0, 32, 0, 4096, 0),
    ("gu", 1, 0, 32, 0, RSPLIT, 0),
    ("gu", 1, 0, 32, RSPLIT, 4096 - RSPLIT, 1),
    ("d", 0, 0, 96, 0, 1024, 0),
    ("d", 0, 96, 32, 0, 1024, 1),
    ("qkv", 0, 0, 32, 0, 1536, 0),
    ("qkv", 1, 0, 32, 0, 1536, 1),
    ("o", 0, 0, 32, 0, 1024, 0),
)


def reduce_kernel(dqkv, dgu, do, dd, gain_terms, out16, ig16, *rest):
    fqkv, fgu, fo, fd, fgain, out_w, ig_w = rest[:7]
    scratch = list(rest[7:])
    send, recv, local = scratch[-3:]
    gsum, ggot = scratch[-5:-3]
    me = y, x, c, z = place()
    partner = dev(y, x, 1 - c, z)
    greet(y, x, c, z)
    links = Links(send, recv, local)
    g1 = links.to(gain_terms.at[:, 1 - c], ggot, partner)
    g2 = links.here(gain_terms.at[:, c], gsum)
    arrays = {"qkv": (dqkv, fqkv), "gu": (dgu, fgu), "o": (do, fo), "d": (dd, fd)}
    work = []
    finals = []
    for name, part, row, rows, col, cols, route in PIECES:
        src, dst = arrays[name]
        bufs = [scratch.pop(0) for _ in range(5)]
        if name in ("qkv", "gu"):
            def at(yy, xx, src=src, part=part, col=col, cols=cols):
                return src.at[yy * 2 + xx, part, :, :, pl.ds(col, cols)]

            def deliver(total, dst=dst, part=part, col=col, cols=cols):
                d = dst.at[c, :, pl.ds(col, cols)]
                i, m = links.take(1), links.m
                links.m += 1
                remote = links.copy(total, d, partner, i, i)
                local = pltpu.make_async_copy(total, d, links.local.at[m])
                mine = c == part
                pl.when(mine)(local.start)
                links.go(remote, jnp.logical_not(mine))

                def finish():
                    pl.when(mine)(local.wait)
                    e = dst.at[1 - c, :, pl.ds(col, cols)]
                    pl.when(mine)(links.copy(e, e, partner, i, i).wait_recv)
                finals.append(finish)
        else:
            def at(yy, xx, src=src, row=row, rows=rows):
                return src.at[yy * 2 + xx, :, pl.ds(row, rows)]

            def deliver(total, dst=dst, row=row, rows=rows):
                finals.append(links.here(total, dst.at[pl.ds(row, rows)]).wait)
        work.append(collect(links, at, me, route, bufs, deliver))
    for w in work:
        w[0]()
    o1 = Outgoing(links, me, out16, out_w)
    o2 = Outgoing(links, me, ig16, ig_w)
    g1.wait_recv()
    g2.wait()
    gsum[...] += ggot[...]
    gb = [scratch.pop(0) for _ in range(5)]
    gw = collect(links, lambda yy, xx: gsum.at[yy * 2 + xx], me, 0, gb,
                 lambda total: finals.append(links.here(total, fgain).wait))
    gw[0]()
    work.insert(5, gw)
    for stage in (1, 2, 3):
        for w in work:
            w[stage]()
    for f in finals:
        f()
    o1.finish()
    o2.finish()
    links.drain()


def reduce(dqkv, dgu, do, dd, gain_terms, out16, ig16):
    scratch = []
    for name, part, row, rows, col, cols, route in PIECES:
        scratch += reduce_shapes(rows, cols, route)
    scratch += reduce_shapes(8, 128, 0, F32)
    return pl.pallas_call(
        reduce_kernel,
        out_shape=(
            jax.ShapeDtypeStruct((2, 32, 1536), F32),
            jax.ShapeDtypeStruct((2, 32, 4096), F32),
            jax.ShapeDtypeStruct((32, 1024), F32),
            jax.ShapeDtypeStruct((128, 1024), F32),
            jax.ShapeDtypeStruct((8, 128), F32),
            jax.ShapeDtypeStruct((2, 2, 128, 1024), BF),
            jax.ShapeDtypeStruct((2, 2, 128, 1024), BF),
        ),
        in_specs=[ANY] * 7,
        out_specs=[ANY] * 7,
        scratch_shapes=scratch + [
            pltpu.VMEM((4, 4, 8, 128), F32),
            pltpu.VMEM((4, 4, 8, 128), F32),
            pltpu.SemaphoreType.DMA((128,)),
            pltpu.SemaphoreType.DMA((128,)),
            pltpu.SemaphoreType.DMA((48,)),
        ],
        compiler_params=pltpu.CompilerParams(collective_id=1, has_side_effects=True, vmem_limit_bytes=VMEM_BYTES),
    )(dqkv.reshape(4, 2, 4, 32, 1536), dgu.reshape(4, 2, 4, 32, 4096), do.reshape(4, 4, 32, 1024),
      dd.reshape(4, 4, 128, 1024), gain_terms, out16, ig16)


def swap_halves(u):
    lane = lax.broadcasted_iota(jnp.int32, u.shape, 1) % HD
    return jnp.where(lane < HD // 2, pltpu.roll(u, 128 - HD // 2, 1), pltpu.roll(u, HD // 2, 1))


def head_mask(shape, h):
    lane = lax.broadcasted_iota(jnp.int32, shape, 1)
    return (lane < HD) if h == 0 else (lane >= HD)


def dot_t(a, b):
    return lax.dot_general(a, b, (((1,), (1,)), ((), ())), preferred_element_type=F32)


def project_kernel(x, gain, shift, w, cos, sin, n1, q, k, v):
    u = x[...].astype(F32)
    d = u - jnp.mean(u, axis=-1, keepdims=True)
    r = lax.rsqrt(jnp.mean(d * d, axis=-1, keepdims=True) + 1e-05)
    n = (d * r * gain[...] + shift[...]).astype(BF)
    n1[...] = n
    for g in range(4):
        for j, o in ((0, q), (1, k)):
            s = jnp.dot(n, w[:, pl.ds(512 * j + 128 * g, 128)], preferred_element_type=F32)
            o[:, pl.ds(128 * g, 128)] = (s * cos[...] + swap_halves(s) * sin[...]).astype(BF)
    v[...] = jnp.dot(n, w[:, pl.ds(1024, 512)], preferred_element_type=F32).astype(BF)


def project(x, gain, shift, w, cos, sin):
    rows = 256
    blk = lambda n: pl.BlockSpec((rows, n), lambda i: (i, 0))
    one = lambda a, b: pl.BlockSpec((a, b), lambda i: (0, 0))
    return pl.pallas_call(
        project_kernel,
        grid=(1024 // rows,),
        out_shape=(jax.ShapeDtypeStruct((1024, 1024), BF),) + (jax.ShapeDtypeStruct((1024, 512), BF),) * 3,
        in_specs=[blk(1024), one(1, 1024), one(1, 1024), one(1024, 1536), blk(128), blk(128)],
        out_specs=[blk(1024), blk(512), blk(512), blk(512)],
        compiler_params=pltpu.CompilerParams(vmem_limit_bytes=VMEM_BYTES),
    )(x, gain, shift, w, cos, sin)


def attend_kernel(q, k, v, o, lse):
    qs = q[...] * jnp.asarray(HD ** -0.5, BF)
    outs, logs = [], []
    for h in (0, 1):
        qh = jnp.where(head_mask(qs.shape, h), qs, jnp.zeros_like(qs))
        s = dot_t(qh, k[...])
        m = jnp.max(s, axis=-1, keepdims=True)
        e = jnp.exp(s - m)
        t = jnp.sum(e, axis=-1, keepdims=True)
        p = (e * (1.0 / t)).astype(BF)
        outs.append(jnp.dot(p, v[...], preferred_element_type=F32))
        logs.append(jnp.broadcast_to(m + jnp.log(t), qs.shape))
    keep = head_mask(qs.shape, 0)
    o[...] = jnp.where(keep, outs[0], outs[1]).astype(BF)
    lse[...] = jnp.where(keep, logs[0], logs[1])


def attend(q, k, v):
    rows = 256
    part = pl.BlockSpec((rows, 128), lambda g, i: (i, g))
    full = pl.BlockSpec((1024, 128), lambda g, i: (0, g))
    return pl.pallas_call(
        attend_kernel,
        grid=(4, 1024 // rows),
        out_shape=(jax.ShapeDtypeStruct((1024, 512), BF), jax.ShapeDtypeStruct((1024, 512), F32)),
        in_specs=[part, full, full],
        out_specs=[part, part],
        compiler_params=pltpu.CompilerParams(vmem_limit_bytes=VMEM_BYTES),
    )(q, k, v)


def attend_back_kernel(q, k, v, do, lse, cos, sin, cosq, sinq, dq, dk, dv, dka, dva):
    i = pl.program_id(1)

    @pl.when(i == 0)
    def _():
        dka[...] = jnp.zeros_like(dka)
        dva[...] = jnp.zeros_like(dva)
    kk, vv, g = k[...], v[...], do[...]
    qs = q[...] * jnp.asarray(HD ** -0.5, BF)
    rows = jnp.transpose(lse[...])
    dks, dvs, dqs = [], [], []
    for h in (0, 1):
        keep = head_mask(kk.shape, h)
        zero = jnp.zeros_like(kk)
        s = dot_t(jnp.where(keep, kk, zero), qs)
        p = jnp.exp(s - rows[h * HD:h * HD + 1])
        dp = dot_t(jnp.where(keep, vv, zero), g)
        pd = p * dp
        ds = (pd - p * jnp.sum(pd, axis=0, keepdims=True)).astype(BF)
        dvs.append(jnp.dot(p.astype(BF), g, preferred_element_type=F32))
        dks.append(jnp.dot(ds, qs, preferred_element_type=F32))
        dqs.append(lax.dot_general(ds, kk, (((0,), (0,)), ((), ())), preferred_element_type=F32))
    keep = head_mask(kk.shape, 0)
    dka[...] += jnp.where(keep, dks[0], dks[1])
    dva[...] += jnp.where(keep, dvs[0], dvs[1])
    u = jnp.where(head_mask(g.shape, 0), dqs[0], dqs[1]) * HD ** -0.5
    dq[...] = (u * cosq[...] - swap_halves(u) * sinq[...]).astype(BF)

    @pl.when(i == pl.num_programs(1) - 1)
    def _():
        u = dka[...]
        dk[...] = (u * cos[...] - swap_halves(u) * sin[...]).astype(BF)
        dv[...] = dva[...].astype(BF)


def attend_back(q, k, v, do, lse, cos, sin):
    rows = 256
    part = pl.BlockSpec((rows, 128), lambda g, i: (i, g))
    full = pl.BlockSpec((1024, 128), lambda g, i: (0, g))
    table = pl.BlockSpec((1024, 128), lambda g, i: (0, 0))
    tpart = pl.BlockSpec((rows, 128), lambda g, i: (i, 0))
    return pl.pallas_call(
        attend_back_kernel,
        grid=(4, 1024 // rows),
        out_shape=(jax.ShapeDtypeStruct((1024, 512), BF),) * 3,
        in_specs=[part, full, full, part, part, table, table, tpart, tpart],
        out_specs=[part, full, full],
        scratch_shapes=[pltpu.VMEM((1024, 128), F32)] * 2,
        compiler_params=pltpu.CompilerParams(vmem_limit_bytes=VMEM_BYTES),
    )(q, k, v, do, lse, cos, sin, cos, sin)


def matmul(left, right):
    return jnp.dot(left, right, preferred_element_type=jnp.float32)


def weight_term(left, right):
    return lax.dot_general(
        left, right, (((0,), (0,)), ((), ())), preferred_element_type=jnp.float32
    )


def through(left, weight):
    return lax.dot_general(
        left, weight, (((1,), (1,)), ((), ())), preferred_element_type=jnp.float32
    )


def normalize(values):
    center = jnp.mean(values, axis=-1, keepdims=True)
    centered = values - center
    variance = jnp.mean(centered * centered, axis=-1, keepdims=True)
    scaling = lax.rsqrt(variance + 1e-05)
    return (centered * scaling, scaling)


def norm_back(upstream, normed, scaling):
    first = jnp.mean(upstream, axis=-1, keepdims=True)
    second = jnp.mean(upstream * normed, axis=-1, keepdims=True)
    return scaling * (upstream - first - normed * second)


def half_tables(c):
    row = jnp.arange(1024, dtype=jnp.int32)
    half, zz, r = row // 512, (row // 128) % 4, row % 128
    owner = jnp.where(half == 0, c, 1 - c)
    positions = (zz * 256 + owner * 128 + r).astype(jnp.float32)
    lane = jnp.arange(128, dtype=jnp.int32)
    freqs = 10000.0 ** (-2.0 * (lane % 32).astype(jnp.float32) / HD)
    angle = positions[:, None] * freqs[None, :]
    return jnp.cos(angle), jnp.where(lane % HD < HD // 2, -1.0, 1.0)[None, :] * jnp.sin(angle)


def column_halves(weights, c):
    own, other = [], []
    for w in weights:
        v = w.reshape(w.shape[0], 4, 2, w.shape[1] // 8)
        own.append(lax.dynamic_index_in_dim(v, c, 2, False).reshape(w.shape[0], -1))
        other.append(lax.dynamic_index_in_dim(v, 1 - c, 2, False).reshape(w.shape[0], -1))
    return jnp.concatenate(own, 1), jnp.concatenate(other, 1)


def paired(
    tokens,
    cotangent,
    species_index,
    species_count,
    loss_weight,
    query_weight,
    key_weight,
    value_weight,
    out_weight,
    gate_weight,
    up_weight,
    down_weight,
    mixer_gain,
    mixer_shift,
    feeder_gain,
    feeder_shift,
):
    dp, z = lax.axis_index("dp"), lax.axis_index("seq")
    c = dp % 2
    flip = [(i, i ^ 1) for i in range(8)]

    def other_core(a):
        return lax.ppermute(a, "dp", flip)

    own_qkv, oth_qkv = column_halves((query_weight, key_weight, value_weight), c)
    own_gu, oth_gu = column_halves((gate_weight, up_weight), c)
    small = jnp.stack([mixer_gain, mixer_shift, feeder_gain, feeder_shift]).astype(F32)
    small = jnp.pad(small, ((0, 4), (0, 96)))
    table = loss_weight * lax.rsqrt(species_count.astype(jnp.float32) / 400.0)
    picks = species_index[:, None] == jnp.arange(table.shape[0], dtype=jnp.int32)[None, :]
    factors = jnp.sum(jnp.where(picks, table[None, :], 0.0), axis=1)
    small = small.at[4, :2].set(factors)
    wqkv, wgu, wo, wd, xw, cw, gains = gather(
        tokens, cotangent, own_qkv, oth_qkv, own_gu, oth_gu, out_weight, down_weight, small)
    wqkv, wgu, wo, wd = (wqkv.reshape(1024, 1536), wgu.reshape(1024, 4096), wo.reshape(512, 1024),
                         wd.reshape(2048, 1024))
    x, cot = xw.reshape(1024, 1024), cw.reshape(1024, 1024)
    gains = gains.reshape(32, 8, 128)
    vectors = gains[:, :4, :32].transpose(1, 0, 2).reshape(4, 1, 1024)
    gain_one, shift_one, gain_two, shift_two = vectors
    column = gains[:, 4, :2].reshape(4, 2, 4, 2)[:, :, 0].reshape(4, 4)
    factor = lax.dynamic_index_in_dim(lax.dynamic_index_in_dim(column, dp // 2, 0, False), z, 0, False)

    cos, sin = half_tables(c)
    norm_one, q, k, v = project(x, gain_one, shift_one, wqkv, cos, sin)
    attended, lse = attend(q, k, v)

    def combine(part):
        return part[:512] + other_core(part[512:])

    x_half = x[:512].astype(F32)
    middle = x_half + combine(matmul(attended, wo))
    normed_two, scaling_two = normalize(middle)
    norm_two = (normed_two * gain_two + shift_two).astype(BF)
    norm_two = jnp.concatenate([norm_two, other_core(norm_two)], 0)
    gu = matmul(norm_two, wgu)
    gate, upward = gu[:, :2048], gu[:, 2048:]
    sigma = jax.nn.sigmoid(gate)
    swish = gate * sigma
    hidden = (swish * upward).astype(BF)
    output = (middle + combine(matmul(hidden, wd))).astype(BF)

    grad_out = factor * cot.astype(F32)
    out_low = grad_out.astype(BF)
    down_part = weight_term(hidden, out_low).astype(BF)
    hidden_grad = through(out_low, wd)
    gate_grad = (hidden_grad * upward * sigma * (1.0 + gate * (1.0 - sigma))).astype(BF)
    upward_grad = (hidden_grad * swish).astype(BF)
    both_grad = jnp.concatenate([gate_grad, upward_grad], 1)
    gu_part = weight_term(norm_two, both_grad).astype(BF)
    norm_two_grad = combine(through(both_grad, wgu))
    feeder_gain_part = jnp.sum(norm_two_grad * normed_two, axis=0)
    feeder_shift_part = jnp.sum(norm_two_grad, axis=0)
    middle_grad = grad_out[:512] + norm_back(norm_two_grad * gain_two, normed_two, scaling_two)
    middle_low = middle_grad.astype(BF)
    middle_low = jnp.concatenate([middle_low, other_core(middle_low)], 0)
    out_part = weight_term(attended, middle_low).astype(BF)
    attended_grad = through(middle_low, wo).astype(BF)
    dq, dk, dv = attend_back(q, k, v, attended_grad, lse, cos, sin)
    dqkv = jnp.concatenate([dq, dk, dv], 1)
    qkv_part = weight_term(norm_one, dqkv).astype(BF)
    norm_one_grad = combine(through(dqkv, wqkv))
    normed_one, scaling_one = normalize(x_half)
    mixer_gain_part = jnp.sum(norm_one_grad * normed_one, axis=0)
    mixer_shift_part = jnp.sum(norm_one_grad, axis=0)
    input_grad = middle_grad + norm_back(norm_one_grad * gain_one, normed_one, scaling_one)

    terms = jnp.stack([mixer_gain_part, mixer_shift_part, feeder_gain_part, feeder_shift_part])
    terms = terms.reshape(4, 32, 32).transpose(1, 0, 2)
    terms = jnp.pad(terms, ((0, 0), (0, 4), (0, 96))).reshape(4, 2, 4, 8, 128)
    gqkv, ggu, go, gd, ggain, out, ig = reduce(
        qkv_part, gu_part, out_part, down_part, terms,
        output.reshape(4, 128, 1024), input_grad.astype(BF).reshape(4, 128, 1024))
    gqkv = gqkv.reshape(2, 32, 3, 4, 128).transpose(2, 1, 3, 0, 4).reshape(3, 32, 1024)
    ggu = ggu.reshape(2, 32, 2, 4, 512).transpose(2, 1, 3, 0, 4).reshape(2, 32, 4096)
    return (
        out.reshape(2, 256, 1024),
        ig.reshape(2, 256, 1024).astype(F32),
        gqkv[0],
        gqkv[1],
        gqkv[2],
        go,
        ggu[0],
        ggu[1],
        gd,
        ggain[0, :32],
        ggain[1, :32],
        ggain[2, :32],
        ggain[3, :32],
    )


def tables(start, count):
    half = HD // 2
    positions = (start + jnp.arange(count, dtype=jnp.int32)).astype(jnp.float32)
    freqs = 10000.0 ** (-2.0 * jnp.arange(half, dtype=jnp.float32) / HD)
    angle = positions[:, None] * freqs[None, :]
    return (jnp.cos(angle)[:, None, :], jnp.sin(angle)[:, None, :])


def rotate(values, cosine, sine):
    half = HD // 2
    first = values[..., :half]
    second = values[..., half:]
    return jnp.concatenate(
        [first * cosine - second * sine, second * cosine + first * sine], axis=-1
    )


def attend_head(operands):
    query_head, key_head, value_head = operands
    scores = jnp.einsum(
        "wtd,wsd->wts", query_head, key_head, preferred_element_type=jnp.float32
    ) * HD ** (-0.5)
    peak = jnp.max(scores, axis=-1, keepdims=True)
    raised = jnp.exp(scores - peak)
    total = jnp.sum(raised, axis=-1, keepdims=True)
    probs = (raised / total).astype(jnp.bfloat16)
    result = jnp.einsum("wts,wsd->wtd", probs, value_head, preferred_element_type=jnp.float32)
    return (result, (peak + jnp.log(total))[..., 0])


def head_back(operands):
    query_head, key_head, value_head, upstream, log_total = operands
    scores = jnp.einsum(
        "wtd,wsd->wts", query_head, key_head, preferred_element_type=jnp.float32
    ) * HD ** (-0.5)
    probs = jnp.exp(scores - log_total[..., None])
    prob_grads = jnp.einsum(
        "wtd,wsd->wts", upstream, value_head, preferred_element_type=jnp.float32
    )
    inner = jnp.sum(probs * prob_grads, axis=-1, keepdims=True)
    score_grads = (probs * (prob_grads - inner)).astype(jnp.bfloat16)
    query_grad = jnp.einsum(
        "wts,wsd->wtd", score_grads, key_head, preferred_element_type=jnp.float32
    ) * HD ** (-0.5)
    key_grad = jnp.einsum(
        "wts,wtd->wsd", score_grads, query_head, preferred_element_type=jnp.float32
    ) * HD ** (-0.5)
    value_grad = jnp.einsum(
        "wts,wtd->wsd", probs.astype(jnp.bfloat16), upstream, preferred_element_type=jnp.float32
    )
    return (query_grad, key_grad, value_grad)


def general(
    tokens,
    cotangent,
    species_index,
    species_count,
    loss_weight,
    query_weight,
    key_weight,
    value_weight,
    out_weight,
    gate_weight,
    up_weight,
    down_weight,
    mixer_gain,
    mixer_shift,
    feeder_gain,
    feeder_shift,
):
    gathered = (
        lax.all_gather(query_weight, ("dp", "seq"), axis=0, tiled=True),
        lax.all_gather(key_weight, ("dp", "seq"), axis=0, tiled=True),
        lax.all_gather(value_weight, ("dp", "seq"), axis=0, tiled=True),
        lax.all_gather(out_weight, ("dp", "seq"), axis=0, tiled=True),
        lax.all_gather(gate_weight, ("dp", "seq"), axis=0, tiled=True),
        lax.all_gather(up_weight, ("dp", "seq"), axis=0, tiled=True),
        lax.all_gather(down_weight, ("dp", "seq"), axis=0, tiled=True),
        lax.all_gather(mixer_gain, ("dp", "seq"), axis=0, tiled=True),
        lax.all_gather(mixer_shift, ("dp", "seq"), axis=0, tiled=True),
        lax.all_gather(feeder_gain, ("dp", "seq"), axis=0, tiled=True),
        lax.all_gather(feeder_shift, ("dp", "seq"), axis=0, tiled=True),
    )
    wq, wk, wv, wo, wg, wu, wd, gain_one, shift_one, gain_two, shift_two = gathered
    windows, steps_dev, width = tokens.shape
    rows = windows * steps_dev
    start = lax.axis_index("seq") * steps_dev
    cosine, sine = tables(start, steps_dev)
    inputs = tokens.astype(jnp.float32).reshape(rows, width)
    normed_one, scaling_one = normalize(inputs)
    norm_one = (normed_one * gain_one.astype(jnp.float32) + shift_one.astype(jnp.float32)).astype(
        jnp.bfloat16
    )
    queries = rotate(
        matmul(norm_one, wq).reshape(windows, steps_dev, HEADS, HD), cosine, sine
    ).astype(jnp.bfloat16)
    keys = rotate(matmul(norm_one, wk).reshape(windows, steps_dev, HEADS, HD), cosine, sine).astype(
        jnp.bfloat16
    )
    values = matmul(norm_one, wv).astype(jnp.bfloat16)
    all_keys, all_values = (
        lax.all_gather(keys.reshape(windows, steps_dev, width), "seq", axis=1, tiled=True),
        lax.all_gather(values.reshape(windows, steps_dev, width), "seq", axis=1, tiled=True),
    )
    length = all_keys.shape[1]
    query_heads = queries.transpose(2, 0, 1, 3)
    key_heads = all_keys.reshape(windows, length, HEADS, HD).transpose(2, 0, 1, 3)
    value_heads = all_values.reshape(windows, length, HEADS, HD).transpose(2, 0, 1, 3)
    head_results, log_totals = lax.map(attend_head, (query_heads, key_heads, value_heads))
    attended = head_results.transpose(1, 2, 0, 3).reshape(rows, width).astype(jnp.bfloat16)
    middle = inputs + matmul(attended, wo)
    normed_two, scaling_two = normalize(middle)
    norm_two = (normed_two * gain_two.astype(jnp.float32) + shift_two.astype(jnp.float32)).astype(
        jnp.bfloat16
    )
    gate = matmul(norm_two, wg)
    upward = matmul(norm_two, wu)
    sigma = jax.nn.sigmoid(gate)
    swish = gate * sigma
    hidden = (swish * upward).astype(jnp.bfloat16)
    output = (middle + matmul(hidden, wd)).astype(jnp.bfloat16).reshape(windows, steps_dev, width)
    table = loss_weight * lax.rsqrt(species_count.astype(jnp.float32) / 400.0)
    picks = species_index[:, None] == jnp.arange(table.shape[0], dtype=jnp.int32)[None, :]
    factor = jnp.sum(jnp.where(picks, table[None, :], 0.0), axis=1)
    grad_out = (factor[:, None, None] * cotangent.astype(jnp.float32)).reshape(rows, width)
    regathered = (
        lax.all_gather(query_weight, ("dp", "seq"), axis=0, tiled=True),
        lax.all_gather(key_weight, ("dp", "seq"), axis=0, tiled=True),
        lax.all_gather(value_weight, ("dp", "seq"), axis=0, tiled=True),
        lax.all_gather(out_weight, ("dp", "seq"), axis=0, tiled=True),
        lax.all_gather(gate_weight, ("dp", "seq"), axis=0, tiled=True),
        lax.all_gather(up_weight, ("dp", "seq"), axis=0, tiled=True),
        lax.all_gather(down_weight, ("dp", "seq"), axis=0, tiled=True),
        lax.all_gather(mixer_gain, ("dp", "seq"), axis=0, tiled=True),
        lax.all_gather(mixer_shift, ("dp", "seq"), axis=0, tiled=True),
        lax.all_gather(feeder_gain, ("dp", "seq"), axis=0, tiled=True),
        lax.all_gather(feeder_shift, ("dp", "seq"), axis=0, tiled=True),
    )
    wq, wk, wv, wo, wg, wu, wd, gain_one, shift_one, gain_two, shift_two = regathered
    out_low = grad_out.astype(jnp.bfloat16)
    down_part = weight_term(hidden, out_low)
    hidden_grad = through(out_low, wd)
    gate_grad = (hidden_grad * upward * sigma * (1.0 + gate * (1.0 - sigma))).astype(jnp.bfloat16)
    upward_grad = (hidden_grad * swish).astype(jnp.bfloat16)
    gate_part = weight_term(norm_two, gate_grad)
    upward_part = weight_term(norm_two, upward_grad)
    norm_two_grad = through(gate_grad, wg) + through(upward_grad, wu)
    feeder_gain_part = jnp.sum(norm_two_grad * normed_two, axis=0)
    feeder_shift_part = jnp.sum(norm_two_grad, axis=0)
    middle_grad = grad_out + norm_back(
        norm_two_grad * gain_two.astype(jnp.float32), normed_two, scaling_two
    )
    middle_low = middle_grad.astype(jnp.bfloat16)
    out_part = weight_term(attended, middle_low)
    attended_grad = through(middle_low, wo).astype(jnp.bfloat16)
    upstream_heads = attended_grad.reshape(windows, steps_dev, HEADS, HD).transpose(2, 0, 1, 3)
    query_heads_grad, key_heads_grad, value_heads_grad = lax.map(
        head_back, (query_heads, key_heads, value_heads, upstream_heads, log_totals)
    )
    key_whole = key_heads_grad.transpose(1, 2, 0, 3).reshape(windows, length, width)
    value_whole = value_heads_grad.transpose(1, 2, 0, 3).reshape(windows, length, width)
    key_mine, value_mine = (
        lax.psum_scatter(
            key_whole.astype(jnp.bfloat16), "seq", scatter_dimension=1, tiled=True
        ).astype(jnp.float32),
        lax.psum_scatter(
            value_whole.astype(jnp.bfloat16), "seq", scatter_dimension=1, tiled=True
        ).astype(jnp.float32),
    )
    query_lin_grad = (
        rotate(query_heads_grad.transpose(1, 2, 0, 3), cosine, -sine)
        .reshape(rows, width)
        .astype(jnp.bfloat16)
    )
    key_lin_grad = (
        rotate(key_mine.reshape(windows, steps_dev, HEADS, HD), cosine, -sine)
        .reshape(rows, width)
        .astype(jnp.bfloat16)
    )
    value_lin_grad = value_mine.reshape(rows, width).astype(jnp.bfloat16)
    query_part = weight_term(norm_one, query_lin_grad)
    key_part = weight_term(norm_one, key_lin_grad)
    value_part = weight_term(norm_one, value_lin_grad)
    norm_one_grad = (
        through(query_lin_grad, wq) + through(key_lin_grad, wk) + through(value_lin_grad, wv)
    )
    mixer_gain_part = jnp.sum(norm_one_grad * normed_one, axis=0)
    mixer_shift_part = jnp.sum(norm_one_grad, axis=0)
    input_grad = middle_grad + norm_back(
        norm_one_grad * gain_one.astype(jnp.float32), normed_one, scaling_one
    )
    summed = (
        lax.psum_scatter(query_part, ("dp", "seq"), scatter_dimension=0, tiled=True),
        lax.psum_scatter(key_part, ("dp", "seq"), scatter_dimension=0, tiled=True),
        lax.psum_scatter(value_part, ("dp", "seq"), scatter_dimension=0, tiled=True),
        lax.psum_scatter(out_part, ("dp", "seq"), scatter_dimension=0, tiled=True),
        lax.psum_scatter(gate_part, ("dp", "seq"), scatter_dimension=0, tiled=True),
        lax.psum_scatter(upward_part, ("dp", "seq"), scatter_dimension=0, tiled=True),
        lax.psum_scatter(down_part, ("dp", "seq"), scatter_dimension=0, tiled=True),
        lax.psum_scatter(mixer_gain_part, ("dp", "seq"), scatter_dimension=0, tiled=True),
        lax.psum_scatter(mixer_shift_part, ("dp", "seq"), scatter_dimension=0, tiled=True),
        lax.psum_scatter(feeder_gain_part, ("dp", "seq"), scatter_dimension=0, tiled=True),
        lax.psum_scatter(feeder_shift_part, ("dp", "seq"), scatter_dimension=0, tiled=True),
    )
    return (
        output,
        input_grad.reshape(windows, steps_dev, width),
        summed[0],
        summed[1],
        summed[2],
        summed[3],
        summed[4],
        summed[5],
        summed[6],
        summed[7],
        summed[8],
        summed[9],
        summed[10],
    )


def solution(mesh):
    in_specs = (
        P("dp", "seq", None),
        P("dp", "seq", None),
        P("dp"),
        P(),
        P(),
    ) + (P(("dp", "seq"), None),) * 7 + (P(("dp", "seq")),) * 4
    out_specs = (P("dp", "seq", None),) * 2 + (P(("dp", "seq"), None),) * 7 + (P(("dp", "seq")),) * 4
    fits = mesh.shape["dp"] == 8 and mesh.shape["seq"] == 4
    return jax.shard_map(
        paired if fits else general, mesh=mesh, in_specs=in_specs, out_specs=out_specs, check_vma=False
    )
```

```python
import jax
import jax.numpy as jnp
from jax import lax
from jax.experimental import pallas as pl
from jax.experimental.pallas import tpu as pltpu
from jax.sharding import PartitionSpec as P

HEADS = 16
HD = 64
MESH = pl.DeviceIdType.MESH
BF = jnp.bfloat16
F32 = jnp.float32
ANY = pl.BlockSpec(memory_space=pl.ANY)
VM = pl.BlockSpec(memory_space=pltpu.VMEM)
VMEM_BYTES = 60 << 20


def place():
    dp, z = lax.axis_index("dp"), lax.axis_index("seq")
    return dp // 4, (dp // 2) % 2, dp % 2, z


def dev(y, x, c, z):
    return ((y * 2 + x) * 2 + c, z)


def both(a, b):
    return jnp.logical_and(a, b)


def greet(y, x, c, z):
    barrier = pltpu.get_barrier_semaphore()
    peers = [dev(y, 1 - x, c, z), dev(1 - y, x, c, z), dev(y, x, 1 - c, z)]
    for k in (1, 2, 3):
        peers += [dev(y, x, c, (z + k) % 4), dev(y, x, 1 - c, (z + k) % 4)]
    for p in peers:
        pl.semaphore_signal(barrier, inc=1, device_id=p, device_id_type=MESH)
    pl.semaphore_wait(barrier, len(peers))


class Links:
    def __init__(self, send, recv, local):
        self.send, self.recv, self.local = send, recv, local
        self.n = 0
        self.m = 0
        self.open = []

    def take(self, count):
        self.n += count
        return self.n - count

    def copy(self, src, dst, device, send, recv):
        return pltpu.make_async_remote_copy(
            src_ref=src, dst_ref=dst, send_sem=self.send.at[send], recv_sem=self.recv.at[recv],
            device_id=device, device_id_type=MESH)

    def go(self, c, ok=None):
        if ok is None:
            c.start()
        else:
            pl.when(ok)(c.start)
        self.open.append((c, ok))
        return c

    def to(self, src, dst, device):
        i = self.take(1)
        return self.go(self.copy(src, dst, device, i, i))

    def later(self, src, dst, device):
        i = self.take(1)
        c = self.copy(src, dst, device, i, i)
        self.open.append((c, None))
        return c

    def here_later(self, src, dst):
        self.m += 1
        return pltpu.make_async_copy(src, dst, self.local.at[self.m - 1])

    def wanted(self, src, dst, device):
        i = self.take(1)
        return self.copy(src, dst, device, i, i)

    def here(self, src, dst):
        self.m += 1
        c = pltpu.make_async_copy(src, dst, self.local.at[self.m - 1])
        c.start()
        return c

    def drain(self):
        for c, ok in self.open:
            if ok is None:
                c.wait_send()
            else:
                pl.when(ok)(c.wait_send)
        self.open = []


def near(z):
    return [(z + side * d, both(z + side * d >= 0, z + side * d <= 3), side)
            for d in (1, 2, 3) for side in (-1, 1)]


class Chain:
    def __init__(self, links, me, at, yy, xx):
        self.links, self.me, self.at, self.yy, self.xx = links, me, at, yy, xx
        self.recv, self.send = links.take(4), links.take(8)

    def copy(self, zz, target, slot):
        y, x, c, _ = self.me
        p = self.at(self.yy, self.xx, zz)
        return self.links.copy(p, p, dev(y, x, c, target), self.send + slot, self.recv + zz)

    def own(self):
        z = self.me[3]
        self.links.go(self.copy(z, z - 1, 0), z > 0)
        self.links.go(self.copy(z, z + 1, 1), z < 3)

    def arrive(self, n, zz, ok, side, then):
        z = self.me[3]

        @pl.when(ok)
        def _():
            self.copy(zz, z, 0).wait_recv()
        self.links.go(self.copy(zz, z - side, 2 + n), both(ok, z < 3 if side < 0 else z > 0))
        then(zz, ok)


class Pair:
    def __init__(self, links, at, yy, xx, target):
        self.links, self.at, self.yy, self.xx, self.target = links, at, yy, xx, target
        self.base = links.take(4)

    def copy(self, zz):
        p = self.at(self.yy, self.xx, zz)
        return self.links.copy(p, p, self.target, self.base + zz, self.base + zz)

    def go(self, zz, ok=None):
        self.links.go(self.copy(zz), ok)

    def wait(self, zz, ok=None):
        c = self.copy(zz)
        if ok is None:
            c.wait_recv()
        else:
            pl.when(ok)(c.wait_recv)


def spread(links, at, me, route):
    y, x, c, z = me
    to_x, to_y = dev(y, 1 - x, c, z), dev(1 - y, x, c, z)
    order = near(z)
    if route == 0:
        chain = Chain(links, me, at, y, x)
        py, px, px2 = Pair(links, at, y, x, to_y), Pair(links, at, y, x, to_x), Pair(links, at, 1 - y, x, to_x)

        def start():
            chain.own()
            py.go(z)
            px.go(z)

        def first():
            py.wait(z)
            px2.go(z)

            def then(zz, ok):
                py.go(zz, ok)
                px.go(zz, ok)
            for n, (zz, ok, side) in enumerate(order):
                chain.arrive(n, zz, ok, side, then)

        def second():
            for zz, ok, side in order:
                py.wait(zz, ok)
                px2.go(zz, ok)

        def last():
            for p in (px, px2):
                for zz in range(4):
                    p.wait(zz)
    else:
        px = Pair(links, at, y, x, to_x)
        ch0, ch1 = Chain(links, me, at, y, x), Chain(links, me, at, y, 1 - x)
        py, py2 = Pair(links, at, y, x, to_y), Pair(links, at, y, 1 - x, to_y)

        def start():
            px.go(z)
            ch0.own()
            py.go(z)

        def first():
            px.wait(z)
            ch1.own()
            py2.go(z)
            for n, (zz, ok, side) in enumerate(order):
                ch0.arrive(n, zz, ok, side, py.go)

        def second():
            for n, (zz, ok, side) in enumerate(order):
                ch1.arrive(n, zz, ok, side, py2.go)

        def last():
            for p in (py, py2):
                for zz in range(4):
                    p.wait(zz)
    return start, first, second, last


class Incoming:
    def __init__(self, links, me, src, mid, dst):
        self.links, self.me, self.src, self.mid, self.dst = links, me, src, mid, dst
        y, x, c, z = me
        self.swap = [links.to(src.at[i, pl.ds((1 - c) * 128, 128)], mid.at[2 * c + i], dev(y, x, 1 - c, z))
                     for i in (0, 1)]
        self.base = links.take(4)

    def send(self):
        y, x, c, z = self.me
        for i in (0, 1):
            self.swap[i].wait_recv()
        self.kept = []
        for w in range(4):
            mine = c == w // 2
            for ok, s in ((mine, self.src.at[w % 2, pl.ds(c * 128, 128)]), (jnp.logical_not(mine), self.mid.at[w])):
                d = self.dst.at[0, z]
                self.links.go(self.links.copy(s, d, dev(y, x, c, w), self.base + w, self.base + z), both(ok, z != w))
                local = pltpu.make_async_copy(s, d, self.links.local.at[self.links.m])
                here = both(ok, z == w)
                pl.when(here)(local.start)
                self.kept.append((local, here))
        self.links.m += 1

    def arrive(self):
        y, x, c, z = self.me
        for local, here in self.kept:
            pl.when(here)(local.wait)
        for zz in range(4):
            d = self.dst.at[0, zz]
            pl.when(zz != z)(self.links.copy(d, d, dev(y, x, c, zz), self.base, self.base + zz).wait_recv)
        self.pair = self.links.to(self.dst.at[0], self.dst.at[1], dev(y, x, 1 - c, z))

    def finish(self):
        self.pair.wait_recv()


SPLIT = 1152


def gather_kernel(tok, cot, own_qkv, oth_qkv, own_gu, oth_gu, wo, wd, gp,
                  oqkv, ogu, oo, od, xw, cw, gains, tmid, cmid, send, recv, local):
    me = y, x, c, z = place()
    yx = y * 2 + x
    partner = dev(y, x, 1 - c, z)
    greet(y, x, c, z)
    links = Links(send, recv, local)
    a = links.to(oth_qkv, oqkv.at[yx, c, z], partner)
    tin = Incoming(links, me, tok, tmid, xw)
    b = links.to(oth_gu, ogu.at[yx, c, z], partner)
    cin = Incoming(links, me, cot, cmid, cw)
    loc = [links.here(own_qkv, oqkv.at[yx, c, z]), links.here(own_gu, ogu.at[yx, c, z]),
           links.here(wo, oo.at[yx, z]), links.here(wd, od.at[yx, z]), links.here(gp, gains.at[yx, c, z])]
    tin.send()
    for q in loc:
        q.wait()
    a.wait_recv()
    b.wait_recv()
    parts = []

    def add(at, route):
        parts.append(spread(links, at, me, route))
    for r in (0, 1):
        add(lambda y, x, z, r=r: oqkv.at[y * 2 + x, r, z], r)
        add(lambda y, x, z, r=r: oo.at[y * 2 + x, z, pl.ds(16 * r, 16)], r)
    add(lambda y, x, z: gains.at[y * 2 + x, c, z], 0)
    add(lambda y, x, z: ogu.at[y * 2 + x, 0, z], 0)
    add(lambda y, x, z: ogu.at[y * 2 + x, 1, z, :, pl.ds(0, SPLIT)], 0)
    add(lambda y, x, z: ogu.at[y * 2 + x, 1, z, :, pl.ds(SPLIT, 4096 - SPLIT)], 1)
    add(lambda y, x, z: od.at[y * 2 + x, z, pl.ds(0, 80)], 0)
    add(lambda y, x, z: od.at[y * 2 + x, z, pl.ds(80, 48)], 1)
    for s in parts:
        s[0]()
    for i, s in enumerate(parts):
        s[1]()
        if i == 3:
            tin.arrive()
    cin.send()
    for s in parts:
        s[2]()
    for s in parts:
        s[3]()
    cin.arrive()
    g = links.to(gains.at[:, c], gains.at[:, c], partner)
    g.wait_recv()
    tin.finish()
    cin.finish()
    links.drain()


def gather(tok, cot, own_qkv, oth_qkv, own_gu, oth_gu, wo, wd, gp):
    return pl.pallas_call(
        gather_kernel,
        out_shape=(
            jax.ShapeDtypeStruct((4, 2, 4, 32, 1536), BF),
            jax.ShapeDtypeStruct((4, 2, 4, 32, 4096), BF),
            jax.ShapeDtypeStruct((4, 4, 32, 1024), BF),
            jax.ShapeDtypeStruct((4, 4, 128, 1024), BF),
            jax.ShapeDtypeStruct((2, 4, 128, 1024), BF),
            jax.ShapeDtypeStruct((2, 4, 128, 1024), BF),
            jax.ShapeDtypeStruct((4, 2, 4, 8, 128), F32),
        ),
        in_specs=[VM] * 9,
        out_specs=[ANY] * 7,
        scratch_shapes=[
            pltpu.VMEM((4, 128, 1024), BF),
            pltpu.VMEM((4, 128, 1024), BF),
            pltpu.SemaphoreType.DMA((400,)),
            pltpu.SemaphoreType.DMA((400,)),
            pltpu.SemaphoreType.DMA((8,)),
        ],
        compiler_params=pltpu.CompilerParams(collective_id=0, has_side_effects=True, vmem_limit_bytes=VMEM_BYTES),
    )(tok, cot, own_qkv, oth_qkv, own_gu, oth_gu, wo, wd, gp)


def at_z(ref, zz):
    return ref.at[zz] if len(ref.shape) == 3 else ref.at[:, zz]


def add_into(dst, a, b):
    def body(i, _):
        at_z(dst, i)[...] = (at_z(a, i)[...].astype(F32) + at_z(b, i)[...].astype(F32)).astype(dst.dtype)
        return 0
    lax.fori_loop(0, 4, body, 0)


def reduce_shapes(piece, route, dtype=BF):
    part = piece[:-3] + piece[-2:]
    big = pltpu.VMEM((2,) + piece, dtype)
    if route < 2:
        return [big, big, pltpu.VMEM(piece, dtype), pltpu.VMEM((3,) + part, dtype), pltpu.VMEM(part, F32)]
    return [big, big, pltpu.VMEM((2, 3) + part, dtype), pltpu.VMEM((2,) + part, dtype), pltpu.VMEM(part, F32)]


def collect(links, at, me, route, bufs, deliver):
    y, x, c, z = me
    to_x, to_y = dev(y, 1 - x, c, z), dev(1 - y, x, c, z)
    zs = [(z + k) % 4 for k in range(4)]
    to_z = [dev(y, x, c, zs[k]) for k in range(4)]
    own, got, third, fourth, total = bufs
    out = deliver(total)

    def finish():
        for q in out:
            q.start()

    if route < 2:
        if route == 0:
            keep, away = [at(1 - y, x), at(y, x)], [at(1 - y, 1 - x), at(y, 1 - x)]
            one, two = to_x, to_y
        else:
            keep, away = [at(y, 1 - x), at(y, x)], [at(1 - y, 1 - x), at(1 - y, x)]
            one, two = to_y, to_x
        load = [links.here_later(keep[n], own.at[n]) for n in (0, 1)]
        give = [links.later(away[n], got.at[n], one) for n in (0, 1)]
        cross = links.later(own.at[0], third, two)
        over_z = [links.later(at_z(own.at[1], zs[k]), fourth.at[k - 1], to_z[k]) for k in (1, 2, 3)]

        def start():
            for q in give + load:
                q.start()

        def first():
            load[0].wait()
            give[0].wait_recv()
            add_into(own.at[0], own.at[0], got.at[0])
            cross.start()

        def second():
            load[1].wait()
            give[1].wait_recv()
            add_into(own.at[1], own.at[1], got.at[1])
            cross.wait_recv()
            add_into(own.at[1], own.at[1], third)
            for q in over_z:
                q.start()

        def last():
            for q in over_z:
                q.wait_recv()
            total[...] = (at_z(own.at[1], z)[...].astype(F32) + fourth[0].astype(F32)
                          + (fourth[1].astype(F32) + fourth[2].astype(F32)))
            finish()
        return start, first, second, last

    load = [links.here_later(at(y, xx), own.at[n]) for n, xx in ((0, 1 - x), (1, x))]
    give = [links.later(at(1 - y, xx), got.at[n], to_y) for n, xx in ((0, 1 - x), (1, x))]
    over_z = [[links.later(at_z(own.at[n], zs[k]), third.at[n, k - 1], to_z[k]) for k in (1, 2, 3)] for n in (0, 1)]
    over_x = links.later(fourth.at[0], fourth.at[1], to_x)

    def start():
        for q in give + load:
            q.start()

    def first(n):
        load[n].wait()
        give[n].wait_recv()
        add_into(own.at[n], own.at[n], got.at[n])
        for q in over_z[n]:
            q.start()

    def second():
        for q in over_z[0]:
            q.wait_recv()
        fourth[0] = (at_z(own.at[0], z)[...].astype(F32) + third[0, 0].astype(F32)
                     + (third[0, 1].astype(F32) + third[0, 2].astype(F32))).astype(fourth.dtype)
        over_x.start()

    def last():
        for q in over_z[1]:
            q.wait_recv()
        over_x.wait_recv()
        total[...] = (at_z(own.at[1], z)[...].astype(F32) + third[1, 0].astype(F32)
                      + (third[1, 1].astype(F32) + third[1, 2].astype(F32)) + fourth[1].astype(F32))
        finish()
    return start, lambda: first(0), lambda: first(1), second, last


class Outgoing:
    def __init__(self, links, me, src, dst):
        y, x, c, z = me
        recv, send = links.take(4), links.take(4)
        self.here, self.away = c == z // 2, c != z // 2
        self.remote, self.back = [], []
        for k in range(4):
            zz = (z + k) % 4
            s, d = src.at[zz], dst.at[z % 2, c]
            self.remote.append(links.copy(s, d, dev(y, x, z // 2, zz), send + k, recv + (z % 2) * 2 + c))
            links.open.append((self.remote[k], None if k else self.away))
            if k == 0:
                self.local = links.here_later(s, d)
        for i in (0, 1):
            for h in (0, 1):
                d = dst.at[i, h]
                mine = both(z == 2 * c + i, h == c)
                self.back.append((links.copy(d, d, dev(y, x, 1 - c, z), send, recv + 2 * i + h), jnp.logical_not(mine)))

    def start(self):
        for q in self.remote[1:]:
            q.start()
        pl.when(self.away)(self.remote[0].start)
        pl.when(self.here)(self.local.start)

    def finish(self):
        pl.when(self.here)(self.local.wait)
        for q, ok in self.back:
            pl.when(ok)(q.wait_recv)


def swap_halves(u):
    lane = lax.broadcasted_iota(jnp.int32, u.shape, 1) % HD
    return jnp.where(lane < HD // 2, pltpu.roll(u, 128 - HD // 2, 1), pltpu.roll(u, HD // 2, 1))


def head_mask(shape, h):
    lane = lax.broadcasted_iota(jnp.int32, shape, 1)
    return (lane < HD) if h == 0 else (lane >= HD)


def dot_t(a, b):
    return lax.dot_general(a, b, (((1,), (1,)), ((), ())), preferred_element_type=F32)


def project_kernel(x, gain, shift, w, cos, sin, n1, q, k, v):
    u = x[...].astype(F32)
    d = u - jnp.mean(u, axis=-1, keepdims=True)
    r = lax.rsqrt(jnp.mean(d * d, axis=-1, keepdims=True) + 1e-05)
    n = (d * r * gain[...] + shift[...]).astype(BF)
    n1[...] = n
    for g in range(4):
        for j, o in ((0, q), (1, k)):
            s = jnp.dot(n, w[:, pl.ds(512 * j + 128 * g, 128)], preferred_element_type=F32)
            o[:, pl.ds(128 * g, 128)] = (s * cos[...] + swap_halves(s) * sin[...]).astype(BF)
    v[...] = jnp.dot(n, w[:, pl.ds(1024, 512)], preferred_element_type=F32).astype(BF)


def project(x, gain, shift, w, cos, sin):
    rows = 256
    blk = lambda n: pl.BlockSpec((rows, n), lambda i: (i, 0))
    one = lambda a, b: pl.BlockSpec((a, b), lambda i: (0, 0))
    return pl.pallas_call(
        project_kernel,
        grid=(1024 // rows,),
        out_shape=(jax.ShapeDtypeStruct((1024, 1024), BF),) + (jax.ShapeDtypeStruct((1024, 512), BF),) * 3,
        in_specs=[blk(1024), one(1, 1024), one(1, 1024), one(1024, 1536), blk(128), blk(128)],
        out_specs=[blk(1024), blk(512), blk(512), blk(512)],
        compiler_params=pltpu.CompilerParams(vmem_limit_bytes=VMEM_BYTES),
    )(x, gain, shift, w, cos, sin)


def attend_kernel(q, k, v, o, lse):
    qs = q[...] * jnp.asarray(HD ** -0.5, BF)
    outs, logs = [], []
    for h in (0, 1):
        qh = jnp.where(head_mask(qs.shape, h), qs, jnp.zeros_like(qs))
        s = dot_t(qh, k[...])
        m = jnp.max(s, axis=-1, keepdims=True)
        e = jnp.exp(s - m)
        t = jnp.sum(e, axis=-1, keepdims=True)
        p = (e * (1.0 / t)).astype(BF)
        outs.append(jnp.dot(p, v[...], preferred_element_type=F32))
        logs.append(jnp.broadcast_to(m + jnp.log(t), qs.shape))
    keep = head_mask(qs.shape, 0)
    o[...] = jnp.where(keep, outs[0], outs[1]).astype(BF)
    lse[...] = jnp.where(keep, logs[0], logs[1])


def attend(q, k, v):
    rows = 256
    part = pl.BlockSpec((rows, 128), lambda g, i: (i, g))
    full = pl.BlockSpec((1024, 128), lambda g, i: (0, g))
    return pl.pallas_call(
        attend_kernel,
        grid=(4, 1024 // rows),
        out_shape=(jax.ShapeDtypeStruct((1024, 512), BF), jax.ShapeDtypeStruct((1024, 512), F32)),
        in_specs=[part, full, full],
        out_specs=[part, part],
        compiler_params=pltpu.CompilerParams(vmem_limit_bytes=VMEM_BYTES),
    )(q, k, v)


def attend_back_step(q, k, v, do, lse, cos, sin, dqkv, dka, dva, g, i):
    lanes = pl.ds(pl.multiple_of(g * 128, 128), 128)
    rows = pl.ds(pl.multiple_of(i * 256, 256), 256)

    @pl.when(i == 0)
    def _():
        dka[...] = jnp.zeros_like(dka)
        dva[...] = jnp.zeros_like(dva)
    kk, vv, go = k[:, lanes], v[:, lanes], do[rows, lanes]
    qs = q[rows, lanes] * jnp.asarray(HD ** -0.5, BF)
    logs = jnp.transpose(lse[rows, lanes])
    dks, dvs, dqs = [], [], []
    for h in (0, 1):
        keep = head_mask(kk.shape, h)
        zero = jnp.zeros_like(kk)
        s = dot_t(jnp.where(keep, kk, zero), qs)
        p = jnp.exp(s - logs[h * HD:h * HD + 1])
        dp = dot_t(jnp.where(keep, vv, zero), go)
        pd = p * dp
        ds = (pd - p * jnp.sum(pd, axis=0, keepdims=True)).astype(BF)
        dvs.append(jnp.dot(p.astype(BF), go, preferred_element_type=F32))
        dks.append(jnp.dot(ds, qs, preferred_element_type=F32))
        dqs.append(lax.dot_general(ds, kk, (((0,), (0,)), ((), ())), preferred_element_type=F32))
    keep = head_mask(kk.shape, 0)
    dka[...] += jnp.where(keep, dks[0], dks[1])
    dva[...] += jnp.where(keep, dvs[0], dvs[1])
    u = jnp.where(head_mask(go.shape, 0), dqs[0], dqs[1]) * HD ** -0.5
    dqkv[rows, lanes] = (u * cos[rows, :] - swap_halves(u) * sin[rows, :]).astype(BF)

    @pl.when(i == 3)
    def _():
        u = dka[...]
        dqkv[:, pl.ds(pl.multiple_of(512 + g * 128, 128), 128)] = (
            u * cos[...] - swap_halves(u) * sin[...]).astype(BF)
        dqkv[:, pl.ds(pl.multiple_of(1024 + g * 128, 128), 128)] = dva[...].astype(BF)


PIECES = (
    ("d", 3, 2),
    ("d", 0, 1),
    ("gu", 5, 0),
    ("o", 0, 0),
    ("gu", 1, 0),
    ("gu", 3, 0),
    ("qkv", 1, 1),
    ("qkv", 0, 1),
    ("d", 1, 0),
    ("gu", 2, 0),
    ("gu", 7, 1),
    ("gu", 4, 0),
    ("d", 2, 0),
    ("gu", 0, 2),
    ("gu", 6, 1),
)
SHAPES = {"d": (4, 32, 1024), "o": (4, 32, 1024), "gu": (2, 4, 32, 512), "qkv": (2, 4, 32, 768)}
ORDER = (
    ((15, 0), (0, 0), (1, 0), (2, 0)), (), (), ((0, 1), (2, 1), (3, 0), (13, 0)), (), ((0, 2),), (),
    ((1, 1), (3, 1), (4, 0)), (), (), ((1, 2), (2, 2)), ((15, 1), (4, 1), (5, 0), (13, 1)), ((0, 3), (13, 2)), (),
    ((3, 2), (5, 1), (8, 0)), ((0, 4), (1, 3), (4, 2), (2, 3)), ((5, 2), (8, 1), (9, 0), (13, 3)),
    ((6, 0), (7, 0), (8, 2), (9, 1), (11, 0)),
    ((3, 3), (16, 0), (4, 3), (6, 1), (5, 3), (10, 0), (11, 1), (12, 0), (13, 4), (17, 0), (8, 3), (6, 2), (7, 1),
     (14, 0), (12, 1), (17, 1), (9, 2), (7, 2), (16, 1), (10, 1), (10, 2), (6, 3), (11, 2), (9, 3), (14, 1),
     (14, 2), (7, 3), (12, 2), (17, 2), (10, 3), (11, 3), (14, 3), (12, 3), (17, 3),),

)


def total_over_devices(links, me, acc, got):
    y, x, c, z = me
    hops = [links.wanted(acc, got.at[i], d) for i, d in
            enumerate((dev(y, x, 1 - c, z), dev(y, 1 - x, c, z), dev(1 - y, x, c, z)))]
    over_z = [links.wanted(acc, got.at[2 + k], dev(y, x, c, (z + k) % 4)) for k in (1, 2, 3)]

    def settle(i):
        hops[i].wait()
        acc[...] += got[i]

    def chip():
        hops[0].start()
        settle(0)
        hops[1].start()

    def second():
        settle(1)
        hops[2].start()

    def third():
        settle(2)
        for q in over_z:
            q.start()

    def last():
        for q in over_z:
            q.wait()
        acc[...] += got[3] + (got[4] + got[5])
    return chip, second, third, last


def back_kernel(dgu, do, dd, out16, q, k, v, ag, lse, cos, sin, n1, w, xh, mg, gain, gterms, *rest):
    fqkv, fgu, fo, fd, fgain, out_w, ig_w = rest[:7]
    scratch = list(rest[7:])
    dqkv, dka, dva, dw, sent, came, ig, gacc, ggot, send, recv, local = scratch[-12:]
    me = y, x, c, z = place()
    partner = dev(y, x, 1 - c, z)
    greet(y, x, c, z)
    links = Links(send, recv, local)
    work = []
    finals = []
    for name, index, route in PIECES:
        bufs = [scratch.pop(0) for _ in range(5)]
        if name in ("qkv", "gu"):
            src, dst = (dw, fqkv) if name == "qkv" else (dgu, fgu)
            cols = SHAPES[name][3]
            lanes = pl.ds(index * cols, cols)

            def at(yy, xx, src=src, lanes=lanes):
                return src.at[yy * 2 + xx, :, :, :, lanes]

            def deliver(total, dst=dst, lanes=lanes):
                there = links.later(total.at[1 - c], dst.at[c, :, lanes], partner)
                here = links.here_later(total.at[c], dst.at[c, :, lanes])
                finals.extend((there.wait_recv, here.wait))
                return there, here
        else:
            src, dst = (dd, fd) if name == "d" else (do, fo)
            rows = pl.ds(index * 32, 32)

            def at(yy, xx, src=src, rows=rows):
                return src.at[yy * 2 + xx, :, rows]

            def deliver(total, dst=dst, rows=rows):
                here = links.here_later(total, dst.at[rows])
                finals.append(here.wait)
                return (here,)
        work.append(collect(links, at, me, route, bufs, deliver))

    o1 = Outgoing(links, me, out16, out_w)
    o2 = Outgoing(links, me, ig, ig_w)
    work += [(o1.start, o1.finish), (o2.start, o2.finish), total_over_devices(links, me, gacc, ggot)]
    swap = links.wanted(sent, came, partner)

    def comm(slot):
        for i, stage in ORDER[slot]:
            work[i][stage]()
    comm(0)

    def step(t, _):
        attend_back_step(q, k, v, ag, lse, cos, sin, dqkv, dka, dva, t // 4, t % 4)
        for slot in range(1, 16):
            if ORDER[slot]:
                pl.when(t == slot - 1)(lambda slot=slot: comm(slot))
        return 0
    lax.fori_loop(0, 16, step, 0)
    comm(16)

    def weight_chunk(j, _):
        cols = pl.ds(pl.multiple_of(j * 256, 256), 256)
        u = lax.dot_general(n1[...], dqkv[:, cols], (((0,), (0,)), ((), ())), preferred_element_type=F32)
        dw[:, :, :, :, cols] = u.astype(BF).reshape(4, 2, 4, 32, 256)
        return 0
    lax.fori_loop(0, 6, weight_chunk, 0)
    comm(17)
    for r in (2, 3):
        sent[pl.ds((r - 2) * 256, 256), :] = dot_t(dqkv[pl.ds(r * 256, 256), :], w[...])
    swap.start()
    mine = [dot_t(dqkv[pl.ds(r * 256, 256), :], w[...]) for r in (0, 1)]
    swap.wait()
    sums = [jnp.zeros((1, 1024), F32)] * 2
    for r in (0, 1):
        rows = pl.ds(r * 256, 256)
        gn = mine[r] + came[rows, :]
        u = xh[rows, :].astype(F32)
        d = u - jnp.mean(u, axis=-1, keepdims=True)
        scaling = lax.rsqrt(jnp.mean(d * d, axis=-1, keepdims=True) + 1e-05)
        normed = d * scaling
        sums = [sums[0] + jnp.sum(gn * normed, axis=0, keepdims=True), sums[1] + jnp.sum(gn, axis=0, keepdims=True)]
        up = gn * gain[...]
        out = mg[rows, :] + scaling * (up - jnp.mean(up, axis=-1, keepdims=True)
                                       - normed * jnp.mean(up * normed, axis=-1, keepdims=True))
        ig[pl.ds(2 * r, 2)] = out.astype(BF).reshape(2, 128, 1024)
    gacc[...] = gterms[...]
    gacc[0:1, :] = sums[0]
    gacc[1:2, :] = sums[1]
    comm(18)
    finals.append(links.here(gacc, fgain).wait)
    for f in finals:
        f()
    links.drain()


def back(dgu, do, dd, out16, q, k, v, ag, lse, cos, sin, n1, w, xh, mg, gain, gterms):
    scratch = []
    for name, index, route in PIECES:
        scratch += reduce_shapes(SHAPES[name], route)
    return pl.pallas_call(
        back_kernel,
        out_shape=(
            jax.ShapeDtypeStruct((2, 32, 1536), F32),
            jax.ShapeDtypeStruct((2, 32, 4096), F32),
            jax.ShapeDtypeStruct((32, 1024), F32),
            jax.ShapeDtypeStruct((128, 1024), F32),
            jax.ShapeDtypeStruct((8, 1024), F32),
            jax.ShapeDtypeStruct((2, 2, 128, 1024), BF),
            jax.ShapeDtypeStruct((2, 2, 128, 1024), BF),
        ),
        in_specs=[ANY] * 4 + [VM] * 13,
        out_specs=[ANY] * 7,
        scratch_shapes=scratch + [
            pltpu.VMEM((1024, 1536), BF),
            pltpu.VMEM((1024, 128), F32),
            pltpu.VMEM((1024, 128), F32),
            pltpu.VMEM((4, 2, 4, 32, 1536), BF),
            pltpu.VMEM((512, 1024), F32),
            pltpu.VMEM((512, 1024), F32),
            pltpu.VMEM((4, 128, 1024), BF),
            pltpu.VMEM((8, 1024), F32),
            pltpu.VMEM((6, 8, 1024), F32),
            pltpu.SemaphoreType.DMA((192,)),
            pltpu.SemaphoreType.DMA((192,)),
            pltpu.SemaphoreType.DMA((64,)),
        ],
        compiler_params=pltpu.CompilerParams(collective_id=1, has_side_effects=True, vmem_limit_bytes=67043328),
    )(dgu.reshape(4, 2, 4, 32, 4096), do.reshape(4, 4, 32, 1024), dd.reshape(4, 4, 128, 1024), out16,
      q, k, v, ag, lse, cos, sin, n1, w, xh, mg, gain, gterms)


def matmul(left, right):
    return jnp.dot(left, right, preferred_element_type=jnp.float32)


def weight_term(left, right):
    return lax.dot_general(
        left, right, (((0,), (0,)), ((), ())), preferred_element_type=jnp.float32
    )


def through(left, weight):
    return lax.dot_general(
        left, weight, (((1,), (1,)), ((), ())), preferred_element_type=jnp.float32
    )


def normalize(values):
    center = jnp.mean(values, axis=-1, keepdims=True)
    centered = values - center
    variance = jnp.mean(centered * centered, axis=-1, keepdims=True)
    scaling = lax.rsqrt(variance + 1e-05)
    return (centered * scaling, scaling)


def norm_back(upstream, normed, scaling):
    first = jnp.mean(upstream, axis=-1, keepdims=True)
    second = jnp.mean(upstream * normed, axis=-1, keepdims=True)
    return scaling * (upstream - first - normed * second)


def half_tables(c):
    row = jnp.arange(1024, dtype=jnp.int32)
    half, zz, r = row // 512, (row // 128) % 4, row % 128
    owner = jnp.where(half == 0, c, 1 - c)
    positions = (zz * 256 + owner * 128 + r).astype(jnp.float32)
    lane = jnp.arange(128, dtype=jnp.int32)
    freqs = 10000.0 ** (-2.0 * (lane % 32).astype(jnp.float32) / HD)
    angle = positions[:, None] * freqs[None, :]
    return jnp.cos(angle), jnp.where(lane % HD < HD // 2, -1.0, 1.0)[None, :] * jnp.sin(angle)


def column_halves(weights, c):
    own, other = [], []
    for w in weights:
        v = w.reshape(w.shape[0], 4, 2, w.shape[1] // 8)
        own.append(lax.dynamic_index_in_dim(v, c, 2, False).reshape(w.shape[0], -1))
        other.append(lax.dynamic_index_in_dim(v, 1 - c, 2, False).reshape(w.shape[0], -1))
    return jnp.concatenate(own, 1), jnp.concatenate(other, 1)


def paired(
    tokens,
    cotangent,
    species_index,
    species_count,
    loss_weight,
    query_weight,
    key_weight,
    value_weight,
    out_weight,
    gate_weight,
    up_weight,
    down_weight,
    mixer_gain,
    mixer_shift,
    feeder_gain,
    feeder_shift,
):
    dp, z = lax.axis_index("dp"), lax.axis_index("seq")
    c = dp % 2
    flip = [(i, i ^ 1) for i in range(8)]

    def other_core(a):
        return lax.ppermute(a, "dp", flip)

    own_qkv, oth_qkv = column_halves((query_weight, key_weight, value_weight), c)
    own_gu, oth_gu = column_halves((gate_weight, up_weight), c)
    small = jnp.stack([mixer_gain, mixer_shift, feeder_gain, feeder_shift]).astype(F32)
    small = jnp.pad(small, ((0, 4), (0, 96)))
    table = loss_weight * lax.rsqrt(species_count.astype(jnp.float32) / 400.0)
    picks = species_index[:, None] == jnp.arange(table.shape[0], dtype=jnp.int32)[None, :]
    factors = jnp.sum(jnp.where(picks, table[None, :], 0.0), axis=1)
    small = small.at[4, :2].set(factors)
    wqkv, wgu, wo, wd, xw, cw, gains = gather(
        tokens, cotangent, own_qkv, oth_qkv, own_gu, oth_gu, out_weight, down_weight, small)
    wqkv, wgu, wo, wd = (wqkv.reshape(1024, 1536), wgu.reshape(1024, 4096), wo.reshape(512, 1024),
                         wd.reshape(2048, 1024))
    x, cot = xw.reshape(1024, 1024), cw.reshape(1024, 1024)
    gains = gains.reshape(32, 8, 128)
    vectors = gains[:, :4, :32].transpose(1, 0, 2).reshape(4, 1, 1024)
    gain_one, shift_one, gain_two, shift_two = vectors
    column = gains[:, 4, :2].reshape(4, 2, 4, 2)[:, :, 0].reshape(4, 4)
    factor = lax.dynamic_index_in_dim(lax.dynamic_index_in_dim(column, dp // 2, 0, False), z, 0, False)

    cos, sin = half_tables(c)
    norm_one, q, k, v = project(x, gain_one, shift_one, wqkv, cos, sin)
    attended, lse = attend(q, k, v)

    def combine(part):
        return part[:512] + other_core(part[512:])

    x_half = x[:512].astype(F32)
    middle = x_half + combine(matmul(attended, wo))
    normed_two, scaling_two = normalize(middle)
    norm_two = (normed_two * gain_two + shift_two).astype(BF)
    norm_two = jnp.concatenate([norm_two, other_core(norm_two)], 0)
    gu = matmul(norm_two, wgu)
    gate, upward = gu[:, :2048], gu[:, 2048:]
    sigma = jax.nn.sigmoid(gate)
    swish = gate * sigma
    hidden = (swish * upward).astype(BF)
    output = (middle + combine(matmul(hidden, wd))).astype(BF)

    grad_out = factor * cot.astype(F32)
    out_low = grad_out.astype(BF)
    down_part = weight_term(hidden, out_low).astype(BF)
    hidden_grad = through(out_low, wd)
    gate_grad = (hidden_grad * upward * sigma * (1.0 + gate * (1.0 - sigma))).astype(BF)
    upward_grad = (hidden_grad * swish).astype(BF)
    both_grad = jnp.concatenate([gate_grad, upward_grad], 1)
    gu_part = weight_term(norm_two, both_grad).astype(BF)
    norm_two_grad = combine(through(both_grad, wgu))
    feeder_gain_part = jnp.sum(norm_two_grad * normed_two, axis=0)
    feeder_shift_part = jnp.sum(norm_two_grad, axis=0)
    middle_grad = grad_out[:512] + norm_back(norm_two_grad * gain_two, normed_two, scaling_two)
    middle_low = middle_grad.astype(BF)
    middle_low = jnp.concatenate([middle_low, other_core(middle_low)], 0)
    out_part = weight_term(attended, middle_low).astype(BF)
    attended_grad = through(middle_low, wo).astype(BF)
    terms = jnp.zeros((8, 1024), F32).at[2].set(feeder_gain_part).at[3].set(feeder_shift_part)
    gqkv, ggu, go, gd, ggain, out, ig = back(
        gu_part, out_part, down_part, output.reshape(4, 128, 1024), q, k, v, attended_grad, lse, cos, sin,
        norm_one, wqkv, x[:512], middle_grad, gain_one, terms)
    ggain = lax.dynamic_slice_in_dim(ggain[:4], (dp * 4 + z) * 32, 32, 1)
    gqkv = gqkv.reshape(2, 32, 3, 4, 128).transpose(2, 1, 3, 0, 4).reshape(3, 32, 1024)
    ggu = ggu.reshape(2, 32, 2, 4, 512).transpose(2, 1, 3, 0, 4).reshape(2, 32, 4096)
    return (
        out.reshape(2, 256, 1024),
        ig.reshape(2, 256, 1024).astype(F32),
        gqkv[0],
        gqkv[1],
        gqkv[2],
        go,
        ggu[0],
        ggu[1],
        gd,
        ggain[0],
        ggain[1],
        ggain[2],
        ggain[3],
    )


def tables(start, count):
    half = HD // 2
    positions = (start + jnp.arange(count, dtype=jnp.int32)).astype(jnp.float32)
    freqs = 10000.0 ** (-2.0 * jnp.arange(half, dtype=jnp.float32) / HD)
    angle = positions[:, None] * freqs[None, :]
    return (jnp.cos(angle)[:, None, :], jnp.sin(angle)[:, None, :])


def rotate(values, cosine, sine):
    half = HD // 2
    first = values[..., :half]
    second = values[..., half:]
    return jnp.concatenate(
        [first * cosine - second * sine, second * cosine + first * sine], axis=-1
    )


def attend_head(operands):
    query_head, key_head, value_head = operands
    scores = jnp.einsum(
        "wtd,wsd->wts", query_head, key_head, preferred_element_type=jnp.float32
    ) * HD ** (-0.5)
    peak = jnp.max(scores, axis=-1, keepdims=True)
    raised = jnp.exp(scores - peak)
    total = jnp.sum(raised, axis=-1, keepdims=True)
    probs = (raised / total).astype(jnp.bfloat16)
    result = jnp.einsum("wts,wsd->wtd", probs, value_head, preferred_element_type=jnp.float32)
    return (result, (peak + jnp.log(total))[..., 0])


def head_back(operands):
    query_head, key_head, value_head, upstream, log_total = operands
    scores = jnp.einsum(
        "wtd,wsd->wts", query_head, key_head, preferred_element_type=jnp.float32
    ) * HD ** (-0.5)
    probs = jnp.exp(scores - log_total[..., None])
    prob_grads = jnp.einsum(
        "wtd,wsd->wts", upstream, value_head, preferred_element_type=jnp.float32
    )
    inner = jnp.sum(probs * prob_grads, axis=-1, keepdims=True)
    score_grads = (probs * (prob_grads - inner)).astype(jnp.bfloat16)
    query_grad = jnp.einsum(
        "wts,wsd->wtd", score_grads, key_head, preferred_element_type=jnp.float32
    ) * HD ** (-0.5)
    key_grad = jnp.einsum(
        "wts,wtd->wsd", score_grads, query_head, preferred_element_type=jnp.float32
    ) * HD ** (-0.5)
    value_grad = jnp.einsum(
        "wts,wtd->wsd", probs.astype(jnp.bfloat16), upstream, preferred_element_type=jnp.float32
    )
    return (query_grad, key_grad, value_grad)


def general(
    tokens,
    cotangent,
    species_index,
    species_count,
    loss_weight,
    query_weight,
    key_weight,
    value_weight,
    out_weight,
    gate_weight,
    up_weight,
    down_weight,
    mixer_gain,
    mixer_shift,
    feeder_gain,
    feeder_shift,
):
    gathered = (
        lax.all_gather(query_weight, ("dp", "seq"), axis=0, tiled=True),
        lax.all_gather(key_weight, ("dp", "seq"), axis=0, tiled=True),
        lax.all_gather(value_weight, ("dp", "seq"), axis=0, tiled=True),
        lax.all_gather(out_weight, ("dp", "seq"), axis=0, tiled=True),
        lax.all_gather(gate_weight, ("dp", "seq"), axis=0, tiled=True),
        lax.all_gather(up_weight, ("dp", "seq"), axis=0, tiled=True),
        lax.all_gather(down_weight, ("dp", "seq"), axis=0, tiled=True),
        lax.all_gather(mixer_gain, ("dp", "seq"), axis=0, tiled=True),
        lax.all_gather(mixer_shift, ("dp", "seq"), axis=0, tiled=True),
        lax.all_gather(feeder_gain, ("dp", "seq"), axis=0, tiled=True),
        lax.all_gather(feeder_shift, ("dp", "seq"), axis=0, tiled=True),
    )
    wq, wk, wv, wo, wg, wu, wd, gain_one, shift_one, gain_two, shift_two = gathered
    windows, steps_dev, width = tokens.shape
    rows = windows * steps_dev
    start = lax.axis_index("seq") * steps_dev
    cosine, sine = tables(start, steps_dev)
    inputs = tokens.astype(jnp.float32).reshape(rows, width)
    normed_one, scaling_one = normalize(inputs)
    norm_one = (normed_one * gain_one.astype(jnp.float32) + shift_one.astype(jnp.float32)).astype(
        jnp.bfloat16
    )
    queries = rotate(
        matmul(norm_one, wq).reshape(windows, steps_dev, HEADS, HD), cosine, sine
    ).astype(jnp.bfloat16)
    keys = rotate(matmul(norm_one, wk).reshape(windows, steps_dev, HEADS, HD), cosine, sine).astype(
        jnp.bfloat16
    )
    values = matmul(norm_one, wv).astype(jnp.bfloat16)
    all_keys, all_values = (
        lax.all_gather(keys.reshape(windows, steps_dev, width), "seq", axis=1, tiled=True),
        lax.all_gather(values.reshape(windows, steps_dev, width), "seq", axis=1, tiled=True),
    )
    length = all_keys.shape[1]
    query_heads = queries.transpose(2, 0, 1, 3)
    key_heads = all_keys.reshape(windows, length, HEADS, HD).transpose(2, 0, 1, 3)
    value_heads = all_values.reshape(windows, length, HEADS, HD).transpose(2, 0, 1, 3)
    head_results, log_totals = lax.map(attend_head, (query_heads, key_heads, value_heads))
    attended = head_results.transpose(1, 2, 0, 3).reshape(rows, width).astype(jnp.bfloat16)
    middle = inputs + matmul(attended, wo)
    normed_two, scaling_two = normalize(middle)
    norm_two = (normed_two * gain_two.astype(jnp.float32) + shift_two.astype(jnp.float32)).astype(
        jnp.bfloat16
    )
    gate = matmul(norm_two, wg)
    upward = matmul(norm_two, wu)
    sigma = jax.nn.sigmoid(gate)
    swish = gate * sigma
    hidden = (swish * upward).astype(jnp.bfloat16)
    output = (middle + matmul(hidden, wd)).astype(jnp.bfloat16).reshape(windows, steps_dev, width)
    table = loss_weight * lax.rsqrt(species_count.astype(jnp.float32) / 400.0)
    picks = species_index[:, None] == jnp.arange(table.shape[0], dtype=jnp.int32)[None, :]
    factor = jnp.sum(jnp.where(picks, table[None, :], 0.0), axis=1)
    grad_out = (factor[:, None, None] * cotangent.astype(jnp.float32)).reshape(rows, width)
    regathered = (
        lax.all_gather(query_weight, ("dp", "seq"), axis=0, tiled=True),
        lax.all_gather(key_weight, ("dp", "seq"), axis=0, tiled=True),
        lax.all_gather(value_weight, ("dp", "seq"), axis=0, tiled=True),
        lax.all_gather(out_weight, ("dp", "seq"), axis=0, tiled=True),
        lax.all_gather(gate_weight, ("dp", "seq"), axis=0, tiled=True),
        lax.all_gather(up_weight, ("dp", "seq"), axis=0, tiled=True),
        lax.all_gather(down_weight, ("dp", "seq"), axis=0, tiled=True),
        lax.all_gather(mixer_gain, ("dp", "seq"), axis=0, tiled=True),
        lax.all_gather(mixer_shift, ("dp", "seq"), axis=0, tiled=True),
        lax.all_gather(feeder_gain, ("dp", "seq"), axis=0, tiled=True),
        lax.all_gather(feeder_shift, ("dp", "seq"), axis=0, tiled=True),
    )
    wq, wk, wv, wo, wg, wu, wd, gain_one, shift_one, gain_two, shift_two = regathered
    out_low = grad_out.astype(jnp.bfloat16)
    down_part = weight_term(hidden, out_low)
    hidden_grad = through(out_low, wd)
    gate_grad = (hidden_grad * upward * sigma * (1.0 + gate * (1.0 - sigma))).astype(jnp.bfloat16)
    upward_grad = (hidden_grad * swish).astype(jnp.bfloat16)
    gate_part = weight_term(norm_two, gate_grad)
    upward_part = weight_term(norm_two, upward_grad)
    norm_two_grad = through(gate_grad, wg) + through(upward_grad, wu)
    feeder_gain_part = jnp.sum(norm_two_grad * normed_two, axis=0)
    feeder_shift_part = jnp.sum(norm_two_grad, axis=0)
    middle_grad = grad_out + norm_back(
        norm_two_grad * gain_two.astype(jnp.float32), normed_two, scaling_two
    )
    middle_low = middle_grad.astype(jnp.bfloat16)
    out_part = weight_term(attended, middle_low)
    attended_grad = through(middle_low, wo).astype(jnp.bfloat16)
    upstream_heads = attended_grad.reshape(windows, steps_dev, HEADS, HD).transpose(2, 0, 1, 3)
    query_heads_grad, key_heads_grad, value_heads_grad = lax.map(
        head_back, (query_heads, key_heads, value_heads, upstream_heads, log_totals)
    )
    key_whole = key_heads_grad.transpose(1, 2, 0, 3).reshape(windows, length, width)
    value_whole = value_heads_grad.transpose(1, 2, 0, 3).reshape(windows, length, width)
    key_mine, value_mine = (
        lax.psum_scatter(
            key_whole.astype(jnp.bfloat16), "seq", scatter_dimension=1, tiled=True
        ).astype(jnp.float32),
        lax.psum_scatter(
            value_whole.astype(jnp.bfloat16), "seq", scatter_dimension=1, tiled=True
        ).astype(jnp.float32),
    )
    query_lin_grad = (
        rotate(query_heads_grad.transpose(1, 2, 0, 3), cosine, -sine)
        .reshape(rows, width)
        .astype(jnp.bfloat16)
    )
    key_lin_grad = (
        rotate(key_mine.reshape(windows, steps_dev, HEADS, HD), cosine, -sine)
        .reshape(rows, width)
        .astype(jnp.bfloat16)
    )
    value_lin_grad = value_mine.reshape(rows, width).astype(jnp.bfloat16)
    query_part = weight_term(norm_one, query_lin_grad)
    key_part = weight_term(norm_one, key_lin_grad)
    value_part = weight_term(norm_one, value_lin_grad)
    norm_one_grad = (
        through(query_lin_grad, wq) + through(key_lin_grad, wk) + through(value_lin_grad, wv)
    )
    mixer_gain_part = jnp.sum(norm_one_grad * normed_one, axis=0)
    mixer_shift_part = jnp.sum(norm_one_grad, axis=0)
    input_grad = middle_grad + norm_back(
        norm_one_grad * gain_one.astype(jnp.float32), normed_one, scaling_one
    )
    summed = (
        lax.psum_scatter(query_part, ("dp", "seq"), scatter_dimension=0, tiled=True),
        lax.psum_scatter(key_part, ("dp", "seq"), scatter_dimension=0, tiled=True),
        lax.psum_scatter(value_part, ("dp", "seq"), scatter_dimension=0, tiled=True),
        lax.psum_scatter(out_part, ("dp", "seq"), scatter_dimension=0, tiled=True),
        lax.psum_scatter(gate_part, ("dp", "seq"), scatter_dimension=0, tiled=True),
        lax.psum_scatter(upward_part, ("dp", "seq"), scatter_dimension=0, tiled=True),
        lax.psum_scatter(down_part, ("dp", "seq"), scatter_dimension=0, tiled=True),
        lax.psum_scatter(mixer_gain_part, ("dp", "seq"), scatter_dimension=0, tiled=True),
        lax.psum_scatter(mixer_shift_part, ("dp", "seq"), scatter_dimension=0, tiled=True),
        lax.psum_scatter(feeder_gain_part, ("dp", "seq"), scatter_dimension=0, tiled=True),
        lax.psum_scatter(feeder_shift_part, ("dp", "seq"), scatter_dimension=0, tiled=True),
    )
    return (
        output,
        input_grad.reshape(windows, steps_dev, width),
        summed[0],
        summed[1],
        summed[2],
        summed[3],
        summed[4],
        summed[5],
        summed[6],
        summed[7],
        summed[8],
        summed[9],
        summed[10],
    )


def solution(mesh):
    in_specs = (
        P("dp", "seq", None),
        P("dp", "seq", None),
        P("dp"),
        P(),
        P(),
    ) + (P(("dp", "seq"), None),) * 7 + (P(("dp", "seq")),) * 4
    out_specs = (P("dp", "seq", None),) * 2 + (P(("dp", "seq"), None),) * 7 + (P(("dp", "seq")),) * 4
    fits = mesh.shape["dp"] == 8 and mesh.shape["seq"] == 4
    return jax.shard_map(
        paired if fits else general, mesh=mesh, in_specs=in_specs, out_specs=out_specs, check_vma=False
    )
```

```python
import jax
import jax.numpy as jnp
from jax import lax
from jax.experimental import pallas as pl
from jax.experimental.pallas import tpu as pltpu
from jax.sharding import PartitionSpec as P

HEADS = 16
HD = 64
MESH = pl.DeviceIdType.MESH
BF = jnp.bfloat16
F32 = jnp.float32
ANY = pl.BlockSpec(memory_space=pl.ANY)
VM = pl.BlockSpec(memory_space=pltpu.VMEM)
VMEM_BYTES = 60 << 20


def place():
    dp, z = lax.axis_index("dp"), lax.axis_index("seq")
    return dp // 4, (dp // 2) % 2, dp % 2, z


def dev(y, x, c, z):
    return ((y * 2 + x) * 2 + c, z)


def both(a, b):
    return jnp.logical_and(a, b)


def greet(y, x, c, z):
    barrier = pltpu.get_barrier_semaphore()
    peers = [dev(y, 1 - x, c, z), dev(1 - y, x, c, z), dev(y, x, 1 - c, z)]
    for k in (1, 2, 3):
        peers += [dev(y, x, c, (z + k) % 4), dev(y, x, 1 - c, (z + k) % 4)]
    for p in peers:
        pl.semaphore_signal(barrier, inc=1, device_id=p, device_id_type=MESH)
    pl.semaphore_wait(barrier, len(peers))


class Links:
    def __init__(self, send, recv, local):
        self.send, self.recv, self.local = send, recv, local
        self.n = 0
        self.m = 0
        self.open = []

    def take(self, count):
        self.n += count
        return self.n - count

    def copy(self, src, dst, device, send, recv):
        return pltpu.make_async_remote_copy(
            src_ref=src, dst_ref=dst, send_sem=self.send.at[send], recv_sem=self.recv.at[recv],
            device_id=device, device_id_type=MESH)

    def go(self, c, ok=None):
        if ok is None:
            c.start()
        else:
            pl.when(ok)(c.start)
        self.open.append((c, ok))
        return c

    def to(self, src, dst, device):
        i = self.take(1)
        return self.go(self.copy(src, dst, device, i, i))

    def later(self, src, dst, device):
        i = self.take(1)
        c = self.copy(src, dst, device, i, i)
        self.open.append((c, None))
        return c

    def here_later(self, src, dst):
        self.m += 1
        return pltpu.make_async_copy(src, dst, self.local.at[self.m - 1])

    def wanted(self, src, dst, device):
        i = self.take(1)
        return self.copy(src, dst, device, i, i)

    def here(self, src, dst):
        self.m += 1
        c = pltpu.make_async_copy(src, dst, self.local.at[self.m - 1])
        c.start()
        return c

    def drain(self):
        for c, ok in self.open:
            if ok is None:
                c.wait_send()
            else:
                pl.when(ok)(c.wait_send)
        self.open = []


def at_z(ref, zz):
    return ref.at[zz] if len(ref.shape) == 3 else ref.at[:, zz]


def add_into(dst, a, b):
    def body(i, _):
        at_z(dst, i)[...] = (at_z(a, i)[...].astype(F32) + at_z(b, i)[...].astype(F32)).astype(dst.dtype)
        return 0
    lax.fori_loop(0, 4, body, 0)


def reduce_shapes(piece, route, dtype=BF):
    part = piece[:-3] + piece[-2:]
    big = pltpu.VMEM((2,) + piece, dtype)
    if route < 2:
        return [big, big, pltpu.VMEM(piece, dtype), pltpu.VMEM((3,) + part, dtype), pltpu.VMEM(part, F32)]
    return [big, big, pltpu.VMEM((2, 3) + part, dtype), pltpu.VMEM((2,) + part, dtype), pltpu.VMEM(part, F32)]


def collect(links, at, me, route, bufs, deliver):
    y, x, c, z = me
    to_x, to_y = dev(y, 1 - x, c, z), dev(1 - y, x, c, z)
    zs = [(z + k) % 4 for k in range(4)]
    to_z = [dev(y, x, c, zs[k]) for k in range(4)]
    own, got, third, fourth, total = bufs
    out = deliver(total)

    def finish():
        for q in out:
            q.start()

    if route < 2:
        if route == 0:
            keep, away = [at(1 - y, x), at(y, x)], [at(1 - y, 1 - x), at(y, 1 - x)]
            one, two = to_x, to_y
        else:
            keep, away = [at(y, 1 - x), at(y, x)], [at(1 - y, 1 - x), at(1 - y, x)]
            one, two = to_y, to_x
        load = [links.here_later(keep[n], own.at[n]) for n in (0, 1)]
        give = [links.later(away[n], got.at[n], one) for n in (0, 1)]
        cross = links.later(own.at[0], third, two)
        over_z = [links.later(at_z(own.at[1], zs[k]), fourth.at[k - 1], to_z[k]) for k in (1, 2, 3)]

        def start():
            for q in give + load:
                q.start()

        def first():
            load[0].wait()
            give[0].wait_recv()
            add_into(own.at[0], own.at[0], got.at[0])
            cross.start()

        def second():
            load[1].wait()
            give[1].wait_recv()
            add_into(own.at[1], own.at[1], got.at[1])
            cross.wait_recv()
            add_into(own.at[1], own.at[1], third)
            for q in over_z:
                q.start()

        def last():
            for q in over_z:
                q.wait_recv()
            total[...] = (at_z(own.at[1], z)[...].astype(F32) + fourth[0].astype(F32)
                          + (fourth[1].astype(F32) + fourth[2].astype(F32)))
            finish()
        return start, first, second, last

    load = [links.here_later(at(y, xx), own.at[n]) for n, xx in ((0, 1 - x), (1, x))]
    give = [links.later(at(1 - y, xx), got.at[n], to_y) for n, xx in ((0, 1 - x), (1, x))]
    over_z = [[links.later(at_z(own.at[n], zs[k]), third.at[n, k - 1], to_z[k]) for k in (1, 2, 3)] for n in (0, 1)]
    over_x = links.later(fourth.at[0], fourth.at[1], to_x)

    def start():
        for q in give + load:
            q.start()

    def first(n):
        load[n].wait()
        give[n].wait_recv()
        add_into(own.at[n], own.at[n], got.at[n])
        for q in over_z[n]:
            q.start()

    def second():
        for q in over_z[0]:
            q.wait_recv()
        fourth[0] = (at_z(own.at[0], z)[...].astype(F32) + third[0, 0].astype(F32)
                     + (third[0, 1].astype(F32) + third[0, 2].astype(F32))).astype(fourth.dtype)
        over_x.start()

    def last():
        for q in over_z[1]:
            q.wait_recv()
        over_x.wait_recv()
        total[...] = (at_z(own.at[1], z)[...].astype(F32) + third[1, 0].astype(F32)
                      + (third[1, 1].astype(F32) + third[1, 2].astype(F32)) + fourth[1].astype(F32))
        finish()
    return start, lambda: first(0), lambda: first(1), second, last


class Outgoing:
    def __init__(self, links, me, src, dst):
        y, x, c, z = me
        recv, send = links.take(4), links.take(4)
        self.here, self.away = c == z // 2, c != z // 2
        self.remote, self.back = [], []
        for k in range(4):
            zz = (z + k) % 4
            s, d = src.at[zz], dst.at[z % 2, c]
            self.remote.append(links.copy(s, d, dev(y, x, z // 2, zz), send + k, recv + (z % 2) * 2 + c))
            links.open.append((self.remote[k], None if k else self.away))
            if k == 0:
                self.local = links.here_later(s, d)
        for i in (0, 1):
            for h in (0, 1):
                d = dst.at[i, h]
                mine = both(z == 2 * c + i, h == c)
                self.back.append((links.copy(d, d, dev(y, x, 1 - c, z), send, recv + 2 * i + h), jnp.logical_not(mine)))

    def start(self):
        for q in self.remote[1:]:
            q.start()
        pl.when(self.away)(self.remote[0].start)
        pl.when(self.here)(self.local.start)

    def finish(self):
        pl.when(self.here)(self.local.wait)
        for q, ok in self.back:
            pl.when(ok)(q.wait_recv)


def swap_halves(u):
    lane = lax.broadcasted_iota(jnp.int32, u.shape, 1) % HD
    return jnp.where(lane < HD // 2, pltpu.roll(u, 128 - HD // 2, 1), pltpu.roll(u, HD // 2, 1))


def head_mask(shape, h):
    lane = lax.broadcasted_iota(jnp.int32, shape, 1)
    return (lane < HD) if h == 0 else (lane >= HD)


def dot_t(a, b):
    return lax.dot_general(a, b, (((1,), (1,)), ((), ())), preferred_element_type=F32)


def project_step(xw, gv, w, cos, sin, n1, q, k, v, r):
    rows = pl.ds(pl.multiple_of(r * 256, 256), 256)
    u = xw[r // 2, pl.ds((r % 2) * 2, 2)].reshape(256, 1024).astype(F32)
    d = u - jnp.mean(u, axis=-1, keepdims=True)
    scaling = lax.rsqrt(jnp.mean(d * d, axis=-1, keepdims=True) + 1e-05)
    n = (d * scaling * gv[0:1, :] + gv[1:2, :]).astype(BF)
    n1[rows, :] = n
    for g in range(4):
        lanes = pl.ds(128 * g, 128)
        for j, o in ((0, q), (1, k)):
            s = jnp.dot(n, w[:, :, :, :, pl.ds(512 * j + 128 * g, 128)].reshape(1024, 128), preferred_element_type=F32)
            o[rows, lanes] = (s * cos[rows, :] + swap_halves(s) * sin[rows, :]).astype(BF)
    s = jnp.dot(n, w[:, :, :, :, pl.ds(1024, 512)].reshape(1024, 512), preferred_element_type=F32)
    v[rows, :] = s.astype(BF)


def attend_step(q, k, v, o, lse, g, i):
    lanes = pl.ds(pl.multiple_of(g * 128, 128), 128)
    rows = pl.ds(pl.multiple_of(i * 256, 256), 256)
    qs = q[rows, lanes] * jnp.asarray(HD ** -0.5, BF)
    kk, vv = k[:, lanes], v[:, lanes]
    outs, logs = [], []
    for h in (0, 1):
        qh = jnp.where(head_mask(qs.shape, h), qs, jnp.zeros_like(qs))
        s = dot_t(qh, kk)
        m = jnp.max(s, axis=-1, keepdims=True)
        e = jnp.exp(s - m)
        t = jnp.sum(e, axis=-1, keepdims=True)
        p = (e * (1.0 / t)).astype(BF)
        outs.append(jnp.dot(p, vv, preferred_element_type=F32))
        logs.append(jnp.broadcast_to(m + jnp.log(t), qs.shape))
    keep = head_mask(qs.shape, 0)
    o[rows, lanes] = jnp.where(keep, outs[0], outs[1]).astype(BF)
    lse[rows, lanes] = jnp.where(keep, logs[0], logs[1])


def attend_back_step(q, k, v, do, lse, cos, sin, dqkv, dka, dva, g, i):
    lanes = pl.ds(pl.multiple_of(g * 128, 128), 128)
    rows = pl.ds(pl.multiple_of(i * 256, 256), 256)

    @pl.when(i == 0)
    def _():
        dka[...] = jnp.zeros_like(dka)
        dva[...] = jnp.zeros_like(dva)
    kk, vv, go = k[:, lanes], v[:, lanes], do[rows, lanes]
    qs = q[rows, lanes] * jnp.asarray(HD ** -0.5, BF)
    logs = jnp.transpose(lse[rows, lanes])
    dks, dvs, dqs = [], [], []
    for h in (0, 1):
        keep = head_mask(kk.shape, h)
        zero = jnp.zeros_like(kk)
        s = dot_t(jnp.where(keep, kk, zero), qs)
        p = jnp.exp(s - logs[h * HD:h * HD + 1])
        dp = dot_t(jnp.where(keep, vv, zero), go)
        pd = p * dp
        ds = (pd - p * jnp.sum(pd, axis=0, keepdims=True)).astype(BF)
        dvs.append(jnp.dot(p.astype(BF), go, preferred_element_type=F32))
        dks.append(jnp.dot(ds, qs, preferred_element_type=F32))
        dqs.append(lax.dot_general(ds, kk, (((0,), (0,)), ((), ())), preferred_element_type=F32))
    keep = head_mask(kk.shape, 0)
    dka[...] += jnp.where(keep, dks[0], dks[1])
    dva[...] += jnp.where(keep, dvs[0], dvs[1])
    u = jnp.where(head_mask(go.shape, 0), dqs[0], dqs[1]) * HD ** -0.5
    dqkv[rows, lanes] = (u * cos[rows, :] - swap_halves(u) * sin[rows, :]).astype(BF)

    @pl.when(i == 3)
    def _():
        u = dka[...]
        dqkv[:, pl.ds(pl.multiple_of(512 + g * 128, 128), 128)] = (
            u * cos[...] - swap_halves(u) * sin[...]).astype(BF)
        dqkv[:, pl.ds(pl.multiple_of(1024 + g * 128, 128), 128)] = dva[...].astype(BF)


class Incoming:
    def __init__(self, links, me, src, mid, dst):
        y, x, c, z = me
        partner = dev(y, x, 1 - c, z)
        self.swap = [links.later(src.at[i, pl.ds((1 - c) * 128, 128)], mid.at[2 * c + i], partner) for i in (0, 1)]
        send, recv = links.take(4), links.take(4)
        self.sends, self.kept, self.got = [], [], []
        m = links.m
        links.m += 1
        for w in range(4):
            d = dst.at[0, z]
            for ok, s in ((c == w // 2, src.at[w % 2, pl.ds(c * 128, 128)]), (c != w // 2, mid.at[w])):
                away, here = both(ok, z != w), both(ok, z == w)
                q = links.copy(s, d, dev(y, x, c, w), send + w, recv + z)
                self.sends.append((q, away))
                links.open.append((q, away))
                self.kept.append((pltpu.make_async_copy(s, d, links.local.at[m]), here))
        for zz in range(4):
            d = dst.at[0, zz]
            self.got.append((links.copy(d, d, dev(y, x, c, zz), send, recv + zz), z != zz))
        self.pair = links.later(dst.at[0], dst.at[1], partner)

    def begin(self):
        for q in self.swap:
            q.start()

    def send(self):
        for q in self.swap:
            q.wait_recv()
        for q, ok in self.sends + self.kept:
            pl.when(ok)(q.start)

    def arrive(self):
        for q, ok in self.kept:
            pl.when(ok)(q.wait)
        for q, ok in self.got:
            pl.when(ok)(q.wait_recv)
        self.pair.start()

    def finish(self):
        self.pair.wait_recv()


def disperse(links, single, bundle, me, route):
    y, x, c, z = me
    to_x, to_y = dev(y, 1 - x, c, z), dev(1 - y, x, c, z)
    mine = y * 2 + x
    if route == 0:
        two, three, other = to_y, to_x, (1 - y) * 2 + x
    else:
        two, three, other = to_x, to_y, y * 2 + 1 - x
    over_z = [links.later(single(mine, z), single(mine, z), dev(y, x, c, (z + k) % 4)) for k in (1, 2, 3)]
    cross = links.later(bundle(mine), bundle(mine), two)
    last = [links.later(bundle(mine), bundle(mine), three), links.later(bundle(other), bundle(other), three)]

    def start():
        for q in over_z:
            q.start()

    def first():
        for q in over_z:
            q.wait_recv()
        cross.start()
        last[0].start()

    def second():
        cross.wait_recv()
        last[1].start()

    def finish():
        for q in last:
            q.wait_recv()
    return start, first, second, finish


FORE_PIECES = (
    ("gu", 6, 0),
    ("d", 1, 1),
    ("d", 0, 0),
    ("o", 0, 1),
    ("qkv", 1, 0),
    ("qkv", 0, 0),
    ("gu", 0, 0),
    ("gu", 7, 0),
    ("gu", 4, 1),
    ("gu", 5, 0),
    ("gu", 1, 1),
    ("gu", 2, 0),
    ("gu", 3, 1),
    ("d", 3, 1),
    ("d", 2, 0),
)
FORE_ORDER = (
    ((0, 0), (1, 0), (2, 0), (3, 0), (4, 0), (5, 0), (15, 0), (6, 0), (17, 0), (7, 0), (0, 1), (8, 0), (1, 1),
     (9, 0), (0, 2), (2, 1), (10, 0), (1, 2), (3, 1), (11, 0), (0, 3), (2, 2), (1, 3), (4, 1), (12, 0), (3, 2),
     (2, 3), (5, 1), (13, 0), (4, 2), (3, 3), (5, 2), (4, 3), (15, 1), (5, 3), (6, 1), (14, 0), (17, 1), (15, 2),
     (6, 2), (17, 2), (7, 1), (17, 3),),
    ((6, 3), (7, 2), (8, 1)), (), ((9, 1),), (), (), ((10, 1), (7, 3)), (), (), ((8, 2), (9, 2)), ((11, 1),), (), (),
    ((12, 1), (16, 0)), (), (), ((10, 2),), ((13, 1),), ((11, 2), (8, 3), (9, 3), (14, 1)), ((12, 2), (10, 3)),
    ((13, 2), (11, 3), (14, 2)), ((16, 1), (12, 3)), ((16, 2), (13, 3), (14, 3)),
)


def fore_kernel(tok, cot, wq, wk, wv, wg, wu, wo, wd, gp, cos, sin, *rest):
    (oqkv, ogu, oo, od, xh, cw, gvo, n1o, qo, ko, vo, atto, lseo, n2o, mido, gateo, upo, hido,
     tmid, cmid, gains, gv, xw, w3, n1, q, k, v, att, lse, wos, sent, came, mid, n2, wgs, wus,
     gate, up, hid, send, recv, local) = rest
    me = y, x, c, z = place()
    yx = y * 2 + x
    partner = dev(y, x, 1 - c, z)
    greet(y, x, c, z)
    links = Links(send, recv, local)
    tin, cin = Incoming(links, me, tok, tmid, xw), Incoming(links, me, cot, cmid, cw)
    tin.begin()
    loc, swaps = [], []

    def columns(src, dst, width, base):
        for g in range(4):
            lanes = pl.ds(base + width * g, width)
            swaps.append(links.to(src.at[:, pl.ds(pl.multiple_of((2 * g + 1 - c) * width, width), width)],
                                  dst.at[yx, c, z, :, lanes], partner))
            loc.append(links.here(src.at[:, pl.ds(pl.multiple_of((2 * g + c) * width, width), width)],
                                  dst.at[yx, c, z, :, lanes]))
    swaps.append(links.to(gp, gains.at[yx, c, z], partner))
    loc.append(links.here(gp, gains.at[yx, c, z]))
    for j, src in enumerate((wq, wk, wv)):
        columns(src, oqkv, 128, 512 * j)
    for j, src in enumerate((wg, wu)):
        columns(src, ogu, 512, 2048 * j)
    loc += [links.here(wo, oo.at[yx, z]), links.here(wd, od.at[yx, z])]
    cin.begin()
    work = []
    for name, index, route in FORE_PIECES:
        if name in ("qkv", "gu"):
            arr, cols = (oqkv, 768) if name == "qkv" else (ogu, 512)
            lanes = pl.ds(index * cols, cols)
            work.append(disperse(links, lambda i, zz, arr=arr, lanes=lanes: arr.at[i, :, zz, :, lanes],
                                 lambda i, arr=arr, lanes=lanes: arr.at[i, :, :, :, lanes], me, route))
        else:
            arr = oo if name == "o" else od
            rows = pl.ds(index * 32, 32)
            work.append(disperse(links, lambda i, zz, arr=arr, rows=rows: arr.at[i, zz, rows],
                                 lambda i, arr=arr, rows=rows: arr.at[i, :, rows], me, route))
    work += [(tin.send, tin.arrive, tin.finish), (cin.send, cin.arrive, cin.finish),
             disperse(links, lambda i, zz: gains.at[i, :, zz], lambda i: gains.at[i], me, 1)]
    swap = links.wanted(sent, came, partner)
    share = links.later(n2.at[pl.ds(0, 512)], n2.at[pl.ds(512, 512)], partner)
    for e in loc:
        e.wait()
    for e in swaps:
        e.wait_recv()

    def comm(slot):
        for i, stage in FORE_ORDER[slot]:
            work[i][stage]()

    keep = []

    def put(src, dst):
        keep.append(links.here(src, dst))
    comm(0)
    links.here(oqkv, w3).wait()
    for i in range(4):
        for j in (0, 1):
            gv[:, pl.ds((2 * i + j) * 128, 128)] = (gains[i, j, 0] + gains[i, j, 1]) + (gains[i, j, 2] + gains[i, j, 3])

    def rows_of(step):
        lax.fori_loop(0, 4, lambda r, _: (step(r), 0)[1], 0)
    rows_of(lambda r: project_step(xw, gv, w3, cos, sin, n1, q, k, v, r))
    for a, b in ((gv, gvo), (n1, n1o), (q, qo), (k, ko), (v, vo), (xw.at[0], xh)):
        put(a, b)
    comm(1)

    def step(t, _):
        attend_step(q, k, v, att, lse, t // 4, t % 4)
        for slot in range(2, 17):
            if FORE_ORDER[slot]:
                pl.when(t == slot - 2)(lambda slot=slot: comm(slot))
        return 0
    lax.fori_loop(0, 16, step, 0)
    comm(17)
    wload = links.here(oo, wos)
    put(att, atto)
    put(lse, lseo)
    wload.wait()

    def terms(r, out, first):
        rows = pl.ds(pl.multiple_of(r * 256, 256), 256)
        out[rows, :] = jnp.dot(att[pl.ds(pl.multiple_of(first + r * 256, 256), 256), :], wos[...].reshape(512, 1024),
                               preferred_element_type=F32)
    lax.fori_loop(0, 2, lambda r, _: (terms(r, sent, 512), 0)[1], 0)
    swap.start()
    lax.fori_loop(0, 2, lambda r, _: (terms(r, mid, 0), 0)[1], 0)
    swap.wait()

    def second_norm(r):
        rows = pl.ds(pl.multiple_of(r * 128, 128), 128)
        u = xw[0, r].astype(F32) + (mid[rows, :] + came[rows, :])
        mid[rows, :] = u
        d = u - jnp.mean(u, axis=-1, keepdims=True)
        scaling = lax.rsqrt(jnp.mean(d * d, axis=-1, keepdims=True) + 1e-05)
        n2[rows, :] = (d * scaling * gv[2:3, :] + gv[3:4, :]).astype(BF)
    rows_of(second_norm)
    share.start()
    put(mid, mido)
    comm(18)
    share.wait_recv()
    put(n2, n2o)
    for j in range(4):
        if j:
            comm(18 + j)
        lanes = pl.ds(512 * j, 512)
        lg = links.here(ogu.at[:, :, :, :, lanes], wgs)
        lu = links.here(ogu.at[:, :, :, :, pl.ds(2048 + 512 * j, 512)], wus)
        lg.wait()
        lu.wait()

        def hidden_units(r, lanes=lanes):
            rows = pl.ds(pl.multiple_of(r * 256, 256), 256)
            n = n2[rows, :]
            a = jnp.dot(n, wgs[...].reshape(1024, 512), preferred_element_type=F32)
            b = jnp.dot(n, wus[...].reshape(1024, 512), preferred_element_type=F32)
            hid[rows, lanes] = (a * jax.nn.sigmoid(a) * b).astype(BF)
            gate[rows, lanes] = a.astype(BF)
            up[rows, lanes] = b.astype(BF)
        rows_of(hidden_units)
        for a, b in ((hid, hido), (gate, gateo), (up, upo)):
            put(a.at[:, lanes], b.at[:, lanes])
    comm(22)
    for e in keep:
        e.wait()
    links.drain()


def fore(tok, cot, wq, wk, wv, wg, wu, wo, wd, gp, cos, sin):
    S = jax.ShapeDtypeStruct
    V = pltpu.VMEM
    return pl.pallas_call(
        fore_kernel,
        out_shape=(
            S((4, 2, 4, 32, 1536), BF), S((4, 2, 4, 32, 4096), BF), S((4, 4, 32, 1024), BF), S((4, 4, 128, 1024), BF),
            S((4, 128, 1024), BF), S((2, 4, 128, 1024), BF), S((8, 1024), F32), S((1024, 1024), BF),
            S((1024, 512), BF), S((1024, 512), BF), S((1024, 512), BF), S((1024, 512), BF), S((1024, 512), F32),
            S((1024, 1024), BF), S((512, 1024), F32), S((1024, 2048), BF), S((1024, 2048), BF), S((1024, 2048), BF),
        ),
        in_specs=[VM] * 12,
        out_specs=[ANY] * 18,
        scratch_shapes=[
            V((4, 128, 1024), BF), V((4, 128, 1024), BF), V((4, 2, 4, 8, 128), F32), V((8, 1024), F32),
            V((2, 4, 128, 1024), BF), V((4, 2, 4, 32, 1536), BF), V((1024, 1024), BF),
            V((1024, 512), BF), V((1024, 512), BF), V((1024, 512), BF), V((1024, 512), BF), V((1024, 512), F32),
            V((4, 4, 32, 1024), BF), V((512, 1024), F32), V((512, 1024), F32), V((512, 1024), F32),
            V((1024, 1024), BF), V((4, 2, 4, 32, 512), BF), V((4, 2, 4, 32, 512), BF),
            V((1024, 2048), BF), V((1024, 2048), BF), V((1024, 2048), BF),
            pltpu.SemaphoreType.DMA((200,)),
            pltpu.SemaphoreType.DMA((200,)),
            pltpu.SemaphoreType.DMA((72,)),
        ],
        compiler_params=pltpu.CompilerParams(collective_id=0, has_side_effects=True, vmem_limit_bytes=67043328),
    )(tok, cot, wq, wk, wv, wg, wu, wo, wd, gp, cos, sin)


PIECES = (
    ("d", 3, 2),
    ("d", 0, 1),
    ("gu", 5, 0),
    ("o", 0, 0),
    ("gu", 1, 0),
    ("gu", 3, 0),
    ("qkv", 1, 1),
    ("qkv", 0, 1),
    ("d", 1, 0),
    ("gu", 2, 0),
    ("gu", 7, 1),
    ("gu", 4, 0),
    ("d", 2, 0),
    ("gu", 0, 2),
    ("gu", 6, 1),
)
SHAPES = {"d": (4, 32, 1024), "o": (4, 32, 1024), "gu": (2, 4, 32, 512), "qkv": (2, 4, 32, 768)}
ORDER = (
    ((15, 0), (0, 0), (1, 0), (2, 0)), (), (), ((0, 1), (2, 1), (3, 0), (13, 0)), (), ((0, 2),), (),
    ((1, 1), (3, 1), (4, 0)), (), (), ((1, 2), (2, 2)), ((15, 1), (4, 1), (5, 0), (13, 1)), ((0, 3), (13, 2)), (),
    ((3, 2), (5, 1), (8, 0)), ((0, 4), (1, 3), (4, 2), (2, 3)), ((5, 2), (8, 1), (9, 0), (13, 3)),
    ((6, 0), (7, 0), (8, 2), (9, 1), (11, 0)),
    ((3, 3), (16, 0), (4, 3), (6, 1), (5, 3), (10, 0), (11, 1), (12, 0), (13, 4), (17, 0), (8, 3), (6, 2), (7, 1),
     (14, 0), (12, 1), (17, 1), (9, 2), (7, 2), (16, 1), (10, 1), (10, 2), (6, 3), (11, 2), (9, 3), (14, 1),
     (14, 2), (7, 3), (12, 2), (17, 2), (10, 3), (11, 3), (14, 3), (12, 3), (17, 3),),

)


def total_over_devices(links, me, acc, got):
    y, x, c, z = me
    hops = [links.wanted(acc, got.at[i], d) for i, d in
            enumerate((dev(y, x, 1 - c, z), dev(y, 1 - x, c, z), dev(1 - y, x, c, z)))]
    over_z = [links.wanted(acc, got.at[2 + k], dev(y, x, c, (z + k) % 4)) for k in (1, 2, 3)]

    def settle(i):
        hops[i].wait()
        acc[...] += got[i]

    def chip():
        hops[0].start()
        settle(0)
        hops[1].start()

    def second():
        settle(1)
        hops[2].start()

    def third():
        settle(2)
        for q in over_z:
            q.start()

    def last():
        for q in over_z:
            q.wait()
        acc[...] += got[3] + (got[4] + got[5])
    return chip, second, third, last


def back_kernel(dgu, do, dd, out16, q, k, v, ag, lse, cos, sin, n1, w, xh, mg, gain, gterms, *rest):
    fqkv, fgu, fo, fd, fgain, out_w, ig_w = rest[:7]
    scratch = list(rest[7:])
    dqkv, dka, dva, dw, sent, came, ig, gacc, ggot, send, recv, local = scratch[-12:]
    me = y, x, c, z = place()
    partner = dev(y, x, 1 - c, z)
    greet(y, x, c, z)
    links = Links(send, recv, local)
    work = []
    finals = []
    for name, index, route in PIECES:
        bufs = [scratch.pop(0) for _ in range(5)]
        if name in ("qkv", "gu"):
            src, dst = (dw, fqkv) if name == "qkv" else (dgu, fgu)
            cols = SHAPES[name][3]
            lanes = pl.ds(index * cols, cols)

            def at(yy, xx, src=src, lanes=lanes):
                return src.at[yy * 2 + xx, :, :, :, lanes]

            def deliver(total, dst=dst, lanes=lanes):
                there = links.later(total.at[1 - c], dst.at[c, :, lanes], partner)
                here = links.here_later(total.at[c], dst.at[c, :, lanes])
                finals.extend((there.wait_recv, here.wait))
                return there, here
        else:
            src, dst = (dd, fd) if name == "d" else (do, fo)
            rows = pl.ds(index * 32, 32)

            def at(yy, xx, src=src, rows=rows):
                return src.at[yy * 2 + xx, :, rows]

            def deliver(total, dst=dst, rows=rows):
                here = links.here_later(total, dst.at[rows])
                finals.append(here.wait)
                return (here,)
        work.append(collect(links, at, me, route, bufs, deliver))

    o1 = Outgoing(links, me, out16, out_w)
    o2 = Outgoing(links, me, ig, ig_w)
    work += [(o1.start, o1.finish), (o2.start, o2.finish), total_over_devices(links, me, gacc, ggot)]
    swap = links.wanted(sent, came, partner)

    def comm(slot):
        for i, stage in ORDER[slot]:
            work[i][stage]()
    comm(0)

    def step(t, _):
        attend_back_step(q, k, v, ag, lse, cos, sin, dqkv, dka, dva, t // 4, t % 4)
        for slot in range(1, 16):
            if ORDER[slot]:
                pl.when(t == slot - 1)(lambda slot=slot: comm(slot))
        return 0
    lax.fori_loop(0, 16, step, 0)
    comm(16)

    def weight_chunk(j, _):
        cols = pl.ds(pl.multiple_of(j * 256, 256), 256)
        u = lax.dot_general(n1[...], dqkv[:, cols], (((0,), (0,)), ((), ())), preferred_element_type=F32)
        dw[:, :, :, :, cols] = u.astype(BF).reshape(4, 2, 4, 32, 256)
        return 0
    lax.fori_loop(0, 6, weight_chunk, 0)
    comm(17)
    for r in (2, 3):
        sent[pl.ds((r - 2) * 256, 256), :] = dot_t(dqkv[pl.ds(r * 256, 256), :], w[...])
    swap.start()
    mine = [dot_t(dqkv[pl.ds(r * 256, 256), :], w[...]) for r in (0, 1)]
    swap.wait()
    sums = [jnp.zeros((1, 1024), F32)] * 2
    for r in (0, 1):
        rows = pl.ds(r * 256, 256)
        gn = mine[r] + came[rows, :]
        u = xh[rows, :].astype(F32)
        d = u - jnp.mean(u, axis=-1, keepdims=True)
        scaling = lax.rsqrt(jnp.mean(d * d, axis=-1, keepdims=True) + 1e-05)
        normed = d * scaling
        sums = [sums[0] + jnp.sum(gn * normed, axis=0, keepdims=True), sums[1] + jnp.sum(gn, axis=0, keepdims=True)]
        up = gn * gain[...]
        out = mg[rows, :] + scaling * (up - jnp.mean(up, axis=-1, keepdims=True)
                                       - normed * jnp.mean(up * normed, axis=-1, keepdims=True))
        ig[pl.ds(2 * r, 2)] = out.astype(BF).reshape(2, 128, 1024)
    gacc[...] = gterms[...]
    gacc[0:1, :] = sums[0]
    gacc[1:2, :] = sums[1]
    comm(18)
    finals.append(links.here(gacc, fgain).wait)
    for f in finals:
        f()
    links.drain()


def back(dgu, do, dd, out16, q, k, v, ag, lse, cos, sin, n1, w, xh, mg, gain, gterms):
    scratch = []
    for name, index, route in PIECES:
        scratch += reduce_shapes(SHAPES[name], route)
    return pl.pallas_call(
        back_kernel,
        out_shape=(
            jax.ShapeDtypeStruct((2, 32, 1536), F32),
            jax.ShapeDtypeStruct((2, 32, 4096), F32),
            jax.ShapeDtypeStruct((32, 1024), F32),
            jax.ShapeDtypeStruct((128, 1024), F32),
            jax.ShapeDtypeStruct((8, 1024), F32),
            jax.ShapeDtypeStruct((2, 2, 128, 1024), BF),
            jax.ShapeDtypeStruct((2, 2, 128, 1024), BF),
        ),
        in_specs=[ANY] * 4 + [VM] * 13,
        out_specs=[ANY] * 7,
        scratch_shapes=scratch + [
            pltpu.VMEM((1024, 1536), BF),
            pltpu.VMEM((1024, 128), F32),
            pltpu.VMEM((1024, 128), F32),
            pltpu.VMEM((4, 2, 4, 32, 1536), BF),
            pltpu.VMEM((512, 1024), F32),
            pltpu.VMEM((512, 1024), F32),
            pltpu.VMEM((4, 128, 1024), BF),
            pltpu.VMEM((8, 1024), F32),
            pltpu.VMEM((6, 8, 1024), F32),
            pltpu.SemaphoreType.DMA((192,)),
            pltpu.SemaphoreType.DMA((192,)),
            pltpu.SemaphoreType.DMA((64,)),
        ],
        compiler_params=pltpu.CompilerParams(collective_id=1, has_side_effects=True, vmem_limit_bytes=67043328),
    )(dgu.reshape(4, 2, 4, 32, 4096), do.reshape(4, 4, 32, 1024), dd.reshape(4, 4, 128, 1024), out16,
      q, k, v, ag, lse, cos, sin, n1, w, xh, mg, gain, gterms)


def matmul(left, right):
    return jnp.dot(left, right, preferred_element_type=jnp.float32)


def weight_term(left, right):
    return lax.dot_general(
        left, right, (((0,), (0,)), ((), ())), preferred_element_type=jnp.float32
    )


def through(left, weight):
    return lax.dot_general(
        left, weight, (((1,), (1,)), ((), ())), preferred_element_type=jnp.float32
    )


def normalize(values):
    center = jnp.mean(values, axis=-1, keepdims=True)
    centered = values - center
    variance = jnp.mean(centered * centered, axis=-1, keepdims=True)
    scaling = lax.rsqrt(variance + 1e-05)
    return (centered * scaling, scaling)


def norm_back(upstream, normed, scaling):
    first = jnp.mean(upstream, axis=-1, keepdims=True)
    second = jnp.mean(upstream * normed, axis=-1, keepdims=True)
    return scaling * (upstream - first - normed * second)


def half_tables(c):
    row = jnp.arange(1024, dtype=jnp.int32)
    half, zz, r = row // 512, (row // 128) % 4, row % 128
    owner = jnp.where(half == 0, c, 1 - c)
    positions = (zz * 256 + owner * 128 + r).astype(jnp.float32)
    lane = jnp.arange(128, dtype=jnp.int32)
    freqs = 10000.0 ** (-2.0 * (lane % 32).astype(jnp.float32) / HD)
    angle = positions[:, None] * freqs[None, :]
    return jnp.cos(angle), jnp.where(lane % HD < HD // 2, -1.0, 1.0)[None, :] * jnp.sin(angle)


def paired(
    tokens,
    cotangent,
    species_index,
    species_count,
    loss_weight,
    query_weight,
    key_weight,
    value_weight,
    out_weight,
    gate_weight,
    up_weight,
    down_weight,
    mixer_gain,
    mixer_shift,
    feeder_gain,
    feeder_shift,
):
    dp, z = lax.axis_index("dp"), lax.axis_index("seq")
    c = dp % 2
    flip = [(i, i ^ 1) for i in range(8)]

    def other_core(a):
        return lax.ppermute(a, "dp", flip)

    small = jnp.stack([mixer_gain, mixer_shift, feeder_gain, feeder_shift]).astype(F32)
    table = loss_weight * lax.rsqrt(species_count.astype(jnp.float32) / 400.0)
    picks = species_index[:, None] == jnp.arange(table.shape[0], dtype=jnp.int32)[None, :]
    factors = jnp.sum(jnp.where(picks, table[None, :], 0.0), axis=1)
    lane = jnp.arange(128, dtype=jnp.int32)[None, :]
    small = jnp.where(lane // 32 == z, jnp.tile(small, (1, 4)), 0.0)
    fifth = jnp.where(z == 0, jnp.where(lane == 0, factors[0], jnp.where(lane == 1, factors[1], 0.0)), 0.0)
    small = jnp.concatenate([small, fifth, jnp.zeros((3, 128), F32)], 0)
    cos, sin = half_tables(c)
    (wqkv, wgu, wo, wd, xh, cw, gv, norm_one, q, k, v, attended, lse, norm_two, middle, gate, upward, hidden) = fore(
        tokens, cotangent, query_weight, key_weight, value_weight, gate_weight, up_weight, out_weight, down_weight,
        small, cos, sin)
    wqkv, wgu, wo, wd = (wqkv.reshape(1024, 1536), wgu.reshape(1024, 4096), wo.reshape(512, 1024),
                         wd.reshape(2048, 1024))
    cot = cw.reshape(1024, 1024)
    xh = xh.reshape(512, 1024)
    gain_one, gain_two = gv[0:1], gv[2:3]
    factor = lax.dynamic_slice(gv, (4, (2 * (dp // 2) + z // 2) * 128 + z % 2), (1, 1))[0, 0]

    def combine(part):
        return part[:512] + other_core(part[512:])

    normed_two, scaling_two = normalize(middle)
    gate, upward = gate.astype(F32), upward.astype(F32)
    sigma = jax.nn.sigmoid(gate)
    swish = gate * sigma
    output = (middle + combine(matmul(hidden, wd))).astype(BF)

    grad_out = factor * cot.astype(F32)
    out_low = grad_out.astype(BF)
    down_part = weight_term(hidden, out_low).astype(BF)
    hidden_grad = through(out_low, wd)
    gate_grad = (hidden_grad * upward * sigma * (1.0 + gate * (1.0 - sigma))).astype(BF)
    upward_grad = (hidden_grad * swish).astype(BF)
    both_grad = jnp.concatenate([gate_grad, upward_grad], 1)
    gu_part = weight_term(norm_two, both_grad).astype(BF)
    norm_two_grad = combine(through(both_grad, wgu))
    feeder_gain_part = jnp.sum(norm_two_grad * normed_two, axis=0)
    feeder_shift_part = jnp.sum(norm_two_grad, axis=0)
    middle_grad = grad_out[:512] + norm_back(norm_two_grad * gain_two, normed_two, scaling_two)
    middle_low = middle_grad.astype(BF)
    middle_low = jnp.concatenate([middle_low, other_core(middle_low)], 0)
    out_part = weight_term(attended, middle_low).astype(BF)
    attended_grad = through(middle_low, wo).astype(BF)
    terms = jnp.zeros((8, 1024), F32).at[2].set(feeder_gain_part).at[3].set(feeder_shift_part)
    gqkv, ggu, go, gd, ggain, out, ig = back(
        gu_part, out_part, down_part, output.reshape(4, 128, 1024), q, k, v, attended_grad, lse, cos, sin,
        norm_one, wqkv, xh, middle_grad, gain_one, terms)
    ggain = lax.dynamic_slice_in_dim(ggain[:4], (dp * 4 + z) * 32, 32, 1)
    gqkv = gqkv.reshape(2, 32, 3, 4, 128).transpose(2, 1, 3, 0, 4).reshape(3, 32, 1024)
    ggu = ggu.reshape(2, 32, 2, 4, 512).transpose(2, 1, 3, 0, 4).reshape(2, 32, 4096)
    return (
        out.reshape(2, 256, 1024),
        ig.reshape(2, 256, 1024).astype(F32),
        gqkv[0],
        gqkv[1],
        gqkv[2],
        go,
        ggu[0],
        ggu[1],
        gd,
        ggain[0],
        ggain[1],
        ggain[2],
        ggain[3],
    )


def tables(start, count):
    half = HD // 2
    positions = (start + jnp.arange(count, dtype=jnp.int32)).astype(jnp.float32)
    freqs = 10000.0 ** (-2.0 * jnp.arange(half, dtype=jnp.float32) / HD)
    angle = positions[:, None] * freqs[None, :]
    return (jnp.cos(angle)[:, None, :], jnp.sin(angle)[:, None, :])


def rotate(values, cosine, sine):
    half = HD // 2
    first = values[..., :half]
    second = values[..., half:]
    return jnp.concatenate(
        [first * cosine - second * sine, second * cosine + first * sine], axis=-1
    )


def attend_head(operands):
    query_head, key_head, value_head = operands
    scores = jnp.einsum(
        "wtd,wsd->wts", query_head, key_head, preferred_element_type=jnp.float32
    ) * HD ** (-0.5)
    peak = jnp.max(scores, axis=-1, keepdims=True)
    raised = jnp.exp(scores - peak)
    total = jnp.sum(raised, axis=-1, keepdims=True)
    probs = (raised / total).astype(jnp.bfloat16)
    result = jnp.einsum("wts,wsd->wtd", probs, value_head, preferred_element_type=jnp.float32)
    return (result, (peak + jnp.log(total))[..., 0])


def head_back(operands):
    query_head, key_head, value_head, upstream, log_total = operands
    scores = jnp.einsum(
        "wtd,wsd->wts", query_head, key_head, preferred_element_type=jnp.float32
    ) * HD ** (-0.5)
    probs = jnp.exp(scores - log_total[..., None])
    prob_grads = jnp.einsum(
        "wtd,wsd->wts", upstream, value_head, preferred_element_type=jnp.float32
    )
    inner = jnp.sum(probs * prob_grads, axis=-1, keepdims=True)
    score_grads = (probs * (prob_grads - inner)).astype(jnp.bfloat16)
    query_grad = jnp.einsum(
        "wts,wsd->wtd", score_grads, key_head, preferred_element_type=jnp.float32
    ) * HD ** (-0.5)
    key_grad = jnp.einsum(
        "wts,wtd->wsd", score_grads, query_head, preferred_element_type=jnp.float32
    ) * HD ** (-0.5)
    value_grad = jnp.einsum(
        "wts,wtd->wsd", probs.astype(jnp.bfloat16), upstream, preferred_element_type=jnp.float32
    )
    return (query_grad, key_grad, value_grad)


def general(
    tokens,
    cotangent,
    species_index,
    species_count,
    loss_weight,
    query_weight,
    key_weight,
    value_weight,
    out_weight,
    gate_weight,
    up_weight,
    down_weight,
    mixer_gain,
    mixer_shift,
    feeder_gain,
    feeder_shift,
):
    gathered = (
        lax.all_gather(query_weight, ("dp", "seq"), axis=0, tiled=True),
        lax.all_gather(key_weight, ("dp", "seq"), axis=0, tiled=True),
        lax.all_gather(value_weight, ("dp", "seq"), axis=0, tiled=True),
        lax.all_gather(out_weight, ("dp", "seq"), axis=0, tiled=True),
        lax.all_gather(gate_weight, ("dp", "seq"), axis=0, tiled=True),
        lax.all_gather(up_weight, ("dp", "seq"), axis=0, tiled=True),
        lax.all_gather(down_weight, ("dp", "seq"), axis=0, tiled=True),
        lax.all_gather(mixer_gain, ("dp", "seq"), axis=0, tiled=True),
        lax.all_gather(mixer_shift, ("dp", "seq"), axis=0, tiled=True),
        lax.all_gather(feeder_gain, ("dp", "seq"), axis=0, tiled=True),
        lax.all_gather(feeder_shift, ("dp", "seq"), axis=0, tiled=True),
    )
    wq, wk, wv, wo, wg, wu, wd, gain_one, shift_one, gain_two, shift_two = gathered
    windows, steps_dev, width = tokens.shape
    rows = windows * steps_dev
    start = lax.axis_index("seq") * steps_dev
    cosine, sine = tables(start, steps_dev)
    inputs = tokens.astype(jnp.float32).reshape(rows, width)
    normed_one, scaling_one = normalize(inputs)
    norm_one = (normed_one * gain_one.astype(jnp.float32) + shift_one.astype(jnp.float32)).astype(
        jnp.bfloat16
    )
    queries = rotate(
        matmul(norm_one, wq).reshape(windows, steps_dev, HEADS, HD), cosine, sine
    ).astype(jnp.bfloat16)
    keys = rotate(matmul(norm_one, wk).reshape(windows, steps_dev, HEADS, HD), cosine, sine).astype(
        jnp.bfloat16
    )
    values = matmul(norm_one, wv).astype(jnp.bfloat16)
    all_keys, all_values = (
        lax.all_gather(keys.reshape(windows, steps_dev, width), "seq", axis=1, tiled=True),
        lax.all_gather(values.reshape(windows, steps_dev, width), "seq", axis=1, tiled=True),
    )
    length = all_keys.shape[1]
    query_heads = queries.transpose(2, 0, 1, 3)
    key_heads = all_keys.reshape(windows, length, HEADS, HD).transpose(2, 0, 1, 3)
    value_heads = all_values.reshape(windows, length, HEADS, HD).transpose(2, 0, 1, 3)
    head_results, log_totals = lax.map(attend_head, (query_heads, key_heads, value_heads))
    attended = head_results.transpose(1, 2, 0, 3).reshape(rows, width).astype(jnp.bfloat16)
    middle = inputs + matmul(attended, wo)
    normed_two, scaling_two = normalize(middle)
    norm_two = (normed_two * gain_two.astype(jnp.float32) + shift_two.astype(jnp.float32)).astype(
        jnp.bfloat16
    )
    gate = matmul(norm_two, wg)
    upward = matmul(norm_two, wu)
    sigma = jax.nn.sigmoid(gate)
    swish = gate * sigma
    hidden = (swish * upward).astype(jnp.bfloat16)
    output = (middle + matmul(hidden, wd)).astype(jnp.bfloat16).reshape(windows, steps_dev, width)
    table = loss_weight * lax.rsqrt(species_count.astype(jnp.float32) / 400.0)
    picks = species_index[:, None] == jnp.arange(table.shape[0], dtype=jnp.int32)[None, :]
    factor = jnp.sum(jnp.where(picks, table[None, :], 0.0), axis=1)
    grad_out = (factor[:, None, None] * cotangent.astype(jnp.float32)).reshape(rows, width)
    regathered = (
        lax.all_gather(query_weight, ("dp", "seq"), axis=0, tiled=True),
        lax.all_gather(key_weight, ("dp", "seq"), axis=0, tiled=True),
        lax.all_gather(value_weight, ("dp", "seq"), axis=0, tiled=True),
        lax.all_gather(out_weight, ("dp", "seq"), axis=0, tiled=True),
        lax.all_gather(gate_weight, ("dp", "seq"), axis=0, tiled=True),
        lax.all_gather(up_weight, ("dp", "seq"), axis=0, tiled=True),
        lax.all_gather(down_weight, ("dp", "seq"), axis=0, tiled=True),
        lax.all_gather(mixer_gain, ("dp", "seq"), axis=0, tiled=True),
        lax.all_gather(mixer_shift, ("dp", "seq"), axis=0, tiled=True),
        lax.all_gather(feeder_gain, ("dp", "seq"), axis=0, tiled=True),
        lax.all_gather(feeder_shift, ("dp", "seq"), axis=0, tiled=True),
    )
    wq, wk, wv, wo, wg, wu, wd, gain_one, shift_one, gain_two, shift_two = regathered
    out_low = grad_out.astype(jnp.bfloat16)
    down_part = weight_term(hidden, out_low)
    hidden_grad = through(out_low, wd)
    gate_grad = (hidden_grad * upward * sigma * (1.0 + gate * (1.0 - sigma))).astype(jnp.bfloat16)
    upward_grad = (hidden_grad * swish).astype(jnp.bfloat16)
    gate_part = weight_term(norm_two, gate_grad)
    upward_part = weight_term(norm_two, upward_grad)
    norm_two_grad = through(gate_grad, wg) + through(upward_grad, wu)
    feeder_gain_part = jnp.sum(norm_two_grad * normed_two, axis=0)
    feeder_shift_part = jnp.sum(norm_two_grad, axis=0)
    middle_grad = grad_out + norm_back(
        norm_two_grad * gain_two.astype(jnp.float32), normed_two, scaling_two
    )
    middle_low = middle_grad.astype(jnp.bfloat16)
    out_part = weight_term(attended, middle_low)
    attended_grad = through(middle_low, wo).astype(jnp.bfloat16)
    upstream_heads = attended_grad.reshape(windows, steps_dev, HEADS, HD).transpose(2, 0, 1, 3)
    query_heads_grad, key_heads_grad, value_heads_grad = lax.map(
        head_back, (query_heads, key_heads, value_heads, upstream_heads, log_totals)
    )
    key_whole = key_heads_grad.transpose(1, 2, 0, 3).reshape(windows, length, width)
    value_whole = value_heads_grad.transpose(1, 2, 0, 3).reshape(windows, length, width)
    key_mine, value_mine = (
        lax.psum_scatter(
            key_whole.astype(jnp.bfloat16), "seq", scatter_dimension=1, tiled=True
        ).astype(jnp.float32),
        lax.psum_scatter(
            value_whole.astype(jnp.bfloat16), "seq", scatter_dimension=1, tiled=True
        ).astype(jnp.float32),
    )
    query_lin_grad = (
        rotate(query_heads_grad.transpose(1, 2, 0, 3), cosine, -sine)
        .reshape(rows, width)
        .astype(jnp.bfloat16)
    )
    key_lin_grad = (
        rotate(key_mine.reshape(windows, steps_dev, HEADS, HD), cosine, -sine)
        .reshape(rows, width)
        .astype(jnp.bfloat16)
    )
    value_lin_grad = value_mine.reshape(rows, width).astype(jnp.bfloat16)
    query_part = weight_term(norm_one, query_lin_grad)
    key_part = weight_term(norm_one, key_lin_grad)
    value_part = weight_term(norm_one, value_lin_grad)
    norm_one_grad = (
        through(query_lin_grad, wq) + through(key_lin_grad, wk) + through(value_lin_grad, wv)
    )
    mixer_gain_part = jnp.sum(norm_one_grad * normed_one, axis=0)
    mixer_shift_part = jnp.sum(norm_one_grad, axis=0)
    input_grad = middle_grad + norm_back(
        norm_one_grad * gain_one.astype(jnp.float32), normed_one, scaling_one
    )
    summed = (
        lax.psum_scatter(query_part, ("dp", "seq"), scatter_dimension=0, tiled=True),
        lax.psum_scatter(key_part, ("dp", "seq"), scatter_dimension=0, tiled=True),
        lax.psum_scatter(value_part, ("dp", "seq"), scatter_dimension=0, tiled=True),
        lax.psum_scatter(out_part, ("dp", "seq"), scatter_dimension=0, tiled=True),
        lax.psum_scatter(gate_part, ("dp", "seq"), scatter_dimension=0, tiled=True),
        lax.psum_scatter(upward_part, ("dp", "seq"), scatter_dimension=0, tiled=True),
        lax.psum_scatter(down_part, ("dp", "seq"), scatter_dimension=0, tiled=True),
        lax.psum_scatter(mixer_gain_part, ("dp", "seq"), scatter_dimension=0, tiled=True),
        lax.psum_scatter(mixer_shift_part, ("dp", "seq"), scatter_dimension=0, tiled=True),
        lax.psum_scatter(feeder_gain_part, ("dp", "seq"), scatter_dimension=0, tiled=True),
        lax.psum_scatter(feeder_shift_part, ("dp", "seq"), scatter_dimension=0, tiled=True),
    )
    return (
        output,
        input_grad.reshape(windows, steps_dev, width),
        summed[0],
        summed[1],
        summed[2],
        summed[3],
        summed[4],
        summed[5],
        summed[6],
        summed[7],
        summed[8],
        summed[9],
        summed[10],
    )


def solution(mesh):
    in_specs = (
        P("dp", "seq", None),
        P("dp", "seq", None),
        P("dp"),
        P(),
        P(),
    ) + (P(("dp", "seq"), None),) * 7 + (P(("dp", "seq")),) * 4
    out_specs = (P("dp", "seq", None),) * 2 + (P(("dp", "seq"), None),) * 7 + (P(("dp", "seq")),) * 4
    fits = mesh.shape["dp"] == 8 and mesh.shape["seq"] == 4
    return jax.shard_map(
        paired if fits else general, mesh=mesh, in_specs=in_specs, out_specs=out_specs, check_vma=False
    )
```

```python
import jax
import jax.numpy as jnp
from jax import lax
from jax.experimental import pallas as pl
from jax.experimental.pallas import tpu as pltpu
from jax.sharding import PartitionSpec as P

HEADS = 16
HD = 64
MESH = pl.DeviceIdType.MESH
BF = jnp.bfloat16
F32 = jnp.float32
ANY = pl.BlockSpec(memory_space=pl.ANY)
VM = pl.BlockSpec(memory_space=pltpu.VMEM)
VMEM_BYTES = 60 << 20


def place():
    dp, z = lax.axis_index("dp"), lax.axis_index("seq")
    return dp // 4, (dp // 2) % 2, dp % 2, z


def dev(y, x, c, z):
    return ((y * 2 + x) * 2 + c, z)


def both(a, b):
    return jnp.logical_and(a, b)


def greet(y, x, c, z):
    barrier = pltpu.get_barrier_semaphore()
    peers = [dev(y, 1 - x, c, z), dev(1 - y, x, c, z), dev(y, x, 1 - c, z)]
    for k in (1, 2, 3):
        peers += [dev(y, x, c, (z + k) % 4), dev(y, x, 1 - c, (z + k) % 4)]
    for p in peers:
        pl.semaphore_signal(barrier, inc=1, device_id=p, device_id_type=MESH)
    pl.semaphore_wait(barrier, len(peers))


class Links:
    def __init__(self, send, recv, local):
        self.send, self.recv, self.local = send, recv, local
        self.n = 0
        self.m = 0
        self.open = []

    def take(self, count):
        self.n += count
        return self.n - count

    def copy(self, src, dst, device, send, recv):
        return pltpu.make_async_remote_copy(
            src_ref=src, dst_ref=dst, send_sem=self.send.at[send], recv_sem=self.recv.at[recv],
            device_id=device, device_id_type=MESH)

    def go(self, c, ok=None):
        if ok is None:
            c.start()
        else:
            pl.when(ok)(c.start)
        self.open.append((c, ok))
        return c

    def to(self, src, dst, device):
        i = self.take(1)
        return self.go(self.copy(src, dst, device, i, i))

    def later(self, src, dst, device):
        i = self.take(1)
        c = self.copy(src, dst, device, i, i)
        self.open.append((c, None))
        return c

    def here_later(self, src, dst):
        self.m += 1
        return pltpu.make_async_copy(src, dst, self.local.at[self.m - 1])

    def wanted(self, src, dst, device):
        i = self.take(1)
        return self.copy(src, dst, device, i, i)

    def here(self, src, dst):
        self.m += 1
        c = pltpu.make_async_copy(src, dst, self.local.at[self.m - 1])
        c.start()
        return c

    def drain(self):
        for c, ok in self.open:
            if ok is None:
                c.wait_send()
            else:
                pl.when(ok)(c.wait_send)
        self.open = []


def at_z(ref, zz):
    return ref.at[zz] if len(ref.shape) == 3 else ref.at[:, zz]


def add_into(dst, *terms):
    def body(i, _):
        total = at_z(terms[0], i)[...].astype(F32)
        for t in terms[1:]:
            total += at_z(t, i)[...].astype(F32)
        at_z(dst, i)[...] = total.astype(dst.dtype)
        return 0
    lax.fori_loop(0, 4, body, 0)


def reduce_shapes(piece, route):
    part = piece[:-3] + piece[-2:]
    if route < 2:
        later = [pltpu.VMEM(piece, BF), pltpu.VMEM((3,) + part, BF)]
    else:
        later = [pltpu.VMEM((2, 3) + part, BF), pltpu.VMEM((2,) + part, BF)]
    return [pltpu.VMEM((2,) + piece, BF)] + later + [pltpu.VMEM(part, F32)]


def collect(links, at, me, route, bufs, deliver):
    y, x, c, z = me
    to_x, to_y = dev(y, 1 - x, c, z), dev(1 - y, x, c, z)
    zs = [(z + k) % 4 for k in range(4)]
    to_z = [dev(y, x, c, zs[k]) for k in range(4)]
    got, third, fourth, total = bufs
    out = deliver(total)

    def finish():
        for q in out:
            q.start()

    if route == 0:
        own, away = [at(1 - y, x), at(y, x)], [at(1 - y, 1 - x), at(y, 1 - x)]
        one, two = to_x, to_y
    else:
        own, away = [at(y, 1 - x), at(y, x)], [at(1 - y, 1 - x), at(1 - y, x)]
        one, two = to_y, to_x
    give = [links.later(away[n], got.at[n], one) for n in (0, 1)]

    def start():
        for q in give:
            q.start()

    if route < 2:
        cross = links.later(own[0], third, two)
        over_z = [links.later(at_z(own[1], zs[k]), fourth.at[k - 1], to_z[k]) for k in (1, 2, 3)]

        def first():
            give[0].wait_recv()
            add_into(own[0], own[0], got.at[0])
            cross.start()

        def second():
            give[1].wait_recv()
            cross.wait_recv()
            add_into(own[1], own[1], got.at[1], third)
            for q in over_z:
                q.start()

        def last():
            for q in over_z:
                q.wait_recv()
            total[...] = (at_z(own[1], z)[...].astype(F32) + fourth[0].astype(F32)
                          + (fourth[1].astype(F32) + fourth[2].astype(F32)))
            finish()
        return start, first, second, last

    over_z = [[links.later(at_z(own[n], zs[k]), third.at[n, k - 1], to_z[k]) for k in (1, 2, 3)] for n in (0, 1)]
    over_x = links.later(fourth.at[0], fourth.at[1], to_x)

    def first(n):
        give[n].wait_recv()
        add_into(own[n], own[n], got.at[n])
        for q in over_z[n]:
            q.start()

    def second():
        for q in over_z[0]:
            q.wait_recv()
        fourth[0] = (at_z(own[0], z)[...].astype(F32) + third[0, 0].astype(F32)
                     + (third[0, 1].astype(F32) + third[0, 2].astype(F32))).astype(fourth.dtype)
        over_x.start()

    def last():
        for q in over_z[1]:
            q.wait_recv()
        over_x.wait_recv()
        total[...] = (at_z(own[1], z)[...].astype(F32) + third[1, 0].astype(F32)
                      + (third[1, 1].astype(F32) + third[1, 2].astype(F32)) + fourth[1].astype(F32))
        finish()
    return start, lambda: first(0), lambda: first(1), second, last


class Outgoing:
    def __init__(self, links, me, src, dst):
        y, x, c, z = me
        recv, send = links.take(4), links.take(4)
        self.here, self.away = c == z // 2, c != z // 2
        self.remote, self.back = [], []
        for k in range(4):
            zz = (z + k) % 4
            s, d = src.at[zz], dst.at[z % 2, c]
            self.remote.append(links.copy(s, d, dev(y, x, z // 2, zz), send + k, recv + (z % 2) * 2 + c))
            links.open.append((self.remote[k], None if k else self.away))
            if k == 0:
                self.local = links.here_later(s, d)
        for i in (0, 1):
            for h in (0, 1):
                d = dst.at[i, h]
                mine = both(z == 2 * c + i, h == c)
                self.back.append((links.copy(d, d, dev(y, x, 1 - c, z), send, recv + 2 * i + h), jnp.logical_not(mine)))

    def start(self):
        for q in self.remote[1:]:
            q.start()
        pl.when(self.away)(self.remote[0].start)
        pl.when(self.here)(self.local.start)

    def finish(self):
        pl.when(self.here)(self.local.wait)
        for q, ok in self.back:
            pl.when(ok)(q.wait_recv)


def swap_halves(u):
    lane = lax.broadcasted_iota(jnp.int32, u.shape, 1) % HD
    return jnp.where(lane < HD // 2, pltpu.roll(u, 128 - HD // 2, 1), pltpu.roll(u, HD // 2, 1))


def head_mask(shape, h):
    lane = lax.broadcasted_iota(jnp.int32, shape, 1)
    return (lane < HD) if h == 0 else (lane >= HD)


def dot_t(a, b):
    return lax.dot_general(a, b, (((1,), (1,)), ((), ())), preferred_element_type=F32)


def project_step(xw, gv, w, cos, sin, n1, q, k, v, r):
    rows = pl.ds(pl.multiple_of(r * 256, 256), 256)
    u = xw[r // 2, pl.ds((r % 2) * 2, 2)].reshape(256, 1024).astype(F32)
    d = u - jnp.mean(u, axis=-1, keepdims=True)
    scaling = lax.rsqrt(jnp.mean(d * d, axis=-1, keepdims=True) + 1e-05)
    n = (d * scaling * gv[0:1, :] + gv[1:2, :]).astype(BF)
    n1[rows, :] = n
    for g in range(4):
        lanes = pl.ds(128 * g, 128)
        t = jnp.dot(n, w[:, :, :, :, pl.ds(384 * g, 384)].reshape(1024, 384), preferred_element_type=F32)
        for j, o in ((0, q), (1, k)):
            s = t[:, 128 * j:128 * j + 128]
            o[rows, lanes] = (s * cos[rows, :] + swap_halves(s) * sin[rows, :]).astype(BF)
        v[rows, lanes] = t[:, 256:].astype(BF)


def attend_step(q, k, v, o, lse, g, i):
    lanes = pl.ds(pl.multiple_of(g * 128, 128), 128)
    rows = pl.ds(pl.multiple_of(i * 256, 256), 256)
    qs = q[rows, lanes] * jnp.asarray(HD ** -0.5, BF)
    kk, vv = k[:, lanes], v[:, lanes]
    outs, logs = [], []
    for h in (0, 1):
        qh = jnp.where(head_mask(qs.shape, h), qs, jnp.zeros_like(qs))
        s = dot_t(qh, kk)
        m = jnp.max(s, axis=-1, keepdims=True)
        e = jnp.exp(s - m)
        t = jnp.sum(e, axis=-1, keepdims=True)
        p = (e * (1.0 / t)).astype(BF)
        outs.append(jnp.dot(p, vv, preferred_element_type=F32))
        logs.append(jnp.broadcast_to(m + jnp.log(t), qs.shape))
    keep = head_mask(qs.shape, 0)
    o[rows, lanes] = jnp.where(keep, outs[0], outs[1]).astype(BF)
    t = jnp.transpose(jnp.where(keep, logs[0], logs[1]))
    lse[pl.ds(2 * g, 1), rows] = t[0:1]
    lse[pl.ds(2 * g + 1, 1), rows] = t[HD:HD + 1]


def attend_back_step(q, k, v, do, lse, cos, sin, dqkv, dka, dva, g, i):
    lanes = pl.ds(pl.multiple_of(g * 128, 128), 128)
    rows = pl.ds(pl.multiple_of(i * 256, 256), 256)

    @pl.when(i == 0)
    def _():
        dka[...] = jnp.zeros_like(dka)
        dva[...] = jnp.zeros_like(dva)
    kk, vv, go = k[:, lanes], v[:, lanes], do[rows, lanes]
    qs = q[rows, lanes] * jnp.asarray(HD ** -0.5, BF)
    logs = lse[pl.ds(2 * g, 1), rows], lse[pl.ds(2 * g + 1, 1), rows]
    dks, dvs, dqs = [], [], []
    for h in (0, 1):
        keep = head_mask(kk.shape, h)
        zero = jnp.zeros_like(kk)
        s = dot_t(jnp.where(keep, kk, zero), qs)
        p = jnp.exp(s - logs[h])
        dp = dot_t(jnp.where(keep, vv, zero), go)
        pd = p * dp
        ds = (pd - p * jnp.sum(pd, axis=0, keepdims=True)).astype(BF)
        dvs.append(jnp.dot(p.astype(BF), go, preferred_element_type=F32))
        dks.append(jnp.dot(ds, qs, preferred_element_type=F32))
        dqs.append(lax.dot_general(ds, kk, (((0,), (0,)), ((), ())), preferred_element_type=F32))
    keep = head_mask(kk.shape, 0)
    dka[...] += jnp.where(keep, dks[0], dks[1])
    dva[...] += jnp.where(keep, dvs[0], dvs[1])
    u = jnp.where(head_mask(go.shape, 0), dqs[0], dqs[1]) * HD ** -0.5
    dqkv[rows, pl.ds(pl.multiple_of(g * 384, 128), 128)] = (
        u * cos[rows, :] - swap_halves(u) * sin[rows, :]).astype(BF)

    @pl.when(i == 3)
    def _():
        u = dka[...]
        dqkv[:, pl.ds(pl.multiple_of(128 + g * 384, 128), 128)] = (
            u * cos[...] - swap_halves(u) * sin[...]).astype(BF)
        dqkv[:, pl.ds(pl.multiple_of(256 + g * 384, 128), 128)] = dva[...].astype(BF)


class Incoming:
    def __init__(self, links, me, src, mid, dst):
        y, x, c, z = me
        partner = dev(y, x, 1 - c, z)
        self.swap = [links.later(src.at[i, pl.ds((1 - c) * 128, 128)], mid.at[2 * c + i], partner) for i in (0, 1)]
        send, recv = links.take(4), links.take(4)
        self.sends, self.kept, self.got = [], [], []
        m = links.m
        links.m += 1
        for w in range(4):
            d = dst.at[0, z]
            for ok, s in ((c == w // 2, src.at[w % 2, pl.ds(c * 128, 128)]), (c != w // 2, mid.at[w])):
                away, here = both(ok, z != w), both(ok, z == w)
                q = links.copy(s, d, dev(y, x, c, w), send + w, recv + z)
                self.sends.append((q, away))
                links.open.append((q, away))
                self.kept.append((pltpu.make_async_copy(s, d, links.local.at[m]), here))
        for zz in range(4):
            d = dst.at[0, zz]
            self.got.append((links.copy(d, d, dev(y, x, c, zz), send, recv + zz), z != zz))
        self.pair = links.later(dst.at[0], dst.at[1], partner)

    def begin(self):
        for q in self.swap:
            q.start()

    def send(self):
        for q in self.swap:
            q.wait_recv()
        for q, ok in self.sends + self.kept:
            pl.when(ok)(q.start)

    def arrive(self):
        for q, ok in self.kept:
            pl.when(ok)(q.wait)
        for q, ok in self.got:
            pl.when(ok)(q.wait_recv)
        self.pair.start()

    def finish(self):
        self.pair.wait_recv()


def disperse(links, single, bundle, me, route):
    y, x, c, z = me
    to_x, to_y = dev(y, 1 - x, c, z), dev(1 - y, x, c, z)
    mine = y * 2 + x
    if route == 0:
        two, three, other = to_y, to_x, (1 - y) * 2 + x
    else:
        two, three, other = to_x, to_y, y * 2 + 1 - x
    over_z = [links.later(single(mine, z), single(mine, z), dev(y, x, c, (z + k) % 4)) for k in (1, 2, 3)]
    cross = links.later(bundle(mine), bundle(mine), two)
    last = [links.later(bundle(mine), bundle(mine), three), links.later(bundle(other), bundle(other), three)]

    def start():
        for q in over_z:
            q.start()

    def first():
        for q in over_z:
            q.wait_recv()
        cross.start()
        last[0].start()

    def second():
        cross.wait_recv()
        last[1].start()

    def finish():
        for q in last:
            q.wait_recv()
    return start, first, second, finish


FORE_PIECES = (
    ("gu", 6, 0),
    ("d", 1, 1),
    ("d", 0, 0),
    ("o", 0, 1),
    ("qkv", 1, 0),
    ("qkv", 0, 0),
    ("gu", 0, 0),
    ("gu", 7, 0),
    ("gu", 4, 1),
    ("gu", 5, 0),
    ("gu", 1, 1),
    ("gu", 2, 0),
    ("gu", 3, 1),
    ("d", 3, 1),
    ("d", 2, 0),
)
FORE_ORDER = (
    ((0, 0), (1, 0), (2, 0), (3, 0), (4, 0), (5, 0), (15, 0), (6, 0), (17, 0), (7, 0), (0, 1), (8, 0), (1, 1),
     (9, 0), (0, 2), (2, 1), (10, 0), (1, 2), (3, 1), (11, 0), (0, 3), (2, 2), (1, 3), (4, 1), (12, 0), (3, 2),
     (2, 3), (5, 1), (13, 0), (4, 2), (3, 3), (5, 2), (4, 3), (15, 1), (5, 3), (6, 1), (14, 0), (17, 1), (15, 2),
     (6, 2), (17, 2), (7, 1), (17, 3),),
    ((6, 3), (7, 2), (8, 1)), (), ((9, 1),), (), (), ((10, 1), (7, 3)), (), (), ((8, 2), (9, 2)), ((11, 1),), (), (),
    ((12, 1), (16, 0)), (), (), ((10, 2),), ((13, 1),), ((11, 2), (8, 3), (9, 3), (14, 1)), ((12, 2), (10, 3)),
    ((13, 2), (11, 3), (14, 2)), ((16, 1), (12, 3)), ((16, 2), (13, 3), (14, 3)),
)


def fore_kernel(tok, cot, wq, wk, wv, wg, wu, wo, wd, gp, cos, sin, *rest):
    (oqkv, ogu, oo, od, xh, cw, gvo, n1o, qo, ko, vo, atto, lseo, n2o, mido, gateo, upo, hido,
     tmid, cmid, gains, gv, xw, w3, n1, q, k, v, att, lse, wos, sent, came, mid, n2, wgs, wus,
     gate, up, hid, send, recv, local) = rest
    me = y, x, c, z = place()
    yx = y * 2 + x
    partner = dev(y, x, 1 - c, z)
    greet(y, x, c, z)
    links = Links(send, recv, local)
    tin, cin = Incoming(links, me, tok, tmid, xw), Incoming(links, me, cot, cmid, cw)
    tin.begin()
    loc, swaps = [], []

    def columns(src, dst, width, base, stride):
        for g in range(4):
            lanes = pl.ds(base + stride * g, width)
            swaps.append(links.to(src.at[:, pl.ds(pl.multiple_of((2 * g + 1 - c) * width, width), width)],
                                  dst.at[yx, c, z, :, lanes], partner))
            loc.append(links.here(src.at[:, pl.ds(pl.multiple_of((2 * g + c) * width, width), width)],
                                  dst.at[yx, c, z, :, lanes]))
    swaps.append(links.to(gp, gains.at[yx, c, z], partner))
    loc.append(links.here(gp, gains.at[yx, c, z]))
    for j, src in enumerate((wq, wk, wv)):
        columns(src, oqkv, 128, 128 * j, 384)
    for j, src in enumerate((wg, wu)):
        columns(src, ogu, 512, 2048 * j, 512)
    loc += [links.here(wo, oo.at[yx, z]), links.here(wd, od.at[yx, z])]
    cin.begin()
    work = []
    for name, index, route in FORE_PIECES:
        if name in ("qkv", "gu"):
            arr, cols = (oqkv, 768) if name == "qkv" else (ogu, 512)
            lanes = pl.ds(index * cols, cols)
            work.append(disperse(links, lambda i, zz, arr=arr, lanes=lanes: arr.at[i, :, zz, :, lanes],
                                 lambda i, arr=arr, lanes=lanes: arr.at[i, :, :, :, lanes], me, route))
        else:
            arr = oo if name == "o" else od
            rows = pl.ds(index * 32, 32)
            work.append(disperse(links, lambda i, zz, arr=arr, rows=rows: arr.at[i, zz, rows],
                                 lambda i, arr=arr, rows=rows: arr.at[i, :, rows], me, route))
    work += [(tin.send, tin.arrive, tin.finish), (cin.send, cin.arrive, cin.finish),
             disperse(links, lambda i, zz: gains.at[i, :, zz], lambda i: gains.at[i], me, 1)]
    swap = links.wanted(sent, came, partner)
    share = links.later(n2.at[pl.ds(0, 512)], n2.at[pl.ds(512, 512)], partner)
    for e in loc:
        e.wait()
    for e in swaps:
        e.wait_recv()

    def comm(slot):
        for i, stage in FORE_ORDER[slot]:
            work[i][stage]()

    keep = []

    def put(src, dst):
        keep.append(links.here(src, dst))
    comm(0)
    links.here(oqkv, w3).wait()
    for i in range(4):
        for j in (0, 1):
            gv[:, pl.ds((2 * i + j) * 128, 128)] = (gains[i, j, 0] + gains[i, j, 1]) + (gains[i, j, 2] + gains[i, j, 3])

    def rows_of(step):
        lax.fori_loop(0, 4, lambda r, _: (step(r), 0)[1], 0)
    rows_of(lambda r: project_step(xw, gv, w3, cos, sin, n1, q, k, v, r))
    for a, b in ((gv, gvo), (n1, n1o), (q, qo), (k, ko), (v, vo), (xw.at[0], xh)):
        put(a, b)
    comm(1)

    def step(t, _):
        attend_step(q, k, v, att, lse, t // 4, t % 4)
        for slot in range(2, 17):
            if FORE_ORDER[slot]:
                pl.when(t == slot - 2)(lambda slot=slot: comm(slot))
        return 0
    lax.fori_loop(0, 16, step, 0)
    comm(17)
    wload = links.here(oo, wos)
    put(att, atto)
    put(lse, lseo)
    wload.wait()

    def terms(r, out, first):
        rows = pl.ds(pl.multiple_of(r * 256, 256), 256)
        out[rows, :] = jnp.dot(att[pl.ds(pl.multiple_of(first + r * 256, 256), 256), :], wos[...].reshape(512, 1024),
                               preferred_element_type=F32)
    lax.fori_loop(0, 2, lambda r, _: (terms(r, sent, 512), 0)[1], 0)
    swap.start()
    lax.fori_loop(0, 2, lambda r, _: (terms(r, mid, 0), 0)[1], 0)
    swap.wait()

    def second_norm(r):
        rows = pl.ds(pl.multiple_of(r * 128, 128), 128)
        u = xw[0, r].astype(F32) + (mid[rows, :] + came[rows, :])
        mid[rows, :] = u
        d = u - jnp.mean(u, axis=-1, keepdims=True)
        scaling = lax.rsqrt(jnp.mean(d * d, axis=-1, keepdims=True) + 1e-05)
        n2[rows, :] = (d * scaling * gv[2:3, :] + gv[3:4, :]).astype(BF)
    rows_of(second_norm)
    share.start()
    put(mid, mido)
    comm(18)
    share.wait_recv()
    put(n2, n2o)
    for j in range(4):
        if j:
            comm(18 + j)
        lanes = pl.ds(512 * j, 512)
        lg = links.here(ogu.at[:, :, :, :, lanes], wgs)
        lu = links.here(ogu.at[:, :, :, :, pl.ds(2048 + 512 * j, 512)], wus)
        lg.wait()
        lu.wait()

        def hidden_units(r, lanes=lanes):
            rows = pl.ds(pl.multiple_of(r * 256, 256), 256)
            n = n2[rows, :]
            a = jnp.dot(n, wgs[...].reshape(1024, 512), preferred_element_type=F32)
            b = jnp.dot(n, wus[...].reshape(1024, 512), preferred_element_type=F32)
            hid[rows, lanes] = (a * jax.nn.sigmoid(a) * b).astype(BF)
            gate[rows, lanes] = a.astype(BF)
            up[rows, lanes] = b.astype(BF)
        rows_of(hidden_units)
        for a, b in ((hid, hido), (gate, gateo), (up, upo)):
            put(a.at[:, lanes], b.at[:, lanes])
    comm(22)
    for e in keep:
        e.wait()
    links.drain()


def fore(tok, cot, wq, wk, wv, wg, wu, wo, wd, gp, cos, sin):
    S = jax.ShapeDtypeStruct
    V = pltpu.VMEM
    return pl.pallas_call(
        fore_kernel,
        out_shape=(
            S((4, 2, 4, 32, 1536), BF), S((4, 2, 4, 32, 4096), BF), S((4, 4, 32, 1024), BF), S((4, 4, 128, 1024), BF),
            S((4, 128, 1024), BF), S((2, 4, 128, 1024), BF), S((8, 1024), F32), S((1024, 1024), BF),
            S((1024, 512), BF), S((1024, 512), BF), S((1024, 512), BF), S((1024, 512), BF), S((8, 1024), F32),
            S((1024, 1024), BF), S((512, 1024), F32), S((1024, 2048), BF), S((1024, 2048), BF), S((1024, 2048), BF),
        ),
        in_specs=[VM] * 12,
        out_specs=[ANY] * 18,
        scratch_shapes=[
            V((4, 128, 1024), BF), V((4, 128, 1024), BF), V((4, 2, 4, 8, 128), F32), V((8, 1024), F32),
            V((2, 4, 128, 1024), BF), V((4, 2, 4, 32, 1536), BF), V((1024, 1024), BF),
            V((1024, 512), BF), V((1024, 512), BF), V((1024, 512), BF), V((1024, 512), BF), V((8, 1024), F32),
            V((4, 4, 32, 1024), BF), V((512, 1024), F32), V((512, 1024), F32), V((512, 1024), F32),
            V((1024, 1024), BF), V((4, 2, 4, 32, 512), BF), V((4, 2, 4, 32, 512), BF),
            V((1024, 2048), BF), V((1024, 2048), BF), V((1024, 2048), BF),
            pltpu.SemaphoreType.DMA((200,)),
            pltpu.SemaphoreType.DMA((200,)),
            pltpu.SemaphoreType.DMA((72,)),
        ],
        compiler_params=pltpu.CompilerParams(collective_id=0, has_side_effects=True, vmem_limit_bytes=67043328),
    )(tok, cot, wq, wk, wv, wg, wu, wo, wd, gp, cos, sin)


PIECES = (
    ("qkv", 2, 1),
    ("d", 0, 0),
    ("d", 1, 0),
    ("gu", 4, 2),
    ("gu", 0, 0),
    ("qkv", 0, 1),
    ("gu", 5, 2),
    ("d", 3, 0),
    ("gu", 1, 0),
    ("gu", 7, 0),
    ("d", 2, 2),
    ("qkv", 3, 1),
    ("gu", 6, 2),
    ("gu", 2, 0),
    ("o", 0, 0),
    ("qkv", 1, 0),
    ("gu", 3, 1),
)
SHAPES = {"d": (4, 32, 1024), "o": (4, 32, 1024), "gu": (2, 4, 32, 512), "qkv": (2, 4, 32, 384)}
ORDER = (
    (), ((1, 0), (2, 0), (10, 0)), ((1, 1), (3, 0), (4, 0), (7, 0), (10, 1)),
    ((1, 2), (2, 1), (3, 1), (6, 0), (8, 0), (10, 2), (10, 3)),
    ((1, 3), (2, 2), (3, 2), (4, 1), (3, 3), (12, 0), (7, 1), (6, 1), (13, 0)),
    ((2, 3), (4, 2), (6, 2), (8, 1), (9, 0)), ((3, 4), (4, 3), (6, 3), (10, 4), (12, 1), (7, 2), (12, 2), (13, 1)),
    ((8, 2), (9, 1), (14, 0)), ((17, 0), (6, 4), (7, 3), (9, 2), (12, 3), (13, 2), (14, 1)), (), ((8, 3), (12, 4)),
    ((14, 2),), (), ((5, 0),), (), (), ((5, 1), (16, 0)), (), ((15, 0),), ((5, 2), (16, 1)), ((17, 1), (15, 1)),
    ((9, 3),), (), ((0, 0), (15, 2), (13, 3)), ((16, 2),), ((0, 1),), ((14, 3),), ((5, 3),), ((0, 2), (11, 0)),
    ((18, 0), (19, 0), (0, 3), (11, 1), (15, 3), (16, 3), (19, 1), (19, 2), (11, 2), (18, 1), (19, 3), (11, 3)),
)


def total_over_devices(links, me, acc, got):
    y, x, c, z = me
    hops = [links.wanted(acc, got.at[i], d) for i, d in
            enumerate((dev(y, x, 1 - c, z), dev(y, 1 - x, c, z), dev(1 - y, x, c, z)))]
    over_z = [links.wanted(acc, got.at[2 + k], dev(y, x, c, (z + k) % 4)) for k in (1, 2, 3)]

    def settle(i):
        hops[i].wait()
        acc[...] += got[i]

    def chip():
        hops[0].start()
        settle(0)
        hops[1].start()

    def second():
        settle(1)
        hops[2].start()

    def third():
        settle(2)
        for q in over_z:
            q.start()

    def last():
        for q in over_z:
            q.wait()
        acc[...] += got[3] + (got[4] + got[5])
    return chip, second, third, last


def rows_dot(a, b):
    return lax.dot_general(a, b, (((0,), (0,)), ((), ())), preferred_element_type=F32)


def each(count, step):
    def body(r, _):
        step(r)
        return 0
    lax.fori_loop(0, count, body, 0)


def block(i, size):
    return pl.ds(pl.multiple_of(i * size, size), size)


def norm_parts(u):
    d = u - jnp.mean(u, axis=-1, keepdims=True)
    scaling = lax.rsqrt(jnp.mean(d * d, axis=-1, keepdims=True) + 1e-05)
    return d * scaling, scaling


def norm_back(upstream, normed, scaling):
    return scaling * (upstream - jnp.mean(upstream, axis=-1, keepdims=True)
                      - normed * jnp.mean(upstream * normed, axis=-1, keepdims=True))


def back_kernel(cw, hido, od, n2o, gateo, upo, ogu, mido, oo, atto, qo, ko, vo, lseo, n1o, oqkv, xh,
                cos, sin, gv, fac, *rest):
    fqkv, fgu, fo, fd, fgain, out_w, ig_w = rest[:7]
    scratch = list(rest[7:])
    (gd, ggu, go, gw, mg, sent, came, mlow, ag, out16, ig, gacc, ggot, send, recv, local, ready) = scratch[-17:]
    me = y, x, c, z = place()
    partner = dev(y, x, 1 - c, z)
    greet(y, x, c, z)
    links = Links(send, recv, local)
    work = []
    finals = []
    for name, index, route in PIECES:
        bufs = [scratch.pop(0) for _ in range(4)]
        if name in ("qkv", "gu"):
            src, dst = (gw, fqkv) if name == "qkv" else (ggu, fgu)
            cols = SHAPES[name][3]
            lanes = pl.ds(index * cols, cols)

            def at(yy, xx, src=src, index=index):
                return src.at[index, yy * 2 + xx]

            def deliver(total, dst=dst, lanes=lanes):
                there = links.later(total.at[1 - c], dst.at[c, :, lanes], partner)
                here = links.here_later(total.at[c], dst.at[c, :, lanes])
                finals.extend((there.wait_recv, here.wait))
                return there, here
        else:
            src, dst = (gd, fd) if name == "d" else (go, fo)
            rows = pl.ds(index * 32, 32)

            def at(yy, xx, src=src, rows=rows):
                return src.at[yy * 2 + xx, :, rows]

            def deliver(total, dst=dst, rows=rows):
                here = links.here_later(total, dst.at[rows])
                finals.append(here.wait)
                return (here,)
        work.append(collect(links, at, me, route, bufs, deliver))
    o1 = Outgoing(links, me, out16, out_w)
    o2 = Outgoing(links, me, ig, ig_w)
    work += [(o1.start, o1.finish), (o2.start, o2.finish), total_over_devices(links, me, gacc, ggot)]
    swaps = [links.wanted(sent, came, partner) for _ in range(3)]
    share = links.later(mlow.at[0], mlow.at[1], partner)

    def comm(slot):
        for i, stage in ORDER[slot]:
            work[i][stage]()

    def swap(n):
        if n:
            pl.semaphore_wait(ready, 1)
        swaps[n].start()

    def read(n):
        if n < 2:
            pl.semaphore_signal(ready, inc=1, device_id=partner, device_id_type=MESH)

    gacc[...] = jnp.zeros_like(gacc)
    factor = fac[...]

    def hidden_layer(low):
        a = links.here(cw, low)

        def down(hv):
            b = links.here(hido, hv)
            a.wait()

            def scale(i):
                low[i // 4, i % 4] = (factor * low[i // 4, i % 4].astype(F32)).astype(BF)
            each(8, scale)
            b.wait()
            comm(0)

            def weights(r):
                u = rows_dot(hv[:, block(r, 256)], low[...].reshape(1024, 1024))
                gd[r // 2, pl.ds((r % 2) * 2, 2)] = u.astype(BF).reshape(2, 128, 1024)
            each(8, weights)
        pl.run_scoped(down, pltpu.VMEM((1024, 2048), BF))

        def units(n2, gate, up, dgate, dup, wg, wu, wd):
            a = links.here(n2o, n2)
            for j in range(4):
                lanes = pl.ds(512 * j, 512)
                got = [links.here(od.at[j], wd), links.here(gateo.at[:, lanes], gate), links.here(upo.at[:, lanes], up),
                       links.here(ogu.at[:, :, :, :, lanes], wg),
                       links.here(ogu.at[:, :, :, :, pl.ds(2048 + 512 * j, 512)], wu)]
                comm(1 + j)
                for q in got:
                    q.wait()

                def grads(r):
                    rows = block(r, 256)
                    g = dot_t(low[r // 2, pl.ds((r % 2) * 2, 2)].reshape(256, 1024), wd[...].reshape(512, 1024))
                    a, b = gate[rows, :].astype(F32), up[rows, :].astype(F32)
                    t = jax.nn.sigmoid(a)
                    dgate[rows, :] = (g * b * t * (1.0 + a * (1.0 - t))).astype(BF)
                    dup[rows, :] = (g * a * t).astype(BF)
                each(4, grads)
                if j == 0:
                    a.wait()

                def weights(r):
                    n = n2[:, block(r, 256)]
                    ggu[j, r] = rows_dot(n, dgate[...]).astype(BF).reshape(2, 4, 32, 512)
                    ggu[4 + j, r] = rows_dot(n, dup[...]).astype(BF).reshape(2, 4, 32, 512)
                each(4, weights)

                def terms(r, out, first):
                    rows = pl.ds(pl.multiple_of(first + r * 256, 256), 256)
                    u = (dot_t(dgate[rows, :], wg[...].reshape(1024, 512))
                         + dot_t(dup[rows, :], wu[...].reshape(1024, 512)))
                    dst = block(r, 256)
                    out[dst, :] = u if j == 0 else out[dst, :] + u
                each(2, lambda r: terms(r, sent, 512))
                if j == 3:
                    swap(0)
                each(2, lambda r: terms(r, mg, 0))
        pl.run_scoped(units, pltpu.VMEM((1024, 1024), BF), *[pltpu.VMEM((1024, 512), BF)] * 4,
                      *[pltpu.VMEM((4, 2, 4, 32, 512), BF)] * 2, pltpu.VMEM((4, 128, 1024), BF))
    pl.run_scoped(hidden_layer, pltpu.VMEM((2, 4, 128, 1024), BF))
    comm(5)

    def second_norm(mid, cot):
        a, b = links.here(mido, mid), links.here(cw.at[0], cot)
        a.wait()
        b.wait()
        swaps[0].wait()

        def part(r):
            rows = block(r, 128)
            gn = mg[rows, :] + came[rows, :]
            normed, scaling = norm_parts(mid[rows, :])
            gacc[2:3, :] += jnp.sum(gn * normed, axis=0, keepdims=True)
            gacc[3:4, :] += jnp.sum(gn, axis=0, keepdims=True)
            u = factor * cot[r].astype(F32) + norm_back(gn * gv[2:3, :], normed, scaling)
            mg[rows, :] = u
            mlow[0, r] = u.astype(BF)
        each(4, part)
        read(0)
        share.start()
    pl.run_scoped(second_norm, pltpu.VMEM((512, 1024), F32), pltpu.VMEM((4, 128, 1024), BF))
    comm(6)

    def out_layer(w, att):
        a, b = links.here(oo, w), links.here(atto, att)
        a.wait()
        b.wait()
        share.wait_recv()

        def weights(r):
            u = rows_dot(att[:, block(r, 256)], mlow[...].reshape(1024, 1024))
            go[pl.ds(2 * r, 2)] = u.astype(BF).reshape(2, 4, 32, 1024)
        each(2, weights)

        def grads(r):
            u = dot_t(mlow[r // 2, pl.ds((r % 2) * 2, 2)].reshape(256, 1024), w[...].reshape(512, 1024))
            ag[block(r, 256), :] = u.astype(BF)
        each(4, grads)
    pl.run_scoped(out_layer, pltpu.VMEM((4, 4, 32, 1024), BF), pltpu.VMEM((1024, 512), BF))
    comm(7)

    def output(hv, w, mid):
        got = [links.here(hido, hv), links.here(od, w), links.here(mido, mid)]
        for q in got:
            q.wait()

        def term(r, first):
            return jnp.dot(hv[pl.ds(pl.multiple_of(first + r * 256, 256), 256), :], w[...].reshape(2048, 1024),
                           preferred_element_type=F32)

        def theirs(r):
            sent[block(r, 256), :] = term(r, 512)
        each(2, theirs)
        swap(1)

        def mine(r):
            mid[block(r, 256), :] += term(r, 0)
        each(2, mine)
        swaps[1].wait()

        def total(r):
            out16[r] = (mid[block(r, 128), :] + came[block(r, 128), :]).astype(BF)
        each(4, total)
        read(1)
    pl.run_scoped(output, pltpu.VMEM((1024, 2048), BF), pltpu.VMEM((4, 4, 128, 1024), BF), pltpu.VMEM((512, 1024), F32))

    def attention(dqkv):
        def heads(q, k, v, lse, n1, dka, dva):
            got = [links.here(a, b) for a, b in ((qo, q), (ko, k), (vo, v), (lseo, lse), (n1o, n1))]
            for e in got:
                e.wait()

            def step(t):
                for slot in range(20):
                    if ORDER[8 + slot]:
                        pl.when(t == slot)(lambda slot=slot: comm(8 + slot))
                g, i = t // 5, t % 5

                @pl.when(i < 4)
                def _():
                    attend_back_step(q, k, v, ag, lse, cos, sin, dqkv, dka, dva, g, i)

                @pl.when(i == 4)
                def _():
                    u = rows_dot(n1[...], dqkv[:, pl.ds(pl.multiple_of(g * 384, 128), 384)])
                    gw[g] = u.astype(BF).reshape(4, 2, 4, 32, 384)
            each(20, step)
        pl.run_scoped(heads, *[pltpu.VMEM((1024, 512), BF)] * 3, pltpu.VMEM((8, 1024), F32),
                      pltpu.VMEM((1024, 1024), BF), *[pltpu.VMEM((1024, 128), F32)] * 2)

        def first_norm(w, tokens, mine):
            got = [links.here(oqkv, w), links.here(xh, tokens)]
            comm(28)
            for e in got:
                e.wait()

            def term(r, out, first):
                out[block(r, 256), :] = dot_t(dqkv[pl.ds(pl.multiple_of(first + r * 256, 256), 256), :],
                                              w[...].reshape(1024, 1536))
            each(2, lambda r: term(r, sent, 512))
            swap(2)
            each(2, lambda r: term(r, mine, 0))
            swaps[2].wait()

            def part(r):
                rows = block(r, 128)
                gn = mine[rows, :] + came[rows, :]
                normed, scaling = norm_parts(tokens[r].astype(F32))
                gacc[0:1, :] += jnp.sum(gn * normed, axis=0, keepdims=True)
                gacc[1:2, :] += jnp.sum(gn, axis=0, keepdims=True)
                ig[r] = (mg[rows, :] + norm_back(gn * gv[0:1, :], normed, scaling)).astype(BF)
            each(4, part)
        pl.run_scoped(first_norm, pltpu.VMEM((4, 2, 4, 32, 1536), BF), pltpu.VMEM((4, 128, 1024), BF),
                      pltpu.VMEM((512, 1024), F32))
    pl.run_scoped(attention, pltpu.VMEM((1024, 1536), BF))
    comm(29)
    finals.append(links.here(gacc, fgain).wait)
    for f in finals:
        f()
    links.drain()


def back(*args):
    scratch = []
    for name, index, route in PIECES:
        scratch += reduce_shapes(SHAPES[name], route)
    return pl.pallas_call(
        back_kernel,
        out_shape=(
            jax.ShapeDtypeStruct((2, 32, 1536), F32),
            jax.ShapeDtypeStruct((2, 32, 4096), F32),
            jax.ShapeDtypeStruct((32, 1024), F32),
            jax.ShapeDtypeStruct((128, 1024), F32),
            jax.ShapeDtypeStruct((8, 1024), F32),
            jax.ShapeDtypeStruct((2, 2, 128, 1024), BF),
            jax.ShapeDtypeStruct((2, 2, 128, 1024), BF),
        ),
        in_specs=[ANY] * 17 + [VM] * 4,
        out_specs=[ANY] * 7,
        scratch_shapes=scratch + [
            pltpu.VMEM((4, 4, 128, 1024), BF),
            pltpu.VMEM((8, 4, 2, 4, 32, 512), BF),
            pltpu.VMEM((4, 4, 32, 1024), BF),
            pltpu.VMEM((4, 4, 2, 4, 32, 384), BF),
            pltpu.VMEM((512, 1024), F32),
            pltpu.VMEM((512, 1024), F32),
            pltpu.VMEM((512, 1024), F32),
            pltpu.VMEM((2, 4, 128, 1024), BF),
            pltpu.VMEM((1024, 512), BF),
            pltpu.VMEM((4, 128, 1024), BF),
            pltpu.VMEM((4, 128, 1024), BF),
            pltpu.VMEM((8, 1024), F32),
            pltpu.VMEM((6, 8, 1024), F32),
            pltpu.SemaphoreType.DMA((192,)),
            pltpu.SemaphoreType.DMA((192,)),
            pltpu.SemaphoreType.DMA((96,)),
            pltpu.SemaphoreType.REGULAR,
        ],
        compiler_params=pltpu.CompilerParams(collective_id=1, has_side_effects=True, vmem_limit_bytes=67043328),
    )(*args)


def half_tables(c):
    row = jnp.arange(1024, dtype=jnp.int32)
    half, zz, r = row // 512, (row // 128) % 4, row % 128
    owner = jnp.where(half == 0, c, 1 - c)
    positions = (zz * 256 + owner * 128 + r).astype(jnp.float32)
    lane = jnp.arange(128, dtype=jnp.int32)
    freqs = 10000.0 ** (-2.0 * (lane % 32).astype(jnp.float32) / HD)
    angle = positions[:, None] * freqs[None, :]
    return jnp.cos(angle), jnp.where(lane % HD < HD // 2, -1.0, 1.0)[None, :] * jnp.sin(angle)


def paired(
    tokens,
    cotangent,
    species_index,
    species_count,
    loss_weight,
    query_weight,
    key_weight,
    value_weight,
    out_weight,
    gate_weight,
    up_weight,
    down_weight,
    mixer_gain,
    mixer_shift,
    feeder_gain,
    feeder_shift,
):
    dp, z = lax.axis_index("dp"), lax.axis_index("seq")
    c = dp % 2
    small = jnp.stack([mixer_gain, mixer_shift, feeder_gain, feeder_shift]).astype(F32)
    table = loss_weight * lax.rsqrt(species_count.astype(jnp.float32) / 400.0)
    picks = species_index[:, None] == jnp.arange(table.shape[0], dtype=jnp.int32)[None, :]
    factors = jnp.sum(jnp.where(picks, table[None, :], 0.0), axis=1)
    lane = jnp.arange(128, dtype=jnp.int32)[None, :]
    small = jnp.where(lane // 32 == z, jnp.tile(small, (1, 4)), 0.0)
    fifth = jnp.where(z == 0, jnp.where(lane == 0, factors[0], jnp.where(lane == 1, factors[1], 0.0)), 0.0)
    small = jnp.concatenate([small, fifth, jnp.zeros((3, 128), F32)], 0)
    cos, sin = half_tables(c)
    (wqkv, wgu, wo, wd, xh, cw, gv, norm_one, q, k, v, attended, lse, norm_two, middle, gate, upward, hidden) = fore(
        tokens, cotangent, query_weight, key_weight, value_weight, gate_weight, up_weight, out_weight, down_weight,
        small, cos, sin)
    factor = lax.dynamic_slice(gv, (4, (2 * (dp // 2) + z // 2) * 128 + z % 2), (1, 1))
    gqkv, ggu, go, gd, ggain, out, ig = back(
        cw, hidden, wd, norm_two, gate, upward, wgu, middle, wo, attended, q, k, v, lse, norm_one, wqkv, xh,
        cos, sin, gv, jnp.broadcast_to(factor, (1, 1024)))
    ggain = lax.dynamic_slice_in_dim(ggain[:4], (dp * 4 + z) * 32, 32, 1)
    gqkv = gqkv.reshape(2, 32, 4, 3, 128).transpose(3, 1, 2, 0, 4).reshape(3, 32, 1024)
    ggu = ggu.reshape(2, 32, 2, 4, 512).transpose(2, 1, 3, 0, 4).reshape(2, 32, 4096)
    return (
        out.reshape(2, 256, 1024),
        ig.reshape(2, 256, 1024).astype(F32),
        gqkv[0],
        gqkv[1],
        gqkv[2],
        go,
        ggu[0],
        ggu[1],
        gd,
        ggain[0],
        ggain[1],
        ggain[2],
        ggain[3],
    )


def matmul(left, right):
    return jnp.dot(left, right, preferred_element_type=jnp.float32)


def weight_term(left, right):
    return lax.dot_general(
        left, right, (((0,), (0,)), ((), ())), preferred_element_type=jnp.float32
    )


def through(left, weight):
    return lax.dot_general(
        left, weight, (((1,), (1,)), ((), ())), preferred_element_type=jnp.float32
    )


def normalize(values):
    center = jnp.mean(values, axis=-1, keepdims=True)
    centered = values - center
    variance = jnp.mean(centered * centered, axis=-1, keepdims=True)
    scaling = lax.rsqrt(variance + 1e-05)
    return (centered * scaling, scaling)


def plain_norm_back(upstream, normed, scaling):
    first = jnp.mean(upstream, axis=-1, keepdims=True)
    second = jnp.mean(upstream * normed, axis=-1, keepdims=True)
    return scaling * (upstream - first - normed * second)


def tables(start, count):
    half = HD // 2
    positions = (start + jnp.arange(count, dtype=jnp.int32)).astype(jnp.float32)
    freqs = 10000.0 ** (-2.0 * jnp.arange(half, dtype=jnp.float32) / HD)
    angle = positions[:, None] * freqs[None, :]
    return (jnp.cos(angle)[:, None, :], jnp.sin(angle)[:, None, :])


def rotate(values, cosine, sine):
    half = HD // 2
    first = values[..., :half]
    second = values[..., half:]
    return jnp.concatenate(
        [first * cosine - second * sine, second * cosine + first * sine], axis=-1
    )


def attend_head(operands):
    query_head, key_head, value_head = operands
    scores = jnp.einsum(
        "wtd,wsd->wts", query_head, key_head, preferred_element_type=jnp.float32
    ) * HD ** (-0.5)
    peak = jnp.max(scores, axis=-1, keepdims=True)
    raised = jnp.exp(scores - peak)
    total = jnp.sum(raised, axis=-1, keepdims=True)
    probs = (raised / total).astype(jnp.bfloat16)
    result = jnp.einsum("wts,wsd->wtd", probs, value_head, preferred_element_type=jnp.float32)
    return (result, (peak + jnp.log(total))[..., 0])


def head_back(operands):
    query_head, key_head, value_head, upstream, log_total = operands
    scores = jnp.einsum(
        "wtd,wsd->wts", query_head, key_head, preferred_element_type=jnp.float32
    ) * HD ** (-0.5)
    probs = jnp.exp(scores - log_total[..., None])
    prob_grads = jnp.einsum(
        "wtd,wsd->wts", upstream, value_head, preferred_element_type=jnp.float32
    )
    inner = jnp.sum(probs * prob_grads, axis=-1, keepdims=True)
    score_grads = (probs * (prob_grads - inner)).astype(jnp.bfloat16)
    query_grad = jnp.einsum(
        "wts,wsd->wtd", score_grads, key_head, preferred_element_type=jnp.float32
    ) * HD ** (-0.5)
    key_grad = jnp.einsum(
        "wts,wtd->wsd", score_grads, query_head, preferred_element_type=jnp.float32
    ) * HD ** (-0.5)
    value_grad = jnp.einsum(
        "wts,wtd->wsd", probs.astype(jnp.bfloat16), upstream, preferred_element_type=jnp.float32
    )
    return (query_grad, key_grad, value_grad)


def general(
    tokens,
    cotangent,
    species_index,
    species_count,
    loss_weight,
    query_weight,
    key_weight,
    value_weight,
    out_weight,
    gate_weight,
    up_weight,
    down_weight,
    mixer_gain,
    mixer_shift,
    feeder_gain,
    feeder_shift,
):
    gathered = (
        lax.all_gather(query_weight, ("dp", "seq"), axis=0, tiled=True),
        lax.all_gather(key_weight, ("dp", "seq"), axis=0, tiled=True),
        lax.all_gather(value_weight, ("dp", "seq"), axis=0, tiled=True),
        lax.all_gather(out_weight, ("dp", "seq"), axis=0, tiled=True),
        lax.all_gather(gate_weight, ("dp", "seq"), axis=0, tiled=True),
        lax.all_gather(up_weight, ("dp", "seq"), axis=0, tiled=True),
        lax.all_gather(down_weight, ("dp", "seq"), axis=0, tiled=True),
        lax.all_gather(mixer_gain, ("dp", "seq"), axis=0, tiled=True),
        lax.all_gather(mixer_shift, ("dp", "seq"), axis=0, tiled=True),
        lax.all_gather(feeder_gain, ("dp", "seq"), axis=0, tiled=True),
        lax.all_gather(feeder_shift, ("dp", "seq"), axis=0, tiled=True),
    )
    wq, wk, wv, wo, wg, wu, wd, gain_one, shift_one, gain_two, shift_two = gathered
    windows, steps_dev, width = tokens.shape
    rows = windows * steps_dev
    start = lax.axis_index("seq") * steps_dev
    cosine, sine = tables(start, steps_dev)
    inputs = tokens.astype(jnp.float32).reshape(rows, width)
    normed_one, scaling_one = normalize(inputs)
    norm_one = (normed_one * gain_one.astype(jnp.float32) + shift_one.astype(jnp.float32)).astype(
        jnp.bfloat16
    )
    queries = rotate(
        matmul(norm_one, wq).reshape(windows, steps_dev, HEADS, HD), cosine, sine
    ).astype(jnp.bfloat16)
    keys = rotate(matmul(norm_one, wk).reshape(windows, steps_dev, HEADS, HD), cosine, sine).astype(
        jnp.bfloat16
    )
    values = matmul(norm_one, wv).astype(jnp.bfloat16)
    all_keys, all_values = (
        lax.all_gather(keys.reshape(windows, steps_dev, width), "seq", axis=1, tiled=True),
        lax.all_gather(values.reshape(windows, steps_dev, width), "seq", axis=1, tiled=True),
    )
    length = all_keys.shape[1]
    query_heads = queries.transpose(2, 0, 1, 3)
    key_heads = all_keys.reshape(windows, length, HEADS, HD).transpose(2, 0, 1, 3)
    value_heads = all_values.reshape(windows, length, HEADS, HD).transpose(2, 0, 1, 3)
    head_results, log_totals = lax.map(attend_head, (query_heads, key_heads, value_heads))
    attended = head_results.transpose(1, 2, 0, 3).reshape(rows, width).astype(jnp.bfloat16)
    middle = inputs + matmul(attended, wo)
    normed_two, scaling_two = normalize(middle)
    norm_two = (normed_two * gain_two.astype(jnp.float32) + shift_two.astype(jnp.float32)).astype(
        jnp.bfloat16
    )
    gate = matmul(norm_two, wg)
    upward = matmul(norm_two, wu)
    sigma = jax.nn.sigmoid(gate)
    swish = gate * sigma
    hidden = (swish * upward).astype(jnp.bfloat16)
    output = (middle + matmul(hidden, wd)).astype(jnp.bfloat16).reshape(windows, steps_dev, width)
    table = loss_weight * lax.rsqrt(species_count.astype(jnp.float32) / 400.0)
    picks = species_index[:, None] == jnp.arange(table.shape[0], dtype=jnp.int32)[None, :]
    factor = jnp.sum(jnp.where(picks, table[None, :], 0.0), axis=1)
    grad_out = (factor[:, None, None] * cotangent.astype(jnp.float32)).reshape(rows, width)
    regathered = (
        lax.all_gather(query_weight, ("dp", "seq"), axis=0, tiled=True),
        lax.all_gather(key_weight, ("dp", "seq"), axis=0, tiled=True),
        lax.all_gather(value_weight, ("dp", "seq"), axis=0, tiled=True),
        lax.all_gather(out_weight, ("dp", "seq"), axis=0, tiled=True),
        lax.all_gather(gate_weight, ("dp", "seq"), axis=0, tiled=True),
        lax.all_gather(up_weight, ("dp", "seq"), axis=0, tiled=True),
        lax.all_gather(down_weight, ("dp", "seq"), axis=0, tiled=True),
        lax.all_gather(mixer_gain, ("dp", "seq"), axis=0, tiled=True),
        lax.all_gather(mixer_shift, ("dp", "seq"), axis=0, tiled=True),
        lax.all_gather(feeder_gain, ("dp", "seq"), axis=0, tiled=True),
        lax.all_gather(feeder_shift, ("dp", "seq"), axis=0, tiled=True),
    )
    wq, wk, wv, wo, wg, wu, wd, gain_one, shift_one, gain_two, shift_two = regathered
    out_low = grad_out.astype(jnp.bfloat16)
    down_part = weight_term(hidden, out_low)
    hidden_grad = through(out_low, wd)
    gate_grad = (hidden_grad * upward * sigma * (1.0 + gate * (1.0 - sigma))).astype(jnp.bfloat16)
    upward_grad = (hidden_grad * swish).astype(jnp.bfloat16)
    gate_part = weight_term(norm_two, gate_grad)
    upward_part = weight_term(norm_two, upward_grad)
    norm_two_grad = through(gate_grad, wg) + through(upward_grad, wu)
    feeder_gain_part = jnp.sum(norm_two_grad * normed_two, axis=0)
    feeder_shift_part = jnp.sum(norm_two_grad, axis=0)
    middle_grad = grad_out + plain_norm_back(
        norm_two_grad * gain_two.astype(jnp.float32), normed_two, scaling_two
    )
    middle_low = middle_grad.astype(jnp.bfloat16)
    out_part = weight_term(attended, middle_low)
    attended_grad = through(middle_low, wo).astype(jnp.bfloat16)
    upstream_heads = attended_grad.reshape(windows, steps_dev, HEADS, HD).transpose(2, 0, 1, 3)
    query_heads_grad, key_heads_grad, value_heads_grad = lax.map(
        head_back, (query_heads, key_heads, value_heads, upstream_heads, log_totals)
    )
    key_whole = key_heads_grad.transpose(1, 2, 0, 3).reshape(windows, length, width)
    value_whole = value_heads_grad.transpose(1, 2, 0, 3).reshape(windows, length, width)
    key_mine, value_mine = (
        lax.psum_scatter(
            key_whole.astype(jnp.bfloat16), "seq", scatter_dimension=1, tiled=True
        ).astype(jnp.float32),
        lax.psum_scatter(
            value_whole.astype(jnp.bfloat16), "seq", scatter_dimension=1, tiled=True
        ).astype(jnp.float32),
    )
    query_lin_grad = (
        rotate(query_heads_grad.transpose(1, 2, 0, 3), cosine, -sine)
        .reshape(rows, width)
        .astype(jnp.bfloat16)
    )
    key_lin_grad = (
        rotate(key_mine.reshape(windows, steps_dev, HEADS, HD), cosine, -sine)
        .reshape(rows, width)
        .astype(jnp.bfloat16)
    )
    value_lin_grad = value_mine.reshape(rows, width).astype(jnp.bfloat16)
    query_part = weight_term(norm_one, query_lin_grad)
    key_part = weight_term(norm_one, key_lin_grad)
    value_part = weight_term(norm_one, value_lin_grad)
    norm_one_grad = (
        through(query_lin_grad, wq) + through(key_lin_grad, wk) + through(value_lin_grad, wv)
    )
    mixer_gain_part = jnp.sum(norm_one_grad * normed_one, axis=0)
    mixer_shift_part = jnp.sum(norm_one_grad, axis=0)
    input_grad = middle_grad + plain_norm_back(
        norm_one_grad * gain_one.astype(jnp.float32), normed_one, scaling_one
    )
    summed = (
        lax.psum_scatter(query_part, ("dp", "seq"), scatter_dimension=0, tiled=True),
        lax.psum_scatter(key_part, ("dp", "seq"), scatter_dimension=0, tiled=True),
        lax.psum_scatter(value_part, ("dp", "seq"), scatter_dimension=0, tiled=True),
        lax.psum_scatter(out_part, ("dp", "seq"), scatter_dimension=0, tiled=True),
        lax.psum_scatter(gate_part, ("dp", "seq"), scatter_dimension=0, tiled=True),
        lax.psum_scatter(upward_part, ("dp", "seq"), scatter_dimension=0, tiled=True),
        lax.psum_scatter(down_part, ("dp", "seq"), scatter_dimension=0, tiled=True),
        lax.psum_scatter(mixer_gain_part, ("dp", "seq"), scatter_dimension=0, tiled=True),
        lax.psum_scatter(mixer_shift_part, ("dp", "seq"), scatter_dimension=0, tiled=True),
        lax.psum_scatter(feeder_gain_part, ("dp", "seq"), scatter_dimension=0, tiled=True),
        lax.psum_scatter(feeder_shift_part, ("dp", "seq"), scatter_dimension=0, tiled=True),
    )
    return (
        output,
        input_grad.reshape(windows, steps_dev, width),
        summed[0],
        summed[1],
        summed[2],
        summed[3],
        summed[4],
        summed[5],
        summed[6],
        summed[7],
        summed[8],
        summed[9],
        summed[10],
    )


def solution(mesh):
    in_specs = (
        P("dp", "seq", None),
        P("dp", "seq", None),
        P("dp"),
        P(),
        P(),
    ) + (P(("dp", "seq"), None),) * 7 + (P(("dp", "seq")),) * 4
    out_specs = (P("dp", "seq", None),) * 2 + (P(("dp", "seq"), None),) * 7 + (P(("dp", "seq")),) * 4
    fits = mesh.shape["dp"] == 8 and mesh.shape["seq"] == 4
    return jax.shard_map(
        paired if fits else general, mesh=mesh, in_specs=in_specs, out_specs=out_specs, check_vma=False
    )
```

```python
import jax
import jax.numpy as jnp
from jax import lax
from jax.experimental import pallas as pl
from jax.experimental.pallas import tpu as pltpu
from jax.sharding import PartitionSpec as P

HEADS = 16
HD = 64
MESH = pl.DeviceIdType.MESH
BF = jnp.bfloat16
F32 = jnp.float32
ANY = pl.BlockSpec(memory_space=pl.ANY)
VM = pl.BlockSpec(memory_space=pltpu.VMEM)
VMEM_BYTES = 60 << 20


def place():
    dp, z = lax.axis_index("dp"), lax.axis_index("seq")
    return dp // 4, (dp // 2) % 2, dp % 2, z


def dev(y, x, c, z):
    return ((y * 2 + x) * 2 + c, z)


def both(a, b):
    return jnp.logical_and(a, b)


def greet(y, x, c, z, meanwhile=None):
    barrier = pltpu.get_barrier_semaphore()
    peers = [dev(y, 1 - x, c, z), dev(1 - y, x, c, z), dev(y, x, 1 - c, z)]
    for k in (1, 2, 3):
        peers += [dev(y, x, c, (z + k) % 4), dev(y, x, 1 - c, (z + k) % 4)]
    for p in peers:
        pl.semaphore_signal(barrier, inc=1, device_id=p, device_id_type=MESH)
    if meanwhile is not None:
        meanwhile()
    pl.semaphore_wait(barrier, len(peers))


class Links:
    def __init__(self, send, recv, local):
        self.send, self.recv, self.local = send, recv, local
        self.n = 0
        self.m = 0
        self.open = []

    def take(self, count):
        self.n += count
        return self.n - count

    def copy(self, src, dst, device, send, recv):
        return pltpu.make_async_remote_copy(
            src_ref=src, dst_ref=dst, send_sem=self.send.at[send], recv_sem=self.recv.at[recv],
            device_id=device, device_id_type=MESH)

    def go(self, c, ok=None):
        if ok is None:
            c.start()
        else:
            pl.when(ok)(c.start)
        self.open.append((c, ok))
        return c

    def to(self, src, dst, device):
        i = self.take(1)
        return self.go(self.copy(src, dst, device, i, i))

    def later(self, src, dst, device):
        i = self.take(1)
        c = self.copy(src, dst, device, i, i)
        self.open.append((c, None))
        return c

    def here_later(self, src, dst):
        self.m += 1
        return pltpu.make_async_copy(src, dst, self.local.at[self.m - 1])

    def wanted(self, src, dst, device):
        i = self.take(1)
        return self.copy(src, dst, device, i, i)

    def here(self, src, dst):
        self.m += 1
        c = pltpu.make_async_copy(src, dst, self.local.at[self.m - 1])
        c.start()
        return c

    def drain(self):
        for c, ok in self.open:
            if ok is None:
                c.wait_send()
            else:
                pl.when(ok)(c.wait_send)
        self.open = []


def at_z(ref, zz):
    return ref.at[zz] if len(ref.shape) == 3 else ref.at[:, zz]


def add_into(dst, *terms):
    def body(i, _):
        total = at_z(terms[0], i)[...].astype(F32)
        for t in terms[1:]:
            total += at_z(t, i)[...].astype(F32)
        at_z(dst, i)[...] = total.astype(dst.dtype)
        return 0
    lax.fori_loop(0, 4, body, 0)


def reduce_shapes(piece, route):
    part = piece[:-3] + piece[-2:]
    if route < 2:
        later = [pltpu.VMEM(piece, BF), pltpu.VMEM((3,) + part, BF)]
    else:
        later = [pltpu.VMEM((2, 3) + part, BF), pltpu.VMEM((2,) + part, BF)]
    return [pltpu.VMEM((2,) + piece, BF)] + later + [pltpu.VMEM(part, F32)]


def collect(links, at, me, route, bufs, deliver):
    y, x, c, z = me
    to_x, to_y = dev(y, 1 - x, c, z), dev(1 - y, x, c, z)
    zs = [(z + k) % 4 for k in range(4)]
    to_z = [dev(y, x, c, zs[k]) for k in range(4)]
    got, third, fourth, total = bufs
    out = deliver(total)

    def finish():
        for q in out:
            q.start()

    if route == 0:
        own, away = [at(1 - y, x), at(y, x)], [at(1 - y, 1 - x), at(y, 1 - x)]
        one, two = to_x, to_y
    else:
        own, away = [at(y, 1 - x), at(y, x)], [at(1 - y, 1 - x), at(1 - y, x)]
        one, two = to_y, to_x
    give = [links.later(away[n], got.at[n], one) for n in (0, 1)]

    def start():
        for q in give:
            q.start()

    if route < 2:
        cross = links.later(own[0], third, two)
        over_z = [links.later(at_z(own[1], zs[k]), fourth.at[k - 1], to_z[k]) for k in (1, 2, 3)]

        def first():
            give[0].wait_recv()
            add_into(own[0], own[0], got.at[0])
            cross.start()

        def second():
            give[1].wait_recv()
            cross.wait_recv()
            add_into(own[1], own[1], got.at[1], third)
            for q in over_z:
                q.start()

        def last():
            for q in over_z:
                q.wait_recv()
            total[...] = (at_z(own[1], z)[...].astype(F32) + fourth[0].astype(F32)
                          + (fourth[1].astype(F32) + fourth[2].astype(F32)))
            finish()
        return start, first, second, last

    over_z = [[links.later(at_z(own[n], zs[k]), third.at[n, k - 1], to_z[k]) for k in (1, 2, 3)] for n in (0, 1)]
    over_x = links.later(fourth.at[0], fourth.at[1], to_x)

    def first(n):
        give[n].wait_recv()
        add_into(own[n], own[n], got.at[n])
        for q in over_z[n]:
            q.start()

    def second():
        for q in over_z[0]:
            q.wait_recv()
        fourth[0] = (at_z(own[0], z)[...].astype(F32) + third[0, 0].astype(F32)
                     + (third[0, 1].astype(F32) + third[0, 2].astype(F32))).astype(fourth.dtype)
        over_x.start()

    def last():
        for q in over_z[1]:
            q.wait_recv()
        over_x.wait_recv()
        total[...] = (at_z(own[1], z)[...].astype(F32) + third[1, 0].astype(F32)
                      + (third[1, 1].astype(F32) + third[1, 2].astype(F32)) + fourth[1].astype(F32))
        finish()
    return start, lambda: first(0), lambda: first(1), second, last


class Outgoing:
    def __init__(self, links, me, src, dst):
        y, x, c, z = me
        recv, send = links.take(4), links.take(4)
        self.here, self.away = c == z // 2, c != z // 2
        self.remote, self.back = [], []
        for k in range(4):
            zz = (z + k) % 4
            s, d = src.at[zz], dst.at[z % 2, c]
            self.remote.append(links.copy(s, d, dev(y, x, z // 2, zz), send + k, recv + (z % 2) * 2 + c))
            links.open.append((self.remote[k], None if k else self.away))
            if k == 0:
                self.local = links.here_later(s, d)
        for i in (0, 1):
            for h in (0, 1):
                d = dst.at[i, h]
                mine = both(z == 2 * c + i, h == c)
                self.back.append((links.copy(d, d, dev(y, x, 1 - c, z), send, recv + 2 * i + h), jnp.logical_not(mine)))

    def start(self):
        for q in self.remote[1:]:
            q.start()
        pl.when(self.away)(self.remote[0].start)
        pl.when(self.here)(self.local.start)

    def finish(self):
        pl.when(self.here)(self.local.wait)
        for q, ok in self.back:
            pl.when(ok)(q.wait_recv)


def swap_halves(u):
    lane = lax.broadcasted_iota(jnp.int32, u.shape, 1) % HD
    return jnp.where(lane < HD // 2, pltpu.roll(u, 128 - HD // 2, 1), pltpu.roll(u, HD // 2, 1))


def head_mask(shape, h):
    lane = lax.broadcasted_iota(jnp.int32, shape, 1)
    return (lane < HD) if h == 0 else (lane >= HD)


def dot_t(a, b):
    return lax.dot_general(a, b, (((1,), (1,)), ((), ())), preferred_element_type=F32)


def project_step(xw, gv, w, cos, sin, n1, q, k, v, r):
    rows = pl.ds(pl.multiple_of(r * 256, 256), 256)
    u = xw[r // 2, pl.ds((r % 2) * 2, 2)].reshape(256, 1024).astype(F32)
    d = u - jnp.mean(u, axis=-1, keepdims=True)
    scaling = lax.rsqrt(jnp.mean(d * d, axis=-1, keepdims=True) + 1e-05)
    n = (d * scaling * gv[0:1, :] + gv[1:2, :]).astype(BF)
    n1[rows, :] = n
    for g in range(4):
        lanes = pl.ds(128 * g, 128)
        t = jnp.dot(n, w[:, :, :, :, pl.ds(384 * g, 384)].reshape(1024, 384), preferred_element_type=F32)
        for j, o in ((0, q), (1, k)):
            s = t[:, 128 * j:128 * j + 128]
            o[rows, lanes] = (s * cos[rows, :] + swap_halves(s) * sin[rows, :]).astype(BF)
        v[rows, lanes] = t[:, 256:].astype(BF)


def attend_step(q, k, v, o, lse, g, i):
    lanes = pl.ds(pl.multiple_of(g * 128, 128), 128)
    rows = pl.ds(pl.multiple_of(i * 256, 256), 256)
    qs = q[rows, lanes] * jnp.asarray(HD ** -0.5, BF)
    kk, vv = k[:, lanes], v[:, lanes]
    outs, logs = [], []
    for h in (0, 1):
        qh = jnp.where(head_mask(qs.shape, h), qs, jnp.zeros_like(qs))
        s = dot_t(qh, kk)
        m = jnp.max(s, axis=-1, keepdims=True)
        e = jnp.exp(s - m)
        t = jnp.sum(e, axis=-1, keepdims=True)
        p = (e * (1.0 / t)).astype(BF)
        outs.append(jnp.dot(p, vv, preferred_element_type=F32))
        logs.append(jnp.broadcast_to(m + jnp.log(t), qs.shape))
    keep = head_mask(qs.shape, 0)
    o[rows, lanes] = jnp.where(keep, outs[0], outs[1]).astype(BF)
    t = jnp.transpose(jnp.where(keep, logs[0], logs[1]))
    lse[pl.ds(2 * g, 1), rows] = t[0:1]
    lse[pl.ds(2 * g + 1, 1), rows] = t[HD:HD + 1]


def attend_back_step(q, k, v, do, lse, cos, sin, dqkv, dka, dva, g, i):
    lanes = pl.ds(pl.multiple_of(g * 128, 128), 128)
    rows = pl.ds(pl.multiple_of(i * 256, 256), 256)

    @pl.when(i == 0)
    def _():
        dka[...] = jnp.zeros_like(dka)
        dva[...] = jnp.zeros_like(dva)
    kk, vv, go = k[:, lanes], v[:, lanes], do[rows, lanes]
    qs = q[rows, lanes] * jnp.asarray(HD ** -0.5, BF)
    logs = lse[pl.ds(2 * g, 1), rows], lse[pl.ds(2 * g + 1, 1), rows]
    dks, dvs, dqs = [], [], []
    for h in (0, 1):
        keep = head_mask(kk.shape, h)
        zero = jnp.zeros_like(kk)
        s = dot_t(jnp.where(keep, kk, zero), qs)
        p = jnp.exp(s - logs[h])
        dp = dot_t(jnp.where(keep, vv, zero), go)
        pd = p * dp
        ds = (pd - p * jnp.sum(pd, axis=0, keepdims=True)).astype(BF)
        dvs.append(jnp.dot(p.astype(BF), go, preferred_element_type=F32))
        dks.append(jnp.dot(ds, qs, preferred_element_type=F32))
        dqs.append(lax.dot_general(ds, kk, (((0,), (0,)), ((), ())), preferred_element_type=F32))
    keep = head_mask(kk.shape, 0)
    dka[...] += jnp.where(keep, dks[0], dks[1])
    dva[...] += jnp.where(keep, dvs[0], dvs[1])
    u = jnp.where(head_mask(go.shape, 0), dqs[0], dqs[1]) * HD ** -0.5
    dqkv[rows, pl.ds(pl.multiple_of(g * 384, 128), 128)] = (
        u * cos[rows, :] - swap_halves(u) * sin[rows, :]).astype(BF)

    @pl.when(i == 3)
    def _():
        u = dka[...]
        dqkv[:, pl.ds(pl.multiple_of(128 + g * 384, 128), 128)] = (
            u * cos[...] - swap_halves(u) * sin[...]).astype(BF)
        dqkv[:, pl.ds(pl.multiple_of(256 + g * 384, 128), 128)] = dva[...].astype(BF)


class Incoming:
    def __init__(self, links, me, src, mid, dst):
        y, x, c, z = me
        partner = dev(y, x, 1 - c, z)
        self.swap = [links.later(src.at[i, pl.ds((1 - c) * 128, 128)], mid.at[2 * c + i], partner) for i in (0, 1)]
        send, recv = links.take(4), links.take(4)
        self.sends, self.kept, self.got = [], [], []
        m = links.m
        links.m += 1
        for w in range(4):
            d = dst.at[0, z]
            for ok, s in ((c == w // 2, src.at[w % 2, pl.ds(c * 128, 128)]), (c != w // 2, mid.at[w])):
                away, here = both(ok, z != w), both(ok, z == w)
                q = links.copy(s, d, dev(y, x, c, w), send + w, recv + z)
                self.sends.append((q, away))
                links.open.append((q, away))
                self.kept.append((pltpu.make_async_copy(s, d, links.local.at[m]), here))
        for zz in range(4):
            d = dst.at[0, zz]
            self.got.append((links.copy(d, d, dev(y, x, c, zz), send, recv + zz), z != zz))
        self.pair = links.later(dst.at[0], dst.at[1], partner)

    def begin(self):
        for q in self.swap:
            q.start()

    def send(self):
        for q in self.swap:
            q.wait_recv()
        for q, ok in self.sends + self.kept:
            pl.when(ok)(q.start)

    def arrive(self):
        for q, ok in self.kept:
            pl.when(ok)(q.wait)
        for q, ok in self.got:
            pl.when(ok)(q.wait_recv)
        self.pair.start()

    def finish(self):
        self.pair.wait_recv()


def disperse(links, single, bundle, me, route):
    y, x, c, z = me
    to_x, to_y = dev(y, 1 - x, c, z), dev(1 - y, x, c, z)
    mine = y * 2 + x
    if route == 0:
        two, three, other = to_y, to_x, (1 - y) * 2 + x
    else:
        two, three, other = to_x, to_y, y * 2 + 1 - x
    over_z = [links.later(single(mine, z), single(mine, z), dev(y, x, c, (z + k) % 4)) for k in (1, 2, 3)]
    cross = links.later(bundle(mine), bundle(mine), two)
    last = [links.later(bundle(mine), bundle(mine), three), links.later(bundle(other), bundle(other), three)]

    def start():
        for q in over_z:
            q.start()

    def first():
        for q in over_z:
            q.wait_recv()
        cross.start()
        last[0].start()

    def second():
        cross.wait_recv()
        last[1].start()

    def finish():
        for q in last:
            q.wait_recv()
    return start, first, second, finish


FORE_PIECES = (
    ("gu", 5, 1),
    ("d", 0, 1),
    ("qkv", 0, 1),
    ("o", 0, 0),
    ("gu", 6, 0),
    ("gu", 1, 0),
    ("gu", 2, 1),
    ("qkv", 1, 0),
    ("gu", 0, 1),
    ("gu", 3, 1),
    ("gu", 4, 0),
    ("d", 1, 0),
    ("d", 3, 1),
    ("gu", 7, 0),
    ("d", 2, 1),
)
FORE_ORDER = (
    ((17, 0), (0, 0), (1, 0), (2, 0), (3, 0), (4, 0), (5, 0), (6, 0), (7, 0), (15, 0), (8, 0), (9, 0), (10, 0),
     (11, 0), (12, 0), (13, 0), (14, 0), (17, 1), (17, 2), (17, 3), (0, 1), (1, 1), (0, 2), (1, 2), (2, 1), (0, 3),
     (3, 1), (1, 3), (2, 2), (4, 1), (5, 1), (6, 1), (3, 2), (2, 3), (7, 1), (6, 2), (4, 2), (3, 3), (5, 2),
     (4, 3), (7, 2), (5, 3), (15, 1), (6, 3), (8, 1), (7, 3), (15, 2),),
    ((8, 2), (9, 1)), ((10, 1),), (), (), (), (), ((11, 1), (8, 3), (9, 2)), (), (), (), ((12, 1),), (), (), (),
    ((10, 2), (13, 1), (16, 0)), (), (), ((9, 3), (10, 3), (11, 2), (12, 2), (14, 1)), (), ((11, 3), (13, 2)),
    ((12, 3), (14, 2), (16, 1), (13, 3)), ((16, 2), (14, 3)),
)


def rotary_tables(near_cos, near_sin, far_cos, far_sin, cos, sin):
    lane = lax.broadcasted_iota(jnp.int32, (128, 128), 1)
    sign = jnp.where(lane % HD < HD // 2, -1.0, 1.0)
    for i in range(8):
        a, b = far_cos[i:i + 1, :], far_sin[i:i + 1, :]
        cos[128 * i:128 * i + 128, :] = near_cos[...] * a - near_sin[...] * b
        sin[128 * i:128 * i + 128, :] = sign * (near_sin[...] * a + near_cos[...] * b)


def fore_kernel(tok, cot, wq, wk, wv, wg, wu, wo, wd, g0, g1, g2, g3, species, count, weight,
                near_cos, near_sin, far_cos, far_sin, *rest):
    (oqkv, ogu, oo, od, xh, cw, gvo, n1o, qo, ko, vo, atto, lseo, n2o, mido, gateo, upo, hido, coso, sino,
     own_qkv, oth_qkv, own_gu, oth_gu, gp, cos, sin,
     tmid, cmid, gains, gv, xw, w3, n1, q, k, v, att, lse, wos, sent, came, mid, n2, wgs, wus,
     gate, up, hid, send, recv, local) = rest
    me = y, x, c, z = place()
    yx = y * 2 + x
    partner = dev(y, x, 1 - c, z)

    def prepare():
        def columns(src, own, oth, width, base, stride):
            for g in range(4):
                lanes = pl.ds(base + stride * g, width)
                own[:, lanes] = src[:, pl.ds(pl.multiple_of((2 * g + c) * width, width), width)]
                oth[:, lanes] = src[:, pl.ds(pl.multiple_of((2 * g + 1 - c) * width, width), width)]
        for j, src in enumerate((wq, wk, wv)):
            columns(src, own_qkv, oth_qkv, 128, 128 * j, 384)
        for j, src in enumerate((wg, wu)):
            columns(src, own_gu, oth_gu, 512, 2048 * j, 512)
        gp[...] = jnp.zeros_like(gp)
        for i, src in enumerate((g0, g1, g2, g3)):
            gp[i:i + 1, 0:32] = src[...].astype(F32)
        gp[...] = pltpu.roll(gp[...], z * 32, 1)
        table = weight[...] * lax.rsqrt(count[...].astype(F32) / 400.0)
        pick = lax.broadcasted_iota(jnp.int32, table.shape, 1)
        lane = lax.broadcasted_iota(jnp.int32, (1, 128), 1)
        row = jnp.zeros((1, 128), F32)
        for i in (0, 1):
            f = jnp.sum(jnp.where(pick == species[i], table, 0.0), axis=1, keepdims=True)
            row = jnp.where(lane == i, f, row)
        gp[4:5, :] = jnp.where(z == 0, row, jnp.zeros_like(row))
    greet(y, x, c, z, prepare)
    links = Links(send, recv, local)
    tin, cin = Incoming(links, me, tok, tmid, xw), Incoming(links, me, cot, cmid, cw)
    tin.begin()
    swaps = [links.to(gp, gains.at[yx, c, z], partner), links.to(oth_qkv, oqkv.at[yx, c, z], partner),
             links.to(oth_gu, ogu.at[yx, c, z], partner)]
    loc = [links.here(gp, gains.at[yx, c, z]), links.here(own_qkv, oqkv.at[yx, c, z]),
           links.here(own_gu, ogu.at[yx, c, z]), links.here(wo, oo.at[yx, z]), links.here(wd, od.at[yx, z])]
    work = []
    for name, index, route in FORE_PIECES:
        if name in ("qkv", "gu"):
            arr, cols = (oqkv, 768) if name == "qkv" else (ogu, 512)
            lanes = pl.ds(index * cols, cols)
            work.append(disperse(links, lambda i, zz, arr=arr, lanes=lanes: arr.at[i, :, zz, :, lanes],
                                 lambda i, arr=arr, lanes=lanes: arr.at[i, :, :, :, lanes], me, route))
        else:
            arr = oo if name == "o" else od
            rows = pl.ds(index * 32, 32)
            work.append(disperse(links, lambda i, zz, arr=arr, rows=rows: arr.at[i, zz, rows],
                                 lambda i, arr=arr, rows=rows: arr.at[i, :, rows], me, route))

    def later():
        cin.begin()
        cin.send()
    work += [(tin.send, tin.arrive, tin.finish), (later, cin.arrive, cin.finish),
             disperse(links, lambda i, zz: gains.at[i, :, zz], lambda i: gains.at[i], me, 1)]
    swap = links.wanted(sent, came, partner)
    share = links.later(n2.at[pl.ds(0, 512)], n2.at[pl.ds(512, 512)], partner)
    for e in loc:
        e.wait()
    for e in swaps:
        e.wait_recv()

    def comm(slot):
        for i, stage in FORE_ORDER[slot]:
            work[i][stage]()

    keep = []

    def put(src, dst):
        keep.append(links.here(src, dst))
    comm(0)
    wload = links.here(oqkv, w3)
    rotary_tables(near_cos, near_sin, far_cos, far_sin, cos, sin)
    put(cos, coso)
    put(sin, sino)
    wload.wait()
    for i in range(4):
        for j in (0, 1):
            gv[:, pl.ds((2 * i + j) * 128, 128)] = (gains[i, j, 0] + gains[i, j, 1]) + (gains[i, j, 2] + gains[i, j, 3])

    def rows_of(step):
        lax.fori_loop(0, 4, lambda r, _: (step(r), 0)[1], 0)
    rows_of(lambda r: project_step(xw, gv, w3, cos, sin, n1, q, k, v, r))
    for a, b in ((gv, gvo), (n1, n1o), (q, qo), (k, ko), (v, vo), (xw.at[0], xh)):
        put(a, b)
    comm(1)

    def step(t, _):
        attend_step(q, k, v, att, lse, t // 4, t % 4)
        for slot in range(2, 17):
            if FORE_ORDER[slot]:
                pl.when(t == slot - 2)(lambda slot=slot: comm(slot))
        return 0
    lax.fori_loop(0, 16, step, 0)
    comm(17)
    wload = links.here(oo, wos)
    put(att, atto)
    put(lse, lseo)
    wload.wait()

    def terms(r, out, first):
        rows = pl.ds(pl.multiple_of(r * 256, 256), 256)
        out[rows, :] = jnp.dot(att[pl.ds(pl.multiple_of(first + r * 256, 256), 256), :], wos[...].reshape(512, 1024),
                               preferred_element_type=F32)
    lax.fori_loop(0, 2, lambda r, _: (terms(r, sent, 512), 0)[1], 0)
    swap.start()
    lax.fori_loop(0, 2, lambda r, _: (terms(r, mid, 0), 0)[1], 0)
    swap.wait()

    def second_norm(r):
        rows = pl.ds(pl.multiple_of(r * 128, 128), 128)
        u = xw[0, r].astype(F32) + (mid[rows, :] + came[rows, :])
        mid[rows, :] = u
        d = u - jnp.mean(u, axis=-1, keepdims=True)
        scaling = lax.rsqrt(jnp.mean(d * d, axis=-1, keepdims=True) + 1e-05)
        n2[rows, :] = (d * scaling * gv[2:3, :] + gv[3:4, :]).astype(BF)
    rows_of(second_norm)
    share.start()
    put(mid, mido)
    comm(18)
    share.wait_recv()
    put(n2, n2o)
    for j in range(4):
        if j:
            comm(18 + j)
        lanes = pl.ds(512 * j, 512)
        lg = links.here(ogu.at[:, :, :, :, lanes], wgs)
        lu = links.here(ogu.at[:, :, :, :, pl.ds(2048 + 512 * j, 512)], wus)
        lg.wait()
        lu.wait()

        def hidden_units(r, lanes=lanes):
            rows = pl.ds(pl.multiple_of(r * 256, 256), 256)
            n = n2[rows, :]
            a = jnp.dot(n, wgs[...].reshape(1024, 512), preferred_element_type=F32)
            b = jnp.dot(n, wus[...].reshape(1024, 512), preferred_element_type=F32)
            hid[rows, lanes] = (a * jax.nn.sigmoid(a) * b).astype(BF)
            gate[rows, lanes] = a.astype(BF)
            up[rows, lanes] = b.astype(BF)
        rows_of(hidden_units)
        for a, b in ((hid, hido), (gate, gateo), (up, upo)):
            put(a.at[:, lanes], b.at[:, lanes])
    comm(22)
    for e in keep:
        e.wait()
    links.drain()


def fore(*args):
    S = jax.ShapeDtypeStruct
    V = pltpu.VMEM
    table = [V((1024, 128), F32)] * 2
    specs = [VM] * 20
    specs[13] = pl.BlockSpec(memory_space=pltpu.SMEM)
    return pl.pallas_call(
        fore_kernel,
        out_shape=(
            S((4, 2, 4, 32, 1536), BF), S((4, 2, 4, 32, 4096), BF), S((4, 4, 32, 1024), BF), S((4, 4, 128, 1024), BF),
            S((4, 128, 1024), BF), S((2, 4, 128, 1024), BF), S((8, 1024), F32), S((1024, 1024), BF),
            S((1024, 512), BF), S((1024, 512), BF), S((1024, 512), BF), S((1024, 512), BF), S((8, 1024), F32),
            S((1024, 1024), BF), S((512, 1024), F32), S((1024, 2048), BF), S((1024, 2048), BF), S((1024, 2048), BF),
            S((1024, 128), F32), S((1024, 128), F32),
        ),
        in_specs=specs,
        out_specs=[ANY] * 20,
        scratch_shapes=[V((32, 1536), BF)] * 2 + [V((32, 4096), BF)] * 2 + [V((8, 128), F32)] + table + [
            V((4, 128, 1024), BF), V((4, 128, 1024), BF), V((4, 2, 4, 8, 128), F32), V((8, 1024), F32),
            V((2, 4, 128, 1024), BF), V((4, 2, 4, 32, 1536), BF), V((1024, 1024), BF),
            V((1024, 512), BF), V((1024, 512), BF), V((1024, 512), BF), V((1024, 512), BF), V((8, 1024), F32),
            V((4, 4, 32, 1024), BF), V((512, 1024), F32), V((512, 1024), F32), V((512, 1024), F32),
            V((1024, 1024), BF), V((4, 2, 4, 32, 512), BF), V((4, 2, 4, 32, 512), BF),
            V((1024, 2048), BF), V((1024, 2048), BF), V((1024, 2048), BF),
            pltpu.SemaphoreType.DMA((200,)),
            pltpu.SemaphoreType.DMA((200,)),
            pltpu.SemaphoreType.DMA((72,)),
        ],
        compiler_params=pltpu.CompilerParams(collective_id=0, has_side_effects=True, vmem_limit_bytes=67043328),
    )(*args)


PIECES = (
    ("gu", 6, 0),
    ("d", 0, 2),
    ("o", 0, 1),
    ("gu", 7, 1),
    ("gu", 1, 0),
    ("d", 3, 0),
    ("gu", 0, 2),
    ("d", 2, 0),
    ("qkv", 0, 1),
    ("gu", 3, 1),
    ("gu", 5, 0),
    ("qkv", 1, 1),
    ("qkv", 3, 1),
    ("gu", 4, 0),
    ("d", 1, 0),
    ("gu", 2, 2),
    ("qkv", 2, 1),
)
SHAPES = {"d": (4, 32, 1024), "o": (4, 32, 1024), "gu": (2, 4, 32, 512), "qkv": (2, 4, 32, 384)}
ORDER = (
    (), ((1, 0), (5, 0), (7, 0)), ((1, 1), (5, 1), (6, 0), (14, 0)), ((1, 2), (1, 3), (4, 0), (5, 2), (7, 1)),
    ((0, 0), (6, 1), (6, 2), (14, 1), (15, 0)), ((1, 4), (4, 1), (5, 3), (6, 3), (7, 2), (13, 0), (14, 2)),
    ((0, 1), (7, 3), (10, 0), (15, 1), (15, 2)), ((2, 0), (4, 2), (6, 4), (14, 3)),
    ((0, 2), (2, 1), (3, 0), (13, 1), (17, 0), (15, 3)), (), ((4, 3), (10, 1)), ((3, 1),), ((0, 3),), ((8, 0),), (),
    ((2, 2), (15, 4)), ((13, 2),), ((3, 2),), ((10, 2),), ((8, 1), (9, 0)), (), (), ((8, 2), (17, 1)), (),
    ((9, 1), (2, 3), (11, 0)), (), (), ((13, 3),), ((9, 2), (11, 1), (12, 0)),
    ((3, 3), (18, 0), (19, 0), (8, 3), (10, 3), (11, 2), (12, 1), (16, 0), (19, 1), (9, 3), (12, 2), (16, 1),
     (19, 2), (16, 2), (18, 1), (11, 3), (12, 3), (19, 3), (16, 3),),

)


def total_over_devices(links, me, acc, got):
    y, x, c, z = me
    hops = [links.wanted(acc, got.at[i], d) for i, d in
            enumerate((dev(y, x, 1 - c, z), dev(y, 1 - x, c, z), dev(1 - y, x, c, z)))]
    over_z = [links.wanted(acc, got.at[2 + k], dev(y, x, c, (z + k) % 4)) for k in (1, 2, 3)]

    def settle(i):
        hops[i].wait()
        acc[...] += got[i]

    def chip():
        hops[0].start()
        settle(0)
        hops[1].start()

    def second():
        settle(1)
        hops[2].start()

    def third():
        settle(2)
        for q in over_z:
            q.start()

    def last():
        for q in over_z:
            q.wait()
        acc[...] += got[3] + (got[4] + got[5])
    return chip, second, third, last


def rows_dot(a, b):
    return lax.dot_general(a, b, (((0,), (0,)), ((), ())), preferred_element_type=F32)


def each(count, step):
    def body(r, _):
        step(r)
        return 0
    lax.fori_loop(0, count, body, 0)


def block(i, size):
    return pl.ds(pl.multiple_of(i * size, size), size)


def norm_parts(u):
    d = u - jnp.mean(u, axis=-1, keepdims=True)
    scaling = lax.rsqrt(jnp.mean(d * d, axis=-1, keepdims=True) + 1e-05)
    return d * scaling, scaling


def norm_back(upstream, normed, scaling):
    return scaling * (upstream - jnp.mean(upstream, axis=-1, keepdims=True)
                      - normed * jnp.mean(upstream * normed, axis=-1, keepdims=True))


def back_kernel(cw, hido, od, n2o, gateo, upo, ogu, mido, oo, atto, qo, ko, vo, lseo, n1o, oqkv, xh,
                cos, sin, gv, *rest):
    fqkv, fgu, fo, fd, fgain, out_w, ig_w = rest[:7]
    scratch = list(rest[7:])
    (gd, ggu, go, gw, mg, sent, came, mlow, ag, out16, ig, gacc, ggot, send, recv, local, ready) = scratch[-17:]
    me = y, x, c, z = place()
    partner = dev(y, x, 1 - c, z)
    greet(y, x, c, z)
    links = Links(send, recv, local)
    work = []
    finals = []
    for name, index, route in PIECES:
        bufs = [scratch.pop(0) for _ in range(4)]
        if name in ("qkv", "gu"):
            src, dst = (gw, fqkv) if name == "qkv" else (ggu, fgu)
            cols = SHAPES[name][3]
            lanes = pl.ds(index * cols, cols)

            def at(yy, xx, src=src, index=index):
                return src.at[index, yy * 2 + xx]

            def deliver(total, dst=dst, lanes=lanes):
                there = links.later(total.at[1 - c], dst.at[c, :, lanes], partner)
                here = links.here_later(total.at[c], dst.at[c, :, lanes])
                finals.extend((there.wait_recv, here.wait))
                return there, here
        else:
            src, dst = (gd, fd) if name == "d" else (go, fo)
            rows = pl.ds(index * 32, 32)

            def at(yy, xx, src=src, rows=rows):
                return src.at[yy * 2 + xx, :, rows]

            def deliver(total, dst=dst, rows=rows):
                here = links.here_later(total, dst.at[rows])
                finals.append(here.wait)
                return (here,)
        work.append(collect(links, at, me, route, bufs, deliver))
    o1 = Outgoing(links, me, out16, out_w)
    o2 = Outgoing(links, me, ig, ig_w)
    work += [(o1.start, o1.finish), (o2.start, o2.finish), total_over_devices(links, me, gacc, ggot)]
    swaps = [links.wanted(sent, came, partner) for _ in range(3)]
    share = links.later(mlow.at[0], mlow.at[1], partner)

    def comm(slot):
        for i, stage in ORDER[slot]:
            work[i][stage]()

    def swap(n):
        if n:
            pl.semaphore_wait(ready, 1)
        swaps[n].start()

    def read(n):
        if n < 2:
            pl.semaphore_signal(ready, inc=1, device_id=partner, device_id_type=MESH)

    gacc[...] = jnp.zeros_like(gacc)
    lane = lax.broadcasted_iota(jnp.int32, (1, 1024), 1)
    here = (2 * (y * 2 + x) + z // 2) * 128 + z % 2
    factor = jnp.sum(jnp.where(lane == here, gv[4:5, :], 0.0), axis=1, keepdims=True)

    def hidden_layer(low):
        a = links.here(cw, low)

        def down(hv):
            b = links.here(hido, hv)
            a.wait()

            def scale(i):
                low[i // 4, i % 4] = (factor * low[i // 4, i % 4].astype(F32)).astype(BF)
            each(8, scale)
            b.wait()
            comm(0)

            def weights(r):
                u = rows_dot(hv[:, block(r, 256)], low[...].reshape(1024, 1024))
                gd[r // 2, pl.ds((r % 2) * 2, 2)] = u.astype(BF).reshape(2, 128, 1024)
            each(8, weights)
        pl.run_scoped(down, pltpu.VMEM((1024, 2048), BF))

        def units(n2, gate, up, dgate, dup, wg, wu, wd):
            a = links.here(n2o, n2)
            for j in range(4):
                lanes = pl.ds(512 * j, 512)
                got = [links.here(od.at[j], wd), links.here(gateo.at[:, lanes], gate), links.here(upo.at[:, lanes], up),
                       links.here(ogu.at[:, :, :, :, lanes], wg),
                       links.here(ogu.at[:, :, :, :, pl.ds(2048 + 512 * j, 512)], wu)]
                comm(1 + j)
                for q in got:
                    q.wait()

                def grads(r):
                    rows = block(r, 256)
                    g = dot_t(low[r // 2, pl.ds((r % 2) * 2, 2)].reshape(256, 1024), wd[...].reshape(512, 1024))
                    a, b = gate[rows, :].astype(F32), up[rows, :].astype(F32)
                    t = jax.nn.sigmoid(a)
                    dgate[rows, :] = (g * b * t * (1.0 + a * (1.0 - t))).astype(BF)
                    dup[rows, :] = (g * a * t).astype(BF)
                each(4, grads)
                if j == 0:
                    a.wait()

                def weights(r):
                    n = n2[:, block(r, 256)]
                    ggu[j, r] = rows_dot(n, dgate[...]).astype(BF).reshape(2, 4, 32, 512)
                    ggu[4 + j, r] = rows_dot(n, dup[...]).astype(BF).reshape(2, 4, 32, 512)
                each(4, weights)

                def terms(r, out, first):
                    rows = pl.ds(pl.multiple_of(first + r * 256, 256), 256)
                    u = (dot_t(dgate[rows, :], wg[...].reshape(1024, 512))
                         + dot_t(dup[rows, :], wu[...].reshape(1024, 512)))
                    dst = block(r, 256)
                    out[dst, :] = u if j == 0 else out[dst, :] + u
                each(2, lambda r: terms(r, sent, 512))
                if j == 3:
                    swap(0)
                each(2, lambda r: terms(r, mg, 0))
        pl.run_scoped(units, pltpu.VMEM((1024, 1024), BF), *[pltpu.VMEM((1024, 512), BF)] * 4,
                      *[pltpu.VMEM((4, 2, 4, 32, 512), BF)] * 2, pltpu.VMEM((4, 128, 1024), BF))
    pl.run_scoped(hidden_layer, pltpu.VMEM((2, 4, 128, 1024), BF))
    comm(5)

    def second_norm(mid, cot):
        a, b = links.here(mido, mid), links.here(cw.at[0], cot)
        a.wait()
        b.wait()
        swaps[0].wait()

        def part(r):
            rows = block(r, 128)
            gn = mg[rows, :] + came[rows, :]
            normed, scaling = norm_parts(mid[rows, :])
            gacc[2:3, :] += jnp.sum(gn * normed, axis=0, keepdims=True)
            gacc[3:4, :] += jnp.sum(gn, axis=0, keepdims=True)
            u = factor * cot[r].astype(F32) + norm_back(gn * gv[2:3, :], normed, scaling)
            mg[rows, :] = u
            mlow[0, r] = u.astype(BF)
        each(4, part)
        read(0)
        share.start()
    pl.run_scoped(second_norm, pltpu.VMEM((512, 1024), F32), pltpu.VMEM((4, 128, 1024), BF))
    comm(6)

    def out_layer(w, att):
        a, b = links.here(oo, w), links.here(atto, att)
        a.wait()
        b.wait()
        share.wait_recv()

        def weights(r):
            u = rows_dot(att[:, block(r, 256)], mlow[...].reshape(1024, 1024))
            go[pl.ds(2 * r, 2)] = u.astype(BF).reshape(2, 4, 32, 1024)
        each(2, weights)

        def grads(r):
            u = dot_t(mlow[r // 2, pl.ds((r % 2) * 2, 2)].reshape(256, 1024), w[...].reshape(512, 1024))
            ag[block(r, 256), :] = u.astype(BF)
        each(4, grads)
    pl.run_scoped(out_layer, pltpu.VMEM((4, 4, 32, 1024), BF), pltpu.VMEM((1024, 512), BF))
    comm(7)

    def output(hv, w, mid):
        got = [links.here(hido, hv), links.here(od, w), links.here(mido, mid)]
        for q in got:
            q.wait()

        def term(r, first):
            return jnp.dot(hv[pl.ds(pl.multiple_of(first + r * 256, 256), 256), :], w[...].reshape(2048, 1024),
                           preferred_element_type=F32)

        def theirs(r):
            sent[block(r, 256), :] = term(r, 512)
        each(2, theirs)
        swap(1)

        def mine(r):
            mid[block(r, 256), :] += term(r, 0)
        each(2, mine)
        swaps[1].wait()

        def total(r):
            out16[r] = (mid[block(r, 128), :] + came[block(r, 128), :]).astype(BF)
        each(4, total)
        read(1)
    pl.run_scoped(output, pltpu.VMEM((1024, 2048), BF), pltpu.VMEM((4, 4, 128, 1024), BF), pltpu.VMEM((512, 1024), F32))

    def attention(dqkv):
        def heads(q, k, v, lse, n1, dka, dva):
            got = [links.here(a, b) for a, b in ((qo, q), (ko, k), (vo, v), (lseo, lse), (n1o, n1))]
            for e in got:
                e.wait()

            def step(t):
                for slot in range(20):
                    if ORDER[8 + slot]:
                        pl.when(t == slot)(lambda slot=slot: comm(8 + slot))
                g, i = t // 5, t % 5

                @pl.when(i < 4)
                def _():
                    attend_back_step(q, k, v, ag, lse, cos, sin, dqkv, dka, dva, g, i)

                @pl.when(i == 4)
                def _():
                    u = rows_dot(n1[...], dqkv[:, pl.ds(pl.multiple_of(g * 384, 128), 384)])
                    gw[g] = u.astype(BF).reshape(4, 2, 4, 32, 384)
            each(20, step)
        pl.run_scoped(heads, *[pltpu.VMEM((1024, 512), BF)] * 3, pltpu.VMEM((8, 1024), F32),
                      pltpu.VMEM((1024, 1024), BF), *[pltpu.VMEM((1024, 128), F32)] * 2)

        def first_norm(w, tokens, mine):
            got = [links.here(oqkv, w), links.here(xh, tokens)]
            comm(28)
            for e in got:
                e.wait()

            def term(r, out, first):
                out[block(r, 256), :] = dot_t(dqkv[pl.ds(pl.multiple_of(first + r * 256, 256), 256), :],
                                              w[...].reshape(1024, 1536))
            each(2, lambda r: term(r, sent, 512))
            swap(2)
            each(2, lambda r: term(r, mine, 0))
            swaps[2].wait()

            def part(r):
                rows = block(r, 128)
                gn = mine[rows, :] + came[rows, :]
                normed, scaling = norm_parts(tokens[r].astype(F32))
                gacc[0:1, :] += jnp.sum(gn * normed, axis=0, keepdims=True)
                gacc[1:2, :] += jnp.sum(gn, axis=0, keepdims=True)
                ig[r] = (mg[rows, :] + norm_back(gn * gv[0:1, :], normed, scaling)).astype(BF)
            each(4, part)
        pl.run_scoped(first_norm, pltpu.VMEM((4, 2, 4, 32, 1536), BF), pltpu.VMEM((4, 128, 1024), BF),
                      pltpu.VMEM((512, 1024), F32))
    pl.run_scoped(attention, pltpu.VMEM((1024, 1536), BF))
    comm(29)
    finals.append(links.here(gacc, fgain).wait)
    for f in finals:
        f()
    links.drain()


def back(*args):
    scratch = []
    for name, index, route in PIECES:
        scratch += reduce_shapes(SHAPES[name], route)
    return pl.pallas_call(
        back_kernel,
        out_shape=(
            jax.ShapeDtypeStruct((2, 32, 1536), F32),
            jax.ShapeDtypeStruct((2, 32, 4096), F32),
            jax.ShapeDtypeStruct((32, 1024), F32),
            jax.ShapeDtypeStruct((128, 1024), F32),
            jax.ShapeDtypeStruct((8, 1024), F32),
            jax.ShapeDtypeStruct((2, 2, 128, 1024), BF),
            jax.ShapeDtypeStruct((2, 2, 128, 1024), BF),
        ),
        in_specs=[ANY] * 17 + [VM] * 3,
        out_specs=[ANY] * 7,
        scratch_shapes=scratch + [
            pltpu.VMEM((4, 4, 128, 1024), BF),
            pltpu.VMEM((8, 4, 2, 4, 32, 512), BF),
            pltpu.VMEM((4, 4, 32, 1024), BF),
            pltpu.VMEM((4, 4, 2, 4, 32, 384), BF),
            pltpu.VMEM((512, 1024), F32),
            pltpu.VMEM((512, 1024), F32),
            pltpu.VMEM((512, 1024), F32),
            pltpu.VMEM((2, 4, 128, 1024), BF),
            pltpu.VMEM((1024, 512), BF),
            pltpu.VMEM((4, 128, 1024), BF),
            pltpu.VMEM((4, 128, 1024), BF),
            pltpu.VMEM((8, 1024), F32),
            pltpu.VMEM((6, 8, 1024), F32),
            pltpu.SemaphoreType.DMA((192,)),
            pltpu.SemaphoreType.DMA((192,)),
            pltpu.SemaphoreType.DMA((96,)),
            pltpu.SemaphoreType.REGULAR,
        ],
        compiler_params=pltpu.CompilerParams(collective_id=1, has_side_effects=True, vmem_limit_bytes=67043328),
    )(*args)


def finish_kernel(fqkv, fgu, fo, fd, fgain, out_w, ig_w, out, ig, gq, gk, gv, go, gg, gu, gd, gains):
    for n in (0, 1):
        for g in range(4):
            for j, dst in enumerate((gq, gk, gv)):
                dst[:, pl.ds(128 * (2 * g + n), 128)] = fqkv[n, :, pl.ds(384 * g + 128 * j, 128)]
            for j, dst in enumerate((gg, gu)):
                dst[:, pl.ds(512 * (2 * g + n), 512)] = fgu[n, :, pl.ds(2048 * j + 512 * g, 512)]
    go[...] = fo[...]
    gd[...] = fd[...]

    def rows(i):
        out[i // 2, pl.ds(pl.multiple_of((i % 2) * 128, 128), 128)] = out_w[i // 2, i % 2]
        ig[i // 2, pl.ds(pl.multiple_of((i % 2) * 128, 128), 128)] = ig_w[i // 2, i % 2].astype(F32)
    each(4, rows)
    first = (lax.axis_index("dp") * 4 + lax.axis_index("seq")) * 32
    gains[...] = pltpu.roll(fgain[...], (1024 - first) % 1024, 1)[:, 0:128]


def finish(*args):
    S = jax.ShapeDtypeStruct
    return pl.pallas_call(
        finish_kernel,
        out_shape=(S((2, 256, 1024), BF), S((2, 256, 1024), F32)) + (S((32, 1024), F32),) * 4
        + (S((32, 4096), F32),) * 2 + (S((128, 1024), F32), S((8, 128), F32)),
        in_specs=[VM] * 7,
        out_specs=[VM] * 10,
        compiler_params=pltpu.CompilerParams(vmem_limit_bytes=VMEM_BYTES),
    )(*args)


def angle_tables(c):
    lane = jnp.arange(128, dtype=jnp.int32)
    freqs = 10000.0 ** (-2.0 * (lane % 32).astype(jnp.float32) / HD)
    block = jnp.arange(8, dtype=jnp.int32)
    far = (block % 4) * 256 + jnp.where(block < 4, c, 1 - c) * 128
    rows = jnp.concatenate([jnp.arange(128, dtype=jnp.int32), far]).astype(jnp.float32)
    angle = rows[:, None] * freqs[None, :]
    cos, sin = jnp.cos(angle), jnp.sin(angle)
    return cos[:128], sin[:128], cos[128:], sin[128:]


def paired(
    tokens,
    cotangent,
    species_index,
    species_count,
    loss_weight,
    query_weight,
    key_weight,
    value_weight,
    out_weight,
    gate_weight,
    up_weight,
    down_weight,
    mixer_gain,
    mixer_shift,
    feeder_gain,
    feeder_shift,
):
    dp, z = lax.axis_index("dp"), lax.axis_index("seq")
    c = dp % 2
    (wqkv, wgu, wo, wd, xh, cw, gv, norm_one, q, k, v, attended, lse, norm_two, middle, gate, upward, hidden,
     cos, sin) = fore(
        tokens, cotangent, query_weight, key_weight, value_weight, gate_weight, up_weight, out_weight, down_weight,
        mixer_gain.reshape(1, 32), mixer_shift.reshape(1, 32), feeder_gain.reshape(1, 32), feeder_shift.reshape(1, 32),
        species_index, species_count.reshape(1, -1), loss_weight.reshape(1, -1), *angle_tables(c))
    parts = back(
        cw, hidden, wd, norm_two, gate, upward, wgu, middle, wo, attended, q, k, v, lse, norm_one, wqkv, xh,
        cos, sin, gv)
    done = finish(*parts)
    return done[:9] + tuple(done[9][i, :32] for i in range(4))


def matmul(left, right):
    return jnp.dot(left, right, preferred_element_type=jnp.float32)


def weight_term(left, right):
    return lax.dot_general(
        left, right, (((0,), (0,)), ((), ())), preferred_element_type=jnp.float32
    )


def through(left, weight):
    return lax.dot_general(
        left, weight, (((1,), (1,)), ((), ())), preferred_element_type=jnp.float32
    )


def normalize(values):
    center = jnp.mean(values, axis=-1, keepdims=True)
    centered = values - center
    variance = jnp.mean(centered * centered, axis=-1, keepdims=True)
    scaling = lax.rsqrt(variance + 1e-05)
    return (centered * scaling, scaling)


def plain_norm_back(upstream, normed, scaling):
    first = jnp.mean(upstream, axis=-1, keepdims=True)
    second = jnp.mean(upstream * normed, axis=-1, keepdims=True)
    return scaling * (upstream - first - normed * second)


def tables(start, count):
    half = HD // 2
    positions = (start + jnp.arange(count, dtype=jnp.int32)).astype(jnp.float32)
    freqs = 10000.0 ** (-2.0 * jnp.arange(half, dtype=jnp.float32) / HD)
    angle = positions[:, None] * freqs[None, :]
    return (jnp.cos(angle)[:, None, :], jnp.sin(angle)[:, None, :])


def rotate(values, cosine, sine):
    half = HD // 2
    first = values[..., :half]
    second = values[..., half:]
    return jnp.concatenate(
        [first * cosine - second * sine, second * cosine + first * sine], axis=-1
    )


def attend_head(operands):
    query_head, key_head, value_head = operands
    scores = jnp.einsum(
        "wtd,wsd->wts", query_head, key_head, preferred_element_type=jnp.float32
    ) * HD ** (-0.5)
    peak = jnp.max(scores, axis=-1, keepdims=True)
    raised = jnp.exp(scores - peak)
    total = jnp.sum(raised, axis=-1, keepdims=True)
    probs = (raised / total).astype(jnp.bfloat16)
    result = jnp.einsum("wts,wsd->wtd", probs, value_head, preferred_element_type=jnp.float32)
    return (result, (peak + jnp.log(total))[..., 0])


def head_back(operands):
    query_head, key_head, value_head, upstream, log_total = operands
    scores = jnp.einsum(
        "wtd,wsd->wts", query_head, key_head, preferred_element_type=jnp.float32
    ) * HD ** (-0.5)
    probs = jnp.exp(scores - log_total[..., None])
    prob_grads = jnp.einsum(
        "wtd,wsd->wts", upstream, value_head, preferred_element_type=jnp.float32
    )
    inner = jnp.sum(probs * prob_grads, axis=-1, keepdims=True)
    score_grads = (probs * (prob_grads - inner)).astype(jnp.bfloat16)
    query_grad = jnp.einsum(
        "wts,wsd->wtd", score_grads, key_head, preferred_element_type=jnp.float32
    ) * HD ** (-0.5)
    key_grad = jnp.einsum(
        "wts,wtd->wsd", score_grads, query_head, preferred_element_type=jnp.float32
    ) * HD ** (-0.5)
    value_grad = jnp.einsum(
        "wts,wtd->wsd", probs.astype(jnp.bfloat16), upstream, preferred_element_type=jnp.float32
    )
    return (query_grad, key_grad, value_grad)


def general(
    tokens,
    cotangent,
    species_index,
    species_count,
    loss_weight,
    query_weight,
    key_weight,
    value_weight,
    out_weight,
    gate_weight,
    up_weight,
    down_weight,
    mixer_gain,
    mixer_shift,
    feeder_gain,
    feeder_shift,
):
    gathered = (
        lax.all_gather(query_weight, ("dp", "seq"), axis=0, tiled=True),
        lax.all_gather(key_weight, ("dp", "seq"), axis=0, tiled=True),
        lax.all_gather(value_weight, ("dp", "seq"), axis=0, tiled=True),
        lax.all_gather(out_weight, ("dp", "seq"), axis=0, tiled=True),
        lax.all_gather(gate_weight, ("dp", "seq"), axis=0, tiled=True),
        lax.all_gather(up_weight, ("dp", "seq"), axis=0, tiled=True),
        lax.all_gather(down_weight, ("dp", "seq"), axis=0, tiled=True),
        lax.all_gather(mixer_gain, ("dp", "seq"), axis=0, tiled=True),
        lax.all_gather(mixer_shift, ("dp", "seq"), axis=0, tiled=True),
        lax.all_gather(feeder_gain, ("dp", "seq"), axis=0, tiled=True),
        lax.all_gather(feeder_shift, ("dp", "seq"), axis=0, tiled=True),
    )
    wq, wk, wv, wo, wg, wu, wd, gain_one, shift_one, gain_two, shift_two = gathered
    windows, steps_dev, width = tokens.shape
    rows = windows * steps_dev
    start = lax.axis_index("seq") * steps_dev
    cosine, sine = tables(start, steps_dev)
    inputs = tokens.astype(jnp.float32).reshape(rows, width)
    normed_one, scaling_one = normalize(inputs)
    norm_one = (normed_one * gain_one.astype(jnp.float32) + shift_one.astype(jnp.float32)).astype(
        jnp.bfloat16
    )
    queries = rotate(
        matmul(norm_one, wq).reshape(windows, steps_dev, HEADS, HD), cosine, sine
    ).astype(jnp.bfloat16)
    keys = rotate(matmul(norm_one, wk).reshape(windows, steps_dev, HEADS, HD), cosine, sine).astype(
        jnp.bfloat16
    )
    values = matmul(norm_one, wv).astype(jnp.bfloat16)
    all_keys, all_values = (
        lax.all_gather(keys.reshape(windows, steps_dev, width), "seq", axis=1, tiled=True),
        lax.all_gather(values.reshape(windows, steps_dev, width), "seq", axis=1, tiled=True),
    )
    length = all_keys.shape[1]
    query_heads = queries.transpose(2, 0, 1, 3)
    key_heads = all_keys.reshape(windows, length, HEADS, HD).transpose(2, 0, 1, 3)
    value_heads = all_values.reshape(windows, length, HEADS, HD).transpose(2, 0, 1, 3)
    head_results, log_totals = lax.map(attend_head, (query_heads, key_heads, value_heads))
    attended = head_results.transpose(1, 2, 0, 3).reshape(rows, width).astype(jnp.bfloat16)
    middle = inputs + matmul(attended, wo)
    normed_two, scaling_two = normalize(middle)
    norm_two = (normed_two * gain_two.astype(jnp.float32) + shift_two.astype(jnp.float32)).astype(
        jnp.bfloat16
    )
    gate = matmul(norm_two, wg)
    upward = matmul(norm_two, wu)
    sigma = jax.nn.sigmoid(gate)
    swish = gate * sigma
    hidden = (swish * upward).astype(jnp.bfloat16)
    output = (middle + matmul(hidden, wd)).astype(jnp.bfloat16).reshape(windows, steps_dev, width)
    table = loss_weight * lax.rsqrt(species_count.astype(jnp.float32) / 400.0)
    picks = species_index[:, None] == jnp.arange(table.shape[0], dtype=jnp.int32)[None, :]
    factor = jnp.sum(jnp.where(picks, table[None, :], 0.0), axis=1)
    grad_out = (factor[:, None, None] * cotangent.astype(jnp.float32)).reshape(rows, width)
    regathered = (
        lax.all_gather(query_weight, ("dp", "seq"), axis=0, tiled=True),
        lax.all_gather(key_weight, ("dp", "seq"), axis=0, tiled=True),
        lax.all_gather(value_weight, ("dp", "seq"), axis=0, tiled=True),
        lax.all_gather(out_weight, ("dp", "seq"), axis=0, tiled=True),
        lax.all_gather(gate_weight, ("dp", "seq"), axis=0, tiled=True),
        lax.all_gather(up_weight, ("dp", "seq"), axis=0, tiled=True),
        lax.all_gather(down_weight, ("dp", "seq"), axis=0, tiled=True),
        lax.all_gather(mixer_gain, ("dp", "seq"), axis=0, tiled=True),
        lax.all_gather(mixer_shift, ("dp", "seq"), axis=0, tiled=True),
        lax.all_gather(feeder_gain, ("dp", "seq"), axis=0, tiled=True),
        lax.all_gather(feeder_shift, ("dp", "seq"), axis=0, tiled=True),
    )
    wq, wk, wv, wo, wg, wu, wd, gain_one, shift_one, gain_two, shift_two = regathered
    out_low = grad_out.astype(jnp.bfloat16)
    down_part = weight_term(hidden, out_low)
    hidden_grad = through(out_low, wd)
    gate_grad = (hidden_grad * upward * sigma * (1.0 + gate * (1.0 - sigma))).astype(jnp.bfloat16)
    upward_grad = (hidden_grad * swish).astype(jnp.bfloat16)
    gate_part = weight_term(norm_two, gate_grad)
    upward_part = weight_term(norm_two, upward_grad)
    norm_two_grad = through(gate_grad, wg) + through(upward_grad, wu)
    feeder_gain_part = jnp.sum(norm_two_grad * normed_two, axis=0)
    feeder_shift_part = jnp.sum(norm_two_grad, axis=0)
    middle_grad = grad_out + plain_norm_back(
        norm_two_grad * gain_two.astype(jnp.float32), normed_two, scaling_two
    )
    middle_low = middle_grad.astype(jnp.bfloat16)
    out_part = weight_term(attended, middle_low)
    attended_grad = through(middle_low, wo).astype(jnp.bfloat16)
    upstream_heads = attended_grad.reshape(windows, steps_dev, HEADS, HD).transpose(2, 0, 1, 3)
    query_heads_grad, key_heads_grad, value_heads_grad = lax.map(
        head_back, (query_heads, key_heads, value_heads, upstream_heads, log_totals)
    )
    key_whole = key_heads_grad.transpose(1, 2, 0, 3).reshape(windows, length, width)
    value_whole = value_heads_grad.transpose(1, 2, 0, 3).reshape(windows, length, width)
    key_mine, value_mine = (
        lax.psum_scatter(
            key_whole.astype(jnp.bfloat16), "seq", scatter_dimension=1, tiled=True
        ).astype(jnp.float32),
        lax.psum_scatter(
            value_whole.astype(jnp.bfloat16), "seq", scatter_dimension=1, tiled=True
        ).astype(jnp.float32),
    )
    query_lin_grad = (
        rotate(query_heads_grad.transpose(1, 2, 0, 3), cosine, -sine)
        .reshape(rows, width)
        .astype(jnp.bfloat16)
    )
    key_lin_grad = (
        rotate(key_mine.reshape(windows, steps_dev, HEADS, HD), cosine, -sine)
        .reshape(rows, width)
        .astype(jnp.bfloat16)
    )
    value_lin_grad = value_mine.reshape(rows, width).astype(jnp.bfloat16)
    query_part = weight_term(norm_one, query_lin_grad)
    key_part = weight_term(norm_one, key_lin_grad)
    value_part = weight_term(norm_one, value_lin_grad)
    norm_one_grad = (
        through(query_lin_grad, wq) + through(key_lin_grad, wk) + through(value_lin_grad, wv)
    )
    mixer_gain_part = jnp.sum(norm_one_grad * normed_one, axis=0)
    mixer_shift_part = jnp.sum(norm_one_grad, axis=0)
    input_grad = middle_grad + plain_norm_back(
        norm_one_grad * gain_one.astype(jnp.float32), normed_one, scaling_one
    )
    summed = (
        lax.psum_scatter(query_part, ("dp", "seq"), scatter_dimension=0, tiled=True),
        lax.psum_scatter(key_part, ("dp", "seq"), scatter_dimension=0, tiled=True),
        lax.psum_scatter(value_part, ("dp", "seq"), scatter_dimension=0, tiled=True),
        lax.psum_scatter(out_part, ("dp", "seq"), scatter_dimension=0, tiled=True),
        lax.psum_scatter(gate_part, ("dp", "seq"), scatter_dimension=0, tiled=True),
        lax.psum_scatter(upward_part, ("dp", "seq"), scatter_dimension=0, tiled=True),
        lax.psum_scatter(down_part, ("dp", "seq"), scatter_dimension=0, tiled=True),
        lax.psum_scatter(mixer_gain_part, ("dp", "seq"), scatter_dimension=0, tiled=True),
        lax.psum_scatter(mixer_shift_part, ("dp", "seq"), scatter_dimension=0, tiled=True),
        lax.psum_scatter(feeder_gain_part, ("dp", "seq"), scatter_dimension=0, tiled=True),
        lax.psum_scatter(feeder_shift_part, ("dp", "seq"), scatter_dimension=0, tiled=True),
    )
    return (
        output,
        input_grad.reshape(windows, steps_dev, width),
        summed[0],
        summed[1],
        summed[2],
        summed[3],
        summed[4],
        summed[5],
        summed[6],
        summed[7],
        summed[8],
        summed[9],
        summed[10],
    )


def solution(mesh):
    in_specs = (
        P("dp", "seq", None),
        P("dp", "seq", None),
        P("dp"),
        P(),
        P(),
    ) + (P(("dp", "seq"), None),) * 7 + (P(("dp", "seq")),) * 4
    out_specs = (P("dp", "seq", None),) * 2 + (P(("dp", "seq"), None),) * 7 + (P(("dp", "seq")),) * 4
    fits = mesh.shape["dp"] == 8 and mesh.shape["seq"] == 4
    return jax.shard_map(
        paired if fits else general, mesh=mesh, in_specs=in_specs, out_specs=out_specs, check_vma=False
    )
```

```python
import jax
import jax.numpy as jnp
from jax import lax
from jax.experimental import pallas as pl
from jax.experimental.pallas import tpu as pltpu
from jax.sharding import PartitionSpec as P

HEADS = 16
HD = 64
MESH = pl.DeviceIdType.MESH
BF = jnp.bfloat16
F32 = jnp.float32
ANY = pl.BlockSpec(memory_space=pl.ANY)
VM = pl.BlockSpec(memory_space=pltpu.VMEM)
VMEM_BYTES = 60 << 20


def place():
    dp, z = lax.axis_index("dp"), lax.axis_index("seq")
    return dp // 4, (dp // 2) % 2, dp % 2, z


def dev(y, x, c, z):
    return ((y * 2 + x) * 2 + c, z)


def both(a, b):
    return jnp.logical_and(a, b)


def greet(y, x, c, z, meanwhile=None):
    barrier = pltpu.get_barrier_semaphore()
    peers = [dev(y, 1 - x, c, z), dev(1 - y, x, c, z), dev(y, x, 1 - c, z)]
    for k in (1, 2, 3):
        peers += [dev(y, x, c, (z + k) % 4), dev(y, x, 1 - c, (z + k) % 4)]
    for p in peers:
        pl.semaphore_signal(barrier, inc=1, device_id=p, device_id_type=MESH)
    if meanwhile is not None:
        meanwhile()
    pl.semaphore_wait(barrier, len(peers))


class Links:
    def __init__(self, send, recv, local):
        self.send, self.recv, self.local = send, recv, local
        self.n = 0
        self.m = 0
        self.open = []

    def take(self, count):
        self.n += count
        return self.n - count

    def copy(self, src, dst, device, send, recv):
        return pltpu.make_async_remote_copy(
            src_ref=src, dst_ref=dst, send_sem=self.send.at[send], recv_sem=self.recv.at[recv],
            device_id=device, device_id_type=MESH)

    def go(self, c, ok=None):
        if ok is None:
            c.start()
        else:
            pl.when(ok)(c.start)
        self.open.append((c, ok))
        return c

    def to(self, src, dst, device):
        i = self.take(1)
        return self.go(self.copy(src, dst, device, i, i))

    def later(self, src, dst, device):
        i = self.take(1)
        c = self.copy(src, dst, device, i, i)
        self.open.append((c, None))
        return c

    def here_later(self, src, dst):
        self.m += 1
        return pltpu.make_async_copy(src, dst, self.local.at[self.m - 1])

    def wanted(self, src, dst, device):
        i = self.take(1)
        return self.copy(src, dst, device, i, i)

    def here(self, src, dst):
        self.m += 1
        c = pltpu.make_async_copy(src, dst, self.local.at[self.m - 1])
        c.start()
        return c

    def drain(self):
        for c, ok in self.open:
            if ok is None:
                c.wait_send()
            else:
                pl.when(ok)(c.wait_send)
        self.open = []


def at_z(ref, zz):
    return ref.at[zz] if len(ref.shape) == 3 else ref.at[:, zz]


def add_into(dst, *terms):
    def body(i, _):
        total = at_z(terms[0], i)[...].astype(F32)
        for t in terms[1:]:
            total += at_z(t, i)[...].astype(F32)
        at_z(dst, i)[...] = total.astype(dst.dtype)
        return 0
    lax.fori_loop(0, 4, body, 0)


def reduce_shapes(piece, route):
    part = piece[:-3] + piece[-2:]
    if route < 2:
        later = [pltpu.VMEM(piece, BF), pltpu.VMEM((3,) + part, BF)]
    else:
        later = [pltpu.VMEM((2, 3) + part, BF), pltpu.VMEM((2,) + part, BF)]
    return [pltpu.VMEM((2,) + piece, BF)] + later + [pltpu.VMEM(part, F32)]


def collect(links, at, me, route, bufs, deliver):
    y, x, c, z = me
    to_x, to_y = dev(y, 1 - x, c, z), dev(1 - y, x, c, z)
    zs = [(z + k) % 4 for k in range(4)]
    to_z = [dev(y, x, c, zs[k]) for k in range(4)]
    got, third, fourth, total = bufs
    out = deliver(total)

    def finish():
        for q in out:
            q.start()

    if route == 0:
        own, away = [at(1 - y, x), at(y, x)], [at(1 - y, 1 - x), at(y, 1 - x)]
        one, two = to_x, to_y
    else:
        own, away = [at(y, 1 - x), at(y, x)], [at(1 - y, 1 - x), at(1 - y, x)]
        one, two = to_y, to_x
    give = [links.later(away[n], got.at[n], one) for n in (0, 1)]

    def start():
        for q in give:
            q.start()

    if route < 2:
        cross = links.later(own[0], third, two)
        over_z = [links.later(at_z(own[1], zs[k]), fourth.at[k - 1], to_z[k]) for k in (1, 2, 3)]

        def first():
            give[0].wait_recv()
            add_into(own[0], own[0], got.at[0])
            cross.start()

        def second():
            give[1].wait_recv()
            cross.wait_recv()
            add_into(own[1], own[1], got.at[1], third)
            for q in over_z:
                q.start()

        def last():
            for q in over_z:
                q.wait_recv()
            total[...] = (at_z(own[1], z)[...].astype(F32) + fourth[0].astype(F32)
                          + (fourth[1].astype(F32) + fourth[2].astype(F32)))
            finish()
        return start, first, second, last

    over_z = [[links.later(at_z(own[n], zs[k]), third.at[n, k - 1], to_z[k]) for k in (1, 2, 3)] for n in (0, 1)]
    over_x = links.later(fourth.at[0], fourth.at[1], to_x)

    def first(n):
        give[n].wait_recv()
        add_into(own[n], own[n], got.at[n])
        for q in over_z[n]:
            q.start()

    def second():
        for q in over_z[0]:
            q.wait_recv()
        fourth[0] = (at_z(own[0], z)[...].astype(F32) + third[0, 0].astype(F32)
                     + (third[0, 1].astype(F32) + third[0, 2].astype(F32))).astype(fourth.dtype)
        over_x.start()

    def last():
        for q in over_z[1]:
            q.wait_recv()
        over_x.wait_recv()
        total[...] = (at_z(own[1], z)[...].astype(F32) + third[1, 0].astype(F32)
                      + (third[1, 1].astype(F32) + third[1, 2].astype(F32)) + fourth[1].astype(F32))
        finish()
    return start, lambda: first(0), lambda: first(1), second, last


class Outgoing:
    def __init__(self, links, me, src, dst):
        y, x, c, z = me
        recv, send = links.take(4), links.take(4)
        self.here, self.away = c == z // 2, c != z // 2
        self.remote, self.back = [], []
        for k in range(4):
            zz = (z + k) % 4
            s, d = src.at[zz], dst.at[z % 2, c]
            self.remote.append(links.copy(s, d, dev(y, x, z // 2, zz), send + k, recv + (z % 2) * 2 + c))
            links.open.append((self.remote[k], None if k else self.away))
            if k == 0:
                self.local = links.here_later(s, d)
        for i in (0, 1):
            for h in (0, 1):
                d = dst.at[i, h]
                mine = both(z == 2 * c + i, h == c)
                self.back.append((links.copy(d, d, dev(y, x, 1 - c, z), send, recv + 2 * i + h), jnp.logical_not(mine)))

    def start(self):
        for q in self.remote[1:]:
            q.start()
        pl.when(self.away)(self.remote[0].start)
        pl.when(self.here)(self.local.start)

    def finish(self):
        pl.when(self.here)(self.local.wait)
        for q, ok in self.back:
            pl.when(ok)(q.wait_recv)


def swap_halves(u):
    lane = lax.broadcasted_iota(jnp.int32, u.shape, 1) % HD
    return jnp.where(lane < HD // 2, pltpu.roll(u, 128 - HD // 2, 1), pltpu.roll(u, HD // 2, 1))


def head_mask(shape, h):
    lane = lax.broadcasted_iota(jnp.int32, shape, 1)
    return (lane < HD) if h == 0 else (lane >= HD)


def dot_t(a, b):
    return lax.dot_general(a, b, (((1,), (1,)), ((), ())), preferred_element_type=F32)


def project_step(xw, gv, w, cos, sin, n1, q, k, v, r):
    rows = pl.ds(pl.multiple_of(r * 256, 256), 256)
    u = xw[r // 2, pl.ds((r % 2) * 2, 2)].reshape(256, 1024).astype(F32)
    d = u - jnp.mean(u, axis=-1, keepdims=True)
    scaling = lax.rsqrt(jnp.mean(d * d, axis=-1, keepdims=True) + 1e-05)
    n = (d * scaling * gv[0:1, :] + gv[1:2, :]).astype(BF)
    n1[rows, :] = n
    for g in range(4):
        lanes = pl.ds(128 * g, 128)
        t = jnp.dot(n, w[:, :, :, :, pl.ds(384 * g, 384)].reshape(1024, 384), preferred_element_type=F32)
        for j, o in ((0, q), (1, k)):
            s = t[:, 128 * j:128 * j + 128]
            o[rows, lanes] = (s * cos[rows, :] + swap_halves(s) * sin[rows, :]).astype(BF)
        v[rows, lanes] = t[:, 256:].astype(BF)


def attend_step(q, k, v, o, lse, g, i):
    lanes = pl.ds(pl.multiple_of(g * 128, 128), 128)
    rows = pl.ds(pl.multiple_of(i * 256, 256), 256)
    qs = q[rows, lanes] * jnp.asarray(HD ** -0.5, BF)
    kk, vv = k[:, lanes], v[:, lanes]
    outs, logs = [], []
    for h in (0, 1):
        qh = jnp.where(head_mask(qs.shape, h), qs, jnp.zeros_like(qs))
        s = dot_t(qh, kk)
        m = jnp.max(s, axis=-1, keepdims=True)
        e = jnp.exp(s - m)
        t = jnp.sum(e, axis=-1, keepdims=True)
        p = (e * (1.0 / t)).astype(BF)
        outs.append(jnp.dot(p, vv, preferred_element_type=F32))
        logs.append(jnp.broadcast_to(m + jnp.log(t), qs.shape))
    keep = head_mask(qs.shape, 0)
    o[rows, lanes] = jnp.where(keep, outs[0], outs[1]).astype(BF)
    t = jnp.transpose(jnp.where(keep, logs[0], logs[1]))
    lse[pl.ds(2 * g, 1), rows] = t[0:1]
    lse[pl.ds(2 * g + 1, 1), rows] = t[HD:HD + 1]


def attend_back_step(q, k, v, do, lse, cos, sin, dqkv, dka, dva, g, i):
    lanes = pl.ds(pl.multiple_of(g * 128, 128), 128)
    rows = pl.ds(pl.multiple_of(i * 256, 256), 256)

    @pl.when(i == 0)
    def _():
        dka[...] = jnp.zeros_like(dka)
        dva[...] = jnp.zeros_like(dva)
    kk, vv, go = k[:, lanes], v[:, lanes], do[rows, lanes]
    qs = q[rows, lanes] * jnp.asarray(HD ** -0.5, BF)
    logs = lse[pl.ds(2 * g, 1), rows], lse[pl.ds(2 * g + 1, 1), rows]
    dks, dvs, dqs = [], [], []
    for h in (0, 1):
        keep = head_mask(kk.shape, h)
        zero = jnp.zeros_like(kk)
        s = dot_t(jnp.where(keep, kk, zero), qs)
        p = jnp.exp(s - logs[h])
        dp = dot_t(jnp.where(keep, vv, zero), go)
        pd = p * dp
        ds = (pd - p * jnp.sum(pd, axis=0, keepdims=True)).astype(BF)
        dvs.append(jnp.dot(p.astype(BF), go, preferred_element_type=F32))
        dks.append(jnp.dot(ds, qs, preferred_element_type=F32))
        dqs.append(lax.dot_general(ds, kk, (((0,), (0,)), ((), ())), preferred_element_type=F32))
    keep = head_mask(kk.shape, 0)
    dka[...] += jnp.where(keep, dks[0], dks[1])
    dva[...] += jnp.where(keep, dvs[0], dvs[1])
    u = jnp.where(head_mask(go.shape, 0), dqs[0], dqs[1]) * HD ** -0.5
    dqkv[rows, pl.ds(pl.multiple_of(g * 384, 128), 128)] = (
        u * cos[rows, :] - swap_halves(u) * sin[rows, :]).astype(BF)

    @pl.when(i == 3)
    def _():
        u = dka[...]
        dqkv[:, pl.ds(pl.multiple_of(128 + g * 384, 128), 128)] = (
            u * cos[...] - swap_halves(u) * sin[...]).astype(BF)
        dqkv[:, pl.ds(pl.multiple_of(256 + g * 384, 128), 128)] = dva[...].astype(BF)


class Incoming:
    def __init__(self, links, me, src, mid, dst):
        y, x, c, z = me
        partner = dev(y, x, 1 - c, z)
        self.swap = [links.later(src.at[i, pl.ds((1 - c) * 128, 128)], mid.at[2 * c + i], partner) for i in (0, 1)]
        send, recv = links.take(4), links.take(4)
        self.sends, self.kept, self.got = [], [], []
        m = links.m
        links.m += 1
        for w in range(4):
            d = dst.at[0, z]
            for ok, s in ((c == w // 2, src.at[w % 2, pl.ds(c * 128, 128)]), (c != w // 2, mid.at[w])):
                away, here = both(ok, z != w), both(ok, z == w)
                q = links.copy(s, d, dev(y, x, c, w), send + w, recv + z)
                self.sends.append((q, away))
                links.open.append((q, away))
                self.kept.append((pltpu.make_async_copy(s, d, links.local.at[m]), here))
        for zz in range(4):
            d = dst.at[0, zz]
            self.got.append((links.copy(d, d, dev(y, x, c, zz), send, recv + zz), z != zz))
        self.pair = links.later(dst.at[0], dst.at[1], partner)

    def begin(self):
        for q in self.swap:
            q.start()

    def send(self):
        for q in self.swap:
            q.wait_recv()
        for q, ok in self.sends + self.kept:
            pl.when(ok)(q.start)

    def arrive(self):
        for q, ok in self.kept:
            pl.when(ok)(q.wait)
        for q, ok in self.got:
            pl.when(ok)(q.wait_recv)
        self.pair.start()

    def finish(self):
        self.pair.wait_recv()


def disperse(links, single, bundle, me, route):
    y, x, c, z = me
    to_x, to_y = dev(y, 1 - x, c, z), dev(1 - y, x, c, z)
    mine = y * 2 + x
    if route == 0:
        two, three, other = to_y, to_x, (1 - y) * 2 + x
    else:
        two, three, other = to_x, to_y, y * 2 + 1 - x
    over_z = [links.later(single(mine, z), single(mine, z), dev(y, x, c, (z + k) % 4)) for k in (1, 2, 3)]
    cross = links.later(bundle(mine), bundle(mine), two)
    last = [links.later(bundle(mine), bundle(mine), three), links.later(bundle(other), bundle(other), three)]

    def start():
        for q in over_z:
            q.start()

    def first():
        for q in over_z:
            q.wait_recv()
        cross.start()
        last[0].start()

    def second():
        cross.wait_recv()
        last[1].start()

    def finish():
        for q in last:
            q.wait_recv()
    return start, first, second, finish


FORE_PIECES = (
    ("gu", 5, 1),
    ("d", 0, 1),
    ("qkv", 0, 1),
    ("o", 0, 0),
    ("gu", 6, 0),
    ("gu", 1, 0),
    ("gu", 2, 1),
    ("qkv", 1, 0),
    ("gu", 0, 1),
    ("gu", 3, 1),
    ("gu", 4, 0),
    ("d", 1, 0),
    ("d", 3, 1),
    ("gu", 7, 0),
    ("d", 2, 1),
)
FORE_ORDER = (
    ((17, 0), (0, 0), (1, 0), (2, 0), (3, 0), (4, 0), (5, 0), (6, 0), (7, 0), (15, 0), (8, 0), (9, 0), (10, 0),
     (11, 0), (12, 0), (13, 0), (14, 0), (17, 1), (17, 2), (17, 3), (0, 1), (1, 1), (0, 2), (1, 2), (2, 1), (0, 3),
     (3, 1), (1, 3), (2, 2), (4, 1), (5, 1), (6, 1), (3, 2), (2, 3), (7, 1), (6, 2), (4, 2), (3, 3), (5, 2),
     (4, 3), (7, 2), (5, 3), (15, 1), (6, 3), (8, 1), (7, 3), (15, 2),),
    ((8, 2), (9, 1)), ((10, 1),), (), (), (), (), ((11, 1), (8, 3), (9, 2)), (), (), (), ((12, 1),), (), (), (),
    ((10, 2), (13, 1), (16, 0)), (), (), ((9, 3), (10, 3), (11, 2), (12, 2), (14, 1)), (), ((11, 3), (13, 2)),
    ((12, 3), (14, 2), (16, 1), (13, 3)), ((16, 2), (14, 3)),
)


def rotary_tables(tab_cos, tab_sin, cos, sin):
    lane = lax.broadcasted_iota(jnp.int32, (128, 128), 1)
    sign = jnp.where(lane % HD < HD // 2, -1.0, 1.0)
    for i in range(8):
        a, b = tab_cos[128 + i:129 + i, :], tab_sin[128 + i:129 + i, :]
        cos[128 * i:128 * i + 128, :] = tab_cos[0:128, :] * a - tab_sin[0:128, :] * b
        sin[128 * i:128 * i + 128, :] = sign * (tab_sin[0:128, :] * a + tab_cos[0:128, :] * b)


def fore_kernel(tok, cot, wq, wk, wv, wg, wu, wo, wd, g0, g1, g2, g3, species, count, weight,
                tab_cos, tab_sin, *rest):
    (oqkv, ogu, oo, od, xh, cw, gvo, n1o, qo, ko, vo, atto, lseo, n2o, mido, gateo, upo, hido, coso, sino,
     own_qkv, oth_qkv, own_gu, oth_gu, gp, cos, sin,
     tmid, cmid, gains, gv, xw, w3, n1, q, k, v, att, lse, wos, sent, came, mid, n2, wgs, wus,
     gate, up, hid, send, recv, local) = rest
    me = y, x, c, z = place()
    yx = y * 2 + x
    partner = dev(y, x, 1 - c, z)

    def prepare():
        def columns(src, own, oth, width, base, stride):
            for g in range(4):
                lanes = pl.ds(base + stride * g, width)
                own[:, lanes] = src[:, pl.ds(pl.multiple_of((2 * g + c) * width, width), width)]
                oth[:, lanes] = src[:, pl.ds(pl.multiple_of((2 * g + 1 - c) * width, width), width)]
        for j, src in enumerate((wq, wk, wv)):
            columns(src, own_qkv, oth_qkv, 128, 128 * j, 384)
        for j, src in enumerate((wg, wu)):
            columns(src, own_gu, oth_gu, 512, 2048 * j, 512)
        gp[...] = jnp.zeros_like(gp)
        for i, src in enumerate((g0, g1, g2, g3)):
            gp[i:i + 1, 0:32] = src[...].astype(F32)
        gp[...] = pltpu.roll(gp[...], z * 32, 1)
        lane = lax.broadcasted_iota(jnp.int32, (1, 128), 1)
        row = jnp.zeros((1, 128), F32)
        for i in (0, 1):
            n = jnp.full((1, 128), count[species[i]].astype(F32), F32)
            row = jnp.where(lane == i, weight[species[i]] * lax.rsqrt(n / 400.0), row)
        gp[4:5, :] = jnp.where(z == 0, row, jnp.zeros_like(row))
    greet(y, x, c, z, prepare)
    links = Links(send, recv, local)
    tin, cin = Incoming(links, me, tok, tmid, xw), Incoming(links, me, cot, cmid, cw)
    tin.begin()
    swaps = [links.to(gp, gains.at[yx, c, z], partner), links.to(oth_qkv, oqkv.at[yx, c, z], partner),
             links.to(oth_gu, ogu.at[yx, c, z], partner)]
    loc = [links.here(gp, gains.at[yx, c, z]), links.here(own_qkv, oqkv.at[yx, c, z]),
           links.here(own_gu, ogu.at[yx, c, z]), links.here(wo, oo.at[yx, z]), links.here(wd, od.at[yx, z])]
    work = []
    for name, index, route in FORE_PIECES:
        if name in ("qkv", "gu"):
            arr, cols = (oqkv, 768) if name == "qkv" else (ogu, 512)
            lanes = pl.ds(index * cols, cols)
            work.append(disperse(links, lambda i, zz, arr=arr, lanes=lanes: arr.at[i, :, zz, :, lanes],
                                 lambda i, arr=arr, lanes=lanes: arr.at[i, :, :, :, lanes], me, route))
        else:
            arr = oo if name == "o" else od
            rows = pl.ds(index * 32, 32)
            work.append(disperse(links, lambda i, zz, arr=arr, rows=rows: arr.at[i, zz, rows],
                                 lambda i, arr=arr, rows=rows: arr.at[i, :, rows], me, route))

    def later():
        cin.begin()
        cin.send()
    work += [(tin.send, tin.arrive, tin.finish), (later, cin.arrive, cin.finish),
             disperse(links, lambda i, zz: gains.at[i, :, zz], lambda i: gains.at[i], me, 1)]
    swap = links.wanted(sent, came, partner)
    share = links.later(n2.at[pl.ds(0, 512)], n2.at[pl.ds(512, 512)], partner)
    for e in loc:
        e.wait()
    for e in swaps:
        e.wait_recv()

    def comm(slot):
        for i, stage in FORE_ORDER[slot]:
            work[i][stage]()

    keep = []

    def put(src, dst):
        keep.append(links.here(src, dst))
    comm(0)
    wload = links.here(oqkv, w3)
    rotary_tables(tab_cos, tab_sin, cos, sin)
    put(cos, coso)
    put(sin, sino)
    wload.wait()
    for i in range(4):
        for j in (0, 1):
            gv[:, pl.ds((2 * i + j) * 128, 128)] = (gains[i, j, 0] + gains[i, j, 1]) + (gains[i, j, 2] + gains[i, j, 3])

    def rows_of(step):
        lax.fori_loop(0, 4, lambda r, _: (step(r), 0)[1], 0)
    rows_of(lambda r: project_step(xw, gv, w3, cos, sin, n1, q, k, v, r))
    for a, b in ((gv, gvo), (n1, n1o), (q, qo), (k, ko), (v, vo), (xw.at[0], xh)):
        put(a, b)
    comm(1)

    def step(t, _):
        attend_step(q, k, v, att, lse, t // 4, t % 4)
        for slot in range(2, 17):
            if FORE_ORDER[slot]:
                pl.when(t == slot - 2)(lambda slot=slot: comm(slot))
        return 0
    lax.fori_loop(0, 16, step, 0)
    comm(17)
    wload = links.here(oo, wos)
    put(att, atto)
    put(lse, lseo)
    wload.wait()

    def terms(r, out, first):
        rows = pl.ds(pl.multiple_of(r * 256, 256), 256)
        out[rows, :] = jnp.dot(att[pl.ds(pl.multiple_of(first + r * 256, 256), 256), :], wos[...].reshape(512, 1024),
                               preferred_element_type=F32)
    lax.fori_loop(0, 2, lambda r, _: (terms(r, sent, 512), 0)[1], 0)
    swap.start()
    lax.fori_loop(0, 2, lambda r, _: (terms(r, mid, 0), 0)[1], 0)
    swap.wait()

    def second_norm(r):
        rows = pl.ds(pl.multiple_of(r * 128, 128), 128)
        u = xw[0, r].astype(F32) + (mid[rows, :] + came[rows, :])
        mid[rows, :] = u
        d = u - jnp.mean(u, axis=-1, keepdims=True)
        scaling = lax.rsqrt(jnp.mean(d * d, axis=-1, keepdims=True) + 1e-05)
        n2[rows, :] = (d * scaling * gv[2:3, :] + gv[3:4, :]).astype(BF)
    rows_of(second_norm)
    share.start()
    put(mid, mido)
    comm(18)
    share.wait_recv()
    put(n2, n2o)
    for j in range(4):
        if j:
            comm(18 + j)
        lanes = pl.ds(512 * j, 512)
        lg = links.here(ogu.at[:, :, :, :, lanes], wgs)
        lu = links.here(ogu.at[:, :, :, :, pl.ds(2048 + 512 * j, 512)], wus)
        lg.wait()
        lu.wait()

        def hidden_units(r, lanes=lanes):
            rows = pl.ds(pl.multiple_of(r * 256, 256), 256)
            n = n2[rows, :]
            a = jnp.dot(n, wgs[...].reshape(1024, 512), preferred_element_type=F32)
            b = jnp.dot(n, wus[...].reshape(1024, 512), preferred_element_type=F32)
            hid[rows, lanes] = (a * jax.nn.sigmoid(a) * b).astype(BF)
            gate[rows, lanes] = a.astype(BF)
            up[rows, lanes] = b.astype(BF)
        rows_of(hidden_units)
        for a, b in ((hid, hido), (gate, gateo), (up, upo)):
            put(a.at[:, lanes], b.at[:, lanes])
    comm(22)
    for e in keep:
        e.wait()
    links.drain()


def fore(*args):
    S = jax.ShapeDtypeStruct
    V = pltpu.VMEM
    table = [V((1024, 128), F32)] * 2
    specs = [VM] * 13 + [pl.BlockSpec(memory_space=pltpu.SMEM)] * 3 + [VM] * 2
    return pl.pallas_call(
        fore_kernel,
        out_shape=(
            S((4, 2, 4, 32, 1536), BF), S((4, 2, 4, 32, 4096), BF), S((4, 4, 32, 1024), BF), S((4, 4, 128, 1024), BF),
            S((4, 128, 1024), BF), S((2, 4, 128, 1024), BF), S((8, 1024), F32), S((1024, 1024), BF),
            S((1024, 512), BF), S((1024, 512), BF), S((1024, 512), BF), S((1024, 512), BF), S((8, 1024), F32),
            S((1024, 1024), BF), S((512, 1024), F32), S((1024, 2048), BF), S((1024, 2048), BF), S((1024, 2048), BF),
            S((1024, 128), F32), S((1024, 128), F32),
        ),
        in_specs=specs,
        out_specs=[ANY] * 20,
        scratch_shapes=[V((32, 1536), BF)] * 2 + [V((32, 4096), BF)] * 2 + [V((8, 128), F32)] + table + [
            V((4, 128, 1024), BF), V((4, 128, 1024), BF), V((4, 2, 4, 8, 128), F32), V((8, 1024), F32),
            V((2, 4, 128, 1024), BF), V((4, 2, 4, 32, 1536), BF), V((1024, 1024), BF),
            V((1024, 512), BF), V((1024, 512), BF), V((1024, 512), BF), V((1024, 512), BF), V((8, 1024), F32),
            V((4, 4, 32, 1024), BF), V((512, 1024), F32), V((512, 1024), F32), V((512, 1024), F32),
            V((1024, 1024), BF), V((4, 2, 4, 32, 512), BF), V((4, 2, 4, 32, 512), BF),
            V((1024, 2048), BF), V((1024, 2048), BF), V((1024, 2048), BF),
            pltpu.SemaphoreType.DMA((200,)),
            pltpu.SemaphoreType.DMA((200,)),
            pltpu.SemaphoreType.DMA((72,)),
        ],
        compiler_params=pltpu.CompilerParams(collective_id=0, has_side_effects=True, vmem_limit_bytes=67043328),
    )(*args)


PIECES = (
    ("gu", 6, 0),
    ("d", 0, 2),
    ("o", 0, 1),
    ("gu", 7, 1),
    ("gu", 1, 0),
    ("d", 3, 0),
    ("gu", 0, 2),
    ("d", 2, 0),
    ("qkv", 0, 1),
    ("gu", 3, 1),
    ("gu", 5, 0),
    ("qkv", 1, 1),
    ("qkv", 3, 1),
    ("gu", 4, 0),
    ("d", 1, 0),
    ("gu", 2, 2),
    ("qkv", 2, 1),
)
SHAPES = {"d": (4, 32, 1024), "o": (4, 32, 1024), "gu": (2, 4, 32, 512), "qkv": (2, 4, 32, 384)}
ORDER = (
    (), ((1, 0), (5, 0), (7, 0)), ((1, 1), (5, 1), (6, 0), (14, 0)), ((1, 2), (1, 3), (4, 0), (5, 2), (7, 1)),
    ((0, 0), (6, 1), (6, 2), (14, 1), (15, 0)), ((1, 4), (4, 1), (5, 3), (6, 3), (7, 2), (13, 0), (14, 2)),
    ((0, 1), (7, 3), (10, 0), (15, 1), (15, 2)), ((2, 0), (4, 2), (6, 4), (14, 3)),
    ((0, 2), (2, 1), (3, 0), (13, 1), (17, 0), (15, 3)), (), ((4, 3), (10, 1)), ((3, 1),), ((0, 3),), ((8, 0),), (),
    ((2, 2), (15, 4)), ((13, 2),), ((3, 2),), ((10, 2),), ((8, 1), (9, 0)), (), (), ((8, 2), (17, 1)), (),
    ((9, 1), (2, 3), (11, 0)), (), (), ((13, 3),), ((9, 2), (11, 1), (12, 0)),
    ((3, 3), (18, 0), (19, 0), (8, 3), (10, 3), (11, 2), (12, 1), (16, 0), (19, 1), (9, 3), (12, 2), (16, 1),
     (19, 2), (16, 2), (18, 1), (11, 3), (12, 3), (19, 3), (16, 3),),

)


def total_over_devices(links, me, acc, got):
    y, x, c, z = me
    hops = [links.wanted(acc, got.at[i], d) for i, d in
            enumerate((dev(y, x, 1 - c, z), dev(y, 1 - x, c, z), dev(1 - y, x, c, z)))]
    over_z = [links.wanted(acc, got.at[2 + k], dev(y, x, c, (z + k) % 4)) for k in (1, 2, 3)]

    def settle(i):
        hops[i].wait()
        acc[...] += got[i]

    def chip():
        hops[0].start()
        settle(0)
        hops[1].start()

    def second():
        settle(1)
        hops[2].start()

    def third():
        settle(2)
        for q in over_z:
            q.start()

    def last():
        for q in over_z:
            q.wait()
        acc[...] += got[3] + (got[4] + got[5])
    return chip, second, third, last


def rows_dot(a, b):
    return lax.dot_general(a, b, (((0,), (0,)), ((), ())), preferred_element_type=F32)


def each(count, step):
    def body(r, _):
        step(r)
        return 0
    lax.fori_loop(0, count, body, 0)


def block(i, size):
    return pl.ds(pl.multiple_of(i * size, size), size)


def norm_parts(u):
    d = u - jnp.mean(u, axis=-1, keepdims=True)
    scaling = lax.rsqrt(jnp.mean(d * d, axis=-1, keepdims=True) + 1e-05)
    return d * scaling, scaling


def norm_back(upstream, normed, scaling):
    return scaling * (upstream - jnp.mean(upstream, axis=-1, keepdims=True)
                      - normed * jnp.mean(upstream * normed, axis=-1, keepdims=True))


def back_kernel(cw, hido, od, n2o, gateo, upo, ogu, mido, oo, atto, qo, ko, vo, lseo, n1o, oqkv, xh,
                cos, sin, gv, *rest):
    fqkv, fgu, fo, fd, fgain, out_w, ig_w = rest[:7]
    scratch = list(rest[7:])
    (gd, ggu, go, gw, mg, sent, came, mlow, ag, out16, ig, gacc, ggot, send, recv, local, ready) = scratch[-17:]
    me = y, x, c, z = place()
    partner = dev(y, x, 1 - c, z)
    greet(y, x, c, z)
    links = Links(send, recv, local)
    work = []
    finals = []
    for name, index, route in PIECES:
        bufs = [scratch.pop(0) for _ in range(4)]
        if name in ("qkv", "gu"):
            src, dst = (gw, fqkv) if name == "qkv" else (ggu, fgu)
            cols = SHAPES[name][3]
            lanes = pl.ds(index * cols, cols)

            def at(yy, xx, src=src, index=index):
                return src.at[index, yy * 2 + xx]

            def deliver(total, dst=dst, lanes=lanes):
                there = links.later(total.at[1 - c], dst.at[c, :, lanes], partner)
                here = links.here_later(total.at[c], dst.at[c, :, lanes])
                finals.extend((there.wait_recv, here.wait))
                return there, here
        else:
            src, dst = (gd, fd) if name == "d" else (go, fo)
            rows = pl.ds(index * 32, 32)

            def at(yy, xx, src=src, rows=rows):
                return src.at[yy * 2 + xx, :, rows]

            def deliver(total, dst=dst, rows=rows):
                here = links.here_later(total, dst.at[rows])
                finals.append(here.wait)
                return (here,)
        work.append(collect(links, at, me, route, bufs, deliver))
    o1 = Outgoing(links, me, out16, out_w)
    o2 = Outgoing(links, me, ig, ig_w)
    work += [(o1.start, o1.finish), (o2.start, o2.finish), total_over_devices(links, me, gacc, ggot)]
    swaps = [links.wanted(sent, came, partner) for _ in range(3)]
    share = links.later(mlow.at[0], mlow.at[1], partner)

    def comm(slot):
        for i, stage in ORDER[slot]:
            work[i][stage]()

    def swap(n):
        if n:
            pl.semaphore_wait(ready, 1)
        swaps[n].start()

    def read(n):
        if n < 2:
            pl.semaphore_signal(ready, inc=1, device_id=partner, device_id_type=MESH)

    gacc[...] = jnp.zeros_like(gacc)
    lane = lax.broadcasted_iota(jnp.int32, (1, 1024), 1)
    here = (2 * (y * 2 + x) + z // 2) * 128 + z % 2
    factor = jnp.sum(jnp.where(lane == here, gv[4:5, :], 0.0), axis=1, keepdims=True)

    def hidden_layer(low):
        a = links.here(cw, low)

        def down(hv):
            b = links.here(hido, hv)
            a.wait()

            def scale(i):
                low[i // 4, i % 4] = (factor * low[i // 4, i % 4].astype(F32)).astype(BF)
            each(8, scale)
            b.wait()
            comm(0)

            def weights(r):
                u = rows_dot(hv[:, block(r, 256)], low[...].reshape(1024, 1024))
                gd[r // 2, pl.ds((r % 2) * 2, 2)] = u.astype(BF).reshape(2, 128, 1024)
            each(8, weights)
        pl.run_scoped(down, pltpu.VMEM((1024, 2048), BF))

        def units(n2, gate, up, dgate, dup, wg, wu, wd):
            a = links.here(n2o, n2)
            for j in range(4):
                lanes = pl.ds(512 * j, 512)
                got = [links.here(od.at[j], wd), links.here(gateo.at[:, lanes], gate), links.here(upo.at[:, lanes], up),
                       links.here(ogu.at[:, :, :, :, lanes], wg),
                       links.here(ogu.at[:, :, :, :, pl.ds(2048 + 512 * j, 512)], wu)]
                comm(1 + j)
                for q in got:
                    q.wait()

                def grads(r):
                    rows = block(r, 256)
                    g = dot_t(low[r // 2, pl.ds((r % 2) * 2, 2)].reshape(256, 1024), wd[...].reshape(512, 1024))
                    a, b = gate[rows, :].astype(F32), up[rows, :].astype(F32)
                    t = jax.nn.sigmoid(a)
                    dgate[rows, :] = (g * b * t * (1.0 + a * (1.0 - t))).astype(BF)
                    dup[rows, :] = (g * a * t).astype(BF)
                each(4, grads)
                if j == 0:
                    a.wait()

                def weights(r):
                    n = n2[:, block(r, 256)]
                    ggu[j, r] = rows_dot(n, dgate[...]).astype(BF).reshape(2, 4, 32, 512)
                    ggu[4 + j, r] = rows_dot(n, dup[...]).astype(BF).reshape(2, 4, 32, 512)
                each(4, weights)

                def terms(r, out, first):
                    rows = pl.ds(pl.multiple_of(first + r * 256, 256), 256)
                    u = (dot_t(dgate[rows, :], wg[...].reshape(1024, 512))
                         + dot_t(dup[rows, :], wu[...].reshape(1024, 512)))
                    dst = block(r, 256)
                    out[dst, :] = u if j == 0 else out[dst, :] + u
                each(2, lambda r: terms(r, sent, 512))
                if j == 3:
                    swap(0)
                each(2, lambda r: terms(r, mg, 0))
        pl.run_scoped(units, pltpu.VMEM((1024, 1024), BF), *[pltpu.VMEM((1024, 512), BF)] * 4,
                      *[pltpu.VMEM((4, 2, 4, 32, 512), BF)] * 2, pltpu.VMEM((4, 128, 1024), BF))
    pl.run_scoped(hidden_layer, pltpu.VMEM((2, 4, 128, 1024), BF))
    comm(5)

    def second_norm(mid, cot):
        a, b = links.here(mido, mid), links.here(cw.at[0], cot)
        a.wait()
        b.wait()
        swaps[0].wait()

        def part(r):
            rows = block(r, 128)
            gn = mg[rows, :] + came[rows, :]
            normed, scaling = norm_parts(mid[rows, :])
            gacc[2:3, :] += jnp.sum(gn * normed, axis=0, keepdims=True)
            gacc[3:4, :] += jnp.sum(gn, axis=0, keepdims=True)
            u = factor * cot[r].astype(F32) + norm_back(gn * gv[2:3, :], normed, scaling)
            mg[rows, :] = u
            mlow[0, r] = u.astype(BF)
        each(4, part)
        read(0)
        share.start()
    pl.run_scoped(second_norm, pltpu.VMEM((512, 1024), F32), pltpu.VMEM((4, 128, 1024), BF))
    comm(6)

    def out_layer(w, att):
        a, b = links.here(oo, w), links.here(atto, att)
        a.wait()
        b.wait()
        share.wait_recv()

        def weights(r):
            u = rows_dot(att[:, block(r, 256)], mlow[...].reshape(1024, 1024))
            go[pl.ds(2 * r, 2)] = u.astype(BF).reshape(2, 4, 32, 1024)
        each(2, weights)

        def grads(r):
            u = dot_t(mlow[r // 2, pl.ds((r % 2) * 2, 2)].reshape(256, 1024), w[...].reshape(512, 1024))
            ag[block(r, 256), :] = u.astype(BF)
        each(4, grads)
    pl.run_scoped(out_layer, pltpu.VMEM((4, 4, 32, 1024), BF), pltpu.VMEM((1024, 512), BF))
    comm(7)

    def output(hv, w, mid):
        got = [links.here(hido, hv), links.here(od, w), links.here(mido, mid)]
        for q in got:
            q.wait()

        def term(r, first):
            return jnp.dot(hv[pl.ds(pl.multiple_of(first + r * 256, 256), 256), :], w[...].reshape(2048, 1024),
                           preferred_element_type=F32)

        def theirs(r):
            sent[block(r, 256), :] = term(r, 512)
        each(2, theirs)
        swap(1)

        def mine(r):
            mid[block(r, 256), :] += term(r, 0)
        each(2, mine)
        swaps[1].wait()

        def total(r):
            out16[r] = (mid[block(r, 128), :] + came[block(r, 128), :]).astype(BF)
        each(4, total)
        read(1)
    pl.run_scoped(output, pltpu.VMEM((1024, 2048), BF), pltpu.VMEM((4, 4, 128, 1024), BF), pltpu.VMEM((512, 1024), F32))

    def attention(dqkv):
        def heads(q, k, v, lse, n1, dka, dva):
            got = [links.here(a, b) for a, b in ((qo, q), (ko, k), (vo, v), (lseo, lse), (n1o, n1))]
            for e in got:
                e.wait()

            def step(t):
                for slot in range(20):
                    if ORDER[8 + slot]:
                        pl.when(t == slot)(lambda slot=slot: comm(8 + slot))
                g, i = t // 5, t % 5

                @pl.when(i < 4)
                def _():
                    attend_back_step(q, k, v, ag, lse, cos, sin, dqkv, dka, dva, g, i)

                @pl.when(i == 4)
                def _():
                    u = rows_dot(n1[...], dqkv[:, pl.ds(pl.multiple_of(g * 384, 128), 384)])
                    gw[g] = u.astype(BF).reshape(4, 2, 4, 32, 384)
            each(20, step)
        pl.run_scoped(heads, *[pltpu.VMEM((1024, 512), BF)] * 3, pltpu.VMEM((8, 1024), F32),
                      pltpu.VMEM((1024, 1024), BF), *[pltpu.VMEM((1024, 128), F32)] * 2)

        def first_norm(w, tokens, mine):
            got = [links.here(oqkv, w), links.here(xh, tokens)]
            comm(28)
            for e in got:
                e.wait()

            def term(r, out, first):
                out[block(r, 256), :] = dot_t(dqkv[pl.ds(pl.multiple_of(first + r * 256, 256), 256), :],
                                              w[...].reshape(1024, 1536))
            each(2, lambda r: term(r, sent, 512))
            swap(2)
            each(2, lambda r: term(r, mine, 0))
            swaps[2].wait()

            def part(r):
                rows = block(r, 128)
                gn = mine[rows, :] + came[rows, :]
                normed, scaling = norm_parts(tokens[r].astype(F32))
                gacc[0:1, :] += jnp.sum(gn * normed, axis=0, keepdims=True)
                gacc[1:2, :] += jnp.sum(gn, axis=0, keepdims=True)
                ig[r] = (mg[rows, :] + norm_back(gn * gv[0:1, :], normed, scaling)).astype(BF)
            each(4, part)
        pl.run_scoped(first_norm, pltpu.VMEM((4, 2, 4, 32, 1536), BF), pltpu.VMEM((4, 128, 1024), BF),
                      pltpu.VMEM((512, 1024), F32))
    pl.run_scoped(attention, pltpu.VMEM((1024, 1536), BF))
    comm(29)
    finals.append(links.here(gacc, fgain).wait)
    for f in finals:
        f()
    links.drain()


def back(*args):
    scratch = []
    for name, index, route in PIECES:
        scratch += reduce_shapes(SHAPES[name], route)
    return pl.pallas_call(
        back_kernel,
        out_shape=(
            jax.ShapeDtypeStruct((2, 32, 1536), F32),
            jax.ShapeDtypeStruct((2, 32, 4096), F32),
            jax.ShapeDtypeStruct((32, 1024), F32),
            jax.ShapeDtypeStruct((128, 1024), F32),
            jax.ShapeDtypeStruct((8, 1024), F32),
            jax.ShapeDtypeStruct((2, 2, 128, 1024), BF),
            jax.ShapeDtypeStruct((2, 2, 128, 1024), BF),
        ),
        in_specs=[ANY] * 17 + [VM] * 3,
        out_specs=[ANY] * 7,
        scratch_shapes=scratch + [
            pltpu.VMEM((4, 4, 128, 1024), BF),
            pltpu.VMEM((8, 4, 2, 4, 32, 512), BF),
            pltpu.VMEM((4, 4, 32, 1024), BF),
            pltpu.VMEM((4, 4, 2, 4, 32, 384), BF),
            pltpu.VMEM((512, 1024), F32),
            pltpu.VMEM((512, 1024), F32),
            pltpu.VMEM((512, 1024), F32),
            pltpu.VMEM((2, 4, 128, 1024), BF),
            pltpu.VMEM((1024, 512), BF),
            pltpu.VMEM((4, 128, 1024), BF),
            pltpu.VMEM((4, 128, 1024), BF),
            pltpu.VMEM((8, 1024), F32),
            pltpu.VMEM((6, 8, 1024), F32),
            pltpu.SemaphoreType.DMA((192,)),
            pltpu.SemaphoreType.DMA((192,)),
            pltpu.SemaphoreType.DMA((96,)),
            pltpu.SemaphoreType.REGULAR,
        ],
        compiler_params=pltpu.CompilerParams(collective_id=1, has_side_effects=True, vmem_limit_bytes=67043328),
    )(*args)


def finish_kernel(fqkv, fgu, fo, fd, fgain, out_w, ig_w, out, ig, gq, gk, gv, go, gg, gu, gd, *gains):
    for n in (0, 1):
        for g in range(4):
            for j, dst in enumerate((gq, gk, gv)):
                dst[:, pl.ds(128 * (2 * g + n), 128)] = fqkv[n, :, pl.ds(384 * g + 128 * j, 128)]
            for j, dst in enumerate((gg, gu)):
                dst[:, pl.ds(512 * (2 * g + n), 512)] = fgu[n, :, pl.ds(2048 * j + 512 * g, 512)]
    go[...] = fo[...]
    gd[...] = fd[...]

    def rows(i):
        out[i // 2, pl.ds(pl.multiple_of((i % 2) * 128, 128), 128)] = out_w[i // 2, i % 2]
        ig[i // 2, pl.ds(pl.multiple_of((i % 2) * 128, 128), 128)] = ig_w[i // 2, i % 2].astype(F32)
    each(4, rows)
    first = (lax.axis_index("dp") * 4 + lax.axis_index("seq")) * 32
    mine = pltpu.roll(fgain[...], (1024 - first) % 1024, 1)
    for i in range(4):
        gains[i][...] = mine[i:i + 1, 0:32]


def finish(*args):
    S = jax.ShapeDtypeStruct
    return pl.pallas_call(
        finish_kernel,
        out_shape=(S((2, 256, 1024), BF), S((2, 256, 1024), F32)) + (S((32, 1024), F32),) * 4
        + (S((32, 4096), F32),) * 2 + (S((128, 1024), F32),) + (S((1, 32), F32),) * 4,
        in_specs=[VM] * 7,
        out_specs=[VM] * 13,
        compiler_params=pltpu.CompilerParams(vmem_limit_bytes=VMEM_BYTES),
    )(*args)


def angle_tables(c):
    lane = jnp.arange(128, dtype=jnp.int32)
    freqs = 10000.0 ** (-2.0 * (lane % 32).astype(jnp.float32) / HD)
    block = jnp.arange(8, dtype=jnp.int32)
    far = (block % 4) * 256 + jnp.where(block < 4, c, 1 - c) * 128
    rows = jnp.concatenate([jnp.arange(128, dtype=jnp.int32), far]).astype(jnp.float32)
    angle = rows[:, None] * freqs[None, :]
    cos, sin = jnp.cos(angle), jnp.sin(angle)
    return cos, sin


def paired(
    tokens,
    cotangent,
    species_index,
    species_count,
    loss_weight,
    query_weight,
    key_weight,
    value_weight,
    out_weight,
    gate_weight,
    up_weight,
    down_weight,
    mixer_gain,
    mixer_shift,
    feeder_gain,
    feeder_shift,
):
    dp, z = lax.axis_index("dp"), lax.axis_index("seq")
    c = dp % 2
    (wqkv, wgu, wo, wd, xh, cw, gv, norm_one, q, k, v, attended, lse, norm_two, middle, gate, upward, hidden,
     cos, sin) = fore(
        tokens, cotangent, query_weight, key_weight, value_weight, gate_weight, up_weight, out_weight, down_weight,
        mixer_gain.reshape(1, 32), mixer_shift.reshape(1, 32), feeder_gain.reshape(1, 32), feeder_shift.reshape(1, 32),
        species_index, species_count, loss_weight, *angle_tables(c))
    parts = back(
        cw, hidden, wd, norm_two, gate, upward, wgu, middle, wo, attended, q, k, v, lse, norm_one, wqkv, xh,
        cos, sin, gv)
    done = finish(*parts)
    return done[:9] + tuple(g.reshape(32) for g in done[9:])


def matmul(left, right):
    return jnp.dot(left, right, preferred_element_type=jnp.float32)


def weight_term(left, right):
    return lax.dot_general(
        left, right, (((0,), (0,)), ((), ())), preferred_element_type=jnp.float32
    )


def through(left, weight):
    return lax.dot_general(
        left, weight, (((1,), (1,)), ((), ())), preferred_element_type=jnp.float32
    )


def normalize(values):
    center = jnp.mean(values, axis=-1, keepdims=True)
    centered = values - center
    variance = jnp.mean(centered * centered, axis=-1, keepdims=True)
    scaling = lax.rsqrt(variance + 1e-05)
    return (centered * scaling, scaling)


def plain_norm_back(upstream, normed, scaling):
    first = jnp.mean(upstream, axis=-1, keepdims=True)
    second = jnp.mean(upstream * normed, axis=-1, keepdims=True)
    return scaling * (upstream - first - normed * second)


def tables(start, count):
    half = HD // 2
    positions = (start + jnp.arange(count, dtype=jnp.int32)).astype(jnp.float32)
    freqs = 10000.0 ** (-2.0 * jnp.arange(half, dtype=jnp.float32) / HD)
    angle = positions[:, None] * freqs[None, :]
    return (jnp.cos(angle)[:, None, :], jnp.sin(angle)[:, None, :])


def rotate(values, cosine, sine):
    half = HD // 2
    first = values[..., :half]
    second = values[..., half:]
    return jnp.concatenate(
        [first * cosine - second * sine, second * cosine + first * sine], axis=-1
    )


def attend_head(operands):
    query_head, key_head, value_head = operands
    scores = jnp.einsum(
        "wtd,wsd->wts", query_head, key_head, preferred_element_type=jnp.float32
    ) * HD ** (-0.5)
    peak = jnp.max(scores, axis=-1, keepdims=True)
    raised = jnp.exp(scores - peak)
    total = jnp.sum(raised, axis=-1, keepdims=True)
    probs = (raised / total).astype(jnp.bfloat16)
    result = jnp.einsum("wts,wsd->wtd", probs, value_head, preferred_element_type=jnp.float32)
    return (result, (peak + jnp.log(total))[..., 0])


def head_back(operands):
    query_head, key_head, value_head, upstream, log_total = operands
    scores = jnp.einsum(
        "wtd,wsd->wts", query_head, key_head, preferred_element_type=jnp.float32
    ) * HD ** (-0.5)
    probs = jnp.exp(scores - log_total[..., None])
    prob_grads = jnp.einsum(
        "wtd,wsd->wts", upstream, value_head, preferred_element_type=jnp.float32
    )
    inner = jnp.sum(probs * prob_grads, axis=-1, keepdims=True)
    score_grads = (probs * (prob_grads - inner)).astype(jnp.bfloat16)
    query_grad = jnp.einsum(
        "wts,wsd->wtd", score_grads, key_head, preferred_element_type=jnp.float32
    ) * HD ** (-0.5)
    key_grad = jnp.einsum(
        "wts,wtd->wsd", score_grads, query_head, preferred_element_type=jnp.float32
    ) * HD ** (-0.5)
    value_grad = jnp.einsum(
        "wts,wtd->wsd", probs.astype(jnp.bfloat16), upstream, preferred_element_type=jnp.float32
    )
    return (query_grad, key_grad, value_grad)


def general(
    tokens,
    cotangent,
    species_index,
    species_count,
    loss_weight,
    query_weight,
    key_weight,
    value_weight,
    out_weight,
    gate_weight,
    up_weight,
    down_weight,
    mixer_gain,
    mixer_shift,
    feeder_gain,
    feeder_shift,
):
    gathered = (
        lax.all_gather(query_weight, ("dp", "seq"), axis=0, tiled=True),
        lax.all_gather(key_weight, ("dp", "seq"), axis=0, tiled=True),
        lax.all_gather(value_weight, ("dp", "seq"), axis=0, tiled=True),
        lax.all_gather(out_weight, ("dp", "seq"), axis=0, tiled=True),
        lax.all_gather(gate_weight, ("dp", "seq"), axis=0, tiled=True),
        lax.all_gather(up_weight, ("dp", "seq"), axis=0, tiled=True),
        lax.all_gather(down_weight, ("dp", "seq"), axis=0, tiled=True),
        lax.all_gather(mixer_gain, ("dp", "seq"), axis=0, tiled=True),
        lax.all_gather(mixer_shift, ("dp", "seq"), axis=0, tiled=True),
        lax.all_gather(feeder_gain, ("dp", "seq"), axis=0, tiled=True),
        lax.all_gather(feeder_shift, ("dp", "seq"), axis=0, tiled=True),
    )
    wq, wk, wv, wo, wg, wu, wd, gain_one, shift_one, gain_two, shift_two = gathered
    windows, steps_dev, width = tokens.shape
    rows = windows * steps_dev
    start = lax.axis_index("seq") * steps_dev
    cosine, sine = tables(start, steps_dev)
    inputs = tokens.astype(jnp.float32).reshape(rows, width)
    normed_one, scaling_one = normalize(inputs)
    norm_one = (normed_one * gain_one.astype(jnp.float32) + shift_one.astype(jnp.float32)).astype(
        jnp.bfloat16
    )
    queries = rotate(
        matmul(norm_one, wq).reshape(windows, steps_dev, HEADS, HD), cosine, sine
    ).astype(jnp.bfloat16)
    keys = rotate(matmul(norm_one, wk).reshape(windows, steps_dev, HEADS, HD), cosine, sine).astype(
        jnp.bfloat16
    )
    values = matmul(norm_one, wv).astype(jnp.bfloat16)
    all_keys, all_values = (
        lax.all_gather(keys.reshape(windows, steps_dev, width), "seq", axis=1, tiled=True),
        lax.all_gather(values.reshape(windows, steps_dev, width), "seq", axis=1, tiled=True),
    )
    length = all_keys.shape[1]
    query_heads = queries.transpose(2, 0, 1, 3)
    key_heads = all_keys.reshape(windows, length, HEADS, HD).transpose(2, 0, 1, 3)
    value_heads = all_values.reshape(windows, length, HEADS, HD).transpose(2, 0, 1, 3)
    head_results, log_totals = lax.map(attend_head, (query_heads, key_heads, value_heads))
    attended = head_results.transpose(1, 2, 0, 3).reshape(rows, width).astype(jnp.bfloat16)
    middle = inputs + matmul(attended, wo)
    normed_two, scaling_two = normalize(middle)
    norm_two = (normed_two * gain_two.astype(jnp.float32) + shift_two.astype(jnp.float32)).astype(
        jnp.bfloat16
    )
    gate = matmul(norm_two, wg)
    upward = matmul(norm_two, wu)
    sigma = jax.nn.sigmoid(gate)
    swish = gate * sigma
    hidden = (swish * upward).astype(jnp.bfloat16)
    output = (middle + matmul(hidden, wd)).astype(jnp.bfloat16).reshape(windows, steps_dev, width)
    table = loss_weight * lax.rsqrt(species_count.astype(jnp.float32) / 400.0)
    picks = species_index[:, None] == jnp.arange(table.shape[0], dtype=jnp.int32)[None, :]
    factor = jnp.sum(jnp.where(picks, table[None, :], 0.0), axis=1)
    grad_out = (factor[:, None, None] * cotangent.astype(jnp.float32)).reshape(rows, width)
    regathered = (
        lax.all_gather(query_weight, ("dp", "seq"), axis=0, tiled=True),
        lax.all_gather(key_weight, ("dp", "seq"), axis=0, tiled=True),
        lax.all_gather(value_weight, ("dp", "seq"), axis=0, tiled=True),
        lax.all_gather(out_weight, ("dp", "seq"), axis=0, tiled=True),
        lax.all_gather(gate_weight, ("dp", "seq"), axis=0, tiled=True),
        lax.all_gather(up_weight, ("dp", "seq"), axis=0, tiled=True),
        lax.all_gather(down_weight, ("dp", "seq"), axis=0, tiled=True),
        lax.all_gather(mixer_gain, ("dp", "seq"), axis=0, tiled=True),
        lax.all_gather(mixer_shift, ("dp", "seq"), axis=0, tiled=True),
        lax.all_gather(feeder_gain, ("dp", "seq"), axis=0, tiled=True),
        lax.all_gather(feeder_shift, ("dp", "seq"), axis=0, tiled=True),
    )
    wq, wk, wv, wo, wg, wu, wd, gain_one, shift_one, gain_two, shift_two = regathered
    out_low = grad_out.astype(jnp.bfloat16)
    down_part = weight_term(hidden, out_low)
    hidden_grad = through(out_low, wd)
    gate_grad = (hidden_grad * upward * sigma * (1.0 + gate * (1.0 - sigma))).astype(jnp.bfloat16)
    upward_grad = (hidden_grad * swish).astype(jnp.bfloat16)
    gate_part = weight_term(norm_two, gate_grad)
    upward_part = weight_term(norm_two, upward_grad)
    norm_two_grad = through(gate_grad, wg) + through(upward_grad, wu)
    feeder_gain_part = jnp.sum(norm_two_grad * normed_two, axis=0)
    feeder_shift_part = jnp.sum(norm_two_grad, axis=0)
    middle_grad = grad_out + plain_norm_back(
        norm_two_grad * gain_two.astype(jnp.float32), normed_two, scaling_two
    )
    middle_low = middle_grad.astype(jnp.bfloat16)
    out_part = weight_term(attended, middle_low)
    attended_grad = through(middle_low, wo).astype(jnp.bfloat16)
    upstream_heads = attended_grad.reshape(windows, steps_dev, HEADS, HD).transpose(2, 0, 1, 3)
    query_heads_grad, key_heads_grad, value_heads_grad = lax.map(
        head_back, (query_heads, key_heads, value_heads, upstream_heads, log_totals)
    )
    key_whole = key_heads_grad.transpose(1, 2, 0, 3).reshape(windows, length, width)
    value_whole = value_heads_grad.transpose(1, 2, 0, 3).reshape(windows, length, width)
    key_mine, value_mine = (
        lax.psum_scatter(
            key_whole.astype(jnp.bfloat16), "seq", scatter_dimension=1, tiled=True
        ).astype(jnp.float32),
        lax.psum_scatter(
            value_whole.astype(jnp.bfloat16), "seq", scatter_dimension=1, tiled=True
        ).astype(jnp.float32),
    )
    query_lin_grad = (
        rotate(query_heads_grad.transpose(1, 2, 0, 3), cosine, -sine)
        .reshape(rows, width)
        .astype(jnp.bfloat16)
    )
    key_lin_grad = (
        rotate(key_mine.reshape(windows, steps_dev, HEADS, HD), cosine, -sine)
        .reshape(rows, width)
        .astype(jnp.bfloat16)
    )
    value_lin_grad = value_mine.reshape(rows, width).astype(jnp.bfloat16)
    query_part = weight_term(norm_one, query_lin_grad)
    key_part = weight_term(norm_one, key_lin_grad)
    value_part = weight_term(norm_one, value_lin_grad)
    norm_one_grad = (
        through(query_lin_grad, wq) + through(key_lin_grad, wk) + through(value_lin_grad, wv)
    )
    mixer_gain_part = jnp.sum(norm_one_grad * normed_one, axis=0)
    mixer_shift_part = jnp.sum(norm_one_grad, axis=0)
    input_grad = middle_grad + plain_norm_back(
        norm_one_grad * gain_one.astype(jnp.float32), normed_one, scaling_one
    )
    summed = (
        lax.psum_scatter(query_part, ("dp", "seq"), scatter_dimension=0, tiled=True),
        lax.psum_scatter(key_part, ("dp", "seq"), scatter_dimension=0, tiled=True),
        lax.psum_scatter(value_part, ("dp", "seq"), scatter_dimension=0, tiled=True),
        lax.psum_scatter(out_part, ("dp", "seq"), scatter_dimension=0, tiled=True),
        lax.psum_scatter(gate_part, ("dp", "seq"), scatter_dimension=0, tiled=True),
        lax.psum_scatter(upward_part, ("dp", "seq"), scatter_dimension=0, tiled=True),
        lax.psum_scatter(down_part, ("dp", "seq"), scatter_dimension=0, tiled=True),
        lax.psum_scatter(mixer_gain_part, ("dp", "seq"), scatter_dimension=0, tiled=True),
        lax.psum_scatter(mixer_shift_part, ("dp", "seq"), scatter_dimension=0, tiled=True),
        lax.psum_scatter(feeder_gain_part, ("dp", "seq"), scatter_dimension=0, tiled=True),
        lax.psum_scatter(feeder_shift_part, ("dp", "seq"), scatter_dimension=0, tiled=True),
    )
    return (
        output,
        input_grad.reshape(windows, steps_dev, width),
        summed[0],
        summed[1],
        summed[2],
        summed[3],
        summed[4],
        summed[5],
        summed[6],
        summed[7],
        summed[8],
        summed[9],
        summed[10],
    )


def solution(mesh):
    in_specs = (
        P("dp", "seq", None),
        P("dp", "seq", None),
        P("dp"),
        P(),
        P(),
    ) + (P(("dp", "seq"), None),) * 7 + (P(("dp", "seq")),) * 4
    out_specs = (P("dp", "seq", None),) * 2 + (P(("dp", "seq"), None),) * 7 + (P(("dp", "seq")),) * 4
    fits = mesh.shape["dp"] == 8 and mesh.shape["seq"] == 4
    return jax.shard_map(
        paired if fits else general, mesh=mesh, in_specs=in_specs, out_specs=out_specs, check_vma=False
    )
```

```python
import jax
import jax.numpy as jnp
from jax import lax
from jax.experimental import pallas as pl
from jax.experimental.pallas import tpu as pltpu
from jax.sharding import PartitionSpec as P

HEADS = 16
HD = 64
MESH = pl.DeviceIdType.MESH
BF = jnp.bfloat16
F32 = jnp.float32
ANY = pl.BlockSpec(memory_space=pl.ANY)
VM = pl.BlockSpec(memory_space=pltpu.VMEM)
VMEM_BYTES = 60 << 20


def place():
    dp, z = lax.axis_index("dp"), lax.axis_index("seq")
    return dp // 4, (dp // 2) % 2, dp % 2, z


def dev(y, x, c, z):
    return ((y * 2 + x) * 2 + c, z)


def both(a, b):
    return jnp.logical_and(a, b)


def greet(y, x, c, z):
    barrier = pltpu.get_barrier_semaphore()
    peers = [dev(y, 1 - x, c, z), dev(1 - y, x, c, z), dev(y, x, 1 - c, z)]
    for k in (1, 2, 3):
        peers += [dev(y, x, c, (z + k) % 4), dev(y, x, 1 - c, (z + k) % 4)]
    for p in peers:
        pl.semaphore_signal(barrier, inc=1, device_id=p, device_id_type=MESH)
    return lambda: pl.semaphore_wait(barrier, len(peers))


class Links:
    def __init__(self, send, recv, local):
        self.send, self.recv, self.local = send, recv, local
        self.n = 0
        self.m = 0
        self.open = []

    def take(self, count):
        self.n += count
        return self.n - count

    def copy(self, src, dst, device, send, recv):
        return pltpu.make_async_remote_copy(
            src_ref=src, dst_ref=dst, send_sem=self.send.at[send], recv_sem=self.recv.at[recv],
            device_id=device, device_id_type=MESH)

    def go(self, c, ok=None):
        if ok is None:
            c.start()
        else:
            pl.when(ok)(c.start)
        self.open.append((c, ok))
        return c

    def to(self, src, dst, device):
        i = self.take(1)
        return self.go(self.copy(src, dst, device, i, i))

    def later(self, src, dst, device):
        i = self.take(1)
        c = self.copy(src, dst, device, i, i)
        self.open.append((c, None))
        return c

    def here_later(self, src, dst):
        self.m += 1
        return pltpu.make_async_copy(src, dst, self.local.at[self.m - 1])

    def wanted(self, src, dst, device):
        i = self.take(1)
        return self.copy(src, dst, device, i, i)

    def here(self, src, dst):
        self.m += 1
        c = pltpu.make_async_copy(src, dst, self.local.at[self.m - 1])
        c.start()
        return c

    def drain(self):
        for c, ok in self.open:
            if ok is None:
                c.wait_send()
            else:
                pl.when(ok)(c.wait_send)
        self.open = []


def at_z(ref, zz):
    return ref.at[zz] if len(ref.shape) == 3 else ref.at[:, zz]


def pair_of(ref, first):
    return ref.at[pl.ds(first, 2)] if len(ref.shape) == 3 else ref.at[:, pl.ds(first, 2)]


def add_into(dst, *terms):
    def body(i, _):
        total = at_z(terms[0], i)[...]
        for t in terms[1:]:
            total += at_z(t, i)[...]
        at_z(dst, i)[...] = total
        return 0
    lax.fori_loop(0, dst.shape[-3], body, 0)


def reduce_shapes(piece):
    part = piece[:-3] + piece[-2:]
    two = piece[:-3] + (2,) + piece[-2:]
    return [pltpu.VMEM((2,) + piece, BF), pltpu.VMEM(piece, BF), pltpu.VMEM(two, BF), pltpu.VMEM(two, BF),
            pltpu.VMEM(part, BF), pltpu.VMEM(part, F32)]


def collect(links, at, me, route, bufs, deliver):
    y, x, c, z = me
    to_x, to_y = dev(y, 1 - x, c, z), dev(1 - y, x, c, z)
    got, third, from_outer, from_inner, from_near, total = bufs
    out = deliver(total)
    if route == 0:
        own, away = [at(1 - y, x), at(y, x)], [at(1 - y, 1 - x), at(y, 1 - x)]
        one, two = to_x, to_y
    else:
        own, away = [at(y, 1 - x), at(y, x)], [at(1 - y, 1 - x), at(1 - y, x)]
        one, two = to_y, to_x
    near = z + 1 - 2 * (z % 2)
    inner = both(z > 0, z < 3)
    outer = jnp.logical_not(inner)
    far_side, near_side = pair_of(own[1], 2 - 2 * (z // 2)), pair_of(own[1], 2 * (z // 2))
    give = [links.later(away[n], got.at[n], one) for n in (0, 1)]
    cross = links.later(own[0], third, two)
    inward = links.wanted(far_side, from_outer, dev(y, x, c, near))
    over = links.wanted(far_side, from_inner, dev(y, x, c, 3 - z))
    links.open += [(inward, outer), (over, inner)]
    settle = links.later(at_z(own[1], near), from_near, dev(y, x, c, near))

    def start():
        for q in give:
            q.start()

    def first():
        give[0].wait_recv()
        add_into(own[0], own[0], got.at[0])
        cross.start()

    def second():
        give[1].wait_recv()
        cross.wait_recv()
        add_into(own[1], own[1], got.at[1], third)

        @pl.when(outer)
        def _():
            inward.start()
            settle.start()

    def inside():
        @pl.when(inner)
        def _():
            inward.wait_recv()
            add_into(far_side, far_side, from_outer)
            over.start()

    def across():
        @pl.when(inner)
        def _():
            over.wait_recv()
            add_into(near_side, near_side, from_inner)
            settle.start()

    def last():
        settle.wait_recv()
        total[...] = at_z(own[1], z)[...].astype(F32) + from_near[...].astype(F32)
        for q in out:
            q.start()
    return start, first, second, inside, across, last


class Outgoing:
    def __init__(self, links, me, src, dst):
        y, x, c, z = me
        recv, send = links.take(4), links.take(4)
        self.here, self.away = c == z // 2, c != z // 2
        self.remote, self.back = [], []
        for k in range(4):
            zz = (z + k) % 4
            s, d = src.at[zz], dst.at[z % 2, c]
            self.remote.append(links.copy(s, d, dev(y, x, z // 2, zz), send + k, recv + (z % 2) * 2 + c))
            links.open.append((self.remote[k], None if k else self.away))
            if k == 0:
                self.local = links.here_later(s, d)
        for i in (0, 1):
            for h in (0, 1):
                d = dst.at[i, h]
                mine = both(z == 2 * c + i, h == c)
                self.back.append((links.copy(d, d, dev(y, x, 1 - c, z), send, recv + 2 * i + h), jnp.logical_not(mine)))

    def start(self):
        for q in self.remote[1:]:
            q.start()
        pl.when(self.away)(self.remote[0].start)
        pl.when(self.here)(self.local.start)

    def finish(self):
        pl.when(self.here)(self.local.wait)
        for q, ok in self.back:
            pl.when(ok)(q.wait_recv)


def swap_halves(u):
    lane = lax.broadcasted_iota(jnp.int32, u.shape, 1) % HD
    return jnp.where(lane < HD // 2, pltpu.roll(u, 128 - HD // 2, 1), pltpu.roll(u, HD // 2, 1))


def head_mask(shape, h):
    lane = lax.broadcasted_iota(jnp.int32, shape, 1)
    return (lane < HD) if h == 0 else (lane >= HD)


def dot_t(a, b):
    return lax.dot_general(a, b, (((1,), (1,)), ((), ())), preferred_element_type=F32)


def project_step(xw, gv, w, cos, sin, n1, q, k, v, r):
    rows = pl.ds(pl.multiple_of(r * 256, 256), 256)
    u = xw[r // 2, pl.ds((r % 2) * 2, 2)].reshape(256, 1024).astype(F32)
    d = u - jnp.mean(u, axis=-1, keepdims=True)
    scaling = lax.rsqrt(jnp.mean(d * d, axis=-1, keepdims=True) + 1e-05)
    n = (d * scaling * gv[0:1, :] + gv[1:2, :]).astype(BF)
    n1[rows, :] = n
    for g in range(4):
        lanes = pl.ds(128 * g, 128)
        t = jnp.dot(n, w[:, :, :, :, pl.ds(384 * g, 384)].reshape(1024, 384), preferred_element_type=F32)
        for j, o in ((0, q), (1, k)):
            s = t[:, 128 * j:128 * j + 128]
            o[rows, lanes] = (s * cos[rows, :] + swap_halves(s) * sin[rows, :]).astype(BF)
        v[rows, lanes] = t[:, 256:].astype(BF)


def attend_step(q, k, v, o, lse, g, i):
    lanes = pl.ds(pl.multiple_of(g * 128, 128), 128)
    rows = pl.ds(pl.multiple_of(i * 256, 256), 256)
    qs = q[rows, lanes] * jnp.asarray(HD ** -0.5, BF)
    kk, vv = k[:, lanes], v[:, lanes]
    outs, logs = [], []
    for h in (0, 1):
        qh = jnp.where(head_mask(qs.shape, h), qs, jnp.zeros_like(qs))
        s = dot_t(qh, kk)
        m = jnp.max(s, axis=-1, keepdims=True)
        e = jnp.exp(s - m)
        t = jnp.sum(e, axis=-1, keepdims=True)
        p = (e * (1.0 / t)).astype(BF)
        outs.append(jnp.dot(p, vv, preferred_element_type=F32))
        logs.append(jnp.broadcast_to(m + jnp.log(t), qs.shape))
    keep = head_mask(qs.shape, 0)
    o[rows, lanes] = jnp.where(keep, outs[0], outs[1]).astype(BF)
    t = jnp.transpose(jnp.where(keep, logs[0], logs[1]))
    lse[pl.ds(2 * g, 1), rows] = t[0:1]
    lse[pl.ds(2 * g + 1, 1), rows] = t[HD:HD + 1]


def attend_back_step(q, k, v, do, lse, cos, sin, dqkv, dka, dva, g, i):
    lanes = pl.ds(pl.multiple_of(g * 128, 128), 128)
    rows = pl.ds(pl.multiple_of(i * 256, 256), 256)

    @pl.when(i == 0)
    def _():
        dka[...] = jnp.zeros_like(dka)
        dva[...] = jnp.zeros_like(dva)
    kk, vv, go = k[:, lanes], v[:, lanes], do[rows, lanes]
    qs = q[rows, lanes] * jnp.asarray(HD ** -0.5, BF)
    logs = lse[pl.ds(2 * g, 1), rows], lse[pl.ds(2 * g + 1, 1), rows]
    dks, dvs, dqs = [], [], []
    for h in (0, 1):
        keep = head_mask(kk.shape, h)
        zero = jnp.zeros_like(kk)
        s = dot_t(jnp.where(keep, kk, zero), qs)
        p = jnp.exp(s - logs[h])
        dp = dot_t(jnp.where(keep, vv, zero), go)
        pd = p * dp
        ds = (pd - p * jnp.sum(pd, axis=0, keepdims=True)).astype(BF)
        dvs.append(jnp.dot(p.astype(BF), go, preferred_element_type=F32))
        dks.append(jnp.dot(ds, qs, preferred_element_type=F32))
        dqs.append(lax.dot_general(ds, kk, (((0,), (0,)), ((), ())), preferred_element_type=F32))
    keep = head_mask(kk.shape, 0)
    dka[...] += jnp.where(keep, dks[0], dks[1])
    dva[...] += jnp.where(keep, dvs[0], dvs[1])
    u = jnp.where(head_mask(go.shape, 0), dqs[0], dqs[1]) * HD ** -0.5
    dqkv[rows, pl.ds(pl.multiple_of(g * 384, 128), 128)] = (
        u * cos[rows, :] - swap_halves(u) * sin[rows, :]).astype(BF)

    @pl.when(i == 3)
    def _():
        u = dka[...]
        dqkv[:, pl.ds(pl.multiple_of(128 + g * 384, 128), 128)] = (
            u * cos[...] - swap_halves(u) * sin[...]).astype(BF)
        dqkv[:, pl.ds(pl.multiple_of(256 + g * 384, 128), 128)] = dva[...].astype(BF)


class Incoming:
    def __init__(self, links, me, src, mid, dst):
        y, x, c, z = me
        partner = dev(y, x, 1 - c, z)
        self.swap = [links.later(src.at[i, pl.ds((1 - c) * 128, 128)], mid.at[2 * c + i], partner) for i in (0, 1)]
        send, recv = links.take(4), links.take(4)
        self.sends, self.kept, self.got = [], [], []
        m = links.m
        links.m += 1
        for w in range(4):
            d = dst.at[0, z]
            for ok, s in ((c == w // 2, src.at[w % 2, pl.ds(c * 128, 128)]), (c != w // 2, mid.at[w])):
                away, here = both(ok, z != w), both(ok, z == w)
                q = links.copy(s, d, dev(y, x, c, w), send + w, recv + z)
                self.sends.append((q, away))
                links.open.append((q, away))
                self.kept.append((pltpu.make_async_copy(s, d, links.local.at[m]), here))
        for zz in range(4):
            d = dst.at[0, zz]
            self.got.append((links.copy(d, d, dev(y, x, c, zz), send, recv + zz), z != zz))
        self.pair = links.later(dst.at[0], dst.at[1], partner)

    def begin(self):
        for q in self.swap:
            q.start()

    def send(self):
        for q in self.swap:
            q.wait_recv()
        for q, ok in self.sends + self.kept:
            pl.when(ok)(q.start)

    def arrive(self):
        for q, ok in self.kept:
            pl.when(ok)(q.wait)
        for q, ok in self.got:
            pl.when(ok)(q.wait_recv)
        self.pair.start()

    def finish(self):
        self.pair.wait_recv()


def disperse(links, single, bundle, me, route):
    y, x, c, z = me
    to_x, to_y = dev(y, 1 - x, c, z), dev(1 - y, x, c, z)
    mine = y * 2 + x
    if route == 0:
        two, three, other = to_y, to_x, (1 - y) * 2 + x
    else:
        two, three, other = to_x, to_y, y * 2 + 1 - x
    over_z = [links.later(single(mine, z), single(mine, z), dev(y, x, c, (z + k) % 4)) for k in (1, 2, 3)]
    cross = links.later(bundle(mine), bundle(mine), two)
    last = [links.later(bundle(mine), bundle(mine), three), links.later(bundle(other), bundle(other), three)]

    def start():
        for q in over_z:
            q.start()

    def first():
        for q in over_z:
            q.wait_recv()
        cross.start()
        last[0].start()

    def second():
        cross.wait_recv()
        last[1].start()

    def finish():
        for q in last:
            q.wait_recv()
    return start, first, second, finish


FORE_PIECES = (
    ("gu", 5, 1),
    ("d", 0, 1),
    ("qkv", 0, 1),
    ("o", 0, 0),
    ("gu", 6, 0),
    ("gu", 1, 0),
    ("gu", 2, 1),
    ("qkv", 1, 0),
    ("gu", 0, 1),
    ("gu", 3, 1),
    ("gu", 4, 0),
    ("d", 1, 0),
    ("d", 3, 1),
    ("gu", 7, 0),
    ("d", 2, 1),
)
FORE_ORDER = (
    ((17, 0), (0, 0), (1, 0), (2, 0), (3, 0), (4, 0), (5, 0), (6, 0), (7, 0), (15, 0), (8, 0), (9, 0), (10, 0),
     (11, 0), (12, 0), (13, 0), (14, 0), (17, 1), (17, 2), (17, 3), (0, 1), (1, 1), (0, 2), (1, 2), (2, 1), (0, 3),
     (3, 1), (1, 3), (2, 2), (4, 1), (5, 1), (6, 1), (3, 2), (2, 3), (7, 1), (6, 2), (4, 2), (3, 3), (5, 2),
     (4, 3), (7, 2), (5, 3), (15, 1), (6, 3), (8, 1), (7, 3), (15, 2),),
    ((8, 2), (9, 1)), ((10, 1),), (), (), (), (), ((11, 1), (8, 3), (9, 2)), (), (), (), ((12, 1),), (), (), (),
    ((10, 2), (13, 1), (16, 0)), (), (), ((9, 3), (10, 3), (11, 2), (12, 2), (14, 1)), (), ((11, 3), (13, 2)),
    ((12, 3), (14, 2), (16, 1), (13, 3)), ((16, 2), (14, 3)),
)


def rotary_tables(tab_cos, tab_sin, cos, sin):
    lane = lax.broadcasted_iota(jnp.int32, (128, 128), 1)
    sign = jnp.where(lane % HD < HD // 2, -1.0, 1.0)
    for i in range(8):
        a, b = tab_cos[128 + i:129 + i, :], tab_sin[128 + i:129 + i, :]
        cos[128 * i:128 * i + 128, :] = tab_cos[0:128, :] * a - tab_sin[0:128, :] * b
        sin[128 * i:128 * i + 128, :] = sign * (tab_sin[0:128, :] * a + tab_cos[0:128, :] * b)


def fore_kernel(tok, cot, wq, wk, wv, wg, wu, wo, wd, g0, g1, g2, g3, species, count, weight,
                tab_cos, tab_sin, *rest):
    (oqkv, ogu, oo, od, xh, cw, gvo, n1o, qo, ko, vo, atto, lseo, n2o, mido, gateo, upo, hido, coso, sino,
     own_qkv, oth_qkv, own_gu, oth_gu, gp, cos, sin,
     tmid, cmid, gains, gv, xw, w3, n1, q, k, v, att, lse, wos, sent, came, mid, n2, wgs, wus,
     gate, up, hid, send, recv, local) = rest
    me = y, x, c, z = place()
    yx = y * 2 + x
    partner = dev(y, x, 1 - c, z)

    def prepare():
        def columns(src, own, oth, width, base, stride):
            for g in range(4):
                lanes = pl.ds(base + stride * g, width)
                own[:, lanes] = src[:, pl.ds(pl.multiple_of((2 * g + c) * width, width), width)]
                oth[:, lanes] = src[:, pl.ds(pl.multiple_of((2 * g + 1 - c) * width, width), width)]
        for j, src in enumerate((wq, wk, wv)):
            columns(src, own_qkv, oth_qkv, 128, 128 * j, 384)
        for j, src in enumerate((wg, wu)):
            columns(src, own_gu, oth_gu, 512, 2048 * j, 512)
        gp[...] = jnp.zeros_like(gp)
        for i, src in enumerate((g0, g1, g2, g3)):
            gp[i:i + 1, 0:32] = src[...].astype(F32)
        gp[...] = pltpu.roll(gp[...], z * 32, 1)
        lane = lax.broadcasted_iota(jnp.int32, (1, 128), 1)
        row = jnp.zeros((1, 128), F32)
        for i in (0, 1):
            n = jnp.full((1, 128), count[species[i]].astype(F32), F32)
            row = jnp.where(lane == i, weight[species[i]] * lax.rsqrt(n / 400.0), row)
        gp[4:5, :] = jnp.where(z == 0, row, jnp.zeros_like(row))
    met = greet(y, x, c, z)
    prepare()
    met()
    links = Links(send, recv, local)
    tin, cin = Incoming(links, me, tok, tmid, xw), Incoming(links, me, cot, cmid, cw)
    tin.begin()
    swaps = [links.to(gp, gains.at[yx, c, z], partner), links.to(oth_qkv, oqkv.at[yx, c, z], partner),
             links.to(oth_gu, ogu.at[yx, c, z], partner)]
    loc = [links.here(gp, gains.at[yx, c, z]), links.here(own_qkv, oqkv.at[yx, c, z]),
           links.here(own_gu, ogu.at[yx, c, z]), links.here(wo, oo.at[yx, z]), links.here(wd, od.at[yx, z])]
    work = []
    for name, index, route in FORE_PIECES:
        if name in ("qkv", "gu"):
            arr, cols = (oqkv, 768) if name == "qkv" else (ogu, 512)
            lanes = pl.ds(index * cols, cols)
            work.append(disperse(links, lambda i, zz, arr=arr, lanes=lanes: arr.at[i, :, zz, :, lanes],
                                 lambda i, arr=arr, lanes=lanes: arr.at[i, :, :, :, lanes], me, route))
        else:
            arr = oo if name == "o" else od
            rows = pl.ds(index * 32, 32)
            work.append(disperse(links, lambda i, zz, arr=arr, rows=rows: arr.at[i, zz, rows],
                                 lambda i, arr=arr, rows=rows: arr.at[i, :, rows], me, route))

    def later():
        cin.begin()
        cin.send()
    work += [(tin.send, tin.arrive, tin.finish), (later, cin.arrive, cin.finish),
             disperse(links, lambda i, zz: gains.at[i, :, zz], lambda i: gains.at[i], me, 1)]
    swap = links.wanted(sent, came, partner)
    share = links.later(n2.at[pl.ds(0, 512)], n2.at[pl.ds(512, 512)], partner)
    for e in loc:
        e.wait()
    for e in swaps:
        e.wait_recv()

    def comm(slot):
        for i, stage in FORE_ORDER[slot]:
            work[i][stage]()

    keep = []

    def put(src, dst):
        keep.append(links.here(src, dst))
    comm(0)
    wload = links.here(oqkv, w3)
    rotary_tables(tab_cos, tab_sin, cos, sin)
    put(cos, coso)
    put(sin, sino)
    wload.wait()
    for i in range(4):
        for j in (0, 1):
            gv[:, pl.ds((2 * i + j) * 128, 128)] = (gains[i, j, 0] + gains[i, j, 1]) + (gains[i, j, 2] + gains[i, j, 3])

    def rows_of(step):
        lax.fori_loop(0, 4, lambda r, _: (step(r), 0)[1], 0)
    rows_of(lambda r: project_step(xw, gv, w3, cos, sin, n1, q, k, v, r))
    for a, b in ((gv, gvo), (n1, n1o), (q, qo), (k, ko), (v, vo), (xw.at[0], xh)):
        put(a, b)
    comm(1)

    def step(t, _):
        attend_step(q, k, v, att, lse, t // 4, t % 4)
        for slot in range(2, 17):
            if FORE_ORDER[slot]:
                pl.when(t == slot - 2)(lambda slot=slot: comm(slot))
        return 0
    lax.fori_loop(0, 16, step, 0)
    comm(17)
    wload = links.here(oo, wos)
    put(att, atto)
    put(lse, lseo)
    wload.wait()

    def terms(r, out, first):
        rows = pl.ds(pl.multiple_of(r * 256, 256), 256)
        out[rows, :] = jnp.dot(att[pl.ds(pl.multiple_of(first + r * 256, 256), 256), :], wos[...].reshape(512, 1024),
                               preferred_element_type=F32)
    lax.fori_loop(0, 2, lambda r, _: (terms(r, sent, 512), 0)[1], 0)
    swap.start()
    lax.fori_loop(0, 2, lambda r, _: (terms(r, mid, 0), 0)[1], 0)
    swap.wait()

    def second_norm(r):
        rows = pl.ds(pl.multiple_of(r * 128, 128), 128)
        u = xw[0, r].astype(F32) + (mid[rows, :] + came[rows, :])
        mid[rows, :] = u
        d = u - jnp.mean(u, axis=-1, keepdims=True)
        scaling = lax.rsqrt(jnp.mean(d * d, axis=-1, keepdims=True) + 1e-05)
        n2[rows, :] = (d * scaling * gv[2:3, :] + gv[3:4, :]).astype(BF)
    rows_of(second_norm)
    share.start()
    put(mid, mido)
    comm(18)
    share.wait_recv()
    put(n2, n2o)
    for j in range(4):
        if j:
            comm(18 + j)
        lanes = pl.ds(512 * j, 512)
        lg = links.here(ogu.at[:, :, :, :, lanes], wgs)
        lu = links.here(ogu.at[:, :, :, :, pl.ds(2048 + 512 * j, 512)], wus)
        lg.wait()
        lu.wait()

        def hidden_units(r, lanes=lanes):
            rows = pl.ds(pl.multiple_of(r * 256, 256), 256)
            n = n2[rows, :]
            a = jnp.dot(n, wgs[...].reshape(1024, 512), preferred_element_type=F32)
            b = jnp.dot(n, wus[...].reshape(1024, 512), preferred_element_type=F32)
            hid[rows, lanes] = (a * jax.nn.sigmoid(a) * b).astype(BF)
            gate[rows, lanes] = a.astype(BF)
            up[rows, lanes] = b.astype(BF)
        rows_of(hidden_units)
        for a, b in ((hid, hido), (gate, gateo), (up, upo)):
            put(a.at[:, lanes], b.at[:, lanes])
    comm(22)
    for e in keep:
        e.wait()
    links.drain()


def fore(*args):
    S = jax.ShapeDtypeStruct
    V = pltpu.VMEM
    table = [V((1024, 128), F32)] * 2
    specs = [VM] * 13 + [pl.BlockSpec(memory_space=pltpu.SMEM)] * 3 + [VM] * 2
    return pl.pallas_call(
        fore_kernel,
        out_shape=(
            S((4, 2, 4, 32, 1536), BF), S((4, 2, 4, 32, 4096), BF), S((4, 4, 32, 1024), BF), S((4, 4, 128, 1024), BF),
            S((4, 128, 1024), BF), S((2, 4, 128, 1024), BF), S((8, 1024), F32), S((1024, 1024), BF),
            S((1024, 512), BF), S((1024, 512), BF), S((1024, 512), BF), S((1024, 512), BF), S((8, 1024), F32),
            S((1024, 1024), BF), S((512, 1024), F32), S((1024, 2048), BF), S((1024, 2048), BF), S((1024, 2048), BF),
            S((1024, 128), F32), S((1024, 128), F32),
        ),
        in_specs=specs,
        out_specs=[ANY] * 20,
        scratch_shapes=[V((32, 1536), BF)] * 2 + [V((32, 4096), BF)] * 2 + [V((8, 128), F32)] + table + [
            V((4, 128, 1024), BF), V((4, 128, 1024), BF), V((4, 2, 4, 8, 128), F32), V((8, 1024), F32),
            V((2, 4, 128, 1024), BF), V((4, 2, 4, 32, 1536), BF), V((1024, 1024), BF),
            V((1024, 512), BF), V((1024, 512), BF), V((1024, 512), BF), V((1024, 512), BF), V((8, 1024), F32),
            V((4, 4, 32, 1024), BF), V((512, 1024), F32), V((512, 1024), F32), V((512, 1024), F32),
            V((1024, 1024), BF), V((4, 2, 4, 32, 512), BF), V((4, 2, 4, 32, 512), BF),
            V((1024, 2048), BF), V((1024, 2048), BF), V((1024, 2048), BF),
            pltpu.SemaphoreType.DMA((200,)),
            pltpu.SemaphoreType.DMA((200,)),
            pltpu.SemaphoreType.DMA((72,)),
        ],
        compiler_params=pltpu.CompilerParams(collective_id=0, has_side_effects=True, vmem_limit_bytes=67043328),
    )(*args)


PIECES = (
    ("d", 1, 1),
    ("gu", 2, 1),
    ("gu", 4, 0),
    ("gu", 1, 1),
    ("gu", 0, 0),
    ("qkv", 1, 1),
    ("gu", 7, 0),
    ("d", 3, 0),
    ("o", 0, 1),
    ("d", 0, 1),
    ("qkv", 2, 1),
    ("gu", 6, 1),
    ("qkv", 0, 0),
    ("d", 2, 1),
    ("gu", 5, 0),
    ("qkv", 3, 1),
    ("gu", 3, 0),
)
SHAPES = {"d": (4, 32, 1024), "o": (4, 32, 1024), "gu": (2, 4, 32, 512), "qkv": (2, 4, 32, 384)}
ORDER = (
    (), ((0, 0), (7, 0)), ((0, 1), (2, 0), (4, 0), (7, 1)), ((0, 2), (3, 0), (7, 2)),
    ((0, 3), (1, 0), (2, 1), (3, 1), (7, 3)), ((0, 4), (1, 1), (4, 1), (6, 0), (7, 4), (9, 0), (14, 0)),
    ((0, 5), (1, 2), (2, 2), (7, 5), (3, 2)), ((2, 3), (4, 2), (6, 1), (1, 3), (8, 0), (16, 0)),
    ((1, 4), (2, 4), (3, 3), (17, 0), (4, 3), (9, 1), (14, 1)), ((6, 2),), (), (), ((8, 1), (13, 0), (16, 1)),
    ((12, 0),), (), (), ((3, 4), (6, 3)), ((1, 5), (2, 5), (14, 2), (9, 2)), ((5, 0),),
    ((13, 1), (8, 2), (14, 3), (9, 3)), (), ((12, 1), (4, 4), (8, 3)), ((6, 4),), ((14, 4), (10, 0)),
    ((17, 1), (16, 2), (16, 3), (9, 4)), ((3, 5), (4, 5), (5, 1), (11, 0), (6, 5), (13, 2), (8, 4), (13, 3), (16, 4)),
    (), ((14, 5), (5, 2), (5, 3), (13, 4)), ((9, 5), (12, 2), (12, 3), (5, 4), (15, 0)),
    ((8, 5), (5, 5), (13, 5), (16, 5), (18, 0), (10, 1), (11, 1), (12, 4), (19, 0), (15, 1), (10, 2), (11, 2),
     (19, 1), (19, 2), (15, 2), (10, 3), (11, 3), (18, 1), (12, 5), (19, 3), (10, 4), (15, 3), (10, 5), (11, 4),
     (15, 4), (11, 5), (15, 5),),

)


def total_over_devices(links, me, acc, got):
    y, x, c, z = me
    hops = [links.wanted(acc, got.at[i], d) for i, d in
            enumerate((dev(y, x, 1 - c, z), dev(y, 1 - x, c, z), dev(1 - y, x, c, z)))]
    over_z = [links.wanted(acc, got.at[2 + k], dev(y, x, c, (z + k) % 4)) for k in (1, 2, 3)]

    def settle(i):
        hops[i].wait()
        acc[...] += got[i]

    def chip():
        hops[0].start()
        settle(0)
        hops[1].start()

    def second():
        settle(1)
        hops[2].start()

    def third():
        settle(2)
        for q in over_z:
            q.start()

    def last():
        for q in over_z:
            q.wait()
        acc[...] += got[3] + (got[4] + got[5])
    return chip, second, third, last


def rows_dot(a, b):
    return lax.dot_general(a, b, (((0,), (0,)), ((), ())), preferred_element_type=F32)


def each(count, step):
    def body(r, _):
        step(r)
        return 0
    lax.fori_loop(0, count, body, 0)


def block(i, size):
    return pl.ds(pl.multiple_of(i * size, size), size)


def norm_parts(u):
    d = u - jnp.mean(u, axis=-1, keepdims=True)
    scaling = lax.rsqrt(jnp.mean(d * d, axis=-1, keepdims=True) + 1e-05)
    return d * scaling, scaling


def norm_back(upstream, normed, scaling):
    return scaling * (upstream - jnp.mean(upstream, axis=-1, keepdims=True)
                      - normed * jnp.mean(upstream * normed, axis=-1, keepdims=True))


def back_kernel(cw, hido, od, n2o, gateo, upo, ogu, mido, oo, atto, qo, ko, vo, lseo, n1o, oqkv, xh,
                cos, sin, gv, *rest):
    fqkv, fgu, fo, fd, fgain, out_w, ig_w = rest[:7]
    scratch = list(rest[7:])
    (gd, ggu, go, gw, mg, sent, came, mlow, ag, out16, ig, gacc, ggot, send, recv, local, ready) = scratch[-17:]
    me = y, x, c, z = place()
    partner = dev(y, x, 1 - c, z)
    met = greet(y, x, c, z)
    links = Links(send, recv, local)
    work = []
    finals = []
    for name, index, route in PIECES:
        bufs = [scratch.pop(0) for _ in range(6)]
        if name in ("qkv", "gu"):
            src, dst = (gw, fqkv) if name == "qkv" else (ggu, fgu)
            cols = SHAPES[name][3]
            lanes = pl.ds(index * cols, cols)

            def at(yy, xx, src=src, index=index):
                return src.at[index, yy * 2 + xx]

            def deliver(total, dst=dst, lanes=lanes):
                there = links.later(total.at[1 - c], dst.at[c, :, lanes], partner)
                here = links.here_later(total.at[c], dst.at[c, :, lanes])
                finals.extend((there.wait_recv, here.wait))
                return there, here
        else:
            src, dst = (gd, fd) if name == "d" else (go, fo)
            rows = pl.ds(index * 32, 32)

            def at(yy, xx, src=src, rows=rows):
                return src.at[yy * 2 + xx, :, rows]

            def deliver(total, dst=dst, rows=rows):
                here = links.here_later(total, dst.at[rows])
                finals.append(here.wait)
                return (here,)
        work.append(collect(links, at, me, route, bufs, deliver))
    o1 = Outgoing(links, me, out16, out_w)
    o2 = Outgoing(links, me, ig, ig_w)
    work += [(o1.start, o1.finish), (o2.start, o2.finish), total_over_devices(links, me, gacc, ggot)]
    swaps = [links.wanted(sent, came, partner) for _ in range(3)]
    share = links.later(mlow.at[0], mlow.at[1], partner)

    def comm(slot):
        for i, stage in ORDER[slot]:
            work[i][stage]()

    def swap(n):
        if n:
            pl.semaphore_wait(ready, 1)
        swaps[n].start()

    def read(n):
        if n < 2:
            pl.semaphore_signal(ready, inc=1, device_id=partner, device_id_type=MESH)

    gacc[...] = jnp.zeros_like(gacc)
    lane = lax.broadcasted_iota(jnp.int32, (1, 1024), 1)
    here = (2 * (y * 2 + x) + z // 2) * 128 + z % 2
    factor = jnp.sum(jnp.where(lane == here, gv[4:5, :], 0.0), axis=1, keepdims=True)

    def hidden_layer(low):
        a = links.here(cw, low)

        def down(hv):
            b = links.here(hido, hv)
            a.wait()

            def scale(i):
                low[i // 4, i % 4] = (factor * low[i // 4, i % 4].astype(F32)).astype(BF)
            each(8, scale)
            b.wait()

            def weights(r):
                u = rows_dot(hv[:, block(r, 256)], low[...].reshape(1024, 1024))
                gd[r // 2, pl.ds((r % 2) * 2, 2)] = u.astype(BF).reshape(2, 128, 1024)
            each(8, weights)
            met()
            comm(0)
        pl.run_scoped(down, pltpu.VMEM((1024, 2048), BF))

        def units(n2, gate, up, dgate, dup, wg, wu, wd):
            a = links.here(n2o, n2)
            for j in range(4):
                lanes = pl.ds(512 * j, 512)
                got = [links.here(od.at[j], wd), links.here(gateo.at[:, lanes], gate), links.here(upo.at[:, lanes], up),
                       links.here(ogu.at[:, :, :, :, lanes], wg),
                       links.here(ogu.at[:, :, :, :, pl.ds(2048 + 512 * j, 512)], wu)]
                comm(1 + j)
                for q in got:
                    q.wait()

                def grads(r):
                    rows = block(r, 256)
                    g = dot_t(low[r // 2, pl.ds((r % 2) * 2, 2)].reshape(256, 1024), wd[...].reshape(512, 1024))
                    a, b = gate[rows, :].astype(F32), up[rows, :].astype(F32)
                    t = jax.nn.sigmoid(a)
                    dgate[rows, :] = (g * b * t * (1.0 + a * (1.0 - t))).astype(BF)
                    dup[rows, :] = (g * a * t).astype(BF)
                each(4, grads)
                if j == 0:
                    a.wait()

                def weights(r):
                    n = n2[:, block(r, 256)]
                    ggu[j, r] = rows_dot(n, dgate[...]).astype(BF).reshape(2, 4, 32, 512)
                    ggu[4 + j, r] = rows_dot(n, dup[...]).astype(BF).reshape(2, 4, 32, 512)
                each(4, weights)

                def terms(r, out, first):
                    rows = pl.ds(pl.multiple_of(first + r * 256, 256), 256)
                    u = (dot_t(dgate[rows, :], wg[...].reshape(1024, 512))
                         + dot_t(dup[rows, :], wu[...].reshape(1024, 512)))
                    dst = block(r, 256)
                    out[dst, :] = u if j == 0 else out[dst, :] + u
                each(2, lambda r: terms(r, sent, 512))
                if j == 3:
                    swap(0)
                each(2, lambda r: terms(r, mg, 0))
        pl.run_scoped(units, pltpu.VMEM((1024, 1024), BF), *[pltpu.VMEM((1024, 512), BF)] * 4,
                      *[pltpu.VMEM((4, 2, 4, 32, 512), BF)] * 2, pltpu.VMEM((4, 128, 1024), BF))
    pl.run_scoped(hidden_layer, pltpu.VMEM((2, 4, 128, 1024), BF))
    comm(5)

    def second_norm(mid, cot):
        a, b = links.here(mido, mid), links.here(cw.at[0], cot)
        a.wait()
        b.wait()
        swaps[0].wait()

        def part(r):
            rows = block(r, 128)
            gn = mg[rows, :] + came[rows, :]
            normed, scaling = norm_parts(mid[rows, :])
            gacc[2:3, :] += jnp.sum(gn * normed, axis=0, keepdims=True)
            gacc[3:4, :] += jnp.sum(gn, axis=0, keepdims=True)
            u = factor * cot[r].astype(F32) + norm_back(gn * gv[2:3, :], normed, scaling)
            mg[rows, :] = u
            mlow[0, r] = u.astype(BF)
        each(4, part)
        read(0)
        share.start()
    pl.run_scoped(second_norm, pltpu.VMEM((512, 1024), F32), pltpu.VMEM((4, 128, 1024), BF))
    comm(6)

    def out_layer(w, att):
        a, b = links.here(oo, w), links.here(atto, att)
        a.wait()
        b.wait()
        share.wait_recv()

        def weights(r):
            u = rows_dot(att[:, block(r, 256)], mlow[...].reshape(1024, 1024))
            go[pl.ds(2 * r, 2)] = u.astype(BF).reshape(2, 4, 32, 1024)
        each(2, weights)

        def grads(r):
            u = dot_t(mlow[r // 2, pl.ds((r % 2) * 2, 2)].reshape(256, 1024), w[...].reshape(512, 1024))
            ag[block(r, 256), :] = u.astype(BF)
        each(4, grads)
    pl.run_scoped(out_layer, pltpu.VMEM((4, 4, 32, 1024), BF), pltpu.VMEM((1024, 512), BF))
    comm(7)

    def output(hv, w, mid):
        got = [links.here(hido, hv), links.here(od, w), links.here(mido, mid)]
        for q in got:
            q.wait()

        def term(r, first):
            return jnp.dot(hv[pl.ds(pl.multiple_of(first + r * 256, 256), 256), :], w[...].reshape(2048, 1024),
                           preferred_element_type=F32)

        def theirs(r):
            sent[block(r, 256), :] = term(r, 512)
        each(2, theirs)
        swap(1)

        def mine(r):
            mid[block(r, 256), :] += term(r, 0)
        each(2, mine)
        swaps[1].wait()

        def total(r):
            out16[r] = (mid[block(r, 128), :] + came[block(r, 128), :]).astype(BF)
        each(4, total)
        read(1)
    pl.run_scoped(output, pltpu.VMEM((1024, 2048), BF), pltpu.VMEM((4, 4, 128, 1024), BF), pltpu.VMEM((512, 1024), F32))

    def attention(dqkv):
        def heads(q, k, v, lse, n1, dka, dva):
            got = [links.here(a, b) for a, b in ((qo, q), (ko, k), (vo, v), (lseo, lse), (n1o, n1))]
            for e in got:
                e.wait()

            def step(t):
                for slot in range(20):
                    if ORDER[8 + slot]:
                        pl.when(t == slot)(lambda slot=slot: comm(8 + slot))
                g, i = t // 5, t % 5

                @pl.when(i < 4)
                def _():
                    attend_back_step(q, k, v, ag, lse, cos, sin, dqkv, dka, dva, g, i)

                @pl.when(i == 4)
                def _():
                    u = rows_dot(n1[...], dqkv[:, pl.ds(pl.multiple_of(g * 384, 128), 384)])
                    gw[g] = u.astype(BF).reshape(4, 2, 4, 32, 384)
            each(20, step)
        pl.run_scoped(heads, *[pltpu.VMEM((1024, 512), BF)] * 3, pltpu.VMEM((8, 1024), F32),
                      pltpu.VMEM((1024, 1024), BF), *[pltpu.VMEM((1024, 128), F32)] * 2)

        def first_norm(w, tokens, mine):
            got = [links.here(oqkv, w), links.here(xh, tokens)]
            comm(28)
            for e in got:
                e.wait()

            def term(r, out, first):
                out[block(r, 256), :] = dot_t(dqkv[pl.ds(pl.multiple_of(first + r * 256, 256), 256), :],
                                              w[...].reshape(1024, 1536))
            each(2, lambda r: term(r, sent, 512))
            swap(2)
            each(2, lambda r: term(r, mine, 0))
            swaps[2].wait()

            def part(r):
                rows = block(r, 128)
                gn = mine[rows, :] + came[rows, :]
                normed, scaling = norm_parts(tokens[r].astype(F32))
                gacc[0:1, :] += jnp.sum(gn * normed, axis=0, keepdims=True)
                gacc[1:2, :] += jnp.sum(gn, axis=0, keepdims=True)
                ig[r] = (mg[rows, :] + norm_back(gn * gv[0:1, :], normed, scaling)).astype(BF)
            each(4, part)
        pl.run_scoped(first_norm, pltpu.VMEM((4, 2, 4, 32, 1536), BF), pltpu.VMEM((4, 128, 1024), BF),
                      pltpu.VMEM((512, 1024), F32))
    pl.run_scoped(attention, pltpu.VMEM((1024, 1536), BF))
    comm(29)
    finals.append(links.here(gacc, fgain).wait)
    for f in finals:
        f()
    links.drain()


def back(*args):
    scratch = []
    for name, index, route in PIECES:
        scratch += reduce_shapes(SHAPES[name])
    return pl.pallas_call(
        back_kernel,
        out_shape=(
            jax.ShapeDtypeStruct((2, 32, 1536), F32),
            jax.ShapeDtypeStruct((2, 32, 4096), F32),
            jax.ShapeDtypeStruct((32, 1024), F32),
            jax.ShapeDtypeStruct((128, 1024), F32),
            jax.ShapeDtypeStruct((8, 1024), F32),
            jax.ShapeDtypeStruct((2, 2, 128, 1024), BF),
            jax.ShapeDtypeStruct((2, 2, 128, 1024), BF),
        ),
        in_specs=[ANY] * 17 + [VM] * 3,
        out_specs=[ANY] * 7,
        scratch_shapes=scratch + [
            pltpu.VMEM((4, 4, 128, 1024), BF),
            pltpu.VMEM((8, 4, 2, 4, 32, 512), BF),
            pltpu.VMEM((4, 4, 32, 1024), BF),
            pltpu.VMEM((4, 4, 2, 4, 32, 384), BF),
            pltpu.VMEM((512, 1024), F32),
            pltpu.VMEM((512, 1024), F32),
            pltpu.VMEM((512, 1024), F32),
            pltpu.VMEM((2, 4, 128, 1024), BF),
            pltpu.VMEM((1024, 512), BF),
            pltpu.VMEM((4, 128, 1024), BF),
            pltpu.VMEM((4, 128, 1024), BF),
            pltpu.VMEM((8, 1024), F32),
            pltpu.VMEM((6, 8, 1024), F32),
            pltpu.SemaphoreType.DMA((192,)),
            pltpu.SemaphoreType.DMA((192,)),
            pltpu.SemaphoreType.DMA((96,)),
            pltpu.SemaphoreType.REGULAR,
        ],
        compiler_params=pltpu.CompilerParams(collective_id=1, has_side_effects=True, vmem_limit_bytes=67043328),
    )(*args)


def finish_kernel(fqkv, fgu, fo, fd, fgain, out_w, ig_w, out, ig, gq, gk, gv, go, gg, gu, gd, *gains):
    for n in (0, 1):
        for g in range(4):
            for j, dst in enumerate((gq, gk, gv)):
                dst[:, pl.ds(128 * (2 * g + n), 128)] = fqkv[n, :, pl.ds(384 * g + 128 * j, 128)]
            for j, dst in enumerate((gg, gu)):
                dst[:, pl.ds(512 * (2 * g + n), 512)] = fgu[n, :, pl.ds(2048 * j + 512 * g, 512)]
    go[...] = fo[...]
    gd[...] = fd[...]

    def rows(i):
        out[i // 2, pl.ds(pl.multiple_of((i % 2) * 128, 128), 128)] = out_w[i // 2, i % 2]
        ig[i // 2, pl.ds(pl.multiple_of((i % 2) * 128, 128), 128)] = ig_w[i // 2, i % 2].astype(F32)
    each(4, rows)
    first = (lax.axis_index("dp") * 4 + lax.axis_index("seq")) * 32
    mine = pltpu.roll(fgain[...], (1024 - first) % 1024, 1)
    for i in range(4):
        gains[i][...] = mine[i:i + 1, 0:32]


def finish(*args):
    S = jax.ShapeDtypeStruct
    return pl.pallas_call(
        finish_kernel,
        out_shape=(S((2, 256, 1024), BF), S((2, 256, 1024), F32)) + (S((32, 1024), F32),) * 4
        + (S((32, 4096), F32),) * 2 + (S((128, 1024), F32),) + (S((1, 32), F32),) * 4,
        in_specs=[VM] * 7,
        out_specs=[VM] * 13,
        compiler_params=pltpu.CompilerParams(vmem_limit_bytes=VMEM_BYTES),
    )(*args)


def angle_tables(c):
    lane = jnp.arange(128, dtype=jnp.int32)
    freqs = 10000.0 ** (-2.0 * (lane % 32).astype(jnp.float32) / HD)
    block = jnp.arange(8, dtype=jnp.int32)
    far = (block % 4) * 256 + jnp.where(block < 4, c, 1 - c) * 128
    rows = jnp.concatenate([jnp.arange(128, dtype=jnp.int32), far]).astype(jnp.float32)
    angle = rows[:, None] * freqs[None, :]
    cos, sin = jnp.cos(angle), jnp.sin(angle)
    return cos, sin


def paired(
    tokens,
    cotangent,
    species_index,
    species_count,
    loss_weight,
    query_weight,
    key_weight,
    value_weight,
    out_weight,
    gate_weight,
    up_weight,
    down_weight,
    mixer_gain,
    mixer_shift,
    feeder_gain,
    feeder_shift,
):
    dp, z = lax.axis_index("dp"), lax.axis_index("seq")
    c = dp % 2
    (wqkv, wgu, wo, wd, xh, cw, gv, norm_one, q, k, v, attended, lse, norm_two, middle, gate, upward, hidden,
     cos, sin) = fore(
        tokens, cotangent, query_weight, key_weight, value_weight, gate_weight, up_weight, out_weight, down_weight,
        mixer_gain.reshape(1, 32), mixer_shift.reshape(1, 32), feeder_gain.reshape(1, 32), feeder_shift.reshape(1, 32),
        species_index, species_count, loss_weight, *angle_tables(c))
    parts = back(
        cw, hidden, wd, norm_two, gate, upward, wgu, middle, wo, attended, q, k, v, lse, norm_one, wqkv, xh,
        cos, sin, gv)
    done = finish(*parts)
    return done[:9] + tuple(g.reshape(32) for g in done[9:])


def matmul(left, right):
    return jnp.dot(left, right, preferred_element_type=jnp.float32)


def weight_term(left, right):
    return lax.dot_general(
        left, right, (((0,), (0,)), ((), ())), preferred_element_type=jnp.float32
    )


def through(left, weight):
    return lax.dot_general(
        left, weight, (((1,), (1,)), ((), ())), preferred_element_type=jnp.float32
    )


def normalize(values):
    center = jnp.mean(values, axis=-1, keepdims=True)
    centered = values - center
    variance = jnp.mean(centered * centered, axis=-1, keepdims=True)
    scaling = lax.rsqrt(variance + 1e-05)
    return (centered * scaling, scaling)


def plain_norm_back(upstream, normed, scaling):
    first = jnp.mean(upstream, axis=-1, keepdims=True)
    second = jnp.mean(upstream * normed, axis=-1, keepdims=True)
    return scaling * (upstream - first - normed * second)


def tables(start, count):
    half = HD // 2
    positions = (start + jnp.arange(count, dtype=jnp.int32)).astype(jnp.float32)
    freqs = 10000.0 ** (-2.0 * jnp.arange(half, dtype=jnp.float32) / HD)
    angle = positions[:, None] * freqs[None, :]
    return (jnp.cos(angle)[:, None, :], jnp.sin(angle)[:, None, :])


def rotate(values, cosine, sine):
    half = HD // 2
    first = values[..., :half]
    second = values[..., half:]
    return jnp.concatenate(
        [first * cosine - second * sine, second * cosine + first * sine], axis=-1
    )


def attend_head(operands):
    query_head, key_head, value_head = operands
    scores = jnp.einsum(
        "wtd,wsd->wts", query_head, key_head, preferred_element_type=jnp.float32
    ) * HD ** (-0.5)
    peak = jnp.max(scores, axis=-1, keepdims=True)
    raised = jnp.exp(scores - peak)
    total = jnp.sum(raised, axis=-1, keepdims=True)
    probs = (raised / total).astype(jnp.bfloat16)
    result = jnp.einsum("wts,wsd->wtd", probs, value_head, preferred_element_type=jnp.float32)
    return (result, (peak + jnp.log(total))[..., 0])


def head_back(operands):
    query_head, key_head, value_head, upstream, log_total = operands
    scores = jnp.einsum(
        "wtd,wsd->wts", query_head, key_head, preferred_element_type=jnp.float32
    ) * HD ** (-0.5)
    probs = jnp.exp(scores - log_total[..., None])
    prob_grads = jnp.einsum(
        "wtd,wsd->wts", upstream, value_head, preferred_element_type=jnp.float32
    )
    inner = jnp.sum(probs * prob_grads, axis=-1, keepdims=True)
    score_grads = (probs * (prob_grads - inner)).astype(jnp.bfloat16)
    query_grad = jnp.einsum(
        "wts,wsd->wtd", score_grads, key_head, preferred_element_type=jnp.float32
    ) * HD ** (-0.5)
    key_grad = jnp.einsum(
        "wts,wtd->wsd", score_grads, query_head, preferred_element_type=jnp.float32
    ) * HD ** (-0.5)
    value_grad = jnp.einsum(
        "wts,wtd->wsd", probs.astype(jnp.bfloat16), upstream, preferred_element_type=jnp.float32
    )
    return (query_grad, key_grad, value_grad)


def general(
    tokens,
    cotangent,
    species_index,
    species_count,
    loss_weight,
    query_weight,
    key_weight,
    value_weight,
    out_weight,
    gate_weight,
    up_weight,
    down_weight,
    mixer_gain,
    mixer_shift,
    feeder_gain,
    feeder_shift,
):
    gathered = (
        lax.all_gather(query_weight, ("dp", "seq"), axis=0, tiled=True),
        lax.all_gather(key_weight, ("dp", "seq"), axis=0, tiled=True),
        lax.all_gather(value_weight, ("dp", "seq"), axis=0, tiled=True),
        lax.all_gather(out_weight, ("dp", "seq"), axis=0, tiled=True),
        lax.all_gather(gate_weight, ("dp", "seq"), axis=0, tiled=True),
        lax.all_gather(up_weight, ("dp", "seq"), axis=0, tiled=True),
        lax.all_gather(down_weight, ("dp", "seq"), axis=0, tiled=True),
        lax.all_gather(mixer_gain, ("dp", "seq"), axis=0, tiled=True),
        lax.all_gather(mixer_shift, ("dp", "seq"), axis=0, tiled=True),
        lax.all_gather(feeder_gain, ("dp", "seq"), axis=0, tiled=True),
        lax.all_gather(feeder_shift, ("dp", "seq"), axis=0, tiled=True),
    )
    wq, wk, wv, wo, wg, wu, wd, gain_one, shift_one, gain_two, shift_two = gathered
    windows, steps_dev, width = tokens.shape
    rows = windows * steps_dev
    start = lax.axis_index("seq") * steps_dev
    cosine, sine = tables(start, steps_dev)
    inputs = tokens.astype(jnp.float32).reshape(rows, width)
    normed_one, scaling_one = normalize(inputs)
    norm_one = (normed_one * gain_one.astype(jnp.float32) + shift_one.astype(jnp.float32)).astype(
        jnp.bfloat16
    )
    queries = rotate(
        matmul(norm_one, wq).reshape(windows, steps_dev, HEADS, HD), cosine, sine
    ).astype(jnp.bfloat16)
    keys = rotate(matmul(norm_one, wk).reshape(windows, steps_dev, HEADS, HD), cosine, sine).astype(
        jnp.bfloat16
    )
    values = matmul(norm_one, wv).astype(jnp.bfloat16)
    all_keys, all_values = (
        lax.all_gather(keys.reshape(windows, steps_dev, width), "seq", axis=1, tiled=True),
        lax.all_gather(values.reshape(windows, steps_dev, width), "seq", axis=1, tiled=True),
    )
    length = all_keys.shape[1]
    query_heads = queries.transpose(2, 0, 1, 3)
    key_heads = all_keys.reshape(windows, length, HEADS, HD).transpose(2, 0, 1, 3)
    value_heads = all_values.reshape(windows, length, HEADS, HD).transpose(2, 0, 1, 3)
    head_results, log_totals = lax.map(attend_head, (query_heads, key_heads, value_heads))
    attended = head_results.transpose(1, 2, 0, 3).reshape(rows, width).astype(jnp.bfloat16)
    middle = inputs + matmul(attended, wo)
    normed_two, scaling_two = normalize(middle)
    norm_two = (normed_two * gain_two.astype(jnp.float32) + shift_two.astype(jnp.float32)).astype(
        jnp.bfloat16
    )
    gate = matmul(norm_two, wg)
    upward = matmul(norm_two, wu)
    sigma = jax.nn.sigmoid(gate)
    swish = gate * sigma
    hidden = (swish * upward).astype(jnp.bfloat16)
    output = (middle + matmul(hidden, wd)).astype(jnp.bfloat16).reshape(windows, steps_dev, width)
    table = loss_weight * lax.rsqrt(species_count.astype(jnp.float32) / 400.0)
    picks = species_index[:, None] == jnp.arange(table.shape[0], dtype=jnp.int32)[None, :]
    factor = jnp.sum(jnp.where(picks, table[None, :], 0.0), axis=1)
    grad_out = (factor[:, None, None] * cotangent.astype(jnp.float32)).reshape(rows, width)
    regathered = (
        lax.all_gather(query_weight, ("dp", "seq"), axis=0, tiled=True),
        lax.all_gather(key_weight, ("dp", "seq"), axis=0, tiled=True),
        lax.all_gather(value_weight, ("dp", "seq"), axis=0, tiled=True),
        lax.all_gather(out_weight, ("dp", "seq"), axis=0, tiled=True),
        lax.all_gather(gate_weight, ("dp", "seq"), axis=0, tiled=True),
        lax.all_gather(up_weight, ("dp", "seq"), axis=0, tiled=True),
        lax.all_gather(down_weight, ("dp", "seq"), axis=0, tiled=True),
        lax.all_gather(mixer_gain, ("dp", "seq"), axis=0, tiled=True),
        lax.all_gather(mixer_shift, ("dp", "seq"), axis=0, tiled=True),
        lax.all_gather(feeder_gain, ("dp", "seq"), axis=0, tiled=True),
        lax.all_gather(feeder_shift, ("dp", "seq"), axis=0, tiled=True),
    )
    wq, wk, wv, wo, wg, wu, wd, gain_one, shift_one, gain_two, shift_two = regathered
    out_low = grad_out.astype(jnp.bfloat16)
    down_part = weight_term(hidden, out_low)
    hidden_grad = through(out_low, wd)
    gate_grad = (hidden_grad * upward * sigma * (1.0 + gate * (1.0 - sigma))).astype(jnp.bfloat16)
    upward_grad = (hidden_grad * swish).astype(jnp.bfloat16)
    gate_part = weight_term(norm_two, gate_grad)
    upward_part = weight_term(norm_two, upward_grad)
    norm_two_grad = through(gate_grad, wg) + through(upward_grad, wu)
    feeder_gain_part = jnp.sum(norm_two_grad * normed_two, axis=0)
    feeder_shift_part = jnp.sum(norm_two_grad, axis=0)
    middle_grad = grad_out + plain_norm_back(
        norm_two_grad * gain_two.astype(jnp.float32), normed_two, scaling_two
    )
    middle_low = middle_grad.astype(jnp.bfloat16)
    out_part = weight_term(attended, middle_low)
    attended_grad = through(middle_low, wo).astype(jnp.bfloat16)
    upstream_heads = attended_grad.reshape(windows, steps_dev, HEADS, HD).transpose(2, 0, 1, 3)
    query_heads_grad, key_heads_grad, value_heads_grad = lax.map(
        head_back, (query_heads, key_heads, value_heads, upstream_heads, log_totals)
    )
    key_whole = key_heads_grad.transpose(1, 2, 0, 3).reshape(windows, length, width)
    value_whole = value_heads_grad.transpose(1, 2, 0, 3).reshape(windows, length, width)
    key_mine, value_mine = (
        lax.psum_scatter(
            key_whole.astype(jnp.bfloat16), "seq", scatter_dimension=1, tiled=True
        ).astype(jnp.float32),
        lax.psum_scatter(
            value_whole.astype(jnp.bfloat16), "seq", scatter_dimension=1, tiled=True
        ).astype(jnp.float32),
    )
    query_lin_grad = (
        rotate(query_heads_grad.transpose(1, 2, 0, 3), cosine, -sine)
        .reshape(rows, width)
        .astype(jnp.bfloat16)
    )
    key_lin_grad = (
        rotate(key_mine.reshape(windows, steps_dev, HEADS, HD), cosine, -sine)
        .reshape(rows, width)
        .astype(jnp.bfloat16)
    )
    value_lin_grad = value_mine.reshape(rows, width).astype(jnp.bfloat16)
    query_part = weight_term(norm_one, query_lin_grad)
    key_part = weight_term(norm_one, key_lin_grad)
    value_part = weight_term(norm_one, value_lin_grad)
    norm_one_grad = (
        through(query_lin_grad, wq) + through(key_lin_grad, wk) + through(value_lin_grad, wv)
    )
    mixer_gain_part = jnp.sum(norm_one_grad * normed_one, axis=0)
    mixer_shift_part = jnp.sum(norm_one_grad, axis=0)
    input_grad = middle_grad + plain_norm_back(
        norm_one_grad * gain_one.astype(jnp.float32), normed_one, scaling_one
    )
    summed = (
        lax.psum_scatter(query_part, ("dp", "seq"), scatter_dimension=0, tiled=True),
        lax.psum_scatter(key_part, ("dp", "seq"), scatter_dimension=0, tiled=True),
        lax.psum_scatter(value_part, ("dp", "seq"), scatter_dimension=0, tiled=True),
        lax.psum_scatter(out_part, ("dp", "seq"), scatter_dimension=0, tiled=True),
        lax.psum_scatter(gate_part, ("dp", "seq"), scatter_dimension=0, tiled=True),
        lax.psum_scatter(upward_part, ("dp", "seq"), scatter_dimension=0, tiled=True),
        lax.psum_scatter(down_part, ("dp", "seq"), scatter_dimension=0, tiled=True),
        lax.psum_scatter(mixer_gain_part, ("dp", "seq"), scatter_dimension=0, tiled=True),
        lax.psum_scatter(mixer_shift_part, ("dp", "seq"), scatter_dimension=0, tiled=True),
        lax.psum_scatter(feeder_gain_part, ("dp", "seq"), scatter_dimension=0, tiled=True),
        lax.psum_scatter(feeder_shift_part, ("dp", "seq"), scatter_dimension=0, tiled=True),
    )
    return (
        output,
        input_grad.reshape(windows, steps_dev, width),
        summed[0],
        summed[1],
        summed[2],
        summed[3],
        summed[4],
        summed[5],
        summed[6],
        summed[7],
        summed[8],
        summed[9],
        summed[10],
    )


def solution(mesh):
    in_specs = (
        P("dp", "seq", None),
        P("dp", "seq", None),
        P("dp"),
        P(),
        P(),
    ) + (P(("dp", "seq"), None),) * 7 + (P(("dp", "seq")),) * 4
    out_specs = (P("dp", "seq", None),) * 2 + (P(("dp", "seq"), None),) * 7 + (P(("dp", "seq")),) * 4
    fits = mesh.shape["dp"] == 8 and mesh.shape["seq"] == 4
    return jax.shard_map(
        paired if fits else general, mesh=mesh, in_specs=in_specs, out_specs=out_specs, check_vma=False
    )
```

```python
import jax
import jax.numpy as jnp
from jax import lax
from jax.experimental import pallas as pl
from jax.experimental.pallas import tpu as pltpu
from jax.sharding import PartitionSpec as P

HEADS = 16
HD = 64
MESH = pl.DeviceIdType.MESH
BF = jnp.bfloat16
F32 = jnp.float32
ANY = pl.BlockSpec(memory_space=pl.ANY)
VM = pl.BlockSpec(memory_space=pltpu.VMEM)
VMEM_BYTES = 60 << 20


def place():
    dp, z = lax.axis_index("dp"), lax.axis_index("seq")
    return dp // 4, (dp // 2) % 2, dp % 2, z


def dev(y, x, c, z):
    return ((y * 2 + x) * 2 + c, z)


def both(a, b):
    return jnp.logical_and(a, b)


def greet(y, x, c, z):
    barrier = pltpu.get_barrier_semaphore()
    peers = [dev(y, 1 - x, c, z), dev(1 - y, x, c, z), dev(y, x, 1 - c, z)]
    for k in (1, 2, 3):
        peers += [dev(y, x, c, (z + k) % 4), dev(y, x, 1 - c, (z + k) % 4)]
    for p in peers:
        pl.semaphore_signal(barrier, inc=1, device_id=p, device_id_type=MESH)
    return lambda: pl.semaphore_wait(barrier, len(peers))


class Links:
    def __init__(self, send, recv, local):
        self.send, self.recv, self.local = send, recv, local
        self.n = 0
        self.m = 0
        self.open = []

    def take(self, count):
        self.n += count
        return self.n - count

    def copy(self, src, dst, device, send, recv):
        return pltpu.make_async_remote_copy(
            src_ref=src, dst_ref=dst, send_sem=self.send.at[send], recv_sem=self.recv.at[recv],
            device_id=device, device_id_type=MESH)

    def go(self, c, ok=None):
        if ok is None:
            c.start()
        else:
            pl.when(ok)(c.start)
        self.open.append((c, ok))
        return c

    def to(self, src, dst, device):
        i = self.take(1)
        return self.go(self.copy(src, dst, device, i, i))

    def later(self, src, dst, device):
        i = self.take(1)
        c = self.copy(src, dst, device, i, i)
        self.open.append((c, None))
        return c

    def here_later(self, src, dst):
        self.m += 1
        return pltpu.make_async_copy(src, dst, self.local.at[self.m - 1])

    def wanted(self, src, dst, device):
        i = self.take(1)
        return self.copy(src, dst, device, i, i)

    def here(self, src, dst):
        self.m += 1
        c = pltpu.make_async_copy(src, dst, self.local.at[self.m - 1])
        c.start()
        return c

    def drain(self):
        for c, ok in self.open:
            if ok is None:
                c.wait_send()
            else:
                pl.when(ok)(c.wait_send)
        self.open = []


def at_z(ref, zz):
    return ref.at[zz] if len(ref.shape) == 3 else ref.at[:, zz]


def pair_of(ref, first):
    return ref.at[pl.ds(first, 2)] if len(ref.shape) == 3 else ref.at[:, pl.ds(first, 2)]


def add_into(dst, *terms):
    def body(i, _):
        total = at_z(terms[0], i)[...]
        for t in terms[1:]:
            total += at_z(t, i)[...]
        at_z(dst, i)[...] = total
        return 0
    lax.fori_loop(0, dst.shape[-3], body, 0)


def reduce_shapes(piece):
    part = piece[:-3] + piece[-2:]
    two = piece[:-3] + (2,) + piece[-2:]
    return [pltpu.VMEM((2,) + piece, BF), pltpu.VMEM(piece, BF), pltpu.VMEM(two, BF), pltpu.VMEM(two, BF),
            pltpu.VMEM(part, BF), pltpu.VMEM(part, F32)]


def collect(links, at, me, route, bufs, deliver):
    y, x, c, z = me
    to_x, to_y = dev(y, 1 - x, c, z), dev(1 - y, x, c, z)
    got, third, from_outer, from_inner, from_near, total = bufs
    out = deliver(total)
    if route == 0:
        own, away = [at(1 - y, x), at(y, x)], [at(1 - y, 1 - x), at(y, 1 - x)]
        one, two = to_x, to_y
    else:
        own, away = [at(y, 1 - x), at(y, x)], [at(1 - y, 1 - x), at(1 - y, x)]
        one, two = to_y, to_x
    near = z + 1 - 2 * (z % 2)
    inner = both(z > 0, z < 3)
    outer = jnp.logical_not(inner)
    far_side, near_side = pair_of(own[1], 2 - 2 * (z // 2)), pair_of(own[1], 2 * (z // 2))
    give = [links.later(away[n], got.at[n], one) for n in (0, 1)]
    cross = links.later(own[0], third, two)
    inward = links.wanted(far_side, from_outer, dev(y, x, c, near))
    over = links.wanted(far_side, from_inner, dev(y, x, c, 3 - z))
    links.open += [(inward, outer), (over, inner)]
    settle = links.later(at_z(own[1], near), from_near, dev(y, x, c, near))

    def start():
        for q in give:
            q.start()

    def first():
        give[0].wait_recv()
        add_into(own[0], own[0], got.at[0])
        cross.start()

    def second():
        give[1].wait_recv()
        cross.wait_recv()
        add_into(own[1], own[1], got.at[1], third)

        @pl.when(outer)
        def _():
            inward.start()
            settle.start()

    def inside():
        @pl.when(inner)
        def _():
            inward.wait_recv()
            add_into(far_side, far_side, from_outer)
            over.start()

    def across():
        @pl.when(inner)
        def _():
            over.wait_recv()
            add_into(near_side, near_side, from_inner)
            settle.start()

    def last():
        settle.wait_recv()
        total[...] = at_z(own[1], z)[...].astype(F32) + from_near[...].astype(F32)
        for q in out:
            q.start()
    return start, first, second, inside, across, last


class Outgoing:
    def __init__(self, links, me, src, dst):
        y, x, c, z = me
        recv, send = links.take(4), links.take(4)
        self.here, self.away = c == z // 2, c != z // 2
        self.remote, self.back = [], []
        for k in range(4):
            zz = (z + k) % 4
            s, d = src.at[zz], dst.at[z % 2, c]
            self.remote.append(links.copy(s, d, dev(y, x, z // 2, zz), send + k, recv + (z % 2) * 2 + c))
            links.open.append((self.remote[k], None if k else self.away))
            if k == 0:
                self.local = links.here_later(s, d)
        for i in (0, 1):
            for h in (0, 1):
                d = dst.at[i, h]
                mine = both(z == 2 * c + i, h == c)
                self.back.append((links.copy(d, d, dev(y, x, 1 - c, z), send, recv + 2 * i + h), jnp.logical_not(mine)))

    def start(self):
        for q in self.remote[1:]:
            q.start()
        pl.when(self.away)(self.remote[0].start)
        pl.when(self.here)(self.local.start)

    def finish(self):
        pl.when(self.here)(self.local.wait)
        for q, ok in self.back:
            pl.when(ok)(q.wait_recv)


def swap_halves(u):
    lane = lax.broadcasted_iota(jnp.int32, u.shape, 1) % HD
    return jnp.where(lane < HD // 2, pltpu.roll(u, 128 - HD // 2, 1), pltpu.roll(u, HD // 2, 1))


def head_mask(shape, h):
    lane = lax.broadcasted_iota(jnp.int32, shape, 1)
    return (lane < HD) if h == 0 else (lane >= HD)


def dot_t(a, b):
    return lax.dot_general(a, b, (((1,), (1,)), ((), ())), preferred_element_type=F32)


def project_step(xw, gv, w, cos, sin, n1, q, k, v, r):
    rows = pl.ds(pl.multiple_of(r * 256, 256), 256)
    u = xw[r // 2, pl.ds((r % 2) * 2, 2)].reshape(256, 1024).astype(F32)
    d = u - jnp.mean(u, axis=-1, keepdims=True)
    scaling = lax.rsqrt(jnp.mean(d * d, axis=-1, keepdims=True) + 1e-05)
    n = (d * scaling * gv[0:1, :] + gv[1:2, :]).astype(BF)
    n1[rows, :] = n
    for g in range(4):
        lanes = pl.ds(128 * g, 128)
        t = jnp.dot(n, w[:, :, :, :, pl.ds(384 * g, 384)].reshape(1024, 384), preferred_element_type=F32)
        for j, o in ((0, q), (1, k)):
            s = t[:, 128 * j:128 * j + 128]
            o[rows, lanes] = (s * cos[rows, :] + swap_halves(s) * sin[rows, :]).astype(BF)
        v[rows, lanes] = t[:, 256:].astype(BF)


def attend_step(q, k, v, o, lse, g, i):
    lanes = pl.ds(pl.multiple_of(g * 128, 128), 128)
    rows = pl.ds(pl.multiple_of(i * 256, 256), 256)
    qs = q[rows, lanes] * jnp.asarray(HD ** -0.5, BF)
    kk, vv = k[:, lanes], v[:, lanes]
    outs, logs = [], []
    for h in (0, 1):
        qh = jnp.where(head_mask(qs.shape, h), qs, jnp.zeros_like(qs))
        s = dot_t(qh, kk)
        m = jnp.max(s, axis=-1, keepdims=True)
        e = jnp.exp(s - m)
        t = jnp.sum(e, axis=-1, keepdims=True)
        p = (e * (1.0 / t)).astype(BF)
        outs.append(jnp.dot(p, vv, preferred_element_type=F32))
        logs.append(jnp.broadcast_to(m + jnp.log(t), qs.shape))
    keep = head_mask(qs.shape, 0)
    o[rows, lanes] = jnp.where(keep, outs[0], outs[1]).astype(BF)
    t = jnp.transpose(jnp.where(keep, logs[0], logs[1]))
    lse[pl.ds(2 * g, 1), rows] = t[0:1]
    lse[pl.ds(2 * g + 1, 1), rows] = t[HD:HD + 1]


def attend_back_step(q, k, v, do, lse, cos, sin, dqkv, dka, dva, g, i):
    lanes = pl.ds(pl.multiple_of(g * 128, 128), 128)
    rows = pl.ds(pl.multiple_of(i * 256, 256), 256)

    @pl.when(i == 0)
    def _():
        dka[...] = jnp.zeros_like(dka)
        dva[...] = jnp.zeros_like(dva)
    kk, vv, go = k[:, lanes], v[:, lanes], do[rows, lanes]
    qs = q[rows, lanes] * jnp.asarray(HD ** -0.5, BF)
    logs = lse[pl.ds(2 * g, 1), rows], lse[pl.ds(2 * g + 1, 1), rows]
    dks, dvs, dqs = [], [], []
    for h in (0, 1):
        keep = head_mask(kk.shape, h)
        zero = jnp.zeros_like(kk)
        s = dot_t(jnp.where(keep, kk, zero), qs)
        p = jnp.exp(s - logs[h])
        dp = dot_t(jnp.where(keep, vv, zero), go)
        pd = p * dp
        ds = (pd - p * jnp.sum(pd, axis=0, keepdims=True)).astype(BF)
        dvs.append(jnp.dot(p.astype(BF), go, preferred_element_type=F32))
        dks.append(jnp.dot(ds, qs, preferred_element_type=F32))
        dqs.append(lax.dot_general(ds, kk, (((0,), (0,)), ((), ())), preferred_element_type=F32))
    keep = head_mask(kk.shape, 0)
    dka[...] += jnp.where(keep, dks[0], dks[1])
    dva[...] += jnp.where(keep, dvs[0], dvs[1])
    u = jnp.where(head_mask(go.shape, 0), dqs[0], dqs[1]) * HD ** -0.5
    dqkv[rows, pl.ds(pl.multiple_of(g * 384, 128), 128)] = (
        u * cos[rows, :] - swap_halves(u) * sin[rows, :]).astype(BF)

    @pl.when(i == 3)
    def _():
        u = dka[...]
        dqkv[:, pl.ds(pl.multiple_of(128 + g * 384, 128), 128)] = (
            u * cos[...] - swap_halves(u) * sin[...]).astype(BF)
        dqkv[:, pl.ds(pl.multiple_of(256 + g * 384, 128), 128)] = dva[...].astype(BF)


class Incoming:
    def __init__(self, links, me, src, mid, dst):
        y, x, c, z = me
        partner = dev(y, x, 1 - c, z)
        self.swap = [links.later(src.at[i, pl.ds((1 - c) * 128, 128)], mid.at[2 * c + i], partner) for i in (0, 1)]
        send, recv = links.take(4), links.take(4)
        self.sends, self.kept, self.got = [], [], []
        m = links.m
        links.m += 1
        for w in range(4):
            d = dst.at[0, z]
            for ok, s in ((c == w // 2, src.at[w % 2, pl.ds(c * 128, 128)]), (c != w // 2, mid.at[w])):
                away, here = both(ok, z != w), both(ok, z == w)
                q = links.copy(s, d, dev(y, x, c, w), send + w, recv + z)
                self.sends.append((q, away))
                links.open.append((q, away))
                self.kept.append((pltpu.make_async_copy(s, d, links.local.at[m]), here))
        for zz in range(4):
            d = dst.at[0, zz]
            self.got.append((links.copy(d, d, dev(y, x, c, zz), send, recv + zz), z != zz))
        self.pair = links.later(dst.at[0], dst.at[1], partner)

    def begin(self):
        for q in self.swap:
            q.start()

    def send(self):
        for q in self.swap:
            q.wait_recv()
        for q, ok in self.sends + self.kept:
            pl.when(ok)(q.start)

    def arrive(self):
        for q, ok in self.kept:
            pl.when(ok)(q.wait)
        for q, ok in self.got:
            pl.when(ok)(q.wait_recv)
        self.pair.start()

    def finish(self):
        self.pair.wait_recv()


def disperse(links, single, bundle, me, route):
    y, x, c, z = me
    to_x, to_y = dev(y, 1 - x, c, z), dev(1 - y, x, c, z)
    mine = y * 2 + x
    if route == 0:
        two, three, other = to_y, to_x, (1 - y) * 2 + x
    else:
        two, three, other = to_x, to_y, y * 2 + 1 - x
    over_z = [links.later(single(mine, z), single(mine, z), dev(y, x, c, (z + k) % 4)) for k in (1, 2, 3)]
    cross = links.later(bundle(mine), bundle(mine), two)
    last = [links.later(bundle(mine), bundle(mine), three), links.later(bundle(other), bundle(other), three)]

    def start():
        for q in over_z:
            q.start()

    def first():
        for q in over_z:
            q.wait_recv()
        cross.start()
        last[0].start()

    def second():
        cross.wait_recv()
        last[1].start()

    def finish():
        for q in last:
            q.wait_recv()
    return start, first, second, finish


FORE_PIECES = (
    ("gu", 6, 1),
    ("qkv", 0, 1),
    ("gu", 7, 0),
    ("o", 0, 0),
    ("gu", 1, 0),
    ("gu", 0, 1),
    ("qkv", 1, 1),
    ("gu", 2, 0),
    ("gu", 5, 0),
    ("d", 3, 0),
    ("gu", 4, 1),
    ("d", 0, 1),
    ("gu", 3, 1),
    ("d", 2, 1),
    ("d", 1, 0),
)
FORE_ORDER = (
    ((17, 0), (0, 0), (1, 0), (2, 0), (3, 0), (4, 0), (5, 0), (6, 0), (15, 0), (7, 0), (8, 0), (9, 0), (10, 0),
     (11, 0), (12, 0), (13, 0), (14, 0), (17, 1), (17, 2), (17, 3), (0, 1), (0, 2), (1, 1), (0, 3), (2, 1), (1, 2),
     (3, 1), (4, 1), (2, 2), (5, 1), (1, 3), (6, 1), (3, 2), (2, 3), (4, 2), (5, 2), (6, 2), (3, 3), (5, 3),
     (4, 3), (15, 1), (7, 1), (6, 3), (15, 2),),
    ((7, 2), (8, 1), (9, 1)), (), ((10, 1),), (), (), ((7, 3), (8, 2), (11, 1)), (), (), (), ((9, 2), (12, 1)), (),
    (), (), ((13, 1),), (), (), ((10, 2), (14, 1), (16, 0)), ((8, 3), (11, 2), (9, 3), (10, 3)), ((12, 2), (14, 2)),
    ((11, 3), (13, 2)), ((16, 1), (12, 3)), ((13, 3), (14, 3), (16, 2)),
)


def rotary_tables(tab_cos, tab_sin, cos, sin):
    lane = lax.broadcasted_iota(jnp.int32, (128, 128), 1)
    sign = jnp.where(lane % HD < HD // 2, -1.0, 1.0)
    for i in range(8):
        a, b = tab_cos[128 + i:129 + i, :], tab_sin[128 + i:129 + i, :]
        cos[128 * i:128 * i + 128, :] = tab_cos[0:128, :] * a - tab_sin[0:128, :] * b
        sin[128 * i:128 * i + 128, :] = sign * (tab_sin[0:128, :] * a + tab_cos[0:128, :] * b)


def fore_kernel(tok, cot, wq, wk, wv, wg, wu, wo, wd, g0, g1, g2, g3, species, count, weight,
                tab_cos, tab_sin, *rest):
    (oqkv, ogu, oo, od, xh, cw, gvo, n1o, qo, ko, vo, atto, lseo, n2o, mido, gateo, upo, hido, coso, sino,
     own_qkv, oth_qkv, own_gu, oth_gu, gp, cos, sin,
     tmid, cmid, gains, gv, xw, w3, n1, q, k, v, att, lse, wos, sent, came, mid, n2, wgs, wus,
     gate, up, hid, send, recv, local) = rest
    me = y, x, c, z = place()
    yx = y * 2 + x
    partner = dev(y, x, 1 - c, z)

    def prepare():
        def columns(src, own, oth, width, base, stride):
            for g in range(4):
                lanes = pl.ds(base + stride * g, width)
                own[:, lanes] = src[:, pl.ds(pl.multiple_of((2 * g + c) * width, width), width)]
                oth[:, lanes] = src[:, pl.ds(pl.multiple_of((2 * g + 1 - c) * width, width), width)]
        for j, src in enumerate((wq, wk, wv)):
            columns(src, own_qkv, oth_qkv, 128, 128 * j, 384)
        for j, src in enumerate((wg, wu)):
            columns(src, own_gu, oth_gu, 512, 2048 * j, 512)
        gp[...] = jnp.zeros_like(gp)
        for i, src in enumerate((g0, g1, g2, g3)):
            gp[i:i + 1, 0:32] = src[...].astype(F32)
        gp[...] = pltpu.roll(gp[...], z * 32, 1)
        lane = lax.broadcasted_iota(jnp.int32, (1, 128), 1)
        row = jnp.zeros((1, 128), F32)
        for i in (0, 1):
            n = jnp.full((1, 128), count[species[i]].astype(F32), F32)
            row = jnp.where(lane == i, weight[species[i]] * lax.rsqrt(n / 400.0), row)
        gp[4:5, :] = jnp.where(z == 0, row, jnp.zeros_like(row))
    met = greet(y, x, c, z)
    prepare()
    met()
    links = Links(send, recv, local)
    tin, cin = Incoming(links, me, tok, tmid, xw), Incoming(links, me, cot, cmid, cw)
    tin.begin()
    swaps = [links.to(gp, gains.at[yx, c, z], partner), links.to(oth_qkv, oqkv.at[yx, c, z], partner),
             links.to(oth_gu, ogu.at[yx, c, z], partner)]
    loc = [links.here(gp, gains.at[yx, c, z]), links.here(own_qkv, oqkv.at[yx, c, z]),
           links.here(own_gu, ogu.at[yx, c, z]), links.here(wo, oo.at[yx, z]), links.here(wd, od.at[yx, z])]
    work = []
    for name, index, route in FORE_PIECES:
        if name in ("qkv", "gu"):
            arr, cols = (oqkv, 768) if name == "qkv" else (ogu, 512)
            lanes = pl.ds(index * cols, cols)
            work.append(disperse(links, lambda i, zz, arr=arr, lanes=lanes: arr.at[i, :, zz, :, lanes],
                                 lambda i, arr=arr, lanes=lanes: arr.at[i, :, :, :, lanes], me, route))
        else:
            arr = oo if name == "o" else od
            rows = pl.ds(index * 32, 32)
            work.append(disperse(links, lambda i, zz, arr=arr, rows=rows: arr.at[i, zz, rows],
                                 lambda i, arr=arr, rows=rows: arr.at[i, :, rows], me, route))

    def later():
        cin.begin()
        cin.send()
    work += [(tin.send, tin.arrive, tin.finish), (later, cin.arrive, cin.finish),
             disperse(links, lambda i, zz: gains.at[i, :, zz], lambda i: gains.at[i], me, 1)]
    swap = links.wanted(sent, came, partner)
    share = links.later(n2.at[pl.ds(0, 512)], n2.at[pl.ds(512, 512)], partner)
    for e in loc:
        e.wait()
    for e in swaps:
        e.wait_recv()

    def comm(slot):
        for i, stage in FORE_ORDER[slot]:
            work[i][stage]()

    keep = []

    def put(src, dst):
        keep.append(links.here(src, dst))
    comm(0)
    wload = links.here(oqkv, w3)
    rotary_tables(tab_cos, tab_sin, cos, sin)
    put(cos, coso)
    put(sin, sino)
    wload.wait()
    for i in range(4):
        for j in (0, 1):
            gv[:, pl.ds((2 * i + j) * 128, 128)] = (gains[i, j, 0] + gains[i, j, 1]) + (gains[i, j, 2] + gains[i, j, 3])

    def rows_of(step):
        lax.fori_loop(0, 4, lambda r, _: (step(r), 0)[1], 0)
    rows_of(lambda r: project_step(xw, gv, w3, cos, sin, n1, q, k, v, r))
    for a, b in ((gv, gvo), (n1, n1o), (q, qo), (k, ko), (v, vo), (xw.at[0], xh)):
        put(a, b)
    comm(1)

    def step(t, _):
        attend_step(q, k, v, att, lse, t // 4, t % 4)
        for slot in range(2, 17):
            if FORE_ORDER[slot]:
                pl.when(t == slot - 2)(lambda slot=slot: comm(slot))
        return 0
    lax.fori_loop(0, 16, step, 0)
    comm(17)
    wload = links.here(oo, wos)
    put(att, atto)
    put(lse, lseo)
    wload.wait()

    def terms(r, out, first):
        rows = pl.ds(pl.multiple_of(r * 256, 256), 256)
        out[rows, :] = jnp.dot(att[pl.ds(pl.multiple_of(first + r * 256, 256), 256), :], wos[...].reshape(512, 1024),
                               preferred_element_type=F32)
    lax.fori_loop(0, 2, lambda r, _: (terms(r, sent, 512), 0)[1], 0)
    swap.start()
    lax.fori_loop(0, 2, lambda r, _: (terms(r, mid, 0), 0)[1], 0)
    swap.wait()

    def second_norm(r):
        rows = pl.ds(pl.multiple_of(r * 128, 128), 128)
        u = xw[0, r].astype(F32) + (mid[rows, :] + came[rows, :])
        mid[rows, :] = u
        d = u - jnp.mean(u, axis=-1, keepdims=True)
        scaling = lax.rsqrt(jnp.mean(d * d, axis=-1, keepdims=True) + 1e-05)
        n2[rows, :] = (d * scaling * gv[2:3, :] + gv[3:4, :]).astype(BF)
    rows_of(second_norm)
    share.start()
    put(mid, mido)
    comm(18)
    share.wait_recv()
    put(n2, n2o)
    for j in range(4):
        if j:
            comm(18 + j)
        lanes = pl.ds(512 * j, 512)
        lg = links.here(ogu.at[:, :, :, :, lanes], wgs)
        lu = links.here(ogu.at[:, :, :, :, pl.ds(2048 + 512 * j, 512)], wus)
        lg.wait()
        lu.wait()

        def hidden_units(r, lanes=lanes):
            rows = pl.ds(pl.multiple_of(r * 256, 256), 256)
            n = n2[rows, :]
            a = jnp.dot(n, wgs[...].reshape(1024, 512), preferred_element_type=F32)
            b = jnp.dot(n, wus[...].reshape(1024, 512), preferred_element_type=F32)
            hid[rows, lanes] = (a * jax.nn.sigmoid(a) * b).astype(BF)
            gate[rows, lanes] = a.astype(BF)
            up[rows, lanes] = b.astype(BF)
        rows_of(hidden_units)
        for a, b in ((hid, hido), (gate, gateo), (up, upo)):
            put(a.at[:, lanes], b.at[:, lanes])
    comm(22)
    for e in keep:
        e.wait()
    links.drain()


def fore(*args):
    S = jax.ShapeDtypeStruct
    V = pltpu.VMEM
    table = [V((1024, 128), F32)] * 2
    specs = [VM] * 13 + [pl.BlockSpec(memory_space=pltpu.SMEM)] * 3 + [VM] * 2
    return pl.pallas_call(
        fore_kernel,
        out_shape=(
            S((4, 2, 4, 32, 1536), BF), S((4, 2, 4, 32, 4096), BF), S((4, 4, 32, 1024), BF), S((4, 4, 128, 1024), BF),
            S((4, 128, 1024), BF), S((2, 4, 128, 1024), BF), S((8, 1024), F32), S((1024, 1024), BF),
            S((1024, 512), BF), S((1024, 512), BF), S((1024, 512), BF), S((1024, 512), BF), S((8, 1024), F32),
            S((1024, 1024), BF), S((512, 1024), F32), S((1024, 2048), BF), S((1024, 2048), BF), S((1024, 2048), BF),
            S((1024, 128), F32), S((1024, 128), F32),
        ),
        in_specs=specs,
        out_specs=[ANY] * 20,
        scratch_shapes=[V((32, 1536), BF)] * 2 + [V((32, 4096), BF)] * 2 + [V((8, 128), F32)] + table + [
            V((4, 128, 1024), BF), V((4, 128, 1024), BF), V((4, 2, 4, 8, 128), F32), V((8, 1024), F32),
            V((2, 4, 128, 1024), BF), V((4, 2, 4, 32, 1536), BF), V((1024, 1024), BF),
            V((1024, 512), BF), V((1024, 512), BF), V((1024, 512), BF), V((1024, 512), BF), V((8, 1024), F32),
            V((4, 4, 32, 1024), BF), V((512, 1024), F32), V((512, 1024), F32), V((512, 1024), F32),
            V((1024, 1024), BF), V((4, 2, 4, 32, 512), BF), V((4, 2, 4, 32, 512), BF),
            V((1024, 2048), BF), V((1024, 2048), BF), V((1024, 2048), BF),
            pltpu.SemaphoreType.DMA((200,)),
            pltpu.SemaphoreType.DMA((200,)),
            pltpu.SemaphoreType.DMA((72,)),
        ],
        compiler_params=pltpu.CompilerParams(collective_id=0, has_side_effects=True, vmem_limit_bytes=67043328),
    )(*args)


PIECES = (
    ("d", 1, 1),
    ("gu", 2, 1),
    ("gu", 4, 0),
    ("gu", 1, 1),
    ("gu", 0, 0),
    ("qkv", 1, 1),
    ("gu", 7, 0),
    ("d", 3, 0),
    ("o", 0, 1),
    ("d", 0, 1),
    ("qkv", 2, 1),
    ("gu", 6, 1),
    ("qkv", 0, 0),
    ("d", 2, 1),
    ("gu", 5, 0),
    ("qkv", 3, 1),
    ("gu", 3, 0),
)
SHAPES = {"d": (4, 32, 1024), "o": (4, 32, 1024), "gu": (2, 4, 32, 512), "qkv": (2, 4, 32, 384)}
ORDER = (
    (), ((0, 0), (7, 0)), ((0, 1), (2, 0), (4, 0), (7, 1)), ((0, 2), (3, 0), (7, 2)),
    ((0, 3), (1, 0), (2, 1), (3, 1), (7, 3)), ((0, 4), (1, 1), (4, 1), (6, 0), (7, 4), (9, 0), (14, 0)),
    ((0, 5), (1, 2), (2, 2), (7, 5), (3, 2)), ((2, 3), (4, 2), (6, 1), (1, 3), (8, 0), (16, 0)),
    ((1, 4), (2, 4), (3, 3), (17, 0), (4, 3), (9, 1), (14, 1)), ((6, 2),), (), (), ((8, 1), (13, 0), (16, 1)),
    ((12, 0),), (), (), ((3, 4), (6, 3)), ((1, 5), (2, 5), (14, 2), (9, 2)), ((5, 0),),
    ((13, 1), (8, 2), (14, 3), (9, 3)), (), ((12, 1), (4, 4), (8, 3)), ((6, 4),), ((14, 4), (10, 0)),
    ((17, 1), (16, 2), (16, 3), (9, 4)), ((3, 5), (4, 5), (5, 1), (11, 0), (6, 5), (13, 2), (8, 4), (13, 3), (16, 4)),
    (), ((14, 5), (5, 2), (5, 3), (13, 4)), ((9, 5), (12, 2), (12, 3), (5, 4), (15, 0)),
    ((8, 5), (5, 5), (13, 5), (16, 5), (18, 0), (10, 1), (11, 1), (12, 4), (19, 0), (15, 1), (10, 2), (11, 2),
     (19, 1), (19, 2), (15, 2), (10, 3), (11, 3), (18, 1), (12, 5), (19, 3), (10, 4), (15, 3), (10, 5), (11, 4),
     (15, 4), (11, 5), (15, 5),),

)


def total_over_devices(links, me, acc, got):
    y, x, c, z = me
    hops = [links.wanted(acc, got.at[i], d) for i, d in
            enumerate((dev(y, x, 1 - c, z), dev(y, 1 - x, c, z), dev(1 - y, x, c, z)))]
    over_z = [links.wanted(acc, got.at[2 + k], dev(y, x, c, (z + k) % 4)) for k in (1, 2, 3)]

    def settle(i):
        hops[i].wait()
        acc[...] += got[i]

    def chip():
        hops[0].start()
        settle(0)
        hops[1].start()

    def second():
        settle(1)
        hops[2].start()

    def third():
        settle(2)
        for q in over_z:
            q.start()

    def last():
        for q in over_z:
            q.wait()
        acc[...] += got[3] + (got[4] + got[5])
    return chip, second, third, last


def rows_dot(a, b):
    return lax.dot_general(a, b, (((0,), (0,)), ((), ())), preferred_element_type=F32)


def each(count, step):
    def body(r, _):
        step(r)
        return 0
    lax.fori_loop(0, count, body, 0)


def block(i, size):
    return pl.ds(pl.multiple_of(i * size, size), size)


def norm_parts(u):
    d = u - jnp.mean(u, axis=-1, keepdims=True)
    scaling = lax.rsqrt(jnp.mean(d * d, axis=-1, keepdims=True) + 1e-05)
    return d * scaling, scaling


def norm_back(upstream, normed, scaling):
    return scaling * (upstream - jnp.mean(upstream, axis=-1, keepdims=True)
                      - normed * jnp.mean(upstream * normed, axis=-1, keepdims=True))


def back_kernel(cw, hido, od, n2o, gateo, upo, ogu, mido, oo, atto, qo, ko, vo, lseo, n1o, oqkv, xh,
                cos, sin, gv, *rest):
    fqkv, fgu, fo, fd, fgain, out_w, ig_w = rest[:7]
    scratch = list(rest[7:])
    (gd, ggu, go, gw, mg, sent, came, mlow, ag, out16, ig, gacc, ggot, send, recv, local, ready) = scratch[-17:]
    me = y, x, c, z = place()
    partner = dev(y, x, 1 - c, z)
    met = greet(y, x, c, z)
    links = Links(send, recv, local)
    work = []
    finals = []
    for name, index, route in PIECES:
        bufs = [scratch.pop(0) for _ in range(6)]
        if name in ("qkv", "gu"):
            src, dst = (gw, fqkv) if name == "qkv" else (ggu, fgu)
            cols = SHAPES[name][3]
            lanes = pl.ds(index * cols, cols)

            def at(yy, xx, src=src, index=index):
                return src.at[index, yy * 2 + xx]

            def deliver(total, dst=dst, lanes=lanes):
                there = links.later(total.at[1 - c], dst.at[c, :, lanes], partner)
                here = links.here_later(total.at[c], dst.at[c, :, lanes])
                finals.extend((there.wait_recv, here.wait))
                return there, here
        else:
            src, dst = (gd, fd) if name == "d" else (go, fo)
            rows = pl.ds(index * 32, 32)

            def at(yy, xx, src=src, rows=rows):
                return src.at[yy * 2 + xx, :, rows]

            def deliver(total, dst=dst, rows=rows):
                here = links.here_later(total, dst.at[rows])
                finals.append(here.wait)
                return (here,)
        work.append(collect(links, at, me, route, bufs, deliver))
    o1 = Outgoing(links, me, out16, out_w)
    o2 = Outgoing(links, me, ig, ig_w)
    work += [(o1.start, o1.finish), (o2.start, o2.finish), total_over_devices(links, me, gacc, ggot)]
    swaps = [links.wanted(sent, came, partner) for _ in range(3)]
    share = links.later(mlow.at[0], mlow.at[1], partner)

    def comm(slot):
        for i, stage in ORDER[slot]:
            work[i][stage]()

    def swap(n):
        if n:
            pl.semaphore_wait(ready, 1)
        swaps[n].start()

    def read(n):
        if n < 2:
            pl.semaphore_signal(ready, inc=1, device_id=partner, device_id_type=MESH)

    gacc[...] = jnp.zeros_like(gacc)
    lane = lax.broadcasted_iota(jnp.int32, (1, 1024), 1)
    here = (2 * (y * 2 + x) + z // 2) * 128 + z % 2
    factor = jnp.sum(jnp.where(lane == here, gv[4:5, :], 0.0), axis=1, keepdims=True)

    def hidden_layer(low):
        a = links.here(cw, low)

        def down(hv):
            b = links.here(hido, hv)
            a.wait()

            def scale(i):
                low[i // 4, i % 4] = (factor * low[i // 4, i % 4].astype(F32)).astype(BF)
            each(8, scale)
            b.wait()

            def weights(r):
                u = rows_dot(hv[:, block(r, 256)], low[...].reshape(1024, 1024))
                gd[r // 2, pl.ds((r % 2) * 2, 2)] = u.astype(BF).reshape(2, 128, 1024)
            each(8, weights)
            met()
            comm(0)
        pl.run_scoped(down, pltpu.VMEM((1024, 2048), BF))

        def units(n2, gate, up, dgate, dup, wg, wu, wd):
            a = links.here(n2o, n2)
            for j in range(4):
                lanes = pl.ds(512 * j, 512)
                got = [links.here(od.at[j], wd), links.here(gateo.at[:, lanes], gate), links.here(upo.at[:, lanes], up),
                       links.here(ogu.at[:, :, :, :, lanes], wg),
                       links.here(ogu.at[:, :, :, :, pl.ds(2048 + 512 * j, 512)], wu)]
                comm(1 + j)
                for q in got:
                    q.wait()

                def grads(r):
                    rows = block(r, 256)
                    g = dot_t(low[r // 2, pl.ds((r % 2) * 2, 2)].reshape(256, 1024), wd[...].reshape(512, 1024))
                    a, b = gate[rows, :].astype(F32), up[rows, :].astype(F32)
                    t = jax.nn.sigmoid(a)
                    dgate[rows, :] = (g * b * t * (1.0 + a * (1.0 - t))).astype(BF)
                    dup[rows, :] = (g * a * t).astype(BF)
                each(4, grads)
                if j == 0:
                    a.wait()

                def weights(r):
                    n = n2[:, block(r, 256)]
                    ggu[j, r] = rows_dot(n, dgate[...]).astype(BF).reshape(2, 4, 32, 512)
                    ggu[4 + j, r] = rows_dot(n, dup[...]).astype(BF).reshape(2, 4, 32, 512)
                each(4, weights)

                def terms(r, out, first):
                    rows = pl.ds(pl.multiple_of(first + r * 256, 256), 256)
                    u = (dot_t(dgate[rows, :], wg[...].reshape(1024, 512))
                         + dot_t(dup[rows, :], wu[...].reshape(1024, 512)))
                    dst = block(r, 256)
                    out[dst, :] = u if j == 0 else out[dst, :] + u
                each(2, lambda r: terms(r, sent, 512))
                if j == 3:
                    swap(0)
                each(2, lambda r: terms(r, mg, 0))
        pl.run_scoped(units, pltpu.VMEM((1024, 1024), BF), *[pltpu.VMEM((1024, 512), BF)] * 4,
                      *[pltpu.VMEM((4, 2, 4, 32, 512), BF)] * 2, pltpu.VMEM((4, 128, 1024), BF))
    pl.run_scoped(hidden_layer, pltpu.VMEM((2, 4, 128, 1024), BF))
    comm(5)

    def second_norm(mid, cot):
        a, b = links.here(mido, mid), links.here(cw.at[0], cot)
        a.wait()
        b.wait()
        swaps[0].wait()

        def part(r):
            rows = block(r, 128)
            gn = mg[rows, :] + came[rows, :]
            normed, scaling = norm_parts(mid[rows, :])
            gacc[2:3, :] += jnp.sum(gn * normed, axis=0, keepdims=True)
            gacc[3:4, :] += jnp.sum(gn, axis=0, keepdims=True)
            u = factor * cot[r].astype(F32) + norm_back(gn * gv[2:3, :], normed, scaling)
            mg[rows, :] = u
            mlow[0, r] = u.astype(BF)
        each(4, part)
        read(0)
        share.start()
    pl.run_scoped(second_norm, pltpu.VMEM((512, 1024), F32), pltpu.VMEM((4, 128, 1024), BF))
    comm(6)

    def out_layer(w, att):
        a, b = links.here(oo, w), links.here(atto, att)
        a.wait()
        b.wait()
        share.wait_recv()

        def weights(r):
            u = rows_dot(att[:, block(r, 256)], mlow[...].reshape(1024, 1024))
            go[pl.ds(2 * r, 2)] = u.astype(BF).reshape(2, 4, 32, 1024)
        each(2, weights)

        def grads(r):
            u = dot_t(mlow[r // 2, pl.ds((r % 2) * 2, 2)].reshape(256, 1024), w[...].reshape(512, 1024))
            ag[block(r, 256), :] = u.astype(BF)
        each(4, grads)
    pl.run_scoped(out_layer, pltpu.VMEM((4, 4, 32, 1024), BF), pltpu.VMEM((1024, 512), BF))
    comm(7)

    def output(hv, w, mid):
        got = [links.here(hido, hv), links.here(od, w), links.here(mido, mid)]
        for q in got:
            q.wait()

        def term(r, first):
            return jnp.dot(hv[pl.ds(pl.multiple_of(first + r * 256, 256), 256), :], w[...].reshape(2048, 1024),
                           preferred_element_type=F32)

        def theirs(r):
            sent[block(r, 256), :] = term(r, 512)
        each(2, theirs)
        swap(1)

        def mine(r):
            mid[block(r, 256), :] += term(r, 0)
        each(2, mine)
        swaps[1].wait()

        def total(r):
            out16[r] = (mid[block(r, 128), :] + came[block(r, 128), :]).astype(BF)
        each(4, total)
        read(1)
    pl.run_scoped(output, pltpu.VMEM((1024, 2048), BF), pltpu.VMEM((4, 4, 128, 1024), BF), pltpu.VMEM((512, 1024), F32))

    def attention(dqkv):
        def heads(q, k, v, lse, n1, dka, dva):
            got = [links.here(a, b) for a, b in ((qo, q), (ko, k), (vo, v), (lseo, lse), (n1o, n1))]
            for e in got:
                e.wait()

            def step(t):
                for slot in range(20):
                    if ORDER[8 + slot]:
                        pl.when(t == slot)(lambda slot=slot: comm(8 + slot))
                g, i = t // 5, t % 5

                @pl.when(i < 4)
                def _():
                    attend_back_step(q, k, v, ag, lse, cos, sin, dqkv, dka, dva, g, i)

                @pl.when(i == 4)
                def _():
                    u = rows_dot(n1[...], dqkv[:, pl.ds(pl.multiple_of(g * 384, 128), 384)])
                    gw[g] = u.astype(BF).reshape(4, 2, 4, 32, 384)
            each(20, step)
        pl.run_scoped(heads, *[pltpu.VMEM((1024, 512), BF)] * 3, pltpu.VMEM((8, 1024), F32),
                      pltpu.VMEM((1024, 1024), BF), *[pltpu.VMEM((1024, 128), F32)] * 2)

        def first_norm(w, tokens, mine):
            got = [links.here(oqkv, w), links.here(xh, tokens)]
            comm(28)
            for e in got:
                e.wait()

            def term(r, out, first):
                out[block(r, 256), :] = dot_t(dqkv[pl.ds(pl.multiple_of(first + r * 256, 256), 256), :],
                                              w[...].reshape(1024, 1536))
            each(2, lambda r: term(r, sent, 512))
            swap(2)
            each(2, lambda r: term(r, mine, 0))
            swaps[2].wait()

            def part(r):
                rows = block(r, 128)
                gn = mine[rows, :] + came[rows, :]
                normed, scaling = norm_parts(tokens[r].astype(F32))
                gacc[0:1, :] += jnp.sum(gn * normed, axis=0, keepdims=True)
                gacc[1:2, :] += jnp.sum(gn, axis=0, keepdims=True)
                ig[r] = (mg[rows, :] + norm_back(gn * gv[0:1, :], normed, scaling)).astype(BF)
            each(4, part)
        pl.run_scoped(first_norm, pltpu.VMEM((4, 2, 4, 32, 1536), BF), pltpu.VMEM((4, 128, 1024), BF),
                      pltpu.VMEM((512, 1024), F32))
    pl.run_scoped(attention, pltpu.VMEM((1024, 1536), BF))
    comm(29)
    finals.append(links.here(gacc, fgain).wait)
    for f in finals:
        f()
    links.drain()


def back(*args):
    scratch = []
    for name, index, route in PIECES:
        scratch += reduce_shapes(SHAPES[name])
    return pl.pallas_call(
        back_kernel,
        out_shape=(
            jax.ShapeDtypeStruct((2, 32, 1536), F32),
            jax.ShapeDtypeStruct((2, 32, 4096), F32),
            jax.ShapeDtypeStruct((32, 1024), F32),
            jax.ShapeDtypeStruct((128, 1024), F32),
            jax.ShapeDtypeStruct((8, 1024), F32),
            jax.ShapeDtypeStruct((2, 2, 128, 1024), BF),
            jax.ShapeDtypeStruct((2, 2, 128, 1024), BF),
        ),
        in_specs=[ANY] * 17 + [VM] * 3,
        out_specs=[ANY] * 7,
        scratch_shapes=scratch + [
            pltpu.VMEM((4, 4, 128, 1024), BF),
            pltpu.VMEM((8, 4, 2, 4, 32, 512), BF),
            pltpu.VMEM((4, 4, 32, 1024), BF),
            pltpu.VMEM((4, 4, 2, 4, 32, 384), BF),
            pltpu.VMEM((512, 1024), F32),
            pltpu.VMEM((512, 1024), F32),
            pltpu.VMEM((512, 1024), F32),
            pltpu.VMEM((2, 4, 128, 1024), BF),
            pltpu.VMEM((1024, 512), BF),
            pltpu.VMEM((4, 128, 1024), BF),
            pltpu.VMEM((4, 128, 1024), BF),
            pltpu.VMEM((8, 1024), F32),
            pltpu.VMEM((6, 8, 1024), F32),
            pltpu.SemaphoreType.DMA((192,)),
            pltpu.SemaphoreType.DMA((192,)),
            pltpu.SemaphoreType.DMA((96,)),
            pltpu.SemaphoreType.REGULAR,
        ],
        compiler_params=pltpu.CompilerParams(collective_id=1, has_side_effects=True, vmem_limit_bytes=67043328),
    )(*args)


def finish_kernel(fqkv, fgu, fo, fd, fgain, out_w, ig_w, out, ig, gq, gk, gv, go, gg, gu, gd, *gains):
    for n in (0, 1):
        for g in range(4):
            for j, dst in enumerate((gq, gk, gv)):
                dst[:, pl.ds(128 * (2 * g + n), 128)] = fqkv[n, :, pl.ds(384 * g + 128 * j, 128)]
            for j, dst in enumerate((gg, gu)):
                dst[:, pl.ds(512 * (2 * g + n), 512)] = fgu[n, :, pl.ds(2048 * j + 512 * g, 512)]
    go[...] = fo[...]
    gd[...] = fd[...]

    def rows(i):
        out[i // 2, pl.ds(pl.multiple_of((i % 2) * 128, 128), 128)] = out_w[i // 2, i % 2]
        ig[i // 2, pl.ds(pl.multiple_of((i % 2) * 128, 128), 128)] = ig_w[i // 2, i % 2].astype(F32)
    each(4, rows)
    first = (lax.axis_index("dp") * 4 + lax.axis_index("seq")) * 32
    mine = pltpu.roll(fgain[...], (1024 - first) % 1024, 1)
    for i in range(4):
        gains[i][...] = mine[i:i + 1, 0:32]


def finish(*args):
    S = jax.ShapeDtypeStruct
    return pl.pallas_call(
        finish_kernel,
        out_shape=(S((2, 256, 1024), BF), S((2, 256, 1024), F32)) + (S((32, 1024), F32),) * 4
        + (S((32, 4096), F32),) * 2 + (S((128, 1024), F32),) + (S((1, 32), F32),) * 4,
        in_specs=[VM] * 7,
        out_specs=[VM] * 13,
        compiler_params=pltpu.CompilerParams(vmem_limit_bytes=VMEM_BYTES),
    )(*args)


def angle_tables(c):
    lane = jnp.arange(128, dtype=jnp.int32)
    freqs = 10000.0 ** (-2.0 * (lane % 32).astype(jnp.float32) / HD)
    block = jnp.arange(8, dtype=jnp.int32)
    far = (block % 4) * 256 + jnp.where(block < 4, c, 1 - c) * 128
    rows = jnp.concatenate([jnp.arange(128, dtype=jnp.int32), far]).astype(jnp.float32)
    angle = rows[:, None] * freqs[None, :]
    cos, sin = jnp.cos(angle), jnp.sin(angle)
    return cos, sin


def paired(
    tokens,
    cotangent,
    species_index,
    species_count,
    loss_weight,
    query_weight,
    key_weight,
    value_weight,
    out_weight,
    gate_weight,
    up_weight,
    down_weight,
    mixer_gain,
    mixer_shift,
    feeder_gain,
    feeder_shift,
):
    dp, z = lax.axis_index("dp"), lax.axis_index("seq")
    c = dp % 2
    (wqkv, wgu, wo, wd, xh, cw, gv, norm_one, q, k, v, attended, lse, norm_two, middle, gate, upward, hidden,
     cos, sin) = fore(
        tokens, cotangent, query_weight, key_weight, value_weight, gate_weight, up_weight, out_weight, down_weight,
        mixer_gain.reshape(1, 32), mixer_shift.reshape(1, 32), feeder_gain.reshape(1, 32), feeder_shift.reshape(1, 32),
        species_index, species_count, loss_weight, *angle_tables(c))
    parts = back(
        cw, hidden, wd, norm_two, gate, upward, wgu, middle, wo, attended, q, k, v, lse, norm_one, wqkv, xh,
        cos, sin, gv)
    done = finish(*parts)
    return done[:9] + tuple(g.reshape(32) for g in done[9:])


def matmul(left, right):
    return jnp.dot(left, right, preferred_element_type=jnp.float32)


def weight_term(left, right):
    return lax.dot_general(
        left, right, (((0,), (0,)), ((), ())), preferred_element_type=jnp.float32
    )


def through(left, weight):
    return lax.dot_general(
        left, weight, (((1,), (1,)), ((), ())), preferred_element_type=jnp.float32
    )


def normalize(values):
    center = jnp.mean(values, axis=-1, keepdims=True)
    centered = values - center
    variance = jnp.mean(centered * centered, axis=-1, keepdims=True)
    scaling = lax.rsqrt(variance + 1e-05)
    return (centered * scaling, scaling)


def plain_norm_back(upstream, normed, scaling):
    first = jnp.mean(upstream, axis=-1, keepdims=True)
    second = jnp.mean(upstream * normed, axis=-1, keepdims=True)
    return scaling * (upstream - first - normed * second)


def tables(start, count):
    half = HD // 2
    positions = (start + jnp.arange(count, dtype=jnp.int32)).astype(jnp.float32)
    freqs = 10000.0 ** (-2.0 * jnp.arange(half, dtype=jnp.float32) / HD)
    angle = positions[:, None] * freqs[None, :]
    return (jnp.cos(angle)[:, None, :], jnp.sin(angle)[:, None, :])


def rotate(values, cosine, sine):
    half = HD // 2
    first = values[..., :half]
    second = values[..., half:]
    return jnp.concatenate(
        [first * cosine - second * sine, second * cosine + first * sine], axis=-1
    )


def attend_head(operands):
    query_head, key_head, value_head = operands
    scores = jnp.einsum(
        "wtd,wsd->wts", query_head, key_head, preferred_element_type=jnp.float32
    ) * HD ** (-0.5)
    peak = jnp.max(scores, axis=-1, keepdims=True)
    raised = jnp.exp(scores - peak)
    total = jnp.sum(raised, axis=-1, keepdims=True)
    probs = (raised / total).astype(jnp.bfloat16)
    result = jnp.einsum("wts,wsd->wtd", probs, value_head, preferred_element_type=jnp.float32)
    return (result, (peak + jnp.log(total))[..., 0])


def head_back(operands):
    query_head, key_head, value_head, upstream, log_total = operands
    scores = jnp.einsum(
        "wtd,wsd->wts", query_head, key_head, preferred_element_type=jnp.float32
    ) * HD ** (-0.5)
    probs = jnp.exp(scores - log_total[..., None])
    prob_grads = jnp.einsum(
        "wtd,wsd->wts", upstream, value_head, preferred_element_type=jnp.float32
    )
    inner = jnp.sum(probs * prob_grads, axis=-1, keepdims=True)
    score_grads = (probs * (prob_grads - inner)).astype(jnp.bfloat16)
    query_grad = jnp.einsum(
        "wts,wsd->wtd", score_grads, key_head, preferred_element_type=jnp.float32
    ) * HD ** (-0.5)
    key_grad = jnp.einsum(
        "wts,wtd->wsd", score_grads, query_head, preferred_element_type=jnp.float32
    ) * HD ** (-0.5)
    value_grad = jnp.einsum(
        "wts,wtd->wsd", probs.astype(jnp.bfloat16), upstream, preferred_element_type=jnp.float32
    )
    return (query_grad, key_grad, value_grad)


def general(
    tokens,
    cotangent,
    species_index,
    species_count,
    loss_weight,
    query_weight,
    key_weight,
    value_weight,
    out_weight,
    gate_weight,
    up_weight,
    down_weight,
    mixer_gain,
    mixer_shift,
    feeder_gain,
    feeder_shift,
):
    gathered = (
        lax.all_gather(query_weight, ("dp", "seq"), axis=0, tiled=True),
        lax.all_gather(key_weight, ("dp", "seq"), axis=0, tiled=True),
        lax.all_gather(value_weight, ("dp", "seq"), axis=0, tiled=True),
        lax.all_gather(out_weight, ("dp", "seq"), axis=0, tiled=True),
        lax.all_gather(gate_weight, ("dp", "seq"), axis=0, tiled=True),
        lax.all_gather(up_weight, ("dp", "seq"), axis=0, tiled=True),
        lax.all_gather(down_weight, ("dp", "seq"), axis=0, tiled=True),
        lax.all_gather(mixer_gain, ("dp", "seq"), axis=0, tiled=True),
        lax.all_gather(mixer_shift, ("dp", "seq"), axis=0, tiled=True),
        lax.all_gather(feeder_gain, ("dp", "seq"), axis=0, tiled=True),
        lax.all_gather(feeder_shift, ("dp", "seq"), axis=0, tiled=True),
    )
    wq, wk, wv, wo, wg, wu, wd, gain_one, shift_one, gain_two, shift_two = gathered
    windows, steps_dev, width = tokens.shape
    rows = windows * steps_dev
    start = lax.axis_index("seq") * steps_dev
    cosine, sine = tables(start, steps_dev)
    inputs = tokens.astype(jnp.float32).reshape(rows, width)
    normed_one, scaling_one = normalize(inputs)
    norm_one = (normed_one * gain_one.astype(jnp.float32) + shift_one.astype(jnp.float32)).astype(
        jnp.bfloat16
    )
    queries = rotate(
        matmul(norm_one, wq).reshape(windows, steps_dev, HEADS, HD), cosine, sine
    ).astype(jnp.bfloat16)
    keys = rotate(matmul(norm_one, wk).reshape(windows, steps_dev, HEADS, HD), cosine, sine).astype(
        jnp.bfloat16
    )
    values = matmul(norm_one, wv).astype(jnp.bfloat16)
    all_keys, all_values = (
        lax.all_gather(keys.reshape(windows, steps_dev, width), "seq", axis=1, tiled=True),
        lax.all_gather(values.reshape(windows, steps_dev, width), "seq", axis=1, tiled=True),
    )
    length = all_keys.shape[1]
    query_heads = queries.transpose(2, 0, 1, 3)
    key_heads = all_keys.reshape(windows, length, HEADS, HD).transpose(2, 0, 1, 3)
    value_heads = all_values.reshape(windows, length, HEADS, HD).transpose(2, 0, 1, 3)
    head_results, log_totals = lax.map(attend_head, (query_heads, key_heads, value_heads))
    attended = head_results.transpose(1, 2, 0, 3).reshape(rows, width).astype(jnp.bfloat16)
    middle = inputs + matmul(attended, wo)
    normed_two, scaling_two = normalize(middle)
    norm_two = (normed_two * gain_two.astype(jnp.float32) + shift_two.astype(jnp.float32)).astype(
        jnp.bfloat16
    )
    gate = matmul(norm_two, wg)
    upward = matmul(norm_two, wu)
    sigma = jax.nn.sigmoid(gate)
    swish = gate * sigma
    hidden = (swish * upward).astype(jnp.bfloat16)
    output = (middle + matmul(hidden, wd)).astype(jnp.bfloat16).reshape(windows, steps_dev, width)
    table = loss_weight * lax.rsqrt(species_count.astype(jnp.float32) / 400.0)
    picks = species_index[:, None] == jnp.arange(table.shape[0], dtype=jnp.int32)[None, :]
    factor = jnp.sum(jnp.where(picks, table[None, :], 0.0), axis=1)
    grad_out = (factor[:, None, None] * cotangent.astype(jnp.float32)).reshape(rows, width)
    regathered = (
        lax.all_gather(query_weight, ("dp", "seq"), axis=0, tiled=True),
        lax.all_gather(key_weight, ("dp", "seq"), axis=0, tiled=True),
        lax.all_gather(value_weight, ("dp", "seq"), axis=0, tiled=True),
        lax.all_gather(out_weight, ("dp", "seq"), axis=0, tiled=True),
        lax.all_gather(gate_weight, ("dp", "seq"), axis=0, tiled=True),
        lax.all_gather(up_weight, ("dp", "seq"), axis=0, tiled=True),
        lax.all_gather(down_weight, ("dp", "seq"), axis=0, tiled=True),
        lax.all_gather(mixer_gain, ("dp", "seq"), axis=0, tiled=True),
        lax.all_gather(mixer_shift, ("dp", "seq"), axis=0, tiled=True),
        lax.all_gather(feeder_gain, ("dp", "seq"), axis=0, tiled=True),
        lax.all_gather(feeder_shift, ("dp", "seq"), axis=0, tiled=True),
    )
    wq, wk, wv, wo, wg, wu, wd, gain_one, shift_one, gain_two, shift_two = regathered
    out_low = grad_out.astype(jnp.bfloat16)
    down_part = weight_term(hidden, out_low)
    hidden_grad = through(out_low, wd)
    gate_grad = (hidden_grad * upward * sigma * (1.0 + gate * (1.0 - sigma))).astype(jnp.bfloat16)
    upward_grad = (hidden_grad * swish).astype(jnp.bfloat16)
    gate_part = weight_term(norm_two, gate_grad)
    upward_part = weight_term(norm_two, upward_grad)
    norm_two_grad = through(gate_grad, wg) + through(upward_grad, wu)
    feeder_gain_part = jnp.sum(norm_two_grad * normed_two, axis=0)
    feeder_shift_part = jnp.sum(norm_two_grad, axis=0)
    middle_grad = grad_out + plain_norm_back(
        norm_two_grad * gain_two.astype(jnp.float32), normed_two, scaling_two
    )
    middle_low = middle_grad.astype(jnp.bfloat16)
    out_part = weight_term(attended, middle_low)
    attended_grad = through(middle_low, wo).astype(jnp.bfloat16)
    upstream_heads = attended_grad.reshape(windows, steps_dev, HEADS, HD).transpose(2, 0, 1, 3)
    query_heads_grad, key_heads_grad, value_heads_grad = lax.map(
        head_back, (query_heads, key_heads, value_heads, upstream_heads, log_totals)
    )
    key_whole = key_heads_grad.transpose(1, 2, 0, 3).reshape(windows, length, width)
    value_whole = value_heads_grad.transpose(1, 2, 0, 3).reshape(windows, length, width)
    key_mine, value_mine = (
        lax.psum_scatter(
            key_whole.astype(jnp.bfloat16), "seq", scatter_dimension=1, tiled=True
        ).astype(jnp.float32),
        lax.psum_scatter(
            value_whole.astype(jnp.bfloat16), "seq", scatter_dimension=1, tiled=True
        ).astype(jnp.float32),
    )
    query_lin_grad = (
        rotate(query_heads_grad.transpose(1, 2, 0, 3), cosine, -sine)
        .reshape(rows, width)
        .astype(jnp.bfloat16)
    )
    key_lin_grad = (
        rotate(key_mine.reshape(windows, steps_dev, HEADS, HD), cosine, -sine)
        .reshape(rows, width)
        .astype(jnp.bfloat16)
    )
    value_lin_grad = value_mine.reshape(rows, width).astype(jnp.bfloat16)
    query_part = weight_term(norm_one, query_lin_grad)
    key_part = weight_term(norm_one, key_lin_grad)
    value_part = weight_term(norm_one, value_lin_grad)
    norm_one_grad = (
        through(query_lin_grad, wq) + through(key_lin_grad, wk) + through(value_lin_grad, wv)
    )
    mixer_gain_part = jnp.sum(norm_one_grad * normed_one, axis=0)
    mixer_shift_part = jnp.sum(norm_one_grad, axis=0)
    input_grad = middle_grad + plain_norm_back(
        norm_one_grad * gain_one.astype(jnp.float32), normed_one, scaling_one
    )
    summed = (
        lax.psum_scatter(query_part, ("dp", "seq"), scatter_dimension=0, tiled=True),
        lax.psum_scatter(key_part, ("dp", "seq"), scatter_dimension=0, tiled=True),
        lax.psum_scatter(value_part, ("dp", "seq"), scatter_dimension=0, tiled=True),
        lax.psum_scatter(out_part, ("dp", "seq"), scatter_dimension=0, tiled=True),
        lax.psum_scatter(gate_part, ("dp", "seq"), scatter_dimension=0, tiled=True),
        lax.psum_scatter(upward_part, ("dp", "seq"), scatter_dimension=0, tiled=True),
        lax.psum_scatter(down_part, ("dp", "seq"), scatter_dimension=0, tiled=True),
        lax.psum_scatter(mixer_gain_part, ("dp", "seq"), scatter_dimension=0, tiled=True),
        lax.psum_scatter(mixer_shift_part, ("dp", "seq"), scatter_dimension=0, tiled=True),
        lax.psum_scatter(feeder_gain_part, ("dp", "seq"), scatter_dimension=0, tiled=True),
        lax.psum_scatter(feeder_shift_part, ("dp", "seq"), scatter_dimension=0, tiled=True),
    )
    return (
        output,
        input_grad.reshape(windows, steps_dev, width),
        summed[0],
        summed[1],
        summed[2],
        summed[3],
        summed[4],
        summed[5],
        summed[6],
        summed[7],
        summed[8],
        summed[9],
        summed[10],
    )


def solution(mesh):
    in_specs = (
        P("dp", "seq", None),
        P("dp", "seq", None),
        P("dp"),
        P(),
        P(),
    ) + (P(("dp", "seq"), None),) * 7 + (P(("dp", "seq")),) * 4
    out_specs = (P("dp", "seq", None),) * 2 + (P(("dp", "seq"), None),) * 7 + (P(("dp", "seq")),) * 4
    fits = mesh.shape["dp"] == 8 and mesh.shape["seq"] == 4
    return jax.shard_map(
        paired if fits else general, mesh=mesh, in_specs=in_specs, out_specs=out_specs, check_vma=False
    )
```

```python
import jax
import jax.numpy as jnp
from jax import lax
from jax.experimental import pallas as pl
from jax.experimental.pallas import tpu as pltpu
from jax.sharding import PartitionSpec as P

HEADS = 16
HD = 64
MESH = pl.DeviceIdType.MESH
BF = jnp.bfloat16
F32 = jnp.float32
ANY = pl.BlockSpec(memory_space=pl.ANY)
VM = pl.BlockSpec(memory_space=pltpu.VMEM)
VMEM_BYTES = 60 << 20


def place():
    dp, z = lax.axis_index("dp"), lax.axis_index("seq")
    return dp // 4, (dp // 2) % 2, dp % 2, z


def dev(y, x, c, z):
    return ((y * 2 + x) * 2 + c, z)


def both(a, b):
    return jnp.logical_and(a, b)


def greet(y, x, c, z):
    barrier = pltpu.get_barrier_semaphore()
    peers = [dev(y, 1 - x, c, z), dev(1 - y, x, c, z), dev(y, x, 1 - c, z)]
    for k in (1, 2, 3):
        peers += [dev(y, x, c, (z + k) % 4), dev(y, x, 1 - c, (z + k) % 4)]
    for p in peers:
        pl.semaphore_signal(barrier, inc=1, device_id=p, device_id_type=MESH)
    return lambda: pl.semaphore_wait(barrier, len(peers))


class Links:
    def __init__(self, send, recv, local):
        self.send, self.recv, self.local = send, recv, local
        self.n = 0
        self.m = 0
        self.open = []

    def take(self, count):
        self.n += count
        return self.n - count

    def copy(self, src, dst, device, send, recv):
        return pltpu.make_async_remote_copy(
            src_ref=src, dst_ref=dst, send_sem=self.send.at[send], recv_sem=self.recv.at[recv],
            device_id=device, device_id_type=MESH)

    def go(self, c, ok=None):
        if ok is None:
            c.start()
        else:
            pl.when(ok)(c.start)
        self.open.append((c, ok))
        return c

    def to(self, src, dst, device):
        i = self.take(1)
        return self.go(self.copy(src, dst, device, i, i))

    def later(self, src, dst, device):
        i = self.take(1)
        c = self.copy(src, dst, device, i, i)
        self.open.append((c, None))
        return c

    def here_later(self, src, dst):
        self.m += 1
        return pltpu.make_async_copy(src, dst, self.local.at[self.m - 1])

    def wanted(self, src, dst, device):
        i = self.take(1)
        return self.copy(src, dst, device, i, i)

    def here(self, src, dst):
        self.m += 1
        c = pltpu.make_async_copy(src, dst, self.local.at[self.m - 1])
        c.start()
        return c

    def drain(self):
        for c, ok in self.open:
            if ok is None:
                c.wait_send()
            else:
                pl.when(ok)(c.wait_send)
        self.open = []


def at_z(ref, zz):
    return ref.at[zz] if len(ref.shape) == 3 else ref.at[:, zz]


def pair_of(ref, first):
    return ref.at[pl.ds(first, 2)] if len(ref.shape) == 3 else ref.at[:, pl.ds(first, 2)]


def add_into(dst, *terms):
    def body(i, _):
        total = at_z(terms[0], i)[...]
        for t in terms[1:]:
            total += at_z(t, i)[...]
        at_z(dst, i)[...] = total
        return 0
    lax.fori_loop(0, dst.shape[-3], body, 0)


def reduce_shapes(piece):
    part = piece[:-3] + piece[-2:]
    two = piece[:-3] + (2,) + piece[-2:]
    return [pltpu.VMEM((2,) + piece, BF), pltpu.VMEM(piece, BF), pltpu.VMEM(two, BF), pltpu.VMEM(two, BF),
            pltpu.VMEM(part, BF), pltpu.VMEM(part, F32)]


def collect(links, at, me, route, bufs, deliver):
    y, x, c, z = me
    to_x, to_y = dev(y, 1 - x, c, z), dev(1 - y, x, c, z)
    got, third, from_outer, from_inner, from_near, total = bufs
    out = deliver(total)
    if route == 0:
        own, away = [at(1 - y, x), at(y, x)], [at(1 - y, 1 - x), at(y, 1 - x)]
        one, two = to_x, to_y
    else:
        own, away = [at(y, 1 - x), at(y, x)], [at(1 - y, 1 - x), at(1 - y, x)]
        one, two = to_y, to_x
    near = z + 1 - 2 * (z % 2)
    inner = both(z > 0, z < 3)
    outer = jnp.logical_not(inner)
    far_side, near_side = pair_of(own[1], 2 - 2 * (z // 2)), pair_of(own[1], 2 * (z // 2))
    give = [links.later(away[n], got.at[n], one) for n in (0, 1)]
    cross = links.later(own[0], third, two)
    inward = links.wanted(far_side, from_outer, dev(y, x, c, near))
    over = links.wanted(far_side, from_inner, dev(y, x, c, 3 - z))
    links.open += [(inward, outer), (over, inner)]
    settle = links.later(at_z(own[1], near), from_near, dev(y, x, c, near))

    def start():
        for q in give:
            q.start()

    def first():
        give[0].wait_recv()
        add_into(own[0], own[0], got.at[0])
        cross.start()

    def second():
        give[1].wait_recv()
        cross.wait_recv()
        add_into(own[1], own[1], got.at[1], third)

        @pl.when(outer)
        def _():
            inward.start()
            settle.start()

    def inside():
        @pl.when(inner)
        def _():
            inward.wait_recv()
            add_into(far_side, far_side, from_outer)
            over.start()

    def across():
        @pl.when(inner)
        def _():
            over.wait_recv()
            add_into(near_side, near_side, from_inner)
            settle.start()

    def last():
        settle.wait_recv()
        total[...] = at_z(own[1], z)[...].astype(F32) + from_near[...].astype(F32)
        for q in out:
            q.start()
    return start, first, second, inside, across, last


class Outgoing:
    def __init__(self, links, me, src, dst):
        y, x, c, z = me
        recv, send = links.take(4), links.take(4)
        self.here, self.away = c == z // 2, c != z // 2
        self.remote, self.back = [], []
        for k in range(4):
            zz = (z + k) % 4
            s, d = src.at[zz], dst.at[z % 2, c]
            self.remote.append(links.copy(s, d, dev(y, x, z // 2, zz), send + k, recv + (z % 2) * 2 + c))
            links.open.append((self.remote[k], None if k else self.away))
            if k == 0:
                self.local = links.here_later(s, d)
        for i in (0, 1):
            for h in (0, 1):
                d = dst.at[i, h]
                mine = both(z == 2 * c + i, h == c)
                self.back.append((links.copy(d, d, dev(y, x, 1 - c, z), send, recv + 2 * i + h), jnp.logical_not(mine)))

    def start(self):
        for q in self.remote[1:]:
            q.start()
        pl.when(self.away)(self.remote[0].start)
        pl.when(self.here)(self.local.start)

    def finish(self):
        pl.when(self.here)(self.local.wait)
        for q, ok in self.back:
            pl.when(ok)(q.wait_recv)


def swap_halves(u):
    lane = lax.broadcasted_iota(jnp.int32, u.shape, 1) % HD
    return jnp.where(lane < HD // 2, pltpu.roll(u, 128 - HD // 2, 1), pltpu.roll(u, HD // 2, 1))


def head_mask(shape, h):
    lane = lax.broadcasted_iota(jnp.int32, shape, 1)
    return (lane < HD) if h == 0 else (lane >= HD)


def dot_t(a, b):
    return lax.dot_general(a, b, (((1,), (1,)), ((), ())), preferred_element_type=F32)


def project_step(xw, gv, w, cos, sin, n1, q, k, v, r):
    rows = pl.ds(pl.multiple_of(r * 256, 256), 256)
    u = xw[r // 2, pl.ds((r % 2) * 2, 2)].reshape(256, 1024).astype(F32)
    d = u - jnp.mean(u, axis=-1, keepdims=True)
    scaling = lax.rsqrt(jnp.mean(d * d, axis=-1, keepdims=True) + 1e-05)
    n = (d * scaling * gv[0:1, :] + gv[1:2, :]).astype(BF)
    n1[rows, :] = n
    for g in range(4):
        lanes = pl.ds(128 * g, 128)
        t = jnp.dot(n, w[:, :, :, :, pl.ds(384 * g, 384)].reshape(1024, 384), preferred_element_type=F32)
        for j, o in ((0, q), (1, k)):
            s = t[:, 128 * j:128 * j + 128]
            o[rows, lanes] = (s * cos[rows, :] + swap_halves(s) * sin[rows, :]).astype(BF)
        v[rows, lanes] = t[:, 256:].astype(BF)


def attend_step(q, k, v, o, lse, g, i):
    lanes = pl.ds(pl.multiple_of(g * 128, 128), 128)
    rows = pl.ds(pl.multiple_of(i * 256, 256), 256)
    qs = q[rows, lanes] * jnp.asarray(HD ** -0.5, BF)
    kk, vv = k[:, lanes], v[:, lanes]
    outs, logs = [], []
    for h in (0, 1):
        qh = jnp.where(head_mask(qs.shape, h), qs, jnp.zeros_like(qs))
        s = dot_t(qh, kk)
        m = jnp.max(s, axis=-1, keepdims=True)
        e = jnp.exp(s - m)
        t = jnp.sum(e, axis=-1, keepdims=True)
        p = (e * (1.0 / t)).astype(BF)
        outs.append(jnp.dot(p, vv, preferred_element_type=F32))
        logs.append(jnp.broadcast_to(m + jnp.log(t), qs.shape))
    keep = head_mask(qs.shape, 0)
    o[rows, lanes] = jnp.where(keep, outs[0], outs[1]).astype(BF)
    t = jnp.transpose(jnp.where(keep, logs[0], logs[1]))
    lse[pl.ds(2 * g, 1), rows] = t[0:1]
    lse[pl.ds(2 * g + 1, 1), rows] = t[HD:HD + 1]


def attend_back_step(q, k, v, do, lse, cos, sin, dqkv, dka, dva, g, i):
    lanes = pl.ds(pl.multiple_of(g * 128, 128), 128)
    rows = pl.ds(pl.multiple_of(i * 256, 256), 256)

    @pl.when(i == 0)
    def _():
        dka[...] = jnp.zeros_like(dka)
        dva[...] = jnp.zeros_like(dva)
    kk, vv, go = k[:, lanes], v[:, lanes], do[rows, lanes]
    qs = q[rows, lanes] * jnp.asarray(HD ** -0.5, BF)
    logs = lse[pl.ds(2 * g, 1), rows], lse[pl.ds(2 * g + 1, 1), rows]
    dks, dvs, dqs = [], [], []
    for h in (0, 1):
        keep = head_mask(kk.shape, h)
        zero = jnp.zeros_like(kk)
        s = dot_t(jnp.where(keep, kk, zero), qs)
        p = jnp.exp(s - logs[h])
        dp = dot_t(jnp.where(keep, vv, zero), go)
        pd = p * dp
        ds = (pd - p * jnp.sum(pd, axis=0, keepdims=True)).astype(BF)
        dvs.append(jnp.dot(p.astype(BF), go, preferred_element_type=F32))
        dks.append(jnp.dot(ds, qs, preferred_element_type=F32))
        dqs.append(lax.dot_general(ds, kk, (((0,), (0,)), ((), ())), preferred_element_type=F32))
    keep = head_mask(kk.shape, 0)
    dka[...] += jnp.where(keep, dks[0], dks[1])
    dva[...] += jnp.where(keep, dvs[0], dvs[1])
    u = jnp.where(head_mask(go.shape, 0), dqs[0], dqs[1]) * HD ** -0.5
    dqkv[rows, pl.ds(pl.multiple_of(g * 384, 128), 128)] = (
        u * cos[rows, :] - swap_halves(u) * sin[rows, :]).astype(BF)

    @pl.when(i == 3)
    def _():
        u = dka[...]
        dqkv[:, pl.ds(pl.multiple_of(128 + g * 384, 128), 128)] = (
            u * cos[...] - swap_halves(u) * sin[...]).astype(BF)
        dqkv[:, pl.ds(pl.multiple_of(256 + g * 384, 128), 128)] = dva[...].astype(BF)


class Incoming:
    def __init__(self, links, me, src, mid, dst):
        y, x, c, z = me
        partner = dev(y, x, 1 - c, z)
        self.swap = [links.later(src.at[i, pl.ds((1 - c) * 128, 128)], mid.at[2 * c + i], partner) for i in (0, 1)]
        send, recv = links.take(4), links.take(4)
        self.sends, self.kept, self.got = [], [], []
        m = links.m
        links.m += 1
        for w in range(4):
            d = dst.at[0, z]
            for ok, s in ((c == w // 2, src.at[w % 2, pl.ds(c * 128, 128)]), (c != w // 2, mid.at[w])):
                away, here = both(ok, z != w), both(ok, z == w)
                q = links.copy(s, d, dev(y, x, c, w), send + w, recv + z)
                self.sends.append((q, away))
                links.open.append((q, away))
                self.kept.append((pltpu.make_async_copy(s, d, links.local.at[m]), here))
        for zz in range(4):
            d = dst.at[0, zz]
            self.got.append((links.copy(d, d, dev(y, x, c, zz), send, recv + zz), z != zz))
        self.pair = links.later(dst.at[0], dst.at[1], partner)

    def begin(self):
        for q in self.swap:
            q.start()

    def send(self):
        for q in self.swap:
            q.wait_recv()
        for q, ok in self.sends + self.kept:
            pl.when(ok)(q.start)

    def arrive(self):
        for q, ok in self.kept:
            pl.when(ok)(q.wait)
        for q, ok in self.got:
            pl.when(ok)(q.wait_recv)
        self.pair.start()

    def finish(self):
        self.pair.wait_recv()


def disperse(links, single, bundle, me, route):
    y, x, c, z = me
    to_x, to_y = dev(y, 1 - x, c, z), dev(1 - y, x, c, z)
    mine = y * 2 + x
    if route == 0:
        two, three, other = to_y, to_x, (1 - y) * 2 + x
    else:
        two, three, other = to_x, to_y, y * 2 + 1 - x
    over_z = [links.later(single(mine, z), single(mine, z), dev(y, x, c, (z + k) % 4)) for k in (1, 2, 3)]
    cross = links.later(bundle(mine), bundle(mine), two)
    last = [links.later(bundle(mine), bundle(mine), three), links.later(bundle(other), bundle(other), three)]

    def start():
        for q in over_z:
            q.start()

    def first():
        for q in over_z:
            q.wait_recv()
        cross.start()
        last[0].start()

    def second():
        cross.wait_recv()
        last[1].start()

    def finish():
        for q in last:
            q.wait_recv()
    return start, first, second, finish


FORE_PIECES = (
    ("gu", 6, 1),
    ("qkv", 0, 1),
    ("gu", 7, 0),
    ("o", 0, 0),
    ("gu", 1, 0),
    ("gu", 0, 1),
    ("qkv", 1, 1),
    ("gu", 2, 0),
    ("gu", 5, 0),
    ("d", 3, 0),
    ("gu", 4, 1),
    ("d", 0, 1),
    ("gu", 3, 1),
    ("d", 2, 1),
    ("d", 1, 0),
)
FORE_ORDER = (
    ((17, 0), (0, 0), (1, 0), (2, 0), (3, 0), (4, 0), (5, 0), (6, 0), (15, 0), (7, 0), (8, 0), (9, 0), (10, 0),
     (11, 0), (12, 0), (13, 0), (14, 0), (17, 1), (17, 2), (17, 3), (0, 1), (0, 2), (1, 1), (0, 3), (2, 1), (1, 2),
     (3, 1), (4, 1), (2, 2), (5, 1), (1, 3), (6, 1), (3, 2), (2, 3), (4, 2), (5, 2), (6, 2), (3, 3), (5, 3),
     (4, 3), (15, 1), (7, 1), (6, 3), (15, 2),),
    ((7, 2), (8, 1), (9, 1)), (), ((10, 1),), (), (), ((7, 3), (8, 2), (11, 1)), (), (), (), ((9, 2), (12, 1)), (),
    (), (), ((13, 1),), (), (), ((10, 2), (14, 1), (16, 0)), ((8, 3), (11, 2), (9, 3), (10, 3)), ((12, 2), (14, 2)),
    ((11, 3), (13, 2)), ((16, 1), (12, 3)), ((13, 3), (14, 3), (16, 2)),
)


def rotary_tables(tab_cos, tab_sin, cos, sin):
    lane = lax.broadcasted_iota(jnp.int32, (128, 128), 1)
    sign = jnp.where(lane % HD < HD // 2, -1.0, 1.0)
    for i in range(8):
        a, b = tab_cos[128 + i:129 + i, :], tab_sin[128 + i:129 + i, :]
        cos[128 * i:128 * i + 128, :] = tab_cos[0:128, :] * a - tab_sin[0:128, :] * b
        sin[128 * i:128 * i + 128, :] = sign * (tab_sin[0:128, :] * a + tab_cos[0:128, :] * b)


def fore_kernel(tok, cot, wq, wk, wv, wg, wu, wo, wd, g0, g1, g2, g3, species, count, weight,
                tab_cos, tab_sin, *rest):
    (oqkv, ogu, oo, od, xh, cw, gvo, n1o, qo, ko, vo, atto, lseo, n2o, mido, gateo, upo, hido, coso, sino,
     own_qkv, oth_qkv, own_gu, oth_gu, gp, cos, sin,
     tmid, cmid, gains, gv, xw, w3, n1, q, k, v, att, lse, wos, sent, came, mid, n2, wgs, wus,
     gate, up, hid, send, recv, local) = rest
    me = y, x, c, z = place()
    yx = y * 2 + x
    partner = dev(y, x, 1 - c, z)

    def prepare():
        def columns(src, own, oth, width, base, stride):
            for g in range(4):
                lanes = pl.ds(base + stride * g, width)
                own[:, lanes] = src[:, pl.ds(pl.multiple_of((2 * g + c) * width, width), width)]
                oth[:, lanes] = src[:, pl.ds(pl.multiple_of((2 * g + 1 - c) * width, width), width)]
        for j, src in enumerate((wq, wk, wv)):
            columns(src, own_qkv, oth_qkv, 128, 128 * j, 384)
        for j, src in enumerate((wg, wu)):
            columns(src, own_gu, oth_gu, 512, 2048 * j, 512)
        gp[...] = jnp.zeros_like(gp)
        for i, src in enumerate((g0, g1, g2, g3)):
            gp[i:i + 1, 0:32] = src[...].astype(F32)
        gp[...] = pltpu.roll(gp[...], z * 32, 1)
        lane = lax.broadcasted_iota(jnp.int32, (1, 128), 1)
        row = jnp.zeros((1, 128), F32)
        for i in (0, 1):
            n = jnp.full((1, 128), count[species[i]].astype(F32), F32)
            row = jnp.where(lane == i, weight[species[i]] * lax.rsqrt(n / 400.0), row)
        gp[4:5, :] = jnp.where(z == 0, row, jnp.zeros_like(row))
    met = greet(y, x, c, z)
    prepare()
    met()
    links = Links(send, recv, local)
    tin, cin = Incoming(links, me, tok, tmid, xw), Incoming(links, me, cot, cmid, cw)
    tin.begin()
    swaps = [links.to(gp, gains.at[yx, c, z], partner), links.to(oth_qkv, oqkv.at[yx, c, z], partner),
             links.to(oth_gu, ogu.at[yx, c, z], partner)]
    loc = [links.here(gp, gains.at[yx, c, z]), links.here(own_qkv, oqkv.at[yx, c, z]),
           links.here(own_gu, ogu.at[yx, c, z]), links.here(wo, oo.at[yx, z]), links.here(wd, od.at[yx, z])]
    work = []
    for name, index, route in FORE_PIECES:
        if name in ("qkv", "gu"):
            arr, cols = (oqkv, 768) if name == "qkv" else (ogu, 512)
            lanes = pl.ds(index * cols, cols)
            work.append(disperse(links, lambda i, zz, arr=arr, lanes=lanes: arr.at[i, :, zz, :, lanes],
                                 lambda i, arr=arr, lanes=lanes: arr.at[i, :, :, :, lanes], me, route))
        else:
            arr = oo if name == "o" else od
            rows = pl.ds(index * 32, 32)
            work.append(disperse(links, lambda i, zz, arr=arr, rows=rows: arr.at[i, zz, rows],
                                 lambda i, arr=arr, rows=rows: arr.at[i, :, rows], me, route))

    def later():
        cin.begin()
        cin.send()
    work += [(tin.send, tin.arrive, tin.finish), (later, cin.arrive, cin.finish),
             disperse(links, lambda i, zz: gains.at[i, :, zz], lambda i: gains.at[i], me, 1)]
    swap = links.wanted(sent, came, partner)
    share = links.later(n2.at[pl.ds(0, 512)], n2.at[pl.ds(512, 512)], partner)
    for e in loc:
        e.wait()
    for e in swaps:
        e.wait_recv()

    def comm(slot):
        for i, stage in FORE_ORDER[slot]:
            work[i][stage]()

    keep = []

    def put(src, dst):
        keep.append(links.here(src, dst))
    comm(0)
    wload = links.here(oqkv, w3)
    rotary_tables(tab_cos, tab_sin, cos, sin)
    put(cos, coso)
    put(sin, sino)
    wload.wait()
    for i in range(4):
        for j in (0, 1):
            gv[:, pl.ds((2 * i + j) * 128, 128)] = (gains[i, j, 0] + gains[i, j, 1]) + (gains[i, j, 2] + gains[i, j, 3])

    def rows_of(step):
        lax.fori_loop(0, 4, lambda r, _: (step(r), 0)[1], 0)
    rows_of(lambda r: project_step(xw, gv, w3, cos, sin, n1, q, k, v, r))
    for a, b in ((gv, gvo), (n1, n1o), (q, qo), (k, ko), (v, vo), (xw.at[0], xh)):
        put(a, b)
    comm(1)

    def step(t, _):
        attend_step(q, k, v, att, lse, t // 4, t % 4)
        for slot in range(2, 17):
            if FORE_ORDER[slot]:
                pl.when(t == slot - 2)(lambda slot=slot: comm(slot))
        return 0
    lax.fori_loop(0, 16, step, 0)
    comm(17)
    wload = links.here(oo, wos)
    put(att, atto)
    put(lse, lseo)
    wload.wait()

    def terms(r, out, first):
        rows = pl.ds(pl.multiple_of(r * 256, 256), 256)
        out[rows, :] = jnp.dot(att[pl.ds(pl.multiple_of(first + r * 256, 256), 256), :], wos[...].reshape(512, 1024),
                               preferred_element_type=F32)
    lax.fori_loop(0, 2, lambda r, _: (terms(r, sent, 512), 0)[1], 0)
    swap.start()
    lax.fori_loop(0, 2, lambda r, _: (terms(r, mid, 0), 0)[1], 0)
    swap.wait()

    def second_norm(r):
        rows = pl.ds(pl.multiple_of(r * 128, 128), 128)
        u = xw[0, r].astype(F32) + (mid[rows, :] + came[rows, :])
        mid[rows, :] = u
        d = u - jnp.mean(u, axis=-1, keepdims=True)
        scaling = lax.rsqrt(jnp.mean(d * d, axis=-1, keepdims=True) + 1e-05)
        n2[rows, :] = (d * scaling * gv[2:3, :] + gv[3:4, :]).astype(BF)
    rows_of(second_norm)
    share.start()
    put(mid, mido)
    comm(18)
    share.wait_recv()
    put(n2, n2o)
    for j in range(4):
        if j:
            comm(18 + j)
        lanes = pl.ds(512 * j, 512)
        lg = links.here(ogu.at[:, :, :, :, lanes], wgs)
        lu = links.here(ogu.at[:, :, :, :, pl.ds(2048 + 512 * j, 512)], wus)
        lg.wait()
        lu.wait()

        def hidden_units(r, lanes=lanes):
            rows = pl.ds(pl.multiple_of(r * 256, 256), 256)
            n = n2[rows, :]
            a = jnp.dot(n, wgs[...].reshape(1024, 512), preferred_element_type=F32)
            b = jnp.dot(n, wus[...].reshape(1024, 512), preferred_element_type=F32)
            hid[rows, lanes] = (a * jax.nn.sigmoid(a) * b).astype(BF)
            gate[rows, lanes] = a.astype(BF)
            up[rows, lanes] = b.astype(BF)
        rows_of(hidden_units)
        for a, b in ((hid, hido), (gate, gateo), (up, upo)):
            put(a.at[:, lanes], b.at[:, lanes])
    comm(22)
    for e in keep:
        e.wait()
    links.drain()


def fore(*args):
    S = jax.ShapeDtypeStruct
    V = pltpu.VMEM
    table = [V((1024, 128), F32)] * 2
    specs = [ANY] * 2 + [VM] * 11 + [pl.BlockSpec(memory_space=pltpu.SMEM)] * 3 + [VM] * 2
    return pl.pallas_call(
        fore_kernel,
        out_shape=(
            S((4, 2, 4, 32, 1536), BF), S((4, 2, 4, 32, 4096), BF), S((4, 4, 32, 1024), BF), S((4, 4, 128, 1024), BF),
            S((4, 128, 1024), BF), S((2, 4, 128, 1024), BF), S((8, 1024), F32), S((1024, 1024), BF),
            S((1024, 512), BF), S((1024, 512), BF), S((1024, 512), BF), S((1024, 512), BF), S((8, 1024), F32),
            S((1024, 1024), BF), S((512, 1024), F32), S((1024, 2048), BF), S((1024, 2048), BF), S((1024, 2048), BF),
            S((1024, 128), F32), S((1024, 128), F32),
        ),
        in_specs=specs,
        out_specs=[ANY] * 20,
        scratch_shapes=[V((32, 1536), BF)] * 2 + [V((32, 4096), BF)] * 2 + [V((8, 128), F32)] + table + [
            V((4, 128, 1024), BF), V((4, 128, 1024), BF), V((4, 2, 4, 8, 128), F32), V((8, 1024), F32),
            V((2, 4, 128, 1024), BF), V((4, 2, 4, 32, 1536), BF), V((1024, 1024), BF),
            V((1024, 512), BF), V((1024, 512), BF), V((1024, 512), BF), V((1024, 512), BF), V((8, 1024), F32),
            V((4, 4, 32, 1024), BF), V((512, 1024), F32), V((512, 1024), F32), V((512, 1024), F32),
            V((1024, 1024), BF), V((4, 2, 4, 32, 512), BF), V((4, 2, 4, 32, 512), BF),
            V((1024, 2048), BF), V((1024, 2048), BF), V((1024, 2048), BF),
            pltpu.SemaphoreType.DMA((200,)),
            pltpu.SemaphoreType.DMA((200,)),
            pltpu.SemaphoreType.DMA((72,)),
        ],
        compiler_params=pltpu.CompilerParams(collective_id=0, has_side_effects=True, vmem_limit_bytes=67043328),
    )(*args)


PIECES = (
    ("d", 1, 1),
    ("gu", 2, 1),
    ("gu", 4, 0),
    ("gu", 1, 1),
    ("gu", 0, 0),
    ("qkv", 1, 1),
    ("gu", 7, 0),
    ("d", 3, 0),
    ("o", 0, 1),
    ("d", 0, 1),
    ("qkv", 2, 1),
    ("gu", 6, 1),
    ("qkv", 0, 0),
    ("d", 2, 1),
    ("gu", 5, 0),
    ("qkv", 3, 1),
    ("gu", 3, 0),
)
SHAPES = {"d": (4, 32, 1024), "o": (4, 32, 1024), "gu": (2, 4, 32, 512), "qkv": (2, 4, 32, 384)}
ORDER = (
    (), ((0, 0), (7, 0)), ((0, 1), (2, 0), (4, 0), (7, 1)), ((0, 2), (3, 0), (7, 2)),
    ((0, 3), (1, 0), (2, 1), (3, 1), (7, 3)), ((0, 4), (1, 1), (4, 1), (6, 0), (7, 4), (9, 0), (14, 0)),
    ((0, 5), (1, 2), (2, 2), (7, 5), (3, 2)), ((2, 3), (4, 2), (6, 1), (1, 3), (8, 0), (16, 0)),
    ((1, 4), (2, 4), (3, 3), (17, 0), (4, 3), (9, 1), (14, 1)), ((6, 2),), (), (), ((8, 1), (13, 0), (16, 1)),
    ((12, 0),), (), (), ((3, 4), (6, 3)), ((1, 5), (2, 5), (14, 2), (9, 2)), ((5, 0),),
    ((13, 1), (8, 2), (14, 3), (9, 3)), (), ((12, 1), (4, 4), (8, 3)), ((6, 4),), ((14, 4), (10, 0)),
    ((17, 1), (16, 2), (16, 3), (9, 4)), ((3, 5), (4, 5), (5, 1), (11, 0), (6, 5), (13, 2), (8, 4), (13, 3), (16, 4)),
    (), ((14, 5), (5, 2), (5, 3), (13, 4)), ((9, 5), (12, 2), (12, 3), (5, 4), (15, 0)),
    ((8, 5), (5, 5), (13, 5), (16, 5), (18, 0), (10, 1), (11, 1), (12, 4), (19, 0), (15, 1), (10, 2), (11, 2),
     (19, 1), (19, 2), (15, 2), (10, 3), (11, 3), (18, 1), (12, 5), (19, 3), (10, 4), (15, 3), (10, 5), (11, 4),
     (15, 4), (11, 5), (15, 5),),

)


def total_over_devices(links, me, acc, got):
    y, x, c, z = me
    hops = [links.wanted(acc, got.at[i], d) for i, d in
            enumerate((dev(y, x, 1 - c, z), dev(y, 1 - x, c, z), dev(1 - y, x, c, z)))]
    over_z = [links.wanted(acc, got.at[2 + k], dev(y, x, c, (z + k) % 4)) for k in (1, 2, 3)]

    def settle(i):
        hops[i].wait()
        acc[...] += got[i]

    def chip():
        hops[0].start()
        settle(0)
        hops[1].start()

    def second():
        settle(1)
        hops[2].start()

    def third():
        settle(2)
        for q in over_z:
            q.start()

    def last():
        for q in over_z:
            q.wait()
        acc[...] += got[3] + (got[4] + got[5])
    return chip, second, third, last


def rows_dot(a, b):
    return lax.dot_general(a, b, (((0,), (0,)), ((), ())), preferred_element_type=F32)


def each(count, step):
    def body(r, _):
        step(r)
        return 0
    lax.fori_loop(0, count, body, 0)


def block(i, size):
    return pl.ds(pl.multiple_of(i * size, size), size)


def norm_parts(u):
    d = u - jnp.mean(u, axis=-1, keepdims=True)
    scaling = lax.rsqrt(jnp.mean(d * d, axis=-1, keepdims=True) + 1e-05)
    return d * scaling, scaling


def norm_back(upstream, normed, scaling):
    return scaling * (upstream - jnp.mean(upstream, axis=-1, keepdims=True)
                      - normed * jnp.mean(upstream * normed, axis=-1, keepdims=True))


def back_kernel(cw, hido, od, n2o, gateo, upo, ogu, mido, oo, atto, qo, ko, vo, lseo, n1o, oqkv, xh,
                cos, sin, gv, *rest):
    fqkv, fgu, fo, fd, fgain, out_w, ig_w = rest[:7]
    scratch = list(rest[7:])
    (gd, ggu, go, gw, mg, sent, came, mlow, ag, out16, ig, gacc, ggot, send, recv, local, ready) = scratch[-17:]
    me = y, x, c, z = place()
    partner = dev(y, x, 1 - c, z)
    met = greet(y, x, c, z)
    links = Links(send, recv, local)
    work = []
    finals = []
    for name, index, route in PIECES:
        bufs = [scratch.pop(0) for _ in range(6)]
        if name in ("qkv", "gu"):
            src, dst = (gw, fqkv) if name == "qkv" else (ggu, fgu)
            cols = SHAPES[name][3]
            lanes = pl.ds(index * cols, cols)

            def at(yy, xx, src=src, index=index):
                return src.at[index, yy * 2 + xx]

            def deliver(total, dst=dst, lanes=lanes):
                there = links.later(total.at[1 - c], dst.at[c, :, lanes], partner)
                here = links.here_later(total.at[c], dst.at[c, :, lanes])
                finals.extend((there.wait_recv, here.wait))
                return there, here
        else:
            src, dst = (gd, fd) if name == "d" else (go, fo)
            rows = pl.ds(index * 32, 32)

            def at(yy, xx, src=src, rows=rows):
                return src.at[yy * 2 + xx, :, rows]

            def deliver(total, dst=dst, rows=rows):
                here = links.here_later(total, dst.at[rows])
                finals.append(here.wait)
                return (here,)
        work.append(collect(links, at, me, route, bufs, deliver))
    o1 = Outgoing(links, me, out16, out_w)
    o2 = Outgoing(links, me, ig, ig_w)
    work += [(o1.start, o1.finish), (o2.start, o2.finish), total_over_devices(links, me, gacc, ggot)]
    swaps = [links.wanted(sent, came, partner) for _ in range(3)]
    share = links.later(mlow.at[0], mlow.at[1], partner)

    def comm(slot):
        for i, stage in ORDER[slot]:
            work[i][stage]()

    def swap(n):
        if n:
            pl.semaphore_wait(ready, 1)
        swaps[n].start()

    def read(n):
        if n < 2:
            pl.semaphore_signal(ready, inc=1, device_id=partner, device_id_type=MESH)

    gacc[...] = jnp.zeros_like(gacc)
    lane = lax.broadcasted_iota(jnp.int32, (1, 1024), 1)
    here = (2 * (y * 2 + x) + z // 2) * 128 + z % 2
    factor = jnp.sum(jnp.where(lane == here, gv[4:5, :], 0.0), axis=1, keepdims=True)

    def hidden_layer(low):
        a = links.here(cw, low)

        def down(hv):
            b = links.here(hido, hv)
            a.wait()

            def scale(i):
                low[i // 4, i % 4] = (factor * low[i // 4, i % 4].astype(F32)).astype(BF)
            each(8, scale)
            b.wait()

            def weights(r):
                u = rows_dot(hv[:, block(r, 256)], low[...].reshape(1024, 1024))
                gd[r // 2, pl.ds((r % 2) * 2, 2)] = u.astype(BF).reshape(2, 128, 1024)
            each(8, weights)
            met()
            comm(0)
        pl.run_scoped(down, pltpu.VMEM((1024, 2048), BF))

        def units(n2, gate, up, dgate, dup, wg, wu, wd):
            a = links.here(n2o, n2)
            for j in range(4):
                lanes = pl.ds(512 * j, 512)
                got = [links.here(od.at[j], wd), links.here(gateo.at[:, lanes], gate), links.here(upo.at[:, lanes], up),
                       links.here(ogu.at[:, :, :, :, lanes], wg),
                       links.here(ogu.at[:, :, :, :, pl.ds(2048 + 512 * j, 512)], wu)]
                comm(1 + j)
                for q in got:
                    q.wait()

                def grads(r):
                    rows = block(r, 256)
                    g = dot_t(low[r // 2, pl.ds((r % 2) * 2, 2)].reshape(256, 1024), wd[...].reshape(512, 1024))
                    a, b = gate[rows, :].astype(F32), up[rows, :].astype(F32)
                    t = jax.nn.sigmoid(a)
                    dgate[rows, :] = (g * b * t * (1.0 + a * (1.0 - t))).astype(BF)
                    dup[rows, :] = (g * a * t).astype(BF)
                each(4, grads)
                if j == 0:
                    a.wait()

                def weights(r):
                    n = n2[:, block(r, 256)]
                    ggu[j, r] = rows_dot(n, dgate[...]).astype(BF).reshape(2, 4, 32, 512)
                    ggu[4 + j, r] = rows_dot(n, dup[...]).astype(BF).reshape(2, 4, 32, 512)
                each(4, weights)

                def terms(r, out, first):
                    rows = pl.ds(pl.multiple_of(first + r * 256, 256), 256)
                    u = (dot_t(dgate[rows, :], wg[...].reshape(1024, 512))
                         + dot_t(dup[rows, :], wu[...].reshape(1024, 512)))
                    dst = block(r, 256)
                    out[dst, :] = u if j == 0 else out[dst, :] + u
                each(2, lambda r: terms(r, sent, 512))
                if j == 3:
                    swap(0)
                each(2, lambda r: terms(r, mg, 0))
        pl.run_scoped(units, pltpu.VMEM((1024, 1024), BF), *[pltpu.VMEM((1024, 512), BF)] * 4,
                      *[pltpu.VMEM((4, 2, 4, 32, 512), BF)] * 2, pltpu.VMEM((4, 128, 1024), BF))
    pl.run_scoped(hidden_layer, pltpu.VMEM((2, 4, 128, 1024), BF))
    comm(5)

    def second_norm(mid, cot):
        a, b = links.here(mido, mid), links.here(cw.at[0], cot)
        a.wait()
        b.wait()
        swaps[0].wait()

        def part(r):
            rows = block(r, 128)
            gn = mg[rows, :] + came[rows, :]
            normed, scaling = norm_parts(mid[rows, :])
            gacc[2:3, :] += jnp.sum(gn * normed, axis=0, keepdims=True)
            gacc[3:4, :] += jnp.sum(gn, axis=0, keepdims=True)
            u = factor * cot[r].astype(F32) + norm_back(gn * gv[2:3, :], normed, scaling)
            mg[rows, :] = u
            mlow[0, r] = u.astype(BF)
        each(4, part)
        read(0)
        share.start()
    pl.run_scoped(second_norm, pltpu.VMEM((512, 1024), F32), pltpu.VMEM((4, 128, 1024), BF))
    comm(6)

    def out_layer(w, att):
        a, b = links.here(oo, w), links.here(atto, att)
        a.wait()
        b.wait()
        share.wait_recv()

        def weights(r):
            u = rows_dot(att[:, block(r, 256)], mlow[...].reshape(1024, 1024))
            go[pl.ds(2 * r, 2)] = u.astype(BF).reshape(2, 4, 32, 1024)
        each(2, weights)

        def grads(r):
            u = dot_t(mlow[r // 2, pl.ds((r % 2) * 2, 2)].reshape(256, 1024), w[...].reshape(512, 1024))
            ag[block(r, 256), :] = u.astype(BF)
        each(4, grads)
    pl.run_scoped(out_layer, pltpu.VMEM((4, 4, 32, 1024), BF), pltpu.VMEM((1024, 512), BF))
    comm(7)

    def output(hv, w, mid):
        got = [links.here(hido, hv), links.here(od, w), links.here(mido, mid)]
        for q in got:
            q.wait()

        def term(r, first):
            return jnp.dot(hv[pl.ds(pl.multiple_of(first + r * 256, 256), 256), :], w[...].reshape(2048, 1024),
                           preferred_element_type=F32)

        def theirs(r):
            sent[block(r, 256), :] = term(r, 512)
        each(2, theirs)
        swap(1)

        def mine(r):
            mid[block(r, 256), :] += term(r, 0)
        each(2, mine)
        swaps[1].wait()

        def total(r):
            out16[r] = (mid[block(r, 128), :] + came[block(r, 128), :]).astype(BF)
        each(4, total)
        read(1)
    pl.run_scoped(output, pltpu.VMEM((1024, 2048), BF), pltpu.VMEM((4, 4, 128, 1024), BF), pltpu.VMEM((512, 1024), F32))

    def attention(dqkv):
        def heads(q, k, v, lse, n1, dka, dva):
            got = [links.here(a, b) for a, b in ((qo, q), (ko, k), (vo, v), (lseo, lse), (n1o, n1))]
            for e in got:
                e.wait()

            def step(t):
                for slot in range(20):
                    if ORDER[8 + slot]:
                        pl.when(t == slot)(lambda slot=slot: comm(8 + slot))
                g, i = t // 5, t % 5

                @pl.when(i < 4)
                def _():
                    attend_back_step(q, k, v, ag, lse, cos, sin, dqkv, dka, dva, g, i)

                @pl.when(i == 4)
                def _():
                    u = rows_dot(n1[...], dqkv[:, pl.ds(pl.multiple_of(g * 384, 128), 384)])
                    gw[g] = u.astype(BF).reshape(4, 2, 4, 32, 384)
            each(20, step)
        pl.run_scoped(heads, *[pltpu.VMEM((1024, 512), BF)] * 3, pltpu.VMEM((8, 1024), F32),
                      pltpu.VMEM((1024, 1024), BF), *[pltpu.VMEM((1024, 128), F32)] * 2)

        def first_norm(w, tokens, mine):
            got = [links.here(oqkv, w), links.here(xh, tokens)]
            comm(28)
            for e in got:
                e.wait()

            def term(r, out, first):
                out[block(r, 256), :] = dot_t(dqkv[pl.ds(pl.multiple_of(first + r * 256, 256), 256), :],
                                              w[...].reshape(1024, 1536))
            each(2, lambda r: term(r, sent, 512))
            swap(2)
            each(2, lambda r: term(r, mine, 0))
            swaps[2].wait()

            def part(r):
                rows = block(r, 128)
                gn = mine[rows, :] + came[rows, :]
                normed, scaling = norm_parts(tokens[r].astype(F32))
                gacc[0:1, :] += jnp.sum(gn * normed, axis=0, keepdims=True)
                gacc[1:2, :] += jnp.sum(gn, axis=0, keepdims=True)
                ig[r] = (mg[rows, :] + norm_back(gn * gv[0:1, :], normed, scaling)).astype(BF)
            each(4, part)
        pl.run_scoped(first_norm, pltpu.VMEM((4, 2, 4, 32, 1536), BF), pltpu.VMEM((4, 128, 1024), BF),
                      pltpu.VMEM((512, 1024), F32))
    pl.run_scoped(attention, pltpu.VMEM((1024, 1536), BF))
    comm(29)
    finals.append(links.here(gacc, fgain).wait)
    for f in finals:
        f()
    links.drain()


def back(*args):
    scratch = []
    for name, index, route in PIECES:
        scratch += reduce_shapes(SHAPES[name])
    return pl.pallas_call(
        back_kernel,
        out_shape=(
            jax.ShapeDtypeStruct((2, 32, 1536), F32),
            jax.ShapeDtypeStruct((2, 32, 4096), F32),
            jax.ShapeDtypeStruct((32, 1024), F32),
            jax.ShapeDtypeStruct((128, 1024), F32),
            jax.ShapeDtypeStruct((8, 1024), F32),
            jax.ShapeDtypeStruct((2, 2, 128, 1024), BF),
            jax.ShapeDtypeStruct((2, 2, 128, 1024), BF),
        ),
        in_specs=[ANY] * 17 + [VM] * 3,
        out_specs=[ANY] * 7,
        scratch_shapes=scratch + [
            pltpu.VMEM((4, 4, 128, 1024), BF),
            pltpu.VMEM((8, 4, 2, 4, 32, 512), BF),
            pltpu.VMEM((4, 4, 32, 1024), BF),
            pltpu.VMEM((4, 4, 2, 4, 32, 384), BF),
            pltpu.VMEM((512, 1024), F32),
            pltpu.VMEM((512, 1024), F32),
            pltpu.VMEM((512, 1024), F32),
            pltpu.VMEM((2, 4, 128, 1024), BF),
            pltpu.VMEM((1024, 512), BF),
            pltpu.VMEM((4, 128, 1024), BF),
            pltpu.VMEM((4, 128, 1024), BF),
            pltpu.VMEM((8, 1024), F32),
            pltpu.VMEM((6, 8, 1024), F32),
            pltpu.SemaphoreType.DMA((192,)),
            pltpu.SemaphoreType.DMA((192,)),
            pltpu.SemaphoreType.DMA((96,)),
            pltpu.SemaphoreType.REGULAR,
        ],
        compiler_params=pltpu.CompilerParams(collective_id=1, has_side_effects=True, vmem_limit_bytes=67043328),
    )(*args)


def finish_kernel(fqkv, fgu, fo, fd, fgain, out_w, ig_w, out, ig, gq, gk, gv, go, gg, gu, gd, *gains):
    for n in (0, 1):
        for g in range(4):
            for j, dst in enumerate((gq, gk, gv)):
                dst[:, pl.ds(128 * (2 * g + n), 128)] = fqkv[n, :, pl.ds(384 * g + 128 * j, 128)]
            for j, dst in enumerate((gg, gu)):
                dst[:, pl.ds(512 * (2 * g + n), 512)] = fgu[n, :, pl.ds(2048 * j + 512 * g, 512)]
    go[...] = fo[...]
    gd[...] = fd[...]

    def rows(i):
        out[i // 2, pl.ds(pl.multiple_of((i % 2) * 128, 128), 128)] = out_w[i // 2, i % 2]
        ig[i // 2, pl.ds(pl.multiple_of((i % 2) * 128, 128), 128)] = ig_w[i // 2, i % 2].astype(F32)
    each(4, rows)
    first = (lax.axis_index("dp") * 4 + lax.axis_index("seq")) * 32
    mine = pltpu.roll(fgain[...], (1024 - first) % 1024, 1)
    for i in range(4):
        gains[i][...] = mine[i:i + 1, 0:32]


def finish(*args):
    S = jax.ShapeDtypeStruct
    return pl.pallas_call(
        finish_kernel,
        out_shape=(S((2, 256, 1024), BF), S((2, 256, 1024), F32)) + (S((32, 1024), F32),) * 4
        + (S((32, 4096), F32),) * 2 + (S((128, 1024), F32),) + (S((1, 32), F32),) * 4,
        in_specs=[VM] * 7,
        out_specs=[VM] * 13,
        compiler_params=pltpu.CompilerParams(vmem_limit_bytes=VMEM_BYTES),
    )(*args)


def angle_tables(c):
    lane = jnp.arange(128, dtype=jnp.int32)
    freqs = 10000.0 ** (-2.0 * (lane % 32).astype(jnp.float32) / HD)
    block = jnp.arange(8, dtype=jnp.int32)
    far = (block % 4) * 256 + jnp.where(block < 4, c, 1 - c) * 128
    rows = jnp.concatenate([jnp.arange(128, dtype=jnp.int32), far]).astype(jnp.float32)
    angle = rows[:, None] * freqs[None, :]
    cos, sin = jnp.cos(angle), jnp.sin(angle)
    return cos, sin


def paired(
    tokens,
    cotangent,
    species_index,
    species_count,
    loss_weight,
    query_weight,
    key_weight,
    value_weight,
    out_weight,
    gate_weight,
    up_weight,
    down_weight,
    mixer_gain,
    mixer_shift,
    feeder_gain,
    feeder_shift,
):
    dp, z = lax.axis_index("dp"), lax.axis_index("seq")
    c = dp % 2
    (wqkv, wgu, wo, wd, xh, cw, gv, norm_one, q, k, v, attended, lse, norm_two, middle, gate, upward, hidden,
     cos, sin) = fore(
        tokens, cotangent, query_weight, key_weight, value_weight, gate_weight, up_weight, out_weight, down_weight,
        mixer_gain.reshape(1, 32), mixer_shift.reshape(1, 32), feeder_gain.reshape(1, 32), feeder_shift.reshape(1, 32),
        species_index, species_count, loss_weight, *angle_tables(c))
    parts = back(
        cw, hidden, wd, norm_two, gate, upward, wgu, middle, wo, attended, q, k, v, lse, norm_one, wqkv, xh,
        cos, sin, gv)
    done = finish(*parts)
    return done[:9] + tuple(g.reshape(32) for g in done[9:])


def matmul(left, right):
    return jnp.dot(left, right, preferred_element_type=jnp.float32)


def weight_term(left, right):
    return lax.dot_general(
        left, right, (((0,), (0,)), ((), ())), preferred_element_type=jnp.float32
    )


def through(left, weight):
    return lax.dot_general(
        left, weight, (((1,), (1,)), ((), ())), preferred_element_type=jnp.float32
    )


def normalize(values):
    center = jnp.mean(values, axis=-1, keepdims=True)
    centered = values - center
    variance = jnp.mean(centered * centered, axis=-1, keepdims=True)
    scaling = lax.rsqrt(variance + 1e-05)
    return (centered * scaling, scaling)


def plain_norm_back(upstream, normed, scaling):
    first = jnp.mean(upstream, axis=-1, keepdims=True)
    second = jnp.mean(upstream * normed, axis=-1, keepdims=True)
    return scaling * (upstream - first - normed * second)


def tables(start, count):
    half = HD // 2
    positions = (start + jnp.arange(count, dtype=jnp.int32)).astype(jnp.float32)
    freqs = 10000.0 ** (-2.0 * jnp.arange(half, dtype=jnp.float32) / HD)
    angle = positions[:, None] * freqs[None, :]
    return (jnp.cos(angle)[:, None, :], jnp.sin(angle)[:, None, :])


def rotate(values, cosine, sine):
    half = HD // 2
    first = values[..., :half]
    second = values[..., half:]
    return jnp.concatenate(
        [first * cosine - second * sine, second * cosine + first * sine], axis=-1
    )


def attend_head(operands):
    query_head, key_head, value_head = operands
    scores = jnp.einsum(
        "wtd,wsd->wts", query_head, key_head, preferred_element_type=jnp.float32
    ) * HD ** (-0.5)
    peak = jnp.max(scores, axis=-1, keepdims=True)
    raised = jnp.exp(scores - peak)
    total = jnp.sum(raised, axis=-1, keepdims=True)
    probs = (raised / total).astype(jnp.bfloat16)
    result = jnp.einsum("wts,wsd->wtd", probs, value_head, preferred_element_type=jnp.float32)
    return (result, (peak + jnp.log(total))[..., 0])


def head_back(operands):
    query_head, key_head, value_head, upstream, log_total = operands
    scores = jnp.einsum(
        "wtd,wsd->wts", query_head, key_head, preferred_element_type=jnp.float32
    ) * HD ** (-0.5)
    probs = jnp.exp(scores - log_total[..., None])
    prob_grads = jnp.einsum(
        "wtd,wsd->wts", upstream, value_head, preferred_element_type=jnp.float32
    )
    inner = jnp.sum(probs * prob_grads, axis=-1, keepdims=True)
    score_grads = (probs * (prob_grads - inner)).astype(jnp.bfloat16)
    query_grad = jnp.einsum(
        "wts,wsd->wtd", score_grads, key_head, preferred_element_type=jnp.float32
    ) * HD ** (-0.5)
    key_grad = jnp.einsum(
        "wts,wtd->wsd", score_grads, query_head, preferred_element_type=jnp.float32
    ) * HD ** (-0.5)
    value_grad = jnp.einsum(
        "wts,wtd->wsd", probs.astype(jnp.bfloat16), upstream, preferred_element_type=jnp.float32
    )
    return (query_grad, key_grad, value_grad)


def general(
    tokens,
    cotangent,
    species_index,
    species_count,
    loss_weight,
    query_weight,
    key_weight,
    value_weight,
    out_weight,
    gate_weight,
    up_weight,
    down_weight,
    mixer_gain,
    mixer_shift,
    feeder_gain,
    feeder_shift,
):
    gathered = (
        lax.all_gather(query_weight, ("dp", "seq"), axis=0, tiled=True),
        lax.all_gather(key_weight, ("dp", "seq"), axis=0, tiled=True),
        lax.all_gather(value_weight, ("dp", "seq"), axis=0, tiled=True),
        lax.all_gather(out_weight, ("dp", "seq"), axis=0, tiled=True),
        lax.all_gather(gate_weight, ("dp", "seq"), axis=0, tiled=True),
        lax.all_gather(up_weight, ("dp", "seq"), axis=0, tiled=True),
        lax.all_gather(down_weight, ("dp", "seq"), axis=0, tiled=True),
        lax.all_gather(mixer_gain, ("dp", "seq"), axis=0, tiled=True),
        lax.all_gather(mixer_shift, ("dp", "seq"), axis=0, tiled=True),
        lax.all_gather(feeder_gain, ("dp", "seq"), axis=0, tiled=True),
        lax.all_gather(feeder_shift, ("dp", "seq"), axis=0, tiled=True),
    )
    wq, wk, wv, wo, wg, wu, wd, gain_one, shift_one, gain_two, shift_two = gathered
    windows, steps_dev, width = tokens.shape
    rows = windows * steps_dev
    start = lax.axis_index("seq") * steps_dev
    cosine, sine = tables(start, steps_dev)
    inputs = tokens.astype(jnp.float32).reshape(rows, width)
    normed_one, scaling_one = normalize(inputs)
    norm_one = (normed_one * gain_one.astype(jnp.float32) + shift_one.astype(jnp.float32)).astype(
        jnp.bfloat16
    )
    queries = rotate(
        matmul(norm_one, wq).reshape(windows, steps_dev, HEADS, HD), cosine, sine
    ).astype(jnp.bfloat16)
    keys = rotate(matmul(norm_one, wk).reshape(windows, steps_dev, HEADS, HD), cosine, sine).astype(
        jnp.bfloat16
    )
    values = matmul(norm_one, wv).astype(jnp.bfloat16)
    all_keys, all_values = (
        lax.all_gather(keys.reshape(windows, steps_dev, width), "seq", axis=1, tiled=True),
        lax.all_gather(values.reshape(windows, steps_dev, width), "seq", axis=1, tiled=True),
    )
    length = all_keys.shape[1]
    query_heads = queries.transpose(2, 0, 1, 3)
    key_heads = all_keys.reshape(windows, length, HEADS, HD).transpose(2, 0, 1, 3)
    value_heads = all_values.reshape(windows, length, HEADS, HD).transpose(2, 0, 1, 3)
    head_results, log_totals = lax.map(attend_head, (query_heads, key_heads, value_heads))
    attended = head_results.transpose(1, 2, 0, 3).reshape(rows, width).astype(jnp.bfloat16)
    middle = inputs + matmul(attended, wo)
    normed_two, scaling_two = normalize(middle)
    norm_two = (normed_two * gain_two.astype(jnp.float32) + shift_two.astype(jnp.float32)).astype(
        jnp.bfloat16
    )
    gate = matmul(norm_two, wg)
    upward = matmul(norm_two, wu)
    sigma = jax.nn.sigmoid(gate)
    swish = gate * sigma
    hidden = (swish * upward).astype(jnp.bfloat16)
    output = (middle + matmul(hidden, wd)).astype(jnp.bfloat16).reshape(windows, steps_dev, width)
    table = loss_weight * lax.rsqrt(species_count.astype(jnp.float32) / 400.0)
    picks = species_index[:, None] == jnp.arange(table.shape[0], dtype=jnp.int32)[None, :]
    factor = jnp.sum(jnp.where(picks, table[None, :], 0.0), axis=1)
    grad_out = (factor[:, None, None] * cotangent.astype(jnp.float32)).reshape(rows, width)
    regathered = (
        lax.all_gather(query_weight, ("dp", "seq"), axis=0, tiled=True),
        lax.all_gather(key_weight, ("dp", "seq"), axis=0, tiled=True),
        lax.all_gather(value_weight, ("dp", "seq"), axis=0, tiled=True),
        lax.all_gather(out_weight, ("dp", "seq"), axis=0, tiled=True),
        lax.all_gather(gate_weight, ("dp", "seq"), axis=0, tiled=True),
        lax.all_gather(up_weight, ("dp", "seq"), axis=0, tiled=True),
        lax.all_gather(down_weight, ("dp", "seq"), axis=0, tiled=True),
        lax.all_gather(mixer_gain, ("dp", "seq"), axis=0, tiled=True),
        lax.all_gather(mixer_shift, ("dp", "seq"), axis=0, tiled=True),
        lax.all_gather(feeder_gain, ("dp", "seq"), axis=0, tiled=True),
        lax.all_gather(feeder_shift, ("dp", "seq"), axis=0, tiled=True),
    )
    wq, wk, wv, wo, wg, wu, wd, gain_one, shift_one, gain_two, shift_two = regathered
    out_low = grad_out.astype(jnp.bfloat16)
    down_part = weight_term(hidden, out_low)
    hidden_grad = through(out_low, wd)
    gate_grad = (hidden_grad * upward * sigma * (1.0 + gate * (1.0 - sigma))).astype(jnp.bfloat16)
    upward_grad = (hidden_grad * swish).astype(jnp.bfloat16)
    gate_part = weight_term(norm_two, gate_grad)
    upward_part = weight_term(norm_two, upward_grad)
    norm_two_grad = through(gate_grad, wg) + through(upward_grad, wu)
    feeder_gain_part = jnp.sum(norm_two_grad * normed_two, axis=0)
    feeder_shift_part = jnp.sum(norm_two_grad, axis=0)
    middle_grad = grad_out + plain_norm_back(
        norm_two_grad * gain_two.astype(jnp.float32), normed_two, scaling_two
    )
    middle_low = middle_grad.astype(jnp.bfloat16)
    out_part = weight_term(attended, middle_low)
    attended_grad = through(middle_low, wo).astype(jnp.bfloat16)
    upstream_heads = attended_grad.reshape(windows, steps_dev, HEADS, HD).transpose(2, 0, 1, 3)
    query_heads_grad, key_heads_grad, value_heads_grad = lax.map(
        head_back, (query_heads, key_heads, value_heads, upstream_heads, log_totals)
    )
    key_whole = key_heads_grad.transpose(1, 2, 0, 3).reshape(windows, length, width)
    value_whole = value_heads_grad.transpose(1, 2, 0, 3).reshape(windows, length, width)
    key_mine, value_mine = (
        lax.psum_scatter(
            key_whole.astype(jnp.bfloat16), "seq", scatter_dimension=1, tiled=True
        ).astype(jnp.float32),
        lax.psum_scatter(
            value_whole.astype(jnp.bfloat16), "seq", scatter_dimension=1, tiled=True
        ).astype(jnp.float32),
    )
    query_lin_grad = (
        rotate(query_heads_grad.transpose(1, 2, 0, 3), cosine, -sine)
        .reshape(rows, width)
        .astype(jnp.bfloat16)
    )
    key_lin_grad = (
        rotate(key_mine.reshape(windows, steps_dev, HEADS, HD), cosine, -sine)
        .reshape(rows, width)
        .astype(jnp.bfloat16)
    )
    value_lin_grad = value_mine.reshape(rows, width).astype(jnp.bfloat16)
    query_part = weight_term(norm_one, query_lin_grad)
    key_part = weight_term(norm_one, key_lin_grad)
    value_part = weight_term(norm_one, value_lin_grad)
    norm_one_grad = (
        through(query_lin_grad, wq) + through(key_lin_grad, wk) + through(value_lin_grad, wv)
    )
    mixer_gain_part = jnp.sum(norm_one_grad * normed_one, axis=0)
    mixer_shift_part = jnp.sum(norm_one_grad, axis=0)
    input_grad = middle_grad + plain_norm_back(
        norm_one_grad * gain_one.astype(jnp.float32), normed_one, scaling_one
    )
    summed = (
        lax.psum_scatter(query_part, ("dp", "seq"), scatter_dimension=0, tiled=True),
        lax.psum_scatter(key_part, ("dp", "seq"), scatter_dimension=0, tiled=True),
        lax.psum_scatter(value_part, ("dp", "seq"), scatter_dimension=0, tiled=True),
        lax.psum_scatter(out_part, ("dp", "seq"), scatter_dimension=0, tiled=True),
        lax.psum_scatter(gate_part, ("dp", "seq"), scatter_dimension=0, tiled=True),
        lax.psum_scatter(upward_part, ("dp", "seq"), scatter_dimension=0, tiled=True),
        lax.psum_scatter(down_part, ("dp", "seq"), scatter_dimension=0, tiled=True),
        lax.psum_scatter(mixer_gain_part, ("dp", "seq"), scatter_dimension=0, tiled=True),
        lax.psum_scatter(mixer_shift_part, ("dp", "seq"), scatter_dimension=0, tiled=True),
        lax.psum_scatter(feeder_gain_part, ("dp", "seq"), scatter_dimension=0, tiled=True),
        lax.psum_scatter(feeder_shift_part, ("dp", "seq"), scatter_dimension=0, tiled=True),
    )
    return (
        output,
        input_grad.reshape(windows, steps_dev, width),
        summed[0],
        summed[1],
        summed[2],
        summed[3],
        summed[4],
        summed[5],
        summed[6],
        summed[7],
        summed[8],
        summed[9],
        summed[10],
    )


def solution(mesh):
    in_specs = (
        P("dp", "seq", None),
        P("dp", "seq", None),
        P("dp"),
        P(),
        P(),
    ) + (P(("dp", "seq"), None),) * 7 + (P(("dp", "seq")),) * 4
    out_specs = (P("dp", "seq", None),) * 2 + (P(("dp", "seq"), None),) * 7 + (P(("dp", "seq")),) * 4
    fits = mesh.shape["dp"] == 8 and mesh.shape["seq"] == 4
    return jax.shard_map(
        paired if fits else general, mesh=mesh, in_specs=in_specs, out_specs=out_specs, check_vma=False
    )
```
